32 devices in a mesh: dp: 8 (over z, y), stream: 2 (over x), tensor: 2 (over core).
Axes of the slice: x: 2, y: 2, z: 4, core: 2. Of those that a mesh axis runs over, the one named last changes fastest.
Arguments:
- word_states: bfloat16 [8, 512, 768], P('dp', 'stream'), may hold values from -6 to 6
- entity_shard: int32 [2, 8, 64, 1], P('stream', 'dp'), may hold values from 0 to 15; in each aligned block of 64 rows (0 to 63, 64 to 127, ..., all dimensions but the last counted through in order) at most 8 rows name the same one
- entity_row: int32 [2, 8, 64], P('stream', 'dp'), may hold values from 0 to 4095
- word_segments: int32 [8, 512], P('dp'), may hold values from 0 to 3, never falling along the last dimension, each value on 1 to 256 neighbouring positions
- entity_segments: int32 [8, 128], P('dp'), may hold values from 0 to 3, never falling along the last dimension, each value on 1 to 64 neighbouring positions
- entity_table: bfloat16 [65536, 256], P(('dp', 'stream')), may hold values from -6 to 6
- adam_first: float32 [65536, 256], P(('dp', 'stream')), may hold values from -4 to 4
- adam_second: float32 [65536, 256], P(('dp', 'stream')), may hold values from 0.1 to 1
- w_entity: bfloat16 [256, 768], replicated, may hold values from -0.375 to 0.375
- norm_gain: float32 [3, 768], replicated, may hold values from 0.5 to 1.5
- norm_bias: float32 [3, 768], replicated, may hold values from -3 to 3
- w_query: bfloat16 [4, 768, 768], P(None, None, 'tensor'), may hold values from -0.21875 to 0.21875
- b_query: float32 [4, 768], P(None, 'tensor'), may hold values from -3 to 3
- w_keyval: bfloat16 [2, 768, 768], P(None, None, 'tensor'), may hold values from -0.21875 to 0.21875
- b_value: float32 [768], P('tensor'), may hold values from -3 to 3
- w_out: bfloat16 [768, 768], P('tensor'), may hold values from -2.5 to 2.5
- b_out: float32 [768], replicated, may hold values from -3 to 3
- w_up: bfloat16 [768, 3072], P(None, 'tensor'), may hold values from -0.21875 to 0.21875
- b_up: float32 [3072], P('tensor'), may hold values from -3 to 3
- w_down: bfloat16 [3072, 768], P('tensor'), may hold values from -0.109375 to 0.109375
- b_down: float32 [768], replicated, may hold values from -3 to 3
- cot_words: bfloat16 [8, 512, 768], P('dp', 'stream'), may hold values from -6 to 6
- cot_entities: bfloat16 [8, 128, 768], P('dp', 'stream'), may hold values from -6 to 6
Outputs:
- out_words: bfloat16 [8, 512, 768], P('dp', ('stream', 'tensor'))
- out_entities: bfloat16 [8, 128, 768], P('dp', ('stream', 'tensor'))
- grad_words: float32 [8, 512, 768], P('dp', ('stream', 'tensor'))
- grad_entity: float32 [256, 768], P(None, ('dp', 'stream'))
- grad_gain: float32 [3, 768], P(None, ('dp', 'stream'))
- grad_norm_bias: float32 [3, 768], P(None, ('dp', 'stream'))
- grad_query: float32 [4, 768, 768], P(None, ('dp', 'stream'), 'tensor')
- grad_query_bias: float32 [4, 768], P(None, 'tensor')
- grad_keyval: float32 [2, 768, 768], P(None, ('dp', 'stream'), 'tensor')
- grad_value_bias: float32 [768], P('tensor')
- grad_out: float32 [768, 768], P('tensor', ('dp', 'stream'))
- grad_out_bias: float32 [768], P(('dp', 'stream'))
- grad_up: float32 [768, 3072], P(('dp', 'stream'), 'tensor')
- grad_up_bias: float32 [3072], P('tensor')
- grad_down: float32 [3072, 768], P('tensor', ('dp', 'stream'))
- grad_down_bias: float32 [768], P(('dp', 'stream'))
- table_update: float32 [65536, 256], P(('dp', 'stream'))
- new_first: float32 [65536, 256], P(('dp', 'stream'))
- new_second: float32 [65536, 256], P(('dp', 'stream'))
The draws below stay inside these ranges and needn't reach their ends.
Inputs may be any that keep to these rules, and one draw needn't show every extreme that they name: Among the 64 entities of one device (an aligned block of entity_shard), at most 8 name the same shard, and in some blocks one shard is named by exactly 8. `word_segments`: never falls along a sequence; every one of the 4 documents holds at least one word. `entity_segments`: never falls along a sequence; every one of the 4 documents holds at least one entity.
All inputs are finite; a program needn't handle non-finite values.
Results may differ from the reference program's by a relative error of at most 0.014.
Values may be sent and summed in bfloat16 or wider, within the bound.
A program may use at most 128 MiB of HBM per device.

```python
import math
import jax
import jax.numpy as jnp
import numpy as np
from jax import lax

D = 768
HEADS = 12
HD = 64
FF = 3072
ER = 256
ROWS_OWN = 4096
WORDS = 512
ENTS = 128
DOCS = 4
SEQ_DEV = 1
SEQS = 8
HALF_ENTS = 64
ENT_ROWS = 65536
CAP = 8
N_DP = 8
N_STREAM = 2


def set_ends(entries, rng, least, high):
    shape = entries.shape
    spot = [jax.random.randint(jax.random.fold_in(rng, axis), (), 0, shape[axis]) for axis in range(len(shape))]
    entries = entries.at[tuple(spot)].set(least)
    longest = shape.index(max(shape))
    spot[longest] = (spot[longest] + 1) % shape[longest]
    return entries.at[tuple(spot)].set(high)


def level_of(rng, extent, pieces, least, largest):
    factor_of, own = 1.0, jax.random.fold_in(rng, 6)
    for dim, parts in pieces:
        steps = jnp.exp(jax.random.uniform(jax.random.fold_in(own, dim), (parts,), jnp.float32, least / len(pieces), largest / len(pieces)))
        factor_of = factor_of * jnp.repeat(steps, extent[dim] // parts).reshape([-1 if axis == dim else 1 for axis in range(len(extent))])
    return factor_of


def profile(amount, total, limit, skew):
    weights = [(1 << 20) // math.isqrt(standing ** skew) + 1 for standing in range(2, amount + 1)]
    surplus, holding = total - limit - (amount - 1), [1] * (amount - 1)
    while surplus > 0:
        candidates = [i for i in range(amount - 1) if holding[i] < limit]
        mass, left = sum([weights[i] for i in candidates]), surplus
        for i in candidates:
            extra = min(limit - holding[i], max(1, left * weights[i] // mass), surplus)
            holding[i] = holding[i] + extra
            surplus = surplus - extra
    return np.array([limit] + holding)


def ragged(key, number_of, total, limit, skew):
    if number_of == 2:
        one = jax.random.randint(key, (), max(1, total - limit), min(limit, total - 1) + 1)
        return jnp.stack([one, total - one])
    sizes = jnp.asarray(profile(number_of, total, limit, skew), jnp.int32)
    twos = (number_of - 1) // 2
    giver, taker = sizes[1:1 + 2 * twos:2], sizes[2:2 + 2 * twos:2]
    slack = jnp.minimum(giver - 1, limit - taker)
    shifted = jax.random.randint(jax.random.fold_in(key, 1), (twos,), 0, 1 << 20) % (slack + 1)
    sizes = sizes.at[1:1 + 2 * twos:2].set(giver - shifted).at[2:2 + 2 * twos:2].set(taker + shifted)
    return sizes[jax.random.permutation(jax.random.fold_in(key, 2), number_of)]


def deal_out(rng, own, number, rows, amount, top, most, lean):
    sequence = jax.random.permutation(rng, amount)
    crowded, common = portions_of(amount, rows * top, most, lean, True), portions_of(amount, rows * top, most, lean, False)
    places = jnp.arange(amount)

    def named(sizes, rotation):
        used = int((sizes > 0).sum())
        fixed = max(1, used // 4)
        passed = fixed + (places - fixed + rotation * (used - fixed)) % max(1, amount - fixed)
        return jnp.zeros((amount,), jnp.int32).at[sequence[jnp.where(places < fixed, places, passed)]].set(jnp.asarray(sizes, jnp.int32))

    sizes = jnp.where(number % 4 == 0, named(crowded, number // 4), named(common, number - number // 4 - 1))
    mixed = jax.random.permutation(jax.random.fold_in(own, 3), amount)
    giver, receiver = mixed[0:amount // 2 * 2:2], mixed[1:amount // 2 * 2:2]
    slack = jnp.minimum(sizes[giver] - 1, most - sizes[receiver]) // 2
    slack = jnp.where((giver == sequence[0]) | (receiver == sequence[0]) | (sizes[receiver] == 0), 0, jnp.maximum(slack, 0))
    passed = jax.random.randint(jax.random.fold_in(own, 4), (amount // 2,), 0, 1 << 20) % (slack + 1)
    sizes = sizes.at[giver].add(-passed).at[receiver].add(passed)
    labels = jnp.searchsorted(jnp.cumsum(sizes), jnp.arange(rows * top), side="right").astype(jnp.int32)
    table = labels.reshape(top, rows).T
    table = table[jax.random.permutation(jax.random.fold_in(own, 1), rows)]
    rotation = jax.random.randint(jax.random.fold_in(own, 2), (rows, 1), 0, top)
    return jnp.take_along_axis(table, (jnp.arange(top)[None, :] + rotation) % top, axis=1)


def portions_of(number_of, total, limit, slope, full):
    loads = [(1 << 20) // math.isqrt(standing ** slope) + 1 for standing in range(1, number_of + 1)]
    largest = limit if full else min(limit, max(-(-total // number_of), total * loads[0] // sum(loads)))
    least = 1 if total - largest >= number_of - 1 else 0
    counts, spare = [largest] + [least] * (number_of - 1), total - largest - least * (number_of - 1)
    while spare > 0:
        candidates = [i for i in range(1, number_of) if counts[i] < largest] or [i for i in range(1, number_of) if counts[i] < limit]
        whole, remaining = sum([loads[i] for i in candidates]), spare
        for i in candidates:
            more = min(limit - counts[i], max(1, remaining * loads[i] // whole), spare)
            counts[i] = counts[i] + more
            spare = spare - more
    return np.array(counts)


def scatter_about(own_key, dims, width, bound, split=(), held_as=jnp.bfloat16):
    level = level_of(own_key, dims, split, -0.22, 0.18) if split else 1.0
    array = jax.random.normal(own_key, dims, jnp.float32) * width * level
    return jnp.minimum(jnp.maximum(array, -bound), bound).astype(held_as)


def setup_inputs(seed: int = 0) -> dict:
    key_of = jax.random.split(jax.random.key(seed), 24)
    word_states = scatter_about(key_of[0], (SEQS, WORDS, D), 1.0, 6.0, ((0, 8), (1, 2)))
    entity_shard_keys = jax.random.split(jax.random.fold_in(key_of[1], 1), N_STREAM * SEQS * HALF_ENTS // (SEQ_DEV * HALF_ENTS))
    entity_shard_turns = jax.random.permutation(jax.random.fold_in(key_of[1], 3), N_STREAM * SEQS * HALF_ENTS // (SEQ_DEV * HALF_ENTS))
    entity_shard = jax.vmap(lambda own, number: deal_out(jax.random.fold_in(key_of[1], 2), own, number, SEQ_DEV * HALF_ENTS, N_DP * N_STREAM, 1, CAP, 1))(entity_shard_keys, entity_shard_turns).reshape((N_STREAM, SEQS, HALF_ENTS, 1))
    entity_row = set_ends(jax.random.randint(key_of[2], (N_STREAM, SEQS, HALF_ENTS), 0, ROWS_OWN), jax.random.fold_in(key_of[2], 1), 0, ROWS_OWN - 1).astype(jnp.int32)
    word_segments = jax.vmap(lambda own: jnp.searchsorted(jnp.cumsum(ragged(own, DOCS, WORDS, WORDS // 2, 2)), jnp.arange(WORDS), side="right"))(jax.random.split(key_of[3], SEQS)).reshape((SEQS, WORDS)).astype(jnp.int32)
    entity_segments = jax.vmap(lambda own: jnp.searchsorted(jnp.cumsum(ragged(own, DOCS, ENTS, ENTS // 2, 2)), jnp.arange(ENTS), side="right"))(jax.random.split(key_of[4], SEQS)).reshape((SEQS, ENTS)).astype(jnp.int32)
    entity_table = scatter_about(key_of[5], (ENT_ROWS, ER), 1.0, 6.0, ((0, 16),))
    adam_first = scatter_about(key_of[6], (ENT_ROWS, ER), 0.5, 4.0, ((0, 16),), jnp.float32)
    adam_second = jnp.clip(jnp.exp(math.log(1.0) - 2.3025851 * jax.random.uniform(key_of[7], (ENT_ROWS, ER), jnp.float32) ** level_of(key_of[7], (ENT_ROWS, ER), ((0, 16),), -0.2, 0.2)), 0.1, 1.0)
    w_entity = scatter_about(key_of[8], (ER, D), ER ** -0.5, 0.375)
    norm_gain = jnp.clip(1.0 + 0.1 * jax.random.normal(key_of[9], (3, D), jnp.float32), 0.5, 1.5)
    norm_bias = scatter_about(key_of[10], (3, D), 0.3, 3.0, (), jnp.float32)
    w_query = scatter_about(key_of[11], (4, D, D), D ** -0.5, 0.21875, ((2, 2),))
    b_query = scatter_about(key_of[12], (4, D), 0.3, 3.0, ((1, 2),), jnp.float32)
    w_keyval = scatter_about(key_of[13], (2, D, D), D ** -0.5, 0.21875, ((2, 2),))
    b_value = scatter_about(key_of[14], (D,), 0.3, 3.0, ((0, 2),), jnp.float32)
    w_out = scatter_about(key_of[15], (D, D), (max(D // 128, 4)) ** -0.5, 2.5, ((0, 2),))
    b_out = scatter_about(key_of[16], (D,), 0.3, 3.0, (), jnp.float32)
    w_up = scatter_about(key_of[17], (D, FF), D ** -0.5, 0.21875, ((1, 2),))
    b_up = scatter_about(key_of[18], (FF,), 0.3, 3.0, ((0, 2),), jnp.float32)
    w_down = scatter_about(key_of[19], (FF, D), FF ** -0.5, 0.109375, ((0, 2),))
    b_down = scatter_about(key_of[20], (D,), 0.3, 3.0, (), jnp.float32)
    cot_words = scatter_about(key_of[21], (SEQS, WORDS, D), 1.0, 6.0, ((0, 8), (1, 2)))
    cot_entities = scatter_about(key_of[22], (SEQS, ENTS, D), 1.0, 6.0, ((0, 8), (1, 2)))
    return {"word_states": word_states, "entity_shard": entity_shard, "entity_row": entity_row, "word_segments": word_segments, "entity_segments": entity_segments, "entity_table": entity_table, "adam_first": adam_first, "adam_second": adam_second, "w_entity": w_entity, "norm_gain": norm_gain, "norm_bias": norm_bias, "w_query": w_query, "b_query": b_query, "w_keyval": w_keyval, "b_value": b_value, "w_out": w_out, "b_out": b_out, "w_up": w_up, "b_up": b_up, "w_down": w_down, "b_down": b_down, "cot_words": cot_words, "cot_entities": cot_entities}


norm_eps = 1e-05
score_scale = 0.125
masked_score = -1e+30
beta_one = 0.9
beta_two = 0.99
adam_steps = 10
adam_eps = 1e-08

@jax.custom_vjp
def low(v):
    return lax.optimization_barrier(v.astype(jnp.bfloat16)).astype(jnp.float32)

@jax.custom_vjp
def low_back(v):
    return v

def low_keep(v):
    return (low(v), None)

def low_pass(kept, grad):
    return (grad,)

def back_keep(v):
    return (v, None)

def back_low(kept, grad):
    return (low(grad),)
low.defvjp(low_keep, low_pass)
low_back.defvjp(back_keep, back_low)

def layer_norm(values_in, gain_row, shift_row):
    center = values_in - lax.optimization_barrier(jnp.mean(values_in, -1, keepdims=True))
    spread = lax.optimization_barrier(jnp.mean(center * center, -1, keepdims=True))
    return center * lax.rsqrt(spread + norm_eps) * gain_row + shift_row

def product(matrix_a, matrix_b):
    return jnp.dot(matrix_a, matrix_b, precision=lax.Precision.HIGHEST)

def forward(params, word_rows, looked, word_seg, ent_seg):
    w_entity, norm_gain, norm_bias, w_query, b_query, w_keyval, b_value, w_out, b_out, w_up, b_up, w_down, b_down = params
    count_words = word_rows.shape[0]
    ent_lin = low_back(product(looked, w_entity))
    x_entity = layer_norm(ent_lin, norm_gain[0], norm_bias[0])
    inputs = jnp.concatenate([word_rows, x_entity], 0)
    inputs_low = low(inputs)
    words_low = inputs_low[:count_words]
    ents_low = inputs_low[count_words:]
    to_words = jnp.concatenate([product(words_low, w_query[0]) + b_query[0], product(ents_low, w_query[2]) + b_query[2]], 0)
    to_ents = jnp.concatenate([product(words_low, w_query[1]) + b_query[1], product(ents_low, w_query[3]) + b_query[3]], 0)
    to_words = low_back(low(to_words))
    to_ents = low_back(low(to_ents))
    keys = low_back(low(product(inputs_low, w_keyval[0])))
    values = low_back(low(product(inputs_low, w_keyval[1]) + b_value))
    total_rows = inputs.shape[0]
    score_words = jnp.einsum('qhd,khd->hqk', to_words.reshape(total_rows, HEADS, HD), keys[:count_words].reshape(count_words, HEADS, HD), precision=lax.Precision.HIGHEST) * score_scale
    score_ents = jnp.einsum('qhd,khd->hqk', to_ents.reshape(total_rows, HEADS, HD), keys[count_words:].reshape(total_rows - count_words, HEADS, HD), precision=lax.Precision.HIGHEST) * score_scale
    scores = low_back(jnp.concatenate([score_words, score_ents], 2))
    segment = jnp.concatenate([word_seg, ent_seg], 0)
    allowed = segment[:, None] == segment[None, :]
    scores = jnp.where(allowed[None], scores, masked_score)
    weights = low(jax.nn.softmax(scores, -1))
    heads_out = jnp.einsum('hqk,khd->qhd', weights, values.reshape(total_rows, HEADS, HD), precision=lax.Precision.HIGHEST).reshape(total_rows, HEADS * HD)
    heads_out = low_back(low(heads_out))
    attn_out = low_back(product(heads_out, w_out) + b_out)
    first = layer_norm(inputs + attn_out, norm_gain[1], norm_bias[1])
    up_value = low_back(product(low(first), w_up) + b_up)
    active = low(jax.nn.gelu(up_value, approximate=False))
    ffn_out = low_back(product(active, w_down) + b_down)
    return layer_norm(first + ffn_out, norm_gain[2], norm_bias[2])

def reference(word_states, entity_shard, entity_row, word_segments, entity_segments, entity_table, adam_first, adam_second, w_entity, norm_gain, norm_bias, w_query, b_query, w_keyval, b_value, w_out, b_out, w_up, b_up, w_down, b_down, cot_words, cot_entities):
    shard_ids = jnp.transpose(entity_shard[..., 0], (1, 0, 2)).astype(jnp.int32)
    row_ids = jnp.transpose(entity_row, (1, 0, 2)).astype(jnp.int32)
    entity_ids = (shard_ids * ROWS_OWN + row_ids).reshape(SEQS, ENTS).astype(jnp.int32)
    looked = jnp.take(entity_table, entity_ids, axis=0).astype(jnp.float32)
    params = tuple((item.astype(jnp.float32) for item in (w_entity, norm_gain, norm_bias, w_query, b_query, w_keyval, b_value, w_out, b_out, w_up, b_up, w_down, b_down)))

    def one_sequence(carry, item):
        word_rows, rows_in, word_seg, ent_seg, cot_w, cot_e = item
        outputs, backward = jax.vjp(lambda prm, first_in, second_in: forward(prm, first_in, second_in, word_seg, ent_seg), params, word_rows.astype(jnp.float32), rows_in)
        cotangent = jnp.concatenate([cot_w, cot_e], 0).astype(jnp.float32)
        grad_params, grad_in, grad_rows = backward(cotangent)
        carry = jax.tree.map(jnp.add, carry, grad_params)
        return (carry, (outputs, grad_in, grad_rows))
    zeros = jax.tree.map(jnp.zeros_like, params)
    grads, (outputs, grad_inputs, grad_rows) = lax.scan(one_sequence, zeros, (word_states, looked, word_segments, entity_segments, cot_words, cot_entities))
    out_words = outputs[:, :WORDS].astype(jnp.bfloat16)
    out_entities = outputs[:, WORDS:].astype(jnp.bfloat16)
    flat_ids = entity_ids.reshape(SEQS * ENTS)
    table_grad = jax.ops.segment_sum(grad_rows.reshape(SEQS * ENTS, ER), flat_ids, ENT_ROWS)
    use_count = jax.ops.segment_sum(jnp.ones((SEQS * ENTS,), jnp.float32), flat_ids, ENT_ROWS)
    touched = (use_count > 0.0)[:, None]
    first_next = beta_one * adam_first + (1.0 - beta_one) * table_grad
    second_next = beta_two * adam_second + (1.0 - beta_two) * table_grad * table_grad
    direction = first_next / (1.0 - beta_one ** adam_steps) / (jnp.sqrt(second_next / (1.0 - beta_two ** adam_steps)) + adam_eps)
    table_update = jnp.where(touched, direction, jnp.zeros_like(direction))
    new_first = jnp.where(touched, first_next, adam_first)
    new_second = jnp.where(touched, second_next, adam_second)
    g_entity, g_gain, g_shift, g_query, g_qbias, g_keyval, g_vbias, g_out, g_obias, g_up, g_ubias, g_down, g_dbias = grads
    return (out_words, out_entities, grad_inputs[:, :WORDS], g_entity, g_gain, g_shift, g_query, g_qbias, g_keyval, g_vbias, g_out, g_obias, g_up, g_ubias, g_down, g_dbias, table_update, new_first, new_second)
```

```python
import functools

import jax
import jax.numpy as jnp
from jax import lax
from jax.experimental import pallas as pl
from jax.experimental.pallas import tpu as pltpu
from jax.sharding import PartitionSpec as P

HD = 64
MESH_ID = pl.DeviceIdType.MESH
CHUNK = 384


def greet(peers):
    barrier = pltpu.get_barrier_semaphore()
    for peer in peers:
        pl.semaphore_signal(barrier, inc=1, device_id=peer, device_id_type=MESH_ID)
    pl.semaphore_wait(barrier, len(peers))


def send(source, target, send_sem, recv_sem, peer):
    return pltpu.make_async_remote_copy(
        src_ref=source,
        dst_ref=target,
        send_sem=send_sem,
        recv_sem=recv_sem,
        device_id=peer,
        device_id_type=MESH_ID,
    )


def pair_kernel(part_ref, total_ref, far, send_sem, recv_sem):
    peer = {"tensor": 1 - lax.axis_index("tensor")}
    greet([peer])
    copy = send(part_ref, far, send_sem, recv_sem, peer)
    copy.start()
    copy.wait()
    total_ref[...] = part_ref[...] + far[...]


def pair_total(part):
    return pl.pallas_call(
        pair_kernel,
        out_shape=jax.ShapeDtypeStruct(part.shape, part.dtype),
        in_specs=[pl.BlockSpec(memory_space=pltpu.VMEM)],
        out_specs=pl.BlockSpec(memory_space=pltpu.VMEM),
        scratch_shapes=[
            pltpu.VMEM(part.shape, part.dtype),
            pltpu.SemaphoreType.DMA,
            pltpu.SemaphoreType.DMA,
        ],
        compiler_params=pltpu.CompilerParams(collective_id=0, has_side_effects=True),
    )(part)


def scatter_kernel(grads, out, near1, near2, part1, part2, far3, s1, r1, s2, r2, s3, r3):
    chunks, deep = grads.shape[0], grads.shape[1]
    dp, x = lax.axis_index("dp"), lax.axis_index("stream")
    y, z = lax.rem(dp, 2), dp // 2
    x_peer, y_peer = {"stream": 1 - x}, {"dp": z * 2 + 1 - y}
    z_peers = [{"dp": lax.rem(z + k, deep) * 2 + y} for k in range(1, deep)]
    greet([x_peer, y_peer] + z_peers)

    def first(c, flip):
        if flip:
            return send(grads.at[c, :, 1 - y], near1.at[c], s1.at[c], r1.at[c], y_peer)
        return send(grads.at[c, :, :, 1 - x], near1.at[c], s1.at[c], r1.at[c], x_peer)

    def second(c, flip):
        if flip:
            return send(part1.at[c, :, 1 - x], near2.at[c], s2.at[c], r2.at[c], x_peer)
        return send(part1.at[c, :, 1 - y], near2.at[c], s2.at[c], r2.at[c], y_peer)

    def third(c, k):
        target = lax.rem(z + k, deep)
        return send(
            part2.at[c, target], far3.at[c, k - 1], s3.at[c, k - 1], r3.at[c, k - 1], z_peers[k - 1]
        )

    def add_first(c, flip):
        own = grads.at[c, :, y] if flip else grads.at[c, :, :, x]
        total = own[...].astype(jnp.float32) + near1[c].astype(jnp.float32)
        part1[c] = total.astype(jnp.bfloat16)

    def add_second(c, flip):
        own = part1.at[c, :, x] if flip else part1.at[c, :, y]
        total = own[...].astype(jnp.float32) + near2[c].astype(jnp.float32)
        part2[c] = total.astype(jnp.bfloat16)

    def to_second(c, flip):
        first(c, flip).wait()
        add_first(c, flip)
        second(c, flip).start()

    def to_third(c, flip):
        second(c, flip).wait()
        add_second(c, flip)
        for k in range(1, deep):
            third(c, k).start()

    ahead = 2
    pairs = chunks // 2

    def each(pair, what):
        what(2 * pair, False)
        what(2 * pair + 1, True)

    for pair in range(ahead):
        each(pair, lambda c, flip: first(c, flip).start())

    def body(pair, carry):
        @pl.when(pair < pairs)
        def _():
            each(pair, to_second)

        @pl.when(pair + ahead < pairs)
        def _():
            each(pair + ahead, lambda c, flip: first(c, flip).start())

        @pl.when(pair >= 1)
        def _():
            each(pair - 1, to_third)

        return carry

    lax.fori_loop(0, pairs + 1, body, 0)

    def finish(c, carry):
        for k in range(1, deep):
            third(c, k).wait()
        total = part2[c, z].astype(jnp.float32)
        for k in range(1, deep):
            total = total + far3[c, k - 1].astype(jnp.float32)
        out[c] = total
        return carry

    lax.fori_loop(0, chunks, finish, 0)


def scatter_total(grads):
    chunks, deep, _, _, rows, width = grads.shape
    low = jnp.bfloat16
    return pl.pallas_call(
        scatter_kernel,
        out_shape=jax.ShapeDtypeStruct((chunks, rows, width), jnp.float32),
        in_specs=[pl.BlockSpec(memory_space=pltpu.VMEM)],
        out_specs=pl.BlockSpec(memory_space=pltpu.VMEM),
        scratch_shapes=[
            pltpu.VMEM((chunks, deep, 2, rows, width), low),
            pltpu.VMEM((chunks, deep, rows, width), low),
            pltpu.VMEM((chunks, deep, 2, rows, width), low),
            pltpu.VMEM((chunks, deep, rows, width), low),
            pltpu.VMEM((chunks, deep - 1, rows, width), low),
            pltpu.SemaphoreType.DMA((chunks,)),
            pltpu.SemaphoreType.DMA((chunks,)),
            pltpu.SemaphoreType.DMA((chunks,)),
            pltpu.SemaphoreType.DMA((chunks,)),
            pltpu.SemaphoreType.DMA((chunks, deep - 1)),
            pltpu.SemaphoreType.DMA((chunks, deep - 1)),
        ],
        compiler_params=pltpu.CompilerParams(
            collective_id=1, has_side_effects=True, vmem_limit_bytes=60 * 2**20
        ),
    )(grads)


norm_eps = 1e-05
score_scale = 0.125
masked_score = -1e30
beta_one = 0.9
beta_two = 0.99
adam_steps = 10
adam_eps = 1e-08


def from_partner(block, axis, apart):
    count = lax.axis_size(axis)
    route = []
    for low in range(count):
        high = low | 1 << apart
        if high != low and high < count:
            route += [(low, high), (high, low)]
    return lax.ppermute(block, axis, route)


def layer_norm(values_in, gain_row, shift_row):
    center = values_in - jnp.mean(values_in, -1, keepdims=True)
    spread = jnp.mean(center * center, -1, keepdims=True)
    return center * lax.rsqrt(spread + norm_eps) * gain_row + shift_row


def gelu_exact(values_in):
    return jax.nn.gelu(values_in, approximate=False)


def matmul(matrix_a, matrix_b):
    return jnp.dot(matrix_a, matrix_b, preferred_element_type=jnp.float32)


def tensor_total(values_in):
    if lax.axis_size("tensor") == 2:
        return pair_total(values_in)
    return lax.psum(values_in, "tensor")


def local(
    word_states,
    entity_shard,
    entity_row,
    word_segments,
    entity_segments,
    entity_table,
    adam_first,
    adam_second,
    w_entity,
    norm_gain,
    norm_bias,
    w_query,
    b_query,
    w_keyval,
    b_value,
    w_out,
    b_out,
    w_up,
    b_up,
    w_down,
    b_down,
    cot_words,
    cot_entities,
):
    seq_count, half_words, width = word_states.shape
    half_ents = entity_row.shape[2]
    table_rows, embed_width = entity_table.shape
    local_width = w_query.shape[2]
    local_heads = local_width // HD
    owners = lax.axis_size(("dp", "stream"))
    stream_index = lax.axis_index("stream")
    parts = lax.axis_size("tensor")
    part_index = lax.axis_index("tensor")
    word_part = half_words // parts
    ent_part = half_ents // parts
    ent_count = seq_count * half_ents
    word_count = seq_count * half_words
    local_rows = half_words + half_ents
    share_words = seq_count * word_part
    owner_flat = entity_shard.reshape(ent_count)
    row_flat = entity_row.reshape(ent_count)

    def pick(block, count):
        shaped = block.reshape(seq_count, parts, count // parts, block.shape[-1])
        return lax.dynamic_index_in_dim(shaped, part_index, 1, keepdims=False).reshape(
            seq_count * (count // parts), block.shape[-1]
        )

    def own_share(rows):
        return jnp.concatenate(
            [pick(rows[:word_count], half_words), pick(rows[word_count:], half_ents)], 0
        )

    capacity = 2 * ent_count // owners
    owner_hits = (owner_flat[:, None] == jnp.arange(owners, dtype=jnp.int32)[None, :]).astype(
        jnp.int32
    )
    before = jnp.cumsum(owner_hits, 0) - owner_hits
    ranking = jnp.sum(before * owner_hits, 1)
    slot_index = owner_flat * capacity + ranking
    request = (
        jnp.full((owners * capacity,), -1, jnp.int32)
        .at[slot_index]
        .set(row_flat)
        .reshape(owners, capacity)
    )
    asked_ids = lax.all_to_all(request, ("dp", "stream"), split_axis=0, concat_axis=0, tiled=True)
    present = asked_ids >= 0
    found_rows = jnp.take(entity_table, jnp.clip(asked_ids, 0, table_rows - 1), axis=0)
    found_rows = jnp.where(present[..., None], found_rows, jnp.zeros_like(found_rows))
    found_rows, asked_rows = (found_rows, asked_ids)
    answered = lax.all_to_all(found_rows, ("dp", "stream"), split_axis=0, concat_axis=0, tiled=True)
    looked = answered.reshape(owners * capacity, embed_width)[slot_index]
    ent_lin = matmul(looked, w_entity)
    x_entity, entity_norm_back = jax.vjp(layer_norm, ent_lin, norm_gain[0], norm_bias[0])
    entity_low = x_entity.astype(jnp.bfloat16)
    word_low = word_states.reshape(word_count, width)
    query_words = (
        jnp.einsum("rd,jdc->jrc", word_low, w_query[:2], preferred_element_type=jnp.float32)
        + b_query[:2, None, :]
    ).astype(jnp.bfloat16)
    query_ents = (
        jnp.einsum("rd,jdc->jrc", entity_low, w_query[2:], preferred_element_type=jnp.float32)
        + b_query[2:, None, :]
    ).astype(jnp.bfloat16)
    value_shift = jnp.stack([jnp.zeros_like(b_value), b_value])[:, None, :]
    keyval_words = (
        jnp.einsum("rd,jdc->jrc", word_low, w_keyval, preferred_element_type=jnp.float32)
        + value_shift
    ).astype(jnp.bfloat16)
    keyval_ents = (
        jnp.einsum("rd,jdc->jrc", entity_low, w_keyval, preferred_element_type=jnp.float32)
        + value_shift
    ).astype(jnp.bfloat16)
    far_words, far_ents = from_partner((keyval_words, keyval_ents), "stream", 0)

    def by_heads(block, count):
        return block.reshape(block.shape[0], seq_count, count, local_heads, HD)

    queries = jnp.concatenate(
        [by_heads(query_words, half_words), by_heads(query_ents, half_ents)], 2
    )
    keyval_w = jnp.concatenate(
        [by_heads(keyval_words, half_words), by_heads(far_words, half_words)], 2
    )
    keyval_e = jnp.concatenate([by_heads(keyval_ents, half_ents), by_heads(far_ents, half_ents)], 2)
    own_wseg = lax.dynamic_slice_in_dim(word_segments, stream_index * half_words, half_words, 1)
    far_wseg = lax.dynamic_slice_in_dim(
        word_segments, (1 - stream_index) * half_words, half_words, 1
    )
    own_eseg = lax.dynamic_slice_in_dim(entity_segments, stream_index * half_ents, half_ents, 1)
    far_eseg = lax.dynamic_slice_in_dim(
        entity_segments, (1 - stream_index) * half_ents, half_ents, 1
    )
    query_seg = jnp.concatenate([own_wseg, own_eseg], 1)
    key_wseg = jnp.concatenate([own_wseg, far_wseg], 1)
    key_eseg = jnp.concatenate([own_eseg, far_eseg], 1)
    allow_words = query_seg[:, None, :, None] == key_wseg[:, None, None, :]
    allow_ents = query_seg[:, None, :, None] == key_eseg[:, None, None, :]

    def scores_of():
        raw_words = (
            jnp.einsum(
                "sqhd,skhd->shqk", queries[0], keyval_w[0], preferred_element_type=jnp.float32
            )
            * score_scale
        )
        raw_ents = (
            jnp.einsum(
                "sqhd,skhd->shqk", queries[1], keyval_e[0], preferred_element_type=jnp.float32
            )
            * score_scale
        )
        return (
            jnp.where(allow_words, raw_words, masked_score),
            jnp.where(allow_ents, raw_ents, masked_score),
        )

    score_words, score_ents = scores_of()
    highest = jnp.maximum(
        jnp.max(score_words, -1, keepdims=True), jnp.max(score_ents, -1, keepdims=True)
    )
    totals = jnp.sum(jnp.exp(score_words - highest), -1, keepdims=True) + jnp.sum(
        jnp.exp(score_ents - highest), -1, keepdims=True
    )
    log_total = highest + jnp.log(totals)
    low_words = jnp.exp(score_words - log_total).astype(jnp.bfloat16)
    low_ents = jnp.exp(score_ents - log_total).astype(jnp.bfloat16)
    heads_out = jnp.einsum(
        "shqk,skhd->sqhd", low_words, keyval_w[1], preferred_element_type=jnp.float32
    )
    heads_out = heads_out + jnp.einsum(
        "shqk,skhd->sqhd", low_ents, keyval_e[1], preferred_element_type=jnp.float32
    )
    heads_out = heads_out.astype(jnp.bfloat16).reshape(seq_count, local_rows, local_width)
    heads_dense = jnp.concatenate(
        [
            heads_out[:, :half_words].reshape(word_count, local_width),
            heads_out[:, half_words:].reshape(ent_count, local_width),
        ],
        0,
    )
    resid_in = jnp.concatenate([word_low.astype(jnp.float32), x_entity], 0)
    cotangent = jnp.concatenate(
        [cot_words.reshape(word_count, width), cot_entities.reshape(ent_count, width)], 0
    ).astype(jnp.float32)
    attn_out = tensor_total(matmul(heads_dense, w_out)) + b_out
    first_norm, first_back = jax.vjp(layer_norm, resid_in + attn_out, norm_gain[1], norm_bias[1])
    first_low = first_norm.astype(jnp.bfloat16)
    up_value = matmul(first_low, w_up) + b_up
    active, gelu_back = jax.vjp(gelu_exact, up_value)
    active_low = active.astype(jnp.bfloat16)
    ffn_out = tensor_total(matmul(active_low, w_down)) + b_down
    final_norm, final_back = jax.vjp(layer_norm, first_norm + ffn_out, norm_gain[2], norm_bias[2])
    final_share = own_share(final_norm)
    grad_final, gain_final, shift_final = final_back(cotangent)
    grad_ffn = grad_final.astype(jnp.bfloat16)
    out_words = final_share[:share_words].reshape(seq_count, word_part, width).astype(jnp.bfloat16)
    out_entities = (
        final_share[share_words:].reshape(seq_count, ent_part, width).astype(jnp.bfloat16)
    )
    grad_down = jnp.einsum("rf,rd->fd", active_low, grad_ffn, preferred_element_type=jnp.float32)
    grad_down_bias = jnp.sum(grad_ffn.astype(jnp.float32), 0)
    (grad_pre,) = gelu_back(
        jnp.einsum("rd,fd->rf", grad_ffn, w_down, preferred_element_type=jnp.float32)
    )
    grad_up_low = grad_pre.astype(jnp.bfloat16)
    grad_up = jnp.einsum("rd,rf->df", first_low, grad_up_low, preferred_element_type=jnp.float32)
    grad_up_bias = jnp.sum(grad_up_low.astype(jnp.float32), 0)
    ffn_term = jnp.einsum("rf,df->rd", grad_up_low, w_up, preferred_element_type=jnp.float32)
    grad_first, gain_first, shift_first = first_back(grad_final + tensor_total(ffn_term))
    grad_attn = grad_first.astype(jnp.bfloat16)
    grad_out = jnp.einsum("rc,rd->cd", heads_dense, grad_attn, preferred_element_type=jnp.float32)
    grad_out_bias = jnp.sum(grad_attn.astype(jnp.float32), 0)
    grad_heads = jnp.einsum(
        "rd,cd->rc", grad_attn, w_out, preferred_element_type=jnp.float32
    ).astype(jnp.bfloat16)
    grad_heads = jnp.concatenate(
        [
            grad_heads[:word_count].reshape(seq_count, half_words, local_heads, HD),
            grad_heads[word_count:].reshape(seq_count, half_ents, local_heads, HD),
        ],
        1,
    )
    score_words, score_ents = scores_of()
    prob_words = jnp.exp(score_words - log_total)
    prob_ents = jnp.exp(score_ents - log_total)
    low_words = prob_words.astype(jnp.bfloat16)
    low_ents = prob_ents.astype(jnp.bfloat16)
    dprob_words = jnp.einsum(
        "sqhd,skhd->shqk", grad_heads, keyval_w[1], preferred_element_type=jnp.float32
    )
    dprob_ents = jnp.einsum(
        "sqhd,skhd->shqk", grad_heads, keyval_e[1], preferred_element_type=jnp.float32
    )
    inner_sum = jnp.sum(prob_words * dprob_words, -1, keepdims=True) + jnp.sum(
        prob_ents * dprob_ents, -1, keepdims=True
    )
    dscore_words = (prob_words * (dprob_words - inner_sum)).astype(jnp.bfloat16)
    dscore_ents = (prob_ents * (dprob_ents - inner_sum)).astype(jnp.bfloat16)
    grad_to_words = (
        jnp.einsum("shqk,skhd->sqhd", dscore_words, keyval_w[0], preferred_element_type=jnp.float32)
        * score_scale
    ).astype(jnp.bfloat16)
    grad_to_ents = (
        jnp.einsum("shqk,skhd->sqhd", dscore_ents, keyval_e[0], preferred_element_type=jnp.float32)
        * score_scale
    ).astype(jnp.bfloat16)
    kv_grad_words = jnp.stack(
        [
            jnp.einsum(
                "shqk,sqhd->skhd", dscore_words, queries[0], preferred_element_type=jnp.float32
            )
            * score_scale,
            jnp.einsum(
                "shqk,sqhd->skhd", low_words, grad_heads, preferred_element_type=jnp.float32
            ),
        ]
    )
    kv_grad_ents = jnp.stack(
        [
            jnp.einsum(
                "shqk,sqhd->skhd", dscore_ents, queries[1], preferred_element_type=jnp.float32
            )
            * score_scale,
            jnp.einsum("shqk,sqhd->skhd", low_ents, grad_heads, preferred_element_type=jnp.float32),
        ]
    )
    back_words, back_ents = (
        from_partner(kv_grad_words[:, :, half_words:].astype(jnp.bfloat16), "stream", 0).astype(
            jnp.float32
        ),
        from_partner(kv_grad_ents[:, :, half_ents:].astype(jnp.bfloat16), "stream", 0).astype(
            jnp.float32
        ),
    )
    grad_kv_words = (
        (kv_grad_words[:, :, :half_words] + back_words)
        .reshape(2, word_count, local_width)
        .astype(jnp.bfloat16)
    )
    grad_kv_ents = (
        (kv_grad_ents[:, :, :half_ents] + back_ents)
        .reshape(2, ent_count, local_width)
        .astype(jnp.bfloat16)
    )
    grad_q_words = jnp.stack([grad_to_words[:, :half_words], grad_to_ents[:, :half_words]]).reshape(
        2, word_count, local_width
    )
    grad_q_ents = jnp.stack([grad_to_words[:, half_words:], grad_to_ents[:, half_words:]]).reshape(
        2, ent_count, local_width
    )
    grad_query = jnp.concatenate(
        [
            jnp.einsum("rd,jrc->jdc", word_low, grad_q_words, preferred_element_type=jnp.float32),
            jnp.einsum("rd,jrc->jdc", entity_low, grad_q_ents, preferred_element_type=jnp.float32),
        ],
        0,
    )
    grad_query_bias = jnp.concatenate(
        [jnp.sum(grad_q_words.astype(jnp.float32), 1), jnp.sum(grad_q_ents.astype(jnp.float32), 1)],
        0,
    )
    grad_keyval = jnp.einsum(
        "rd,jrc->jdc", word_low, grad_kv_words, preferred_element_type=jnp.float32
    ) + jnp.einsum("rd,jrc->jdc", entity_low, grad_kv_ents, preferred_element_type=jnp.float32)
    grad_value_bias = jnp.sum(grad_kv_words[1].astype(jnp.float32), 0) + jnp.sum(
        grad_kv_ents[1].astype(jnp.float32), 0
    )
    input_words = jnp.einsum(
        "jrc,jdc->rd", grad_q_words, w_query[:2], preferred_element_type=jnp.float32
    ) + jnp.einsum("jrc,jdc->rd", grad_kv_words, w_keyval, preferred_element_type=jnp.float32)
    input_ents = jnp.einsum(
        "jrc,jdc->rd", grad_q_ents, w_query[2:], preferred_element_type=jnp.float32
    ) + jnp.einsum("jrc,jdc->rd", grad_kv_ents, w_keyval, preferred_element_type=jnp.float32)
    input_term = jnp.concatenate([input_words, input_ents], 0)
    grad_input = grad_first + tensor_total(input_term)
    grad_share = own_share(grad_input)
    grad_lin, gain_entity, shift_entity = entity_norm_back(grad_input[word_count:])
    grad_lin_low = grad_lin.astype(jnp.bfloat16)
    gain_grads = jnp.stack([gain_entity, gain_first, gain_final])
    shift_grads = jnp.stack([shift_entity, shift_first, shift_final])
    grad_words = grad_share[:share_words].reshape(seq_count, word_part, width)
    grad_entity = jnp.einsum("re,rd->ed", looked, grad_lin_low, preferred_element_type=jnp.float32)
    grad_looked = jnp.einsum(
        "rd,ed->re", grad_lin_low, w_entity, preferred_element_type=jnp.float32
    )
    outgoing = (
        jnp.zeros((owners * capacity, embed_width), jnp.float32)
        .at[slot_index]
        .set(grad_looked)
        .reshape(owners, capacity, embed_width)
    )
    incoming = lax.all_to_all(
        outgoing.astype(jnp.bfloat16), ("dp", "stream"), split_axis=0, concat_axis=0, tiled=True
    ).astype(outgoing.dtype)
    target = jnp.where(asked_rows >= 0, asked_rows, table_rows).reshape(-1)
    gradient_sum = (
        jnp.zeros((table_rows, embed_width), jnp.float32)
        .at[target]
        .add(incoming.reshape(-1, embed_width), mode="drop")
    )
    use_count = jnp.zeros((table_rows,), jnp.float32).at[target].add(1.0, mode="drop")
    touched = (use_count > 0.0)[:, None]
    first_next = beta_one * adam_first + (1.0 - beta_one) * gradient_sum
    second_next = beta_two * adam_second + (1.0 - beta_two) * gradient_sum * gradient_sum
    direction = (
        first_next
        / (1.0 - beta_one**adam_steps)
        / (jnp.sqrt(second_next / (1.0 - beta_two**adam_steps)) + adam_eps)
    )
    table_update = jnp.where(touched, direction, jnp.zeros_like(direction))
    new_first = jnp.where(touched, first_next, adam_first)
    new_second = jnp.where(touched, second_next, adam_second)
    groups = ("dp", "stream")
    share = width // owners
    if parts == 2 and lax.axis_size("stream") == 2 and share % 16 == 0 and local_width == CHUNK:
        pieces = (
            [block.T for block in jnp.split(grad_down, grad_down.shape[0] // CHUNK, 0)]
            + jnp.split(grad_up, grad_up.shape[1] // CHUNK, 1)
            + [grad_out.T, *grad_query, *grad_keyval]
            + [jnp.pad(grad_entity.T, ((0, 0), (0, CHUNK - embed_width)))]
        )
        stacked = jnp.stack([piece.astype(jnp.bfloat16) for piece in pieces])
        reduced = scatter_total(
            stacked.reshape(len(pieces), owners // 4, 2, 2, share, CHUNK)
        )
        downs = grad_down.shape[0] // CHUNK
        ups = grad_up.shape[1] // CHUNK
        red_down = jnp.transpose(reduced[:downs], (0, 2, 1)).reshape(grad_down.shape[0], share)
        red_up = jnp.transpose(reduced[downs : downs + ups], (1, 0, 2)).reshape(share, -1)
        base = downs + ups
        red_out = reduced[base].T
        red_query = reduced[base + 1 : base + 5]
        red_keyval = reduced[base + 5 : base + 7]
        red_entity = reduced[base + 7, :, :embed_width].T
    else:
        red_entity, red_query, red_keyval, red_out, red_up, red_down = (
            lax.psum_scatter(grad_entity, groups, scatter_dimension=1, tiled=True),
            lax.psum_scatter(grad_query, groups, scatter_dimension=1, tiled=True),
            lax.psum_scatter(grad_keyval, groups, scatter_dimension=1, tiled=True),
            lax.psum_scatter(grad_out, groups, scatter_dimension=1, tiled=True),
            lax.psum_scatter(grad_up, groups, scatter_dimension=0, tiled=True),
            lax.psum_scatter(grad_down, groups, scatter_dimension=1, tiled=True),
        )
    across = jnp.concatenate([gain_grads, shift_grads, grad_out_bias[None], grad_down_bias[None]], 0)
    small = [across, grad_query_bias, grad_value_bias, grad_up_bias]
    flat = lax.psum(jnp.concatenate([item.reshape(-1) for item in small]), groups)
    totals = []
    for item in small:
        totals.append(flat[: item.size].reshape(item.shape))
        flat = flat[item.size :]
    across, red_query_bias, red_value_bias, red_up_bias = totals
    own = lax.axis_index(groups) * share
    across = lax.dynamic_slice_in_dim(across, own, share, 1)
    red_gain, red_shift, red_out_bias, red_down_bias = across[:3], across[3:6], across[6], across[7]
    return (
        out_words,
        out_entities,
        grad_words,
        red_entity,
        red_gain,
        red_shift,
        red_query,
        red_query_bias,
        red_keyval,
        red_value_bias,
        red_out,
        red_out_bias,
        red_up,
        red_up_bias,
        red_down,
        red_down_bias,
        table_update,
        new_first,
        new_second,
    )


def solution(mesh):
    placed = (
        P("dp", "stream", None),
        P("stream", "dp", None, None),
        P("stream", "dp", None),
        P("dp", None),
        P("dp", None),
        P(("dp", "stream"), None),
        P(("dp", "stream"), None),
        P(("dp", "stream"), None),
        P(),
        P(),
        P(),
        P(None, None, "tensor"),
        P(None, "tensor"),
        P(None, None, "tensor"),
        P("tensor"),
        P("tensor", None),
        P(),
        P(None, "tensor"),
        P("tensor"),
        P("tensor", None),
        P(),
        P("dp", "stream", None),
        P("dp", "stream", None),
    )
    return jax.shard_map(
        local,
        mesh=mesh,
        in_specs=placed,
        out_specs=(
            P("dp", ("stream", "tensor"), None),
            P("dp", ("stream", "tensor"), None),
            P("dp", ("stream", "tensor"), None),
            P(None, ("dp", "stream")),
            P(None, ("dp", "stream")),
            P(None, ("dp", "stream")),
            P(None, ("dp", "stream"), "tensor"),
            P(None, "tensor"),
            P(None, ("dp", "stream"), "tensor"),
            P("tensor"),
            P("tensor", ("dp", "stream")),
            P(("dp", "stream")),
            P(("dp", "stream"), "tensor"),
            P("tensor"),
            P("tensor", ("dp", "stream")),
            P(("dp", "stream")),
            P(("dp", "stream"), None),
            P(("dp", "stream"), None),
            P(("dp", "stream"), None),
        ),
        check_vma=False,
    )
```

```python
import functools
import math
import types

import jax
import jax.numpy as jnp
from jax import lax
from jax.experimental import pallas as pl
from jax.experimental.pallas import tpu as pltpu
from jax.sharding import PartitionSpec as P

HD = 64
MESH_ID = pl.DeviceIdType.MESH


norm_eps = 1e-05
score_scale = 0.125
masked_score = -1e30
beta_one = 0.9
beta_two = 0.99
adam_steps = 10
adam_eps = 1e-08


def from_partner(block, axis, apart):
    count = lax.axis_size(axis)
    route = []
    for low in range(count):
        high = low | 1 << apart
        if high != low and high < count:
            route += [(low, high), (high, low)]
    return lax.ppermute(block, axis, route)


def layer_norm(values_in, gain_row, shift_row):
    center = values_in - jnp.mean(values_in, -1, keepdims=True)
    spread = jnp.mean(center * center, -1, keepdims=True)
    return center * lax.rsqrt(spread + norm_eps) * gain_row + shift_row


def gelu_exact(values_in):
    return jax.nn.gelu(values_in, approximate=False)


def matmul(matrix_a, matrix_b):
    return jnp.dot(matrix_a, matrix_b, preferred_element_type=jnp.float32)


def tensor_total(values_in):
    return lax.psum(values_in, "tensor")


def send(source, target, send_sem, recv_sem, peer):
    return pltpu.make_async_remote_copy(
        src_ref=source,
        dst_ref=target,
        send_sem=send_sem,
        recv_sem=recv_sem,
        device_id=peer,
        device_id_type=MESH_ID,
    )


def row_sum(block):
    return jnp.sum(block, 0, keepdims=True)


def lane_mean(block):
    return jnp.mean(block, -1, keepdims=True)


def dot_nn(left, right):
    return jnp.dot(left, right, preferred_element_type=jnp.float32)


def dot_nt(left, right):
    return lax.dot_general(
        left, right, (((1,), (1,)), ((), ())), preferred_element_type=jnp.float32
    )


def dot_tn(left, right):
    return lax.dot_general(
        left, right, (((0,), (0,)), ((), ())), preferred_element_type=jnp.float32
    )


def normalize(rows):
    center = rows - lane_mean(rows)
    scale = lax.rsqrt(lane_mean(center * center) + norm_eps)
    return center * scale, scale


def normalize_back(grad, normed, scale, gain):
    inner = grad * gain
    return scale * (inner - lane_mean(inner) - normed * lane_mean(inner * normed))


def aligned(index, step):
    return pl.ds(pl.multiple_of(index * step, step), step)


def layer_kernel(names, flips, schedule, *refs):
    r = types.SimpleNamespace(**dict(zip(names, refs, strict=True)))
    low, full = jnp.bfloat16, jnp.float32
    dp, x, t = lax.axis_index("dp"), lax.axis_index("stream"), lax.axis_index("tensor")
    y, z = lax.rem(dp, 2), dp // 2
    deep = lax.axis_size("dp") // 2
    owners = 4 * deep
    half_words, width = r.words.shape
    half_ents = r.shard.shape[1]
    rows, words = half_words + half_ents, 2 * half_words
    everyone = 2 * rows
    capacity = r.ask.shape[1]
    slots = owners * capacity
    heads = r.prob.shape[0]
    share = width // owners
    side = heads * HD
    hidden = r.w_up.shape[1]
    block = half_ents
    blocks = rows // block
    word_blocks = half_words // block
    wide = 256

    core, x_peer, y_peer = {"tensor": 1 - t}, {"stream": 1 - x}, {"dp": z * 2 + 1 - y}
    z_peers = [{"dp": lax.rem(z + k, deep) * 2 + y} for k in range(1, deep)]
    flat = dp * 2 + x
    others = []
    for k in range(1, owners):
        other = lax.rem(flat + k, owners)
        others.append((other, {"dp": other // 2, "stream": lax.rem(other, 2)}))

    barrier = pltpu.get_barrier_semaphore()
    for peer in [core] + [peer for _, peer in others]:
        pl.semaphore_signal(barrier, inc=1, device_id=peer, device_id_type=MESH_ID)

    loads = {}

    def load(source, target):
        loads[id(target)] = pltpu.make_async_copy(source, target, r.load_s.at[len(loads)])
        loads[id(target)].start()

    def loaded(target):
        loads.pop(id(target)).wait()

    load(r.hbm_query, r.w_query)
    load(r.hbm_keyval, r.w_keyval)
    load(r.hbm_table, r.table)
    load(r.hbm_entity, r.w_entity)
    load(r.hbm_out, r.w_out)
    load(r.hbm_up, r.w_up)
    load(r.hbm_down, r.w_down)

    shard_row = r.shard[...]
    shard_all = jnp.broadcast_to(shard_row.astype(full), (half_ents, half_ents)).T
    shard_all = shard_all.astype(jnp.int32)
    shard_col = shard_all[:, 0:1]
    below = lax.broadcasted_iota(jnp.int32, (half_ents, half_ents), 0)
    beside = lax.broadcasted_iota(jnp.int32, (half_ents, half_ents), 1)
    same = shard_all == shard_row
    rank_row = row_sum(jnp.where(same & (below < beside), 1.0, 0.0)).astype(jnp.int32)
    rank_col = jnp.sum(jnp.where(same & (beside < below), 1.0, 0.0), 1, keepdims=True)
    rank_col = rank_col.astype(jnp.int32)
    slot_row = shard_row * capacity + rank_row
    in_slot = lax.broadcasted_iota(jnp.int32, (slots, half_ents), 0) == slot_row
    wanted = jnp.sum(
        jnp.where(in_slot, (r.row[...] + 1).astype(full), 0.0), 1, keepdims=True
    )
    wanted = wanted.astype(jnp.int32) - 1
    r.ask[...] = jnp.broadcast_to(wanted, (slots, 128)).reshape(owners, capacity, 128)
    r.outbox[...] = jnp.where(in_slot, 1.0, 0.0).astype(low)
    answer_col = shard_col * (2 * capacity) + x * capacity + rank_col
    answer_lane = lax.broadcasted_iota(jnp.int32, (half_ents, 2 * slots), 1)
    r.select[aligned(x, half_ents), :] = jnp.where(answer_lane == answer_col, 1.0, 0.0).astype(low)
    r.asked[flat] = r.ask[flat]
    r.x_all[aligned(x, half_words), :] = r.words[...]
    r.x_own[0:half_words, :] = r.words[...].astype(full)
    r.cotangent[0:half_words, :] = r.cot_words[...]
    r.cotangent[half_words:rows, :] = r.cot_ents[...]
    r.vec[0] = jnp.zeros(r.vec.shape[1:], full)

    pl.semaphore_wait(barrier, owners)

    def ask_copy(k):
        other, peer = others[k]
        return send(r.ask.at[other], r.asked.at[flat], r.ask_s.at[k], r.ask_r.at[k], peer)

    def answer_copy(k):
        other, peer = others[k]
        return send(
            r.found.at[other // 2], r.answer.at[flat], r.answer_s.at[k], r.answer_r.at[k], peer
        )

    def slope_copy(k):
        other, peer = others[k]
        return send(r.slope.at[other], r.slopes.at[flat], r.slope_s.at[k], r.slope_r.at[k], peer)

    for k in range(owners - 1):
        ask_copy(k).start()
    my_select = r.select.at[aligned(x, half_ents), :]
    select_copy = send(my_select, my_select, r.pair_s.at[0], r.pair_r.at[0], x_peer)
    select_copy.start()
    my_words = r.x_all.at[aligned(x, half_words), :]
    words_copy = send(r.words, my_words, r.pair_s.at[1], r.pair_r.at[1], x_peer)
    words_copy.start()

    loaded(r.w_query)
    loaded(r.w_keyval)

    def gather_columns(which):
        for h in range(heads):
            own = slice(which * side + h * HD, which * side + (h + 1) * HD)
            for place, words_part, ents_part in (
                (0, r.w_query[0, :, own], r.w_query[2, :, own]),
                (1, r.w_query[1, :, own], r.w_query[3, :, own]),
                (2, r.w_keyval[0, :, own], None),
                (3, r.w_keyval[1, :, own], None),
            ):
                lanes = slice((4 * h + place) * HD, (4 * h + place + 1) * HD)
                r.cat_words[:, lanes] = words_part
                r.cat_ents[:, lanes] = words_part if ents_part is None else ents_part
            zero = jnp.zeros((1, HD), full)
            value = r.b_value[...].reshape(1, -1)[:, own]
            query = r.b_query[:, own]
            lanes = slice(4 * h * HD, 4 * (h + 1) * HD)
            r.bias_words[:, lanes] = jnp.concatenate([query[0:1], query[1:2], zero, value], 1)
            r.bias_ents[:, lanes] = jnp.concatenate([query[2:3], query[3:4], zero, value], 1)

    for which in range(2):

        @pl.when(x == which)
        def _(which=which):
            gather_columns(which)

    def project(start, count, weight, bias):
        def body(h, carry):
            lanes = aligned(h, 4 * HD)
            total = dot_nn(r.x_all[pl.ds(start, count), :], weight[:, lanes]) + bias[:, lanes]
            r.qkv[pl.ds(start, count), lanes] = total.astype(low)
            return carry

        lax.fori_loop(0, heads, body, 0)

    project(pl.multiple_of(x * half_words, half_words), half_words, r.cat_words, r.bias_words)

    segments = jnp.concatenate([r.word_seg[...], r.ent_seg[...]], 1)
    for i in range(everyone // 128):
        own_seg = jnp.broadcast_to(segments[:, i * 128 : (i + 1) * 128].astype(full), (128, 128)).T
        equal = own_seg[:, 0:1].astype(jnp.int32) == segments
        r.mask[i * 128 : (i + 1) * 128, :] = jnp.where(equal, 0.0, masked_score).astype(low)

    for k in range(owners - 1):
        ask_copy(k).wait()
    ids = r.asked[...].reshape(slots, 128)
    lane = lax.broadcasted_iota(jnp.int32, (slots, 128), 1)

    def pick_body(j, carry):
        r.pick[:, aligned(j, 128)] = jnp.where(ids == lane + 128 * j, 1.0, 0.0).astype(low)
        return carry

    lax.fori_loop(0, r.table.shape[0] // 128, pick_body, 0)
    loaded(r.table)
    found = dot_nn(r.pick[...], r.table[...]).astype(low)
    r.found[...] = found.reshape(r.found.shape)
    r.answer[flat] = r.found[dp]
    for k in range(owners - 1):
        answer_copy(k).start()

    words_copy.wait()
    project(pl.multiple_of((1 - x) * half_words, half_words), half_words, r.cat_words, r.bias_words)
    r.words_t[...] = r.x_all[0:words, :].T

    select_copy.wait()
    for k in range(owners - 1):
        answer_copy(k).wait()
    looked = dot_nn(r.select[...], r.answer[...].reshape(2 * slots, r.table.shape[1])).astype(low)
    r.looked[...] = looked
    loaded(r.w_entity)
    ent_lin = dot_nn(looked, r.w_entity[...])
    normed, _ = normalize(ent_lin)
    x_entity = normed * r.gain[0:1, :] + r.shift[0:1, :]
    r.ent_lin[...] = ent_lin
    r.x_ent[...] = x_entity
    r.x_all[words:everyone, :] = x_entity.astype(low)
    r.x_own[half_words:rows, :] = r.x_ent[aligned(x, half_ents), :]
    project(words, 2 * half_ents, r.cat_ents, r.bias_ents)
    r.ents_t[...] = r.x_all[words:everyone, :].T
    for h in range(heads):
        r.key[h] = r.qkv[:, h * 4 * HD + 2 * HD : h * 4 * HD + 3 * HD]
        r.value[h] = r.qkv[:, h * 4 * HD + 3 * HD : h * 4 * HD + 4 * HD]

    def row_start(i, which):
        start = jnp.where(
            i < word_blocks, which * half_words + i * block, words + which * half_ents
        )
        return pl.ds(pl.multiple_of(start, block), block)

    def attend(which, target):
        def body(i, carry):
            here = row_start(i, which)
            outs = []
            for h in range(heads):
                query = r.qkv[here, h * 4 * HD : h * 4 * HD + 2 * HD]
                score = jnp.concatenate(
                    [
                        dot_nt(query[:, :HD], r.key[h, 0:words, :]),
                        dot_nt(query[:, HD:], r.key[h, words:everyone, :]),
                    ],
                    1,
                )
                score = score * score_scale + r.mask[here, :].astype(full)
                power = jnp.exp(score - jnp.max(score, 1, keepdims=True))
                prob = power / jnp.sum(power, 1, keepdims=True)
                r.prob[h, here, :] = prob
                outs.append(dot_nn(prob.astype(low), r.value[h]))
            target[aligned(i, block), :] = jnp.concatenate(outs, 1).astype(low)
            return carry

        lax.fori_loop(0, blocks, body, 0)

    attend(1 - x, r.heads_far)
    heads_copy = send(r.heads_far, r.heads_in, r.pair_s.at[2], r.pair_r.at[2], x_peer)
    heads_copy.start()
    attend(x, r.heads_near)
    heads_copy.wait()

    @pl.when(x == 0)
    def _():
        r.heads_all[:, 0:side] = r.heads_near[...]
        r.heads_all[:, side:] = r.heads_in[...]

    @pl.when(x == 1)
    def _():
        r.heads_all[:, 0:side] = r.heads_in[...]
        r.heads_all[:, side:] = r.heads_near[...]

    def swap(which, turn, first, count):
        part = pl.ds(first, count)
        return send(
            r.mail_out.at[which, part], r.mail_in.at[which, part], r.swap_s.at[turn],
            r.swap_r.at[turn], core,
        )

    def columns(count, fill):
        def body(j, carry):
            fill(aligned(j, wide), j)
            return carry

        lax.fori_loop(0, count // wide, body, 0)

    def fill_attn(lanes, _):
        r.mail_out[0, 0:rows, lanes] = dot_nn(r.heads_all[...], r.w_out[:, lanes])

    loaded(r.w_out)
    columns(width, fill_attn)
    attn_swap = swap(0, 0, 0, rows)
    attn_swap.start()
    attn_swap.wait()

    def over_rows(body):
        def step(i, carry):
            body(aligned(i, block))
            return carry

        lax.fori_loop(0, blocks, step, 0)

    def first_norm(here):
        attn = r.mail_out[0, here, :] + r.mail_in[0, here, :] + r.b_out[...].reshape(1, -1)
        normed, scale = normalize(r.x_own[here, :] + attn)
        r.normed[here, :] = normed
        r.scale[here, :] = jnp.broadcast_to(scale, (block, 128))
        r.first[here, :] = (normed * r.gain[1:2, :] + r.shift[1:2, :]).astype(low)

    over_rows(first_norm)

    def fill_up(lanes, _):
        up = dot_nn(r.first[...], r.w_up[:, lanes]) + r.b_up[lanes].reshape(1, -1)
        chance = 0.5 + 0.5 * lax.erf(up * (0.5**0.5))
        r.act[:, lanes] = (up * chance).astype(low)
        r.slope_up[:, lanes] = chance + up * (jnp.exp(-0.5 * up * up) * (0.5 / math.pi) ** 0.5)

    loaded(r.w_up)
    columns(hidden, fill_up)

    def fill_down(lanes, _):
        r.mail_out[1, 0:rows, lanes] = dot_nn(r.act[...], r.w_down[:, lanes])

    loaded(r.w_down)
    columns(width, fill_down)
    ffn_swap = swap(1, 1, 0, rows)
    ffn_swap.start()
    r.first_t[...] = r.first[...].T
    ffn_swap.wait()

    vec = r.vec.at[0]

    def second_norm(here):
        ffn = r.mail_out[1, here, :] + r.mail_in[1, here, :] + r.b_down[...].reshape(1, -1)
        entering = r.normed[here, :] * r.gain[1:2, :] + r.shift[1:2, :]
        normed, scale = normalize(entering + ffn)
        r.final[here, :] = (normed * r.gain[2:3, :] + r.shift[2:3, :]).astype(low)
        grad = r.cotangent[here, :].astype(full)
        vec[2:3, :] += row_sum(grad * normed)
        vec[5:6, :] += row_sum(grad)
        back = normalize_back(grad, normed, scale, r.gain[2:3, :])
        r.grad_second[here, :] = back
        r.grad_low[here, :] = back.astype(low)
        vec[7:8, :] += row_sum(back.astype(low).astype(full))

    over_rows(second_norm)

    def halves(source, c, axis_flip):
        if axis_flip:
            return source.at[c, :, 1 - y], source.at[c, :, y]
        return source.at[c, :, :, 1 - x], source.at[c, :, :, x]

    def stage_one(kit, c, flip):
        away, _ = halves(kit.grads, c, flip)
        return send(away, kit.near.at[c], kit.s1.at[c], kit.r1.at[c], y_peer if flip else x_peer)

    def stage_two(kit, c, flip):
        away = kit.near.at[c, :, 1 - x] if flip else kit.near.at[c, :, 1 - y]
        return send(away, kit.next.at[c], kit.s2.at[c], kit.r2.at[c], x_peer if flip else y_peer)

    def stage_three(kit, c, k):
        return send(
            kit.next.at[c, lax.rem(z + k, deep)],
            kit.far.at[c, k - 1],
            kit.s3.at[c, k - 1],
            kit.r3.at[c, k - 1],
            z_peers[k - 1],
        )

    def to_two(kit, c, flip):
        stage_one(kit, c, flip).wait()
        _, own = halves(kit.grads, c, flip)

        def body(i, carry):
            total = own[i].astype(full) + kit.near[c, i].astype(full)
            kit.near[c, i] = total.astype(low)
            return carry

        lax.fori_loop(0, deep, body, 0)
        stage_two(kit, c, flip).start()

    def to_three(kit, c, flip):
        stage_two(kit, c, flip).wait()
        own = kit.near.at[c, :, x] if flip else kit.near.at[c, :, y]

        def body(i, carry):
            total = own[i].astype(full) + kit.next[c, i].astype(full)
            kit.next[c, i] = total.astype(low)
            return carry

        lax.fori_loop(0, deep, body, 0)
        for k in range(1, deep):
            stage_three(kit, c, k).start()

    def finish(kit, c):
        for k in range(1, deep):
            stage_three(kit, c, k).wait()
        total = kit.next[c, z].astype(full)
        for k in range(1, deep):
            total = total + kit.far[c, k - 1].astype(full)
        kit.out[c] = total

    kit_a = types.SimpleNamespace(
        grads=r.grads, near=r.near, next=r.next, far=r.far, out=r.out_a,
        s1=r.a_s1, r1=r.a_r1, s2=r.a_s2, r2=r.a_r2, s3=r.a_s3, r3=r.a_r3,
    )
    kit_e = types.SimpleNamespace(
        grads=r.e_grads, near=r.e_near, next=r.e_next, far=r.e_far, out=r.e_sum,
        s1=r.e_s1, r1=r.e_r1, s2=r.e_s2, r2=r.e_r2, s3=r.e_s3, r3=r.e_r3,
    )

    def head_one(h):
        return send(r.q_grads.at[h, :, 1 - y], r.q_near.at[h], r.q_s1.at[h], r.q_r1.at[h], y_peer)

    def head_two(h, k):
        return send(
            r.q_near.at[h, lax.rem(z + k, deep)],
            r.q_far.at[h, k - 1],
            r.q_s2.at[h, k - 1],
            r.q_r2.at[h, k - 1],
            z_peers[k - 1],
        )

    def head_three(h):
        return send(r.q_sum.at[h, 1 - x], r.q_in.at[h], r.q_s3.at[h], r.q_r3.at[h], x_peer)

    def head_to_two(h):
        head_one(h).wait()

        def body(i, carry):
            total = r.q_grads[h, i, y].astype(full) + r.q_near[h, i].astype(full)
            r.q_near[h, i] = total.astype(low)
            return carry

        lax.fori_loop(0, deep, body, 0)
        for k in range(1, deep):
            head_two(h, k).start()

    def head_to_three(h):
        for k in range(1, deep):
            head_two(h, k).wait()
        total = r.q_near[h, z].astype(full)
        for k in range(1, deep):
            total = total + r.q_far[h, k - 1].astype(full)
        r.q_sum[h] = total
        head_three(h).start()
        r.out_q[h, x] = r.q_sum[h, x]

    def head_finish(h):
        head_three(h).wait()
        r.out_q[h, 1 - x] = r.q_in[h]

    band = 4 * share
    chunk = r.grads.shape[5]

    def make_grad(c, left_t, right, lanes):
        def body(i, carry):
            part = dot_nn(left_t[aligned(i, band), :], right[:, lanes])
            r.grads[c, i] = part.astype(low).reshape(2, 2, share, chunk)
            return carry

        lax.fori_loop(0, deep, body, 0)
        stage_one(kit_a, c, flips[c]).start()

    downs = hidden // chunk
    r.grad_t[...] = r.grad_low[...].T
    for c in range(downs):
        make_grad(c, r.grad_t, r.act, slice(c * chunk, (c + 1) * chunk))

    def fill_dup(lanes, j):
        grad_act = dot_nt(r.grad_low[...], r.w_down[lanes, :])
        grad_up = (grad_act * r.slope_up[:, lanes]).astype(low)
        r.grad_up[:, lanes] = grad_up
        vec[pl.ds(8 + j // (width // wide), 1), aligned(lax.rem(j, width // wide), wide)] = row_sum(
            grad_up.astype(full)
        )

    columns(hidden, fill_dup)

    def fill_back(lanes, _):
        r.mail_out[0, 0:rows, lanes] = dot_nt(r.grad_up[...], r.w_up[lanes, :])

    columns(width, fill_back)
    back_swap = swap(0, 2, 0, rows)
    back_swap.start()
    r.out_words[...] = r.final[pl.ds(pl.multiple_of(t * (half_words // 2), half_words // 2), half_words // 2), :]
    r.out_ents[...] = r.final[
        pl.ds(pl.multiple_of(half_words + t * (half_ents // 2), half_ents // 2), half_ents // 2), :
    ]
    for c in range(downs):
        make_grad(downs + c, r.first_t, r.grad_up, slice(c * chunk, (c + 1) * chunk))
    back_swap.wait()

    def first_back(here):
        grad = r.grad_second[here, :] + r.mail_out[0, here, :] + r.mail_in[0, here, :]
        normed = r.normed[here, :]
        vec[1:2, :] += row_sum(grad * normed)
        vec[4:5, :] += row_sum(grad)
        back = normalize_back(grad, normed, r.scale[here, 0:1], r.gain[1:2, :])
        r.grad_first[here, :] = back
        r.grad_low[here, :] = back.astype(low)
        vec[6:7, :] += row_sum(back.astype(low).astype(full))

    over_rows(first_back)
    near_rows = aligned(x, side)
    far_rows = aligned(1 - x, side)
    r.back_far[...] = dot_nt(r.grad_low[...], r.w_out[far_rows, :]).astype(low)
    mine = [(aligned(x, half_words), 0, half_words)]
    mine.append((pl.ds(pl.multiple_of(words + x * half_ents, half_ents), half_ents), half_words, half_ents))
    back_copies = [
        send(
            r.back_far.at[pl.ds(first, count), :], r.back_heads.at[place, :],
            r.pair_s.at[3 + n], r.pair_r.at[3 + n], x_peer,
        )
        for n, (place, first, count) in enumerate(mine)
    ]
    for copy in back_copies:
        copy.start()
    near = dot_nt(r.grad_low[...], r.w_out[near_rows, :]).astype(low)
    for place, first, count in mine:
        r.back_heads[place, :] = near[first : first + count, :]
    r.grad_t[...] = r.grad_low[...].T
    outs = 2 * downs
    make_grad(outs, r.grad_t, r.heads_all, slice(0, chunk))

    def ticks(events):
        for kind, c in events:
            if kind == "f":
                to_two(kit_a, c, flips[c])
            if kind == "s":
                to_three(kit_a, c, flips[c])
            if kind == "q":
                head_to_two(c)
            if kind == "r":
                head_to_three(c)

    ticks(schedule[0])
    for copy in back_copies:
        copy.wait()

    pair = 2 * HD
    for h in range(heads):
        base = h * 4 * HD

        def score_back(i, carry):
            here = aligned(i, block)
            prob = r.prob[h, here, :]
            grad_prob = dot_nt(r.back_heads[here, h * HD : (h + 1) * HD], r.value[h])
            inner = jnp.sum(prob * grad_prob, 1, keepdims=True)
            grad_score = (prob * (grad_prob - inner)).astype(low)
            r.grad_score[here, :] = grad_score
            r.prob_low[here, :] = prob.astype(low)
            queries = jnp.concatenate(
                [
                    dot_nn(grad_score[:, :words], r.key[h, 0:words, :]),
                    dot_nn(grad_score[:, words:], r.key[h, words:everyone, :]),
                ],
                1,
            )
            r.grad_qkv[here, base : base + pair] = (queries * score_scale).astype(low)
            return carry

        lax.fori_loop(0, everyone // block, score_back, 0)
        ticks(schedule[1 + 2 * h])
        query_t = r.qkv[:, base : base + pair].T
        keys_t = dot_nn(query_t, r.grad_score[...])
        keys_t = jnp.concatenate([keys_t[:HD, :words], keys_t[HD:, words:]], 1) * score_scale
        values_t = dot_nn(r.back_heads[:, h * HD : (h + 1) * HD].T, r.prob_low[...])
        r.grad_qkv[:, base + pair : base + 2 * pair] = (
            jnp.concatenate([keys_t, values_t], 0).T.astype(low)
        )

        def head_grad(i, carry):
            here = aligned(i, band)
            of_words = dot_nn(r.words_t[here, :], r.grad_qkv[0:words, base : base + pair])
            of_ents = dot_nn(r.ents_t[here, :], r.grad_qkv[words:everyone, base : base + pair])
            keyval = r.grad_qkv[:, base + pair : base + 2 * pair]
            of_keyval = dot_nn(r.words_t[here, :], keyval[:words]) + dot_nn(
                r.ents_t[here, :], keyval[words:]
            )
            for n, part in enumerate([of_words, of_ents, of_keyval]):
                r.q_grads[h, i, :, :, :, n * pair : (n + 1) * pair] = part.astype(low).reshape(
                    2, 2, share, pair
                )
            return carry

        lax.fori_loop(0, deep, head_grad, 0)
        head_one(h).start()
        sums = jnp.concatenate(
            [
                row_sum(r.grad_qkv[0:words, base : base + pair].astype(full)),
                row_sum(r.grad_qkv[words:everyone, base : base + pair].astype(full)),
                row_sum(r.grad_qkv[:, base + pair : base + 2 * pair].astype(full)),
            ],
            1,
        )
        place = h * 3 * pair
        vec[pl.ds(10 + 2 * x + place // width, 1), place % width : place % width + 3 * pair] = sums
        ticks(schedule[2 + 2 * h])

    quarter = half_words // 2

    def input_grad(place, weight):
        return dot_nt(r.grad_qkv[place, :], weight[...])

    ents_part = input_grad(slice(words, everyone), r.cat_ents)
    r.mail_out[1, words // 2 :, :] = ents_part
    ents_swap = swap(1, 3, words // 2, 2 * half_ents)
    ents_swap.start()
    for n in range(2):
        r.mail_out[1, n * quarter : (n + 1) * quarter, :] = input_grad(
            aligned(2 * n + 1 - t, quarter), r.cat_words
        )
    words_swap = swap(1, 4, 0, words // 2)
    words_swap.start()
    for n in range(2):
        r.input_part[n] = input_grad(aligned(2 * n + t, quarter), r.cat_words)
    ents_swap.wait()
    ents_place = pl.multiple_of(words // 2 + (1 - x) * half_ents, half_ents)
    ents_far = pl.ds(ents_place, half_ents)
    ents_near = pl.ds(pl.multiple_of(words // 2 + x * half_ents, half_ents), half_ents)
    r.ents_back[...] = (r.mail_out[1, ents_far, :] + r.mail_in[1, ents_far, :]).astype(low)
    ents_copy = send(r.ents_back, r.ents_in, r.pair_s.at[5], r.pair_r.at[5], x_peer)
    ents_copy.start()
    words_swap.wait()
    far_place = aligned(1 - x, quarter)
    r.words_back[...] = (r.input_part[1 - x] + r.mail_in[1, far_place, :]).astype(low)
    words_back_copy = send(r.words_back, r.words_in, r.pair_s.at[6], r.pair_r.at[6], x_peer)
    words_back_copy.start()
    ents_copy.wait()

    grad = r.grad_first[half_words:rows, :] + (r.mail_out[1, ents_near, :] + r.mail_in[1, ents_near, :])
    grad = grad + r.ents_in[...].astype(full)
    own_ents = aligned(x, half_ents)
    normed, scale = normalize(r.ent_lin[own_ents, :])
    vec[0:1, :] = row_sum(grad * normed)
    vec[3:4, :] = row_sum(grad)
    lin_low = normalize_back(grad, normed, scale, r.gain[0:1, :]).astype(low)
    slope = dot_nt(lin_low, r.w_entity[...]).astype(low)
    r.slope[...] = dot_nn(r.outbox[...], slope).reshape(owners, capacity, -1)
    r.slopes[flat] = r.slope[flat]
    for k in range(owners - 1):
        slope_copy(k).start()
    looked_half = r.looked[own_ents, aligned(t, 128)]
    r.ents_grad[...] = dot_tn(lin_low, looked_half).astype(low)

    def ents_body(i, carry):
        r.e_grads[0, i] = r.ents_grad[aligned(i, band), :].reshape(2, 2, share, 128)
        return carry

    lax.fori_loop(0, deep, ents_body, 0)
    stage_one(kit_e, 0, False).start()
    vec_copies = [send(r.vec.at[0], r.vec_in.at[0], r.vec_s.at[0], r.vec_r.at[0], x_peer)]
    vec_copies[0].start()
    words_back_copy.wait()
    r.grad_words[...] = (
        r.grad_first[aligned(t, quarter), :]
        + (r.input_part[x] + r.mail_in[1, aligned(x, quarter), :])
        + r.words_in[...].astype(full)
    )
    ticks(schedule[7])
    to_two(kit_e, 0, False)
    vec_copies[0].wait()
    r.vec[1] = r.vec[0] + r.vec_in[0]
    vec_copies.append(send(r.vec.at[1], r.vec_in.at[1], r.vec_s.at[1], r.vec_r.at[1], y_peer))
    vec_copies[1].start()
    ticks(schedule[8])
    to_three(kit_e, 0, False)
    vec_copies[1].wait()
    r.vec[2] = r.vec[1] + r.vec_in[1]
    for k in range(1, deep):
        vec_copies.append(
            send(r.vec.at[2], r.vec_in.at[1 + k], r.vec_s.at[1 + k], r.vec_r.at[1 + k], z_peers[k - 1])
        )
        vec_copies[-1].start()
    for k in range(owners - 1):
        slope_copy(k).wait()
    ids_t = r.asked[...].reshape(slots, 128).astype(full).T
    r.ids_out[...] = ids_t[0:8, :].astype(jnp.int32)
    r.slopes_out[...] = r.slopes[...].reshape(slots, -1).astype(low)
    for c in range(2 * downs + 1):
        finish(kit_a, c)
    ticks(schedule[9])
    total = r.vec[2]
    for k in range(1, deep):
        vec_copies[1 + k].wait()
        total = total + r.vec_in[1 + k]
    r.vec_out[...] = total
    r.across_out[...] = pltpu.roll(total[0:8, :], width - flat * share, 1)[:, 0:128]
    finish(kit_e, 0)
    ents_out = send(r.e_sum.at[0], r.e_in, r.pair_s.at[7], r.pair_r.at[7], core)
    ents_out.start()
    r.out_e[t] = r.e_sum[0]
    for h in range(heads):
        head_finish(h)
    ents_out.wait()
    r.out_e[1 - t] = r.e_in[...]


def finish_kernel(names, *refs):
    r = types.SimpleNamespace(**dict(zip(names, refs, strict=True)))
    low, full = jnp.bfloat16, jnp.float32
    step = pl.program_id(0)
    count, embed = r.adam_first.shape
    slots = r.ids.shape[1]
    row = lax.broadcasted_iota(jnp.int32, (count, slots), 0) + step * count
    chosen = jnp.where(row == r.ids[0:1, :], 1.0, 0.0)
    touched = jnp.max(chosen, 1, keepdims=True) > 0.0
    grad = dot_nn(chosen.astype(low), r.slopes[...])
    first, second = r.adam_first[...], r.adam_second[...]
    first_next = beta_one * first + (1.0 - beta_one) * grad
    second_next = beta_two * second + (1.0 - beta_two) * grad * grad
    direction = (
        first_next
        * (1.0 / (1.0 - beta_one**adam_steps))
        / (jnp.sqrt(second_next * (1.0 / (1.0 - beta_two**adam_steps))) + adam_eps)
    )
    r.table_update[...] = jnp.where(touched, direction, 0.0)
    r.new_first[...] = jnp.where(touched, first_next, first)
    r.new_second[...] = jnp.where(touched, second_next, second)

    chunks, share, chunk = r.out_a.shape
    downs = chunks // 2
    heads, side = r.out_q.shape[0], r.out_q.shape[0] * HD
    last = pl.num_programs(0) - 1

    @pl.when(step == 0)
    def _():
        for c in range(downs):
            r.red_down[c * chunk : (c + 1) * chunk, :] = r.out_a[c].T
            r.red_up[:, c * chunk : (c + 1) * chunk] = r.out_a[downs + c]
        r.red_out[...] = r.out_a[2 * downs].T

    @pl.when(step == last // 2)
    def _():
        for n in range(2):
            r.red_entity[n * 128 : (n + 1) * 128, :] = r.out_e[n].T
            for h in range(heads):
                place = h * 6 * HD
                line = 10 + 2 * n + place // r.vec.shape[1]
                for j in range(6):
                    lanes = slice(n * side + h * HD, n * side + (h + 1) * HD)
                    part = r.out_q[h, n, :, j * HD : (j + 1) * HD]
                    begin = place % r.vec.shape[1] + j * HD
                    line_part = r.vec[line : line + 1, begin : begin + HD]
                    if j < 4:
                        r.red_query[j, :, lanes] = part
                        r.red_query_bias[j : j + 1, lanes] = line_part
                    else:
                        r.red_keyval[j - 4, :, lanes] = part
                    if j == 5:
                        r.value_row[:, lanes] = line_part
        r.red_gain[...] = r.across[0:3, 0:share]
        r.red_shift[...] = r.across[3:6, 0:share]
        r.red_value_bias[...] = r.value_row[...].reshape(-1)
        r.red_out_bias[...] = r.across[6:7, 0:share].reshape(-1)
        r.red_down_bias[...] = r.across[7:8, 0:share].reshape(-1)
        width = r.vec.shape[1]
        for n in range(2):
            r.red_up_bias[n * width : (n + 1) * width] = r.vec[8 + n : 9 + n, :].reshape(-1)


SCHEDULE = (
    [("f", 0), ("f", 1)],
    [("f", 2)],
    [("s", 0), ("s", 1), ("f", 3)],
    [("f", 4)],
    [("s", 2), ("f", 5), ("s", 3)],
    [("f", 6), ("s", 4)],
    [("f", 7), ("s", 5), ("f", 8)],
    [("s", 6), ("s", 7), ("s", 8), ("q", 0)],
    [("q", 1), ("q", 2)],
    [("r", 0), ("r", 1), ("r", 2)],
)
FLIPS = (False, True, False, False, True, False, False, True, False)


def fused_local(
    word_states,
    entity_shard,
    entity_row,
    word_segments,
    entity_segments,
    entity_table,
    adam_first,
    adam_second,
    w_entity,
    norm_gain,
    norm_bias,
    w_query,
    b_query,
    w_keyval,
    b_value,
    w_out,
    b_out,
    w_up,
    b_up,
    w_down,
    b_down,
    cot_words,
    cot_entities,
):
    low, full = jnp.bfloat16, jnp.float32
    _, half_words, width = word_states.shape
    half_ents = entity_row.shape[2]
    rows, everyone = half_words + half_ents, 2 * (half_words + half_ents)
    words, ents = 2 * half_words, 2 * half_ents
    table_rows, embed = entity_table.shape
    local_width, hidden = w_query.shape[2], w_up.shape[1]
    owners = lax.axis_size(("dp", "stream"))
    deep = lax.axis_size("dp") // 2
    share = width // owners
    capacity = 2 * half_ents // owners
    side = local_width // 2
    heads = side // HD
    chunk = local_width
    chunks = 2 * (hidden // chunk) + 1

    operands = dict(
        words=word_states.reshape(half_words, width),
        shard=entity_shard.reshape(1, half_ents),
        row=entity_row.reshape(1, half_ents),
        word_seg=word_segments,
        ent_seg=entity_segments,
        gain=norm_gain,
        shift=norm_bias,
        b_query=b_query,
        b_value=b_value,
        b_out=b_out,
        b_up=b_up,
        b_down=b_down,
        cot_words=cot_words.reshape(half_words, width),
        cot_ents=cot_entities.reshape(half_ents, width),
    )
    streamed = dict(
        hbm_query=w_query,
        hbm_keyval=w_keyval,
        hbm_table=entity_table,
        hbm_entity=w_entity,
        hbm_out=w_out,
        hbm_up=w_up,
        hbm_down=w_down,
    )
    results = dict(
        out_words=((half_words // 2, width), low),
        out_ents=((half_ents // 2, width), low),
        grad_words=((half_words // 2, width), full),
        out_a=((chunks, share, chunk), full),
        out_e=((2, share, 128), full),
        out_q=((heads, 2, share, chunk), full),
        vec_out=((16, width), full),
        across_out=((8, 128), full),
        ids_out=((8, owners * capacity), jnp.int32),
        slopes_out=((owners * capacity, embed), low),
    )
    mail_rows = max(rows, words // 2 + ents)
    dma = pltpu.SemaphoreType.DMA
    scratch = dict(
        w_query=(w_query.shape, low),
        w_keyval=(w_keyval.shape, low),
        table=(entity_table.shape, low),
        w_entity=(w_entity.shape, low),
        w_out=(w_out.shape, low),
        w_up=(w_up.shape, low),
        w_down=(w_down.shape, low),
        cat_words=((width, 4 * side), low),
        cat_ents=((width, 4 * side), low),
        bias_words=((1, 4 * side), full),
        bias_ents=((1, 4 * side), full),
        cotangent=((rows, width), low),
        ask=((owners, capacity, 128), jnp.int32),
        asked=((owners, capacity, 128), jnp.int32),
        outbox=((owners * capacity, half_ents), low),
        select=((ents, owners * 2 * capacity), low),
        pick=((owners * capacity, table_rows), low),
        found=((owners // 2, 2 * capacity, embed), low),
        answer=((owners, 2 * capacity, embed), low),
        looked=((ents, embed), low),
        ent_lin=((ents, width), full),
        x_ent=((ents, width), full),
        x_all=((everyone, width), low),
        x_own=((rows, width), full),
        words_t=((width, words), low),
        ents_t=((width, ents), low),
        mask=((everyone, everyone), low),
        qkv=((everyone, 4 * side), low),
        key=((heads, everyone, HD), low),
        value=((heads, everyone, HD), low),
        prob=((heads, everyone, everyone), full),
        heads_far=((rows, side), low),
        heads_near=((rows, side), low),
        heads_in=((rows, side), low),
        heads_all=((rows, 2 * side), low),
        mail_out=((2, mail_rows, width), full),
        mail_in=((2, mail_rows, width), full),
        normed=((rows, width), full),
        scale=((rows, 128), full),
        first=((rows, width), low),
        first_t=((width, rows), low),
        act=((rows, hidden), low),
        slope_up=((rows, hidden), full),
        final=((rows, width), low),
        grad_second=((rows, width), full),
        grad_low=((rows, width), low),
        grad_t=((width, rows), low),
        grad_up=((rows, hidden), low),
        grad_first=((rows, width), full),
        back_far=((rows, side), low),
        back_heads=((everyone, side), low),
        grad_score=((everyone, everyone), low),
        prob_low=((everyone, everyone), low),
        grad_qkv=((everyone, 4 * side), low),
        input_part=((2, half_words // 2, width), full),
        ents_back=((half_ents, width), low),
        ents_in=((half_ents, width), low),
        words_back=((half_words // 2, width), low),
        words_in=((half_words // 2, width), low),
        slope=((owners, capacity, embed), full),
        slopes=((owners, capacity, embed), full),
        ents_grad=((width, 128), low),
        e_sum=((1, share, 128), full),
        e_in=((share, 128), full),
        vec=((3, 16, width), full),
        vec_in=((deep + 1, 16, width), full),
        grads=((chunks, deep, 2, 2, share, chunk), low),
        near=((chunks, deep, 2, share, chunk), low),
        next=((chunks, deep, share, chunk), low),
        far=((chunks, deep - 1, share, chunk), low),
        e_grads=((1, deep, 2, 2, share, 128), low),
        e_near=((1, deep, 2, share, 128), low),
        e_next=((1, deep, share, 128), low),
        e_far=((1, deep - 1, share, 128), low),
        q_grads=((heads, deep, 2, 2, share, chunk), low),
        q_near=((heads, deep, 2, share, chunk), low),
        q_far=((heads, deep - 1, 2, share, chunk), low),
        q_sum=((heads, 2, share, chunk), full),
        q_in=((heads, share, chunk), full),
    )
    signals = dict(
        load_s=(7,),
        ask_s=(owners - 1,),
        ask_r=(owners - 1,),
        answer_s=(owners - 1,),
        answer_r=(owners - 1,),
        slope_s=(owners - 1,),
        slope_r=(owners - 1,),
        pair_s=(8,),
        pair_r=(8,),
        swap_s=(5,),
        swap_r=(5,),
        vec_s=(deep + 1,),
        vec_r=(deep + 1,),
    )
    one, many = (1,), (1, deep - 1)
    signals.update(e_s1=one, e_r1=one, e_s2=one, e_r2=one, e_s3=many, e_r3=many)
    one, many = (chunks,), (chunks, deep - 1)
    signals.update(a_s1=one, a_r1=one, a_s2=one, a_r2=one, a_s3=many, a_r3=many)
    one, many = (heads,), (heads, deep - 1)
    signals.update(q_s1=one, q_r1=one, q_s2=many, q_r2=many, q_s3=one, q_r3=one)
    names = [*operands, *streamed, *results, *scratch, *signals]
    kernel = functools.partial(layer_kernel, names, FLIPS, SCHEDULE)
    made = pl.pallas_call(
        kernel,
        name="layer",
        out_shape=[jax.ShapeDtypeStruct(*item) for item in results.values()],
        in_specs=[pl.BlockSpec(memory_space=pltpu.VMEM)] * len(operands)
        + [pl.BlockSpec(memory_space=pl.ANY)] * len(streamed),
        out_specs=[pl.BlockSpec(memory_space=pltpu.VMEM)] * len(results),
        scratch_shapes=[pltpu.VMEM(*item) for item in scratch.values()]
        + [dma(shape) for shape in signals.values()],
        compiler_params=pltpu.CompilerParams(
            collective_id=0, has_side_effects=True, vmem_limit_bytes=67_043_328
        ),
    )(*operands.values(), *streamed.values())
    got = types.SimpleNamespace(**dict(zip(results, made, strict=True)))

    step = table_rows // 8
    table = pl.BlockSpec((step, embed), lambda i: (i, 0))

    def whole(shape):
        return pl.BlockSpec(shape, lambda i: (0,) * len(shape))

    given = dict(
        adam_first=adam_first,
        adam_second=adam_second,
        ids=got.ids_out,
        slopes=got.slopes_out,
        out_a=got.out_a,
        out_e=got.out_e,
        out_q=got.out_q,
        vec=got.vec_out,
        across=got.across_out,
    )
    final = dict(
        red_entity=(embed, share),
        red_gain=(3, share),
        red_shift=(3, share),
        red_query=(4, share, local_width),
        red_query_bias=(4, local_width),
        red_keyval=(2, share, local_width),
        red_value_bias=(local_width,),
        red_out=(local_width, share),
        red_out_bias=(share,),
        red_up=(share, hidden),
        red_up_bias=(hidden,),
        red_down=(hidden, share),
        red_down_bias=(share,),
        table_update=adam_first.shape,
        new_first=adam_first.shape,
        new_second=adam_first.shape,
    )
    finished = pl.pallas_call(
        functools.partial(finish_kernel, [*given, *final, *dict(value_row=0)]),
        name="finish",
        grid=(8,),
        out_shape=[jax.ShapeDtypeStruct(shape, full) for shape in final.values()],
        in_specs=[table, table] + [whole(item.shape) for item in list(given.values())[2:]],
        out_specs=[whole(shape) for shape in list(final.values())[:-3]] + [table] * 3,
        scratch_shapes=[pltpu.VMEM((1, local_width), full)],
        compiler_params=pltpu.CompilerParams(vmem_limit_bytes=40 * 2**20),
    )(*given.values())
    return (got.out_words[None], got.out_ents[None], got.grad_words[None], *finished)


def plain_local(
    word_states,
    entity_shard,
    entity_row,
    word_segments,
    entity_segments,
    entity_table,
    adam_first,
    adam_second,
    w_entity,
    norm_gain,
    norm_bias,
    w_query,
    b_query,
    w_keyval,
    b_value,
    w_out,
    b_out,
    w_up,
    b_up,
    w_down,
    b_down,
    cot_words,
    cot_entities,
):
    seq_count, half_words, width = word_states.shape
    half_ents = entity_row.shape[2]
    table_rows, embed_width = entity_table.shape
    local_width = w_query.shape[2]
    local_heads = local_width // HD
    owners = lax.axis_size(("dp", "stream"))
    stream_index = lax.axis_index("stream")
    parts = lax.axis_size("tensor")
    part_index = lax.axis_index("tensor")
    word_part = half_words // parts
    ent_part = half_ents // parts
    ent_count = seq_count * half_ents
    word_count = seq_count * half_words
    local_rows = half_words + half_ents
    share_words = seq_count * word_part
    owner_flat = entity_shard.reshape(ent_count)
    row_flat = entity_row.reshape(ent_count)

    def pick(block, count):
        shaped = block.reshape(seq_count, parts, count // parts, block.shape[-1])
        return lax.dynamic_index_in_dim(shaped, part_index, 1, keepdims=False).reshape(
            seq_count * (count // parts), block.shape[-1]
        )

    def own_share(rows):
        return jnp.concatenate(
            [pick(rows[:word_count], half_words), pick(rows[word_count:], half_ents)], 0
        )

    capacity = 2 * ent_count // owners
    owner_hits = (owner_flat[:, None] == jnp.arange(owners, dtype=jnp.int32)[None, :]).astype(
        jnp.int32
    )
    before = jnp.cumsum(owner_hits, 0) - owner_hits
    ranking = jnp.sum(before * owner_hits, 1)
    slot_index = owner_flat * capacity + ranking
    request = (
        jnp.full((owners * capacity,), -1, jnp.int32)
        .at[slot_index]
        .set(row_flat)
        .reshape(owners, capacity)
    )
    asked_ids = lax.all_to_all(request, ("dp", "stream"), split_axis=0, concat_axis=0, tiled=True)
    present = asked_ids >= 0
    found_rows = jnp.take(entity_table, jnp.clip(asked_ids, 0, table_rows - 1), axis=0)
    found_rows = jnp.where(present[..., None], found_rows, jnp.zeros_like(found_rows))
    found_rows, asked_rows = (found_rows, asked_ids)
    answered = lax.all_to_all(found_rows, ("dp", "stream"), split_axis=0, concat_axis=0, tiled=True)
    looked = answered.reshape(owners * capacity, embed_width)[slot_index]
    ent_lin = matmul(looked, w_entity)
    x_entity, entity_norm_back = jax.vjp(layer_norm, ent_lin, norm_gain[0], norm_bias[0])
    entity_low = x_entity.astype(jnp.bfloat16)
    word_low = word_states.reshape(word_count, width)
    query_words = (
        jnp.einsum("rd,jdc->jrc", word_low, w_query[:2], preferred_element_type=jnp.float32)
        + b_query[:2, None, :]
    ).astype(jnp.bfloat16)
    query_ents = (
        jnp.einsum("rd,jdc->jrc", entity_low, w_query[2:], preferred_element_type=jnp.float32)
        + b_query[2:, None, :]
    ).astype(jnp.bfloat16)
    value_shift = jnp.stack([jnp.zeros_like(b_value), b_value])[:, None, :]
    keyval_words = (
        jnp.einsum("rd,jdc->jrc", word_low, w_keyval, preferred_element_type=jnp.float32)
        + value_shift
    ).astype(jnp.bfloat16)
    keyval_ents = (
        jnp.einsum("rd,jdc->jrc", entity_low, w_keyval, preferred_element_type=jnp.float32)
        + value_shift
    ).astype(jnp.bfloat16)
    far_words, far_ents = from_partner((keyval_words, keyval_ents), "stream", 0)

    def by_heads(block, count):
        return block.reshape(block.shape[0], seq_count, count, local_heads, HD)

    queries = jnp.concatenate(
        [by_heads(query_words, half_words), by_heads(query_ents, half_ents)], 2
    )
    keyval_w = jnp.concatenate(
        [by_heads(keyval_words, half_words), by_heads(far_words, half_words)], 2
    )
    keyval_e = jnp.concatenate([by_heads(keyval_ents, half_ents), by_heads(far_ents, half_ents)], 2)
    own_wseg = lax.dynamic_slice_in_dim(word_segments, stream_index * half_words, half_words, 1)
    far_wseg = lax.dynamic_slice_in_dim(
        word_segments, (1 - stream_index) * half_words, half_words, 1
    )
    own_eseg = lax.dynamic_slice_in_dim(entity_segments, stream_index * half_ents, half_ents, 1)
    far_eseg = lax.dynamic_slice_in_dim(
        entity_segments, (1 - stream_index) * half_ents, half_ents, 1
    )
    query_seg = jnp.concatenate([own_wseg, own_eseg], 1)
    key_wseg = jnp.concatenate([own_wseg, far_wseg], 1)
    key_eseg = jnp.concatenate([own_eseg, far_eseg], 1)
    allow_words = query_seg[:, None, :, None] == key_wseg[:, None, None, :]
    allow_ents = query_seg[:, None, :, None] == key_eseg[:, None, None, :]

    def scores_of():
        raw_words = (
            jnp.einsum(
                "sqhd,skhd->shqk", queries[0], keyval_w[0], preferred_element_type=jnp.float32
            )
            * score_scale
        )
        raw_ents = (
            jnp.einsum(
                "sqhd,skhd->shqk", queries[1], keyval_e[0], preferred_element_type=jnp.float32
            )
            * score_scale
        )
        return (
            jnp.where(allow_words, raw_words, masked_score),
            jnp.where(allow_ents, raw_ents, masked_score),
        )

    score_words, score_ents = scores_of()
    highest = jnp.maximum(
        jnp.max(score_words, -1, keepdims=True), jnp.max(score_ents, -1, keepdims=True)
    )
    totals = jnp.sum(jnp.exp(score_words - highest), -1, keepdims=True) + jnp.sum(
        jnp.exp(score_ents - highest), -1, keepdims=True
    )
    log_total = highest + jnp.log(totals)
    low_words = jnp.exp(score_words - log_total).astype(jnp.bfloat16)
    low_ents = jnp.exp(score_ents - log_total).astype(jnp.bfloat16)
    heads_out = jnp.einsum(
        "shqk,skhd->sqhd", low_words, keyval_w[1], preferred_element_type=jnp.float32
    )
    heads_out = heads_out + jnp.einsum(
        "shqk,skhd->sqhd", low_ents, keyval_e[1], preferred_element_type=jnp.float32
    )
    heads_out = heads_out.astype(jnp.bfloat16).reshape(seq_count, local_rows, local_width)
    heads_dense = jnp.concatenate(
        [
            heads_out[:, :half_words].reshape(word_count, local_width),
            heads_out[:, half_words:].reshape(ent_count, local_width),
        ],
        0,
    )
    resid_in = jnp.concatenate([word_low.astype(jnp.float32), x_entity], 0)
    cotangent = jnp.concatenate(
        [cot_words.reshape(word_count, width), cot_entities.reshape(ent_count, width)], 0
    ).astype(jnp.float32)
    attn_out = tensor_total(matmul(heads_dense, w_out)) + b_out
    first_norm, first_back = jax.vjp(layer_norm, resid_in + attn_out, norm_gain[1], norm_bias[1])
    first_low = first_norm.astype(jnp.bfloat16)
    up_value = matmul(first_low, w_up) + b_up
    active, gelu_back = jax.vjp(gelu_exact, up_value)
    active_low = active.astype(jnp.bfloat16)
    ffn_out = tensor_total(matmul(active_low, w_down)) + b_down
    final_norm, final_back = jax.vjp(layer_norm, first_norm + ffn_out, norm_gain[2], norm_bias[2])
    final_share = own_share(final_norm)
    grad_final, gain_final, shift_final = final_back(cotangent)
    grad_ffn = grad_final.astype(jnp.bfloat16)
    out_words = final_share[:share_words].reshape(seq_count, word_part, width).astype(jnp.bfloat16)
    out_entities = (
        final_share[share_words:].reshape(seq_count, ent_part, width).astype(jnp.bfloat16)
    )
    grad_down = jnp.einsum("rf,rd->fd", active_low, grad_ffn, preferred_element_type=jnp.float32)
    grad_down_bias = jnp.sum(grad_ffn.astype(jnp.float32), 0)
    (grad_pre,) = gelu_back(
        jnp.einsum("rd,fd->rf", grad_ffn, w_down, preferred_element_type=jnp.float32)
    )
    grad_up_low = grad_pre.astype(jnp.bfloat16)
    grad_up = jnp.einsum("rd,rf->df", first_low, grad_up_low, preferred_element_type=jnp.float32)
    grad_up_bias = jnp.sum(grad_up_low.astype(jnp.float32), 0)
    ffn_term = jnp.einsum("rf,df->rd", grad_up_low, w_up, preferred_element_type=jnp.float32)
    grad_first, gain_first, shift_first = first_back(grad_final + tensor_total(ffn_term))
    grad_attn = grad_first.astype(jnp.bfloat16)
    grad_out = jnp.einsum("rc,rd->cd", heads_dense, grad_attn, preferred_element_type=jnp.float32)
    grad_out_bias = jnp.sum(grad_attn.astype(jnp.float32), 0)
    grad_heads = jnp.einsum(
        "rd,cd->rc", grad_attn, w_out, preferred_element_type=jnp.float32
    ).astype(jnp.bfloat16)
    grad_heads = jnp.concatenate(
        [
            grad_heads[:word_count].reshape(seq_count, half_words, local_heads, HD),
            grad_heads[word_count:].reshape(seq_count, half_ents, local_heads, HD),
        ],
        1,
    )
    score_words, score_ents = scores_of()
    prob_words = jnp.exp(score_words - log_total)
    prob_ents = jnp.exp(score_ents - log_total)
    low_words = prob_words.astype(jnp.bfloat16)
    low_ents = prob_ents.astype(jnp.bfloat16)
    dprob_words = jnp.einsum(
        "sqhd,skhd->shqk", grad_heads, keyval_w[1], preferred_element_type=jnp.float32
    )
    dprob_ents = jnp.einsum(
        "sqhd,skhd->shqk", grad_heads, keyval_e[1], preferred_element_type=jnp.float32
    )
    inner_sum = jnp.sum(prob_words * dprob_words, -1, keepdims=True) + jnp.sum(
        prob_ents * dprob_ents, -1, keepdims=True
    )
    dscore_words = (prob_words * (dprob_words - inner_sum)).astype(jnp.bfloat16)
    dscore_ents = (prob_ents * (dprob_ents - inner_sum)).astype(jnp.bfloat16)
    grad_to_words = (
        jnp.einsum("shqk,skhd->sqhd", dscore_words, keyval_w[0], preferred_element_type=jnp.float32)
        * score_scale
    ).astype(jnp.bfloat16)
    grad_to_ents = (
        jnp.einsum("shqk,skhd->sqhd", dscore_ents, keyval_e[0], preferred_element_type=jnp.float32)
        * score_scale
    ).astype(jnp.bfloat16)
    kv_grad_words = jnp.stack(
        [
            jnp.einsum(
                "shqk,sqhd->skhd", dscore_words, queries[0], preferred_element_type=jnp.float32
            )
            * score_scale,
            jnp.einsum(
                "shqk,sqhd->skhd", low_words, grad_heads, preferred_element_type=jnp.float32
            ),
        ]
    )
    kv_grad_ents = jnp.stack(
        [
            jnp.einsum(
                "shqk,sqhd->skhd", dscore_ents, queries[1], preferred_element_type=jnp.float32
            )
            * score_scale,
            jnp.einsum("shqk,sqhd->skhd", low_ents, grad_heads, preferred_element_type=jnp.float32),
        ]
    )
    back_words, back_ents = (
        from_partner(kv_grad_words[:, :, half_words:].astype(jnp.bfloat16), "stream", 0).astype(
            jnp.float32
        ),
        from_partner(kv_grad_ents[:, :, half_ents:].astype(jnp.bfloat16), "stream", 0).astype(
            jnp.float32
        ),
    )
    grad_kv_words = (
        (kv_grad_words[:, :, :half_words] + back_words)
        .reshape(2, word_count, local_width)
        .astype(jnp.bfloat16)
    )
    grad_kv_ents = (
        (kv_grad_ents[:, :, :half_ents] + back_ents)
        .reshape(2, ent_count, local_width)
        .astype(jnp.bfloat16)
    )
    grad_q_words = jnp.stack([grad_to_words[:, :half_words], grad_to_ents[:, :half_words]]).reshape(
        2, word_count, local_width
    )
    grad_q_ents = jnp.stack([grad_to_words[:, half_words:], grad_to_ents[:, half_words:]]).reshape(
        2, ent_count, local_width
    )
    grad_query = jnp.concatenate(
        [
            jnp.einsum("rd,jrc->jdc", word_low, grad_q_words, preferred_element_type=jnp.float32),
            jnp.einsum("rd,jrc->jdc", entity_low, grad_q_ents, preferred_element_type=jnp.float32),
        ],
        0,
    )
    grad_query_bias = jnp.concatenate(
        [jnp.sum(grad_q_words.astype(jnp.float32), 1), jnp.sum(grad_q_ents.astype(jnp.float32), 1)],
        0,
    )
    grad_keyval = jnp.einsum(
        "rd,jrc->jdc", word_low, grad_kv_words, preferred_element_type=jnp.float32
    ) + jnp.einsum("rd,jrc->jdc", entity_low, grad_kv_ents, preferred_element_type=jnp.float32)
    grad_value_bias = jnp.sum(grad_kv_words[1].astype(jnp.float32), 0) + jnp.sum(
        grad_kv_ents[1].astype(jnp.float32), 0
    )
    input_words = jnp.einsum(
        "jrc,jdc->rd", grad_q_words, w_query[:2], preferred_element_type=jnp.float32
    ) + jnp.einsum("jrc,jdc->rd", grad_kv_words, w_keyval, preferred_element_type=jnp.float32)
    input_ents = jnp.einsum(
        "jrc,jdc->rd", grad_q_ents, w_query[2:], preferred_element_type=jnp.float32
    ) + jnp.einsum("jrc,jdc->rd", grad_kv_ents, w_keyval, preferred_element_type=jnp.float32)
    input_term = jnp.concatenate([input_words, input_ents], 0)
    grad_input = grad_first + tensor_total(input_term)
    grad_share = own_share(grad_input)
    grad_lin, gain_entity, shift_entity = entity_norm_back(grad_input[word_count:])
    grad_lin_low = grad_lin.astype(jnp.bfloat16)
    gain_grads = jnp.stack([gain_entity, gain_first, gain_final])
    shift_grads = jnp.stack([shift_entity, shift_first, shift_final])
    grad_words = grad_share[:share_words].reshape(seq_count, word_part, width)
    grad_entity = jnp.einsum("re,rd->ed", looked, grad_lin_low, preferred_element_type=jnp.float32)
    grad_looked = jnp.einsum(
        "rd,ed->re", grad_lin_low, w_entity, preferred_element_type=jnp.float32
    )
    outgoing = (
        jnp.zeros((owners * capacity, embed_width), jnp.float32)
        .at[slot_index]
        .set(grad_looked)
        .reshape(owners, capacity, embed_width)
    )
    incoming = lax.all_to_all(
        outgoing.astype(jnp.bfloat16), ("dp", "stream"), split_axis=0, concat_axis=0, tiled=True
    ).astype(outgoing.dtype)
    target = jnp.where(asked_rows >= 0, asked_rows, table_rows).reshape(-1)
    gradient_sum = (
        jnp.zeros((table_rows, embed_width), jnp.float32)
        .at[target]
        .add(incoming.reshape(-1, embed_width), mode="drop")
    )
    use_count = jnp.zeros((table_rows,), jnp.float32).at[target].add(1.0, mode="drop")
    touched = (use_count > 0.0)[:, None]
    first_next = beta_one * adam_first + (1.0 - beta_one) * gradient_sum
    second_next = beta_two * adam_second + (1.0 - beta_two) * gradient_sum * gradient_sum
    direction = (
        first_next
        / (1.0 - beta_one**adam_steps)
        / (jnp.sqrt(second_next / (1.0 - beta_two**adam_steps)) + adam_eps)
    )
    table_update = jnp.where(touched, direction, jnp.zeros_like(direction))
    new_first = jnp.where(touched, first_next, adam_first)
    new_second = jnp.where(touched, second_next, adam_second)
    (
        red_entity,
        red_gain,
        red_shift,
        red_query,
        red_keyval,
        red_out,
        red_out_bias,
        red_up,
        red_down,
        red_down_bias,
    ) = (
        lax.psum_scatter(grad_entity, ("dp", "stream"), scatter_dimension=1, tiled=True),
        lax.psum_scatter(gain_grads, ("dp", "stream"), scatter_dimension=1, tiled=True),
        lax.psum_scatter(shift_grads, ("dp", "stream"), scatter_dimension=1, tiled=True),
        lax.psum_scatter(grad_query, ("dp", "stream"), scatter_dimension=1, tiled=True),
        lax.psum_scatter(grad_keyval, ("dp", "stream"), scatter_dimension=1, tiled=True),
        lax.psum_scatter(grad_out, ("dp", "stream"), scatter_dimension=1, tiled=True),
        lax.psum_scatter(grad_out_bias, ("dp", "stream"), scatter_dimension=0, tiled=True),
        lax.psum_scatter(grad_up, ("dp", "stream"), scatter_dimension=0, tiled=True),
        lax.psum_scatter(grad_down, ("dp", "stream"), scatter_dimension=1, tiled=True),
        lax.psum_scatter(grad_down_bias, ("dp", "stream"), scatter_dimension=0, tiled=True),
    )
    red_query_bias, red_value_bias, red_up_bias = lax.psum(
        (grad_query_bias, grad_value_bias, grad_up_bias), ("dp", "stream")
    )
    return (
        out_words,
        out_entities,
        grad_words,
        red_entity,
        red_gain,
        red_shift,
        red_query,
        red_query_bias,
        red_keyval,
        red_value_bias,
        red_out,
        red_out_bias,
        red_up,
        red_up_bias,
        red_down,
        red_down_bias,
        table_update,
        new_first,
        new_second,
    )


def solution(mesh):
    placed = (
        P("dp", "stream", None),
        P("stream", "dp", None, None),
        P("stream", "dp", None),
        P("dp", None),
        P("dp", None),
        P(("dp", "stream"), None),
        P(("dp", "stream"), None),
        P(("dp", "stream"), None),
        P(),
        P(),
        P(),
        P(None, None, "tensor"),
        P(None, "tensor"),
        P(None, None, "tensor"),
        P("tensor"),
        P("tensor", None),
        P(),
        P(None, "tensor"),
        P("tensor"),
        P("tensor", None),
        P(),
        P("dp", "stream", None),
        P("dp", "stream", None),
    )
    fits = mesh.shape["stream"] == 2 and mesh.shape["tensor"] == 2 and mesh.shape["dp"] % 2 == 0

    def local(*blocks):
        width, owners = blocks[0].shape[2], mesh.shape["dp"] * mesh.shape["stream"]
        if fits and width % (16 * owners) == 0 and blocks[0].shape[0] == 1:
            return fused_local(*blocks)
        return plain_local(*blocks)

    return jax.shard_map(
        local,
        mesh=mesh,
        in_specs=placed,
        out_specs=(
            P("dp", ("stream", "tensor"), None),
            P("dp", ("stream", "tensor"), None),
            P("dp", ("stream", "tensor"), None),
            P(None, ("dp", "stream")),
            P(None, ("dp", "stream")),
            P(None, ("dp", "stream")),
            P(None, ("dp", "stream"), "tensor"),
            P(None, "tensor"),
            P(None, ("dp", "stream"), "tensor"),
            P("tensor"),
            P("tensor", ("dp", "stream")),
            P(("dp", "stream")),
            P(("dp", "stream"), "tensor"),
            P("tensor"),
            P("tensor", ("dp", "stream")),
            P(("dp", "stream")),
            P(("dp", "stream"), None),
            P(("dp", "stream"), None),
            P(("dp", "stream"), None),
        ),
        check_vma=False,
    )
```

```python
import functools
import math
import types

import jax
import jax.numpy as jnp
from jax import lax
from jax.experimental import pallas as pl
from jax.experimental.pallas import tpu as pltpu
from jax.sharding import PartitionSpec as P

HD = 64
MESH_ID = pl.DeviceIdType.MESH


norm_eps = 1e-05
score_scale = 0.125
masked_score = -1e30
beta_one = 0.9
beta_two = 0.99
adam_steps = 10
adam_eps = 1e-08


def from_partner(block, axis, apart):
    count = lax.axis_size(axis)
    route = []
    for low in range(count):
        high = low | 1 << apart
        if high != low and high < count:
            route += [(low, high), (high, low)]
    return lax.ppermute(block, axis, route)


def layer_norm(values_in, gain_row, shift_row):
    center = values_in - jnp.mean(values_in, -1, keepdims=True)
    spread = jnp.mean(center * center, -1, keepdims=True)
    return center * lax.rsqrt(spread + norm_eps) * gain_row + shift_row


def gelu_exact(values_in):
    return jax.nn.gelu(values_in, approximate=False)


def matmul(matrix_a, matrix_b):
    return jnp.dot(matrix_a, matrix_b, preferred_element_type=jnp.float32)


def tensor_total(values_in):
    return lax.psum(values_in, "tensor")


def send(source, target, send_sem, recv_sem, peer):
    return pltpu.make_async_remote_copy(
        src_ref=source,
        dst_ref=target,
        send_sem=send_sem,
        recv_sem=recv_sem,
        device_id=peer,
        device_id_type=MESH_ID,
    )


def row_sum(block):
    return jnp.sum(block, 0, keepdims=True)


def lane_mean(block):
    return jnp.mean(block, -1, keepdims=True)


def dot_nn(left, right):
    return jnp.dot(left, right, preferred_element_type=jnp.float32)


def dot_nt(left, right):
    return lax.dot_general(
        left, right, (((1,), (1,)), ((), ())), preferred_element_type=jnp.float32
    )


def dot_tn(left, right):
    return lax.dot_general(
        left, right, (((0,), (0,)), ((), ())), preferred_element_type=jnp.float32
    )


def normalize(rows):
    center = rows - lane_mean(rows)
    scale = lax.rsqrt(lane_mean(center * center) + norm_eps)
    return center * scale, scale


def normalize_back(grad, normed, scale, gain):
    inner = grad * gain
    return scale * (inner - lane_mean(inner) - normed * lane_mean(inner * normed))


def aligned(index, step):
    return pl.ds(pl.multiple_of(index * step, step), step)


def layer_kernel(names, flips, schedule, *refs):
    r = types.SimpleNamespace(**dict(zip(names, refs, strict=True)))
    low, full = jnp.bfloat16, jnp.float32
    dp, x, t = lax.axis_index("dp"), lax.axis_index("stream"), lax.axis_index("tensor")
    y, z = lax.rem(dp, 2), dp // 2
    deep = lax.axis_size("dp") // 2
    owners = 4 * deep
    _, half_words, width = r.hbm_words.shape
    half_ents = r.shard.shape[1]
    rows, words = half_words + half_ents, 2 * half_words
    everyone = 2 * rows
    capacity = r.ask.shape[1]
    slots = owners * capacity
    heads = r.prob.shape[0]
    share = width // owners
    side = heads * HD
    hidden = r.w_up.shape[1]
    block = half_ents
    blocks = rows // block
    word_blocks = half_words // block
    wide = 256

    core, x_peer, y_peer = {"tensor": 1 - t}, {"stream": 1 - x}, {"dp": z * 2 + 1 - y}
    z_peers = [{"dp": lax.rem(z + k, deep) * 2 + y} for k in range(1, deep)]
    flat = dp * 2 + x
    others = []
    for k in range(1, owners):
        other = lax.rem(flat + k, owners)
        others.append((other, {"dp": other // 2, "stream": lax.rem(other, 2)}))

    barrier = pltpu.get_barrier_semaphore()
    for peer in [core] + [peer for _, peer in others]:
        pl.semaphore_signal(barrier, inc=1, device_id=peer, device_id_type=MESH_ID)

    loads = {}

    def load(source, target):
        loads[id(target)] = pltpu.make_async_copy(source, target, r.load_s.at[len(loads)])
        loads[id(target)].start()

    def loaded(target):
        loads.pop(id(target)).wait()

    my_words = r.x_all.at[aligned(x, half_words), :]
    load(r.hbm_words.at[0], my_words)
    load(r.hbm_query, r.w_query)
    load(r.hbm_keyval, r.w_keyval)
    load(r.hbm_table, r.table)
    load(r.hbm_entity, r.w_entity)
    cot_words, cot_ents = r.cotangent.at[0:half_words, :], r.cotangent.at[half_words:rows, :]
    load(r.hbm_cot_words.at[0], cot_words)
    load(r.hbm_cot_ents.at[0], cot_ents)
    load(r.hbm_out, r.w_out)
    load(r.hbm_up, r.w_up)
    load(r.hbm_down, r.w_down)

    shard_row = r.shard[...]
    shard_all = jnp.broadcast_to(shard_row.astype(full), (half_ents, half_ents)).T
    shard_all = shard_all.astype(jnp.int32)
    shard_col = shard_all[:, 0:1]
    below = lax.broadcasted_iota(jnp.int32, (half_ents, half_ents), 0)
    beside = lax.broadcasted_iota(jnp.int32, (half_ents, half_ents), 1)
    same = shard_all == shard_row
    rank_row = row_sum(jnp.where(same & (below < beside), 1.0, 0.0)).astype(jnp.int32)
    rank_col = jnp.sum(jnp.where(same & (beside < below), 1.0, 0.0), 1, keepdims=True)
    rank_col = rank_col.astype(jnp.int32)
    slot_row = shard_row * capacity + rank_row
    in_slot = lax.broadcasted_iota(jnp.int32, (slots, half_ents), 0) == slot_row
    wanted = jnp.sum(
        jnp.where(in_slot, (r.row[...] + 1).astype(full), 0.0), 1, keepdims=True
    )
    wanted = wanted.astype(jnp.int32) - 1
    r.ask[...] = jnp.broadcast_to(wanted, (slots, 128)).reshape(owners, capacity, 128)
    r.outbox[...] = jnp.where(in_slot, 1.0, 0.0).astype(low)
    answer_col = shard_col * (2 * capacity) + x * capacity + rank_col
    answer_lane = lax.broadcasted_iota(jnp.int32, (half_ents, 2 * slots), 1)
    r.select[aligned(x, half_ents), :] = jnp.where(answer_lane == answer_col, 1.0, 0.0).astype(low)
    r.asked[flat] = r.ask[flat]
    r.vec[0] = jnp.zeros(r.vec.shape[1:], full)

    loaded(r.w_query)
    loaded(r.w_keyval)

    def gather_columns(which):
        for h in range(heads):
            own = slice(which * side + h * HD, which * side + (h + 1) * HD)
            for place, words_part, ents_part in (
                (0, r.w_query[0, :, own], r.w_query[2, :, own]),
                (1, r.w_query[1, :, own], r.w_query[3, :, own]),
                (2, r.w_keyval[0, :, own], None),
                (3, r.w_keyval[1, :, own], None),
            ):
                lanes = slice((4 * h + place) * HD, (4 * h + place + 1) * HD)
                r.cat_words[:, lanes] = words_part
                r.cat_ents[:, lanes] = words_part if ents_part is None else ents_part
            zero = jnp.zeros((1, HD), full)
            value = r.b_value[...].reshape(1, -1)[:, own]
            query = r.b_query[:, own]
            lanes = slice(4 * h * HD, 4 * (h + 1) * HD)
            r.bias_words[:, lanes] = jnp.concatenate([query[0:1], query[1:2], zero, value], 1)
            r.bias_ents[:, lanes] = jnp.concatenate([query[2:3], query[3:4], zero, value], 1)

    for which in range(2):

        @pl.when(x == which)
        def _(which=which):
            gather_columns(which)

    loaded(my_words)
    r.x_own[0:half_words, :] = my_words[...].astype(full)
    pl.semaphore_wait(barrier, owners)

    def ask_copy(k):
        other, peer = others[k]
        return send(r.ask.at[other], r.asked.at[flat], r.ask_s.at[k], r.ask_r.at[k], peer)

    def answer_copy(k):
        other, peer = others[k]
        return send(
            r.found.at[other // 2], r.answer.at[flat], r.answer_s.at[k], r.answer_r.at[k], peer
        )

    def slope_copy(k):
        other, peer = others[k]
        return send(r.slope.at[other], r.slopes.at[flat], r.slope_s.at[k], r.slope_r.at[k], peer)

    for k in range(owners - 1):
        ask_copy(k).start()
    my_select = r.select.at[aligned(x, half_ents), :]
    select_copy = send(my_select, my_select, r.pair_s.at[0], r.pair_r.at[0], x_peer)
    select_copy.start()
    words_copy = send(my_words, my_words, r.pair_s.at[1], r.pair_r.at[1], x_peer)
    words_copy.start()

    is_query = lax.broadcasted_iota(jnp.int32, (1, 4 * HD), 1) < 2 * HD
    scaling = jnp.where(is_query, score_scale, 1.0)

    def project(start, count, weight, bias):
        def body(h, carry):
            lanes = aligned(h, 4 * HD)
            total = dot_nn(r.x_all[pl.ds(start, count), :], weight[:, lanes]) + bias[:, lanes]
            r.qkv[pl.ds(start, count), lanes] = (total * scaling).astype(low)
            return carry

        lax.fori_loop(0, heads, body, 0)

    project(pl.multiple_of(x * half_words, half_words), half_words, r.cat_words, r.bias_words)

    segments = jnp.concatenate([r.word_seg[...], r.ent_seg[...]], 1)
    for i in range(everyone // 128):
        own_seg = jnp.broadcast_to(segments[:, i * 128 : (i + 1) * 128].astype(full), (128, 128)).T
        equal = own_seg[:, 0:1].astype(jnp.int32) == segments
        r.mask[i * 128 : (i + 1) * 128, :] = jnp.where(equal, 0.0, masked_score).astype(low)

    for k in range(owners - 1):
        ask_copy(k).wait()
    ids = r.asked[...].reshape(slots, 128)
    lane = lax.broadcasted_iota(jnp.int32, (slots, 128), 1)
    loaded(r.table)
    piece = 4 * 128

    def pick_body(j, found):
        ones = [jnp.where(ids == lane + (j * piece + n * 128), 1.0, 0.0) for n in range(4)]
        return found + dot_nn(jnp.concatenate(ones, 1).astype(low), r.table[aligned(j, piece), :])

    found = jnp.zeros((slots, r.table.shape[1]), full)
    found = lax.fori_loop(0, r.table.shape[0] // piece, pick_body, found).astype(low)
    r.found[...] = found.reshape(r.found.shape)
    r.answer[flat] = r.found[dp]
    for k in range(owners - 1):
        answer_copy(k).start()

    words_copy.wait()
    project(pl.multiple_of((1 - x) * half_words, half_words), half_words, r.cat_words, r.bias_words)
    r.words_t[...] = r.x_all[0:words, :].T

    select_copy.wait()
    for k in range(owners - 1):
        answer_copy(k).wait()
    looked = dot_nn(r.select[...], r.answer[...].reshape(2 * slots, r.table.shape[1])).astype(low)
    r.looked[...] = looked
    loaded(r.w_entity)
    ent_lin = dot_nn(looked, r.w_entity[...])
    normed, _ = normalize(ent_lin)
    x_entity = normed * r.gain[0:1, :] + r.shift[0:1, :]
    r.ent_lin[...] = ent_lin
    r.x_ent[...] = x_entity
    r.x_all[words:everyone, :] = x_entity.astype(low)
    r.x_own[half_words:rows, :] = r.x_ent[aligned(x, half_ents), :]
    project(words, 2 * half_ents, r.cat_ents, r.bias_ents)
    r.ents_t[...] = r.x_all[words:everyone, :].T
    for h in range(heads):
        r.key[h] = r.qkv[:, h * 4 * HD + 2 * HD : h * 4 * HD + 3 * HD]
        r.value[h] = r.qkv[:, h * 4 * HD + 3 * HD : h * 4 * HD + 4 * HD]

    def both_kinds(which):
        of_words = pl.ds(pl.multiple_of(which * half_words, half_words), half_words)
        of_ents = pl.ds(pl.multiple_of(words + which * half_ents, half_ents), half_ents)
        return (of_words, slice(0, half_words)), (of_ents, slice(half_words, rows))

    def soften(start):
        def body(i, carry):
            here = pl.ds(pl.multiple_of(start + i * SOFT, SOFT), SOFT)
            bias = r.mask[here, :].astype(full)
            for h in range(heads):
                score = r.prob[h, here, :] + bias
                power = jnp.exp(score - jnp.max(score, 1, keepdims=True))
                r.prob[h, here, :] = power * (1.0 / jnp.sum(power, 1, keepdims=True))
            return carry

        return body

    def attend(which, target):
        for here, _ in both_kinds(which):
            for h in range(heads):
                query = r.qkv[here, h * 4 * HD : h * 4 * HD + 2 * HD]
                r.prob[h, here, 0:words] = dot_nt(query[:, :HD], r.key[h, 0:words, :])
                r.prob[h, here, words:] = dot_nt(query[:, HD:], r.key[h, words:everyone, :])
        lax.fori_loop(0, half_words // SOFT, soften(which * half_words), 0)
        lax.fori_loop(0, half_ents // SOFT, soften(words + which * half_ents), 0)
        for here, there in both_kinds(which):
            for h in range(heads):
                out = dot_nn(r.prob[h, here, :].astype(low), r.value[h])
                target[there, h * HD : (h + 1) * HD] = out.astype(low)

    attend(1 - x, r.heads_far)
    heads_copy = send(r.heads_far, r.heads_in, r.pair_s.at[2], r.pair_r.at[2], x_peer)
    heads_copy.start()
    attend(x, r.heads_near)
    heads_copy.wait()

    @pl.when(x == 0)
    def _():
        r.heads_all[:, 0:side] = r.heads_near[...]
        r.heads_all[:, side:] = r.heads_in[...]

    @pl.when(x == 1)
    def _():
        r.heads_all[:, 0:side] = r.heads_in[...]
        r.heads_all[:, side:] = r.heads_near[...]

    def strip(which, turn, j):
        part = (which, slice(0, rows), aligned(j, wide))
        return send(
            r.mail_out.at[part], r.mail_in.at[part], r.strip_s.at[turn, j], r.strip_r.at[turn, j], core
        )

    def wait_strips(which, turn):
        for j in range(width // wide):
            strip(which, turn, j).wait()

    def swap(which, turn, first, count):
        part = pl.ds(first, count)
        return send(
            r.mail_out.at[which, part], r.mail_in.at[which, part], r.swap_s.at[turn],
            r.swap_r.at[turn], core,
        )

    def columns(count, fill):
        def body(j, carry):
            fill(aligned(j, wide), j)
            return carry

        lax.fori_loop(0, count // wide, body, 0)

    def fill_attn(lanes, j):
        r.mail_out[0, 0:rows, lanes] = dot_nn(r.heads_all[...], r.w_out[:, lanes])
        strip(0, 0, j).start()

    loaded(r.w_out)
    columns(width, fill_attn)
    wait_strips(0, 0)

    def over_rows(body):
        def step(i, carry):
            body(aligned(i, block))
            return carry

        lax.fori_loop(0, blocks, step, 0)

    def first_norm(here):
        attn = r.mail_out[0, here, :] + r.mail_in[0, here, :] + r.b_out[...].reshape(1, -1)
        normed, scale = normalize(r.x_own[here, :] + attn)
        r.normed[here, :] = normed
        r.scale[here, :] = jnp.broadcast_to(scale, (block, 128))
        r.first[here, :] = (normed * r.gain[1:2, :] + r.shift[1:2, :]).astype(low)

    over_rows(first_norm)

    def fill_up(lanes, _):
        up = dot_nn(r.first[...], r.w_up[:, lanes]) + r.b_up[lanes].reshape(1, -1)
        chance = 0.5 + 0.5 * lax.erf(up * (0.5**0.5))
        r.act[:, lanes] = (up * chance).astype(low)
        r.slope_up[:, lanes] = chance + up * (jnp.exp(-0.5 * up * up) * (0.5 / math.pi) ** 0.5)

    loaded(r.w_up)
    columns(hidden, fill_up)

    def fill_down(lanes, j):
        r.mail_out[1, 0:rows, lanes] = dot_nn(r.act[...], r.w_down[:, lanes])
        strip(1, 1, j).start()

    loaded(r.w_down)
    columns(width, fill_down)
    wait_strips(1, 1)

    vec = r.vec.at[0]

    def second_norm(here):
        ffn = r.mail_out[1, here, :] + r.mail_in[1, here, :] + r.b_down[...].reshape(1, -1)
        entering = r.normed[here, :] * r.gain[1:2, :] + r.shift[1:2, :]
        normed, scale = normalize(entering + ffn)
        r.final[here, :] = (normed * r.gain[2:3, :] + r.shift[2:3, :]).astype(low)
        grad = r.cotangent[here, :].astype(full)
        vec[2:3, :] += row_sum(grad * normed)
        vec[5:6, :] += row_sum(grad)
        back = normalize_back(grad, normed, scale, r.gain[2:3, :])
        r.grad_second[here, :] = back
        r.grad_low[here, :] = back.astype(low)
        vec[7:8, :] += row_sum(back.astype(low).astype(full))

    loaded(cot_words)
    loaded(cot_ents)
    over_rows(second_norm)

    def halves(source, c, axis_flip):
        if axis_flip:
            return source.at[c, :, 1 - y], source.at[c, :, y]
        return source.at[c, :, :, 1 - x], source.at[c, :, :, x]

    def stage_one(kit, c, flip):
        away, _ = halves(kit.grads, c, flip)
        return send(away, kit.near.at[c], kit.s1.at[c], kit.r1.at[c], y_peer if flip else x_peer)

    def stage_two(kit, c, flip):
        away = kit.near.at[c, :, 1 - x] if flip else kit.near.at[c, :, 1 - y]
        return send(away, kit.next.at[c], kit.s2.at[c], kit.r2.at[c], x_peer if flip else y_peer)

    def stage_three(kit, c, k):
        return send(
            kit.next.at[c, lax.rem(z + k, deep)],
            kit.far.at[c, k - 1],
            kit.s3.at[c, k - 1],
            kit.r3.at[c, k - 1],
            z_peers[k - 1],
        )

    def to_two(kit, c, flip):
        stage_one(kit, c, flip).wait()
        _, own = halves(kit.grads, c, flip)

        def body(i, carry):
            kit.near[c, i] = own[i] + kit.near[c, i]
            return carry

        lax.fori_loop(0, deep, body, 0)
        stage_two(kit, c, flip).start()

    def to_three(kit, c, flip):
        stage_two(kit, c, flip).wait()
        own = kit.near.at[c, :, x] if flip else kit.near.at[c, :, y]

        def body(i, carry):
            kit.next[c, i] = own[i] + kit.next[c, i]
            return carry

        lax.fori_loop(0, deep, body, 0)
        for k in range(1, deep):
            stage_three(kit, c, k).start()

    def finish(kit, c):
        for k in range(1, deep):
            stage_three(kit, c, k).wait()
        total = kit.next[c, z].astype(full)
        for k in range(1, deep):
            total = total + kit.far[c, k - 1].astype(full)
        kit.out[c] = total

    kit_a = types.SimpleNamespace(
        grads=r.grads, near=r.near, next=r.next, far=r.far, out=r.out_a,
        s1=r.a_s1, r1=r.a_r1, s2=r.a_s2, r2=r.a_r2, s3=r.a_s3, r3=r.a_r3,
    )
    kit_e = types.SimpleNamespace(
        grads=r.e_grads, near=r.e_near, next=r.e_next, far=r.e_far, out=r.e_sum,
        s1=r.e_s1, r1=r.e_r1, s2=r.e_s2, r2=r.e_r2, s3=r.e_s3, r3=r.e_r3,
    )

    def head_one(h):
        return send(r.q_grads.at[h, :, 1 - y], r.q_near.at[h], r.q_s1.at[h], r.q_r1.at[h], y_peer)

    def head_two(h, k):
        return send(
            r.q_near.at[h, lax.rem(z + k, deep)],
            r.q_far.at[h, k - 1],
            r.q_s2.at[h, k - 1],
            r.q_r2.at[h, k - 1],
            z_peers[k - 1],
        )

    def head_three(h):
        return send(r.q_sum.at[h, 1 - x], r.q_in.at[h], r.q_s3.at[h], r.q_r3.at[h], x_peer)

    def head_to_two(h):
        head_one(h).wait()

        def body(i, carry):
            r.q_near[h, i] = r.q_grads[h, i, y] + r.q_near[h, i]
            return carry

        lax.fori_loop(0, deep, body, 0)
        for k in range(1, deep):
            head_two(h, k).start()

    def head_to_three(h):
        for k in range(1, deep):
            head_two(h, k).wait()
        total = r.q_near[h, z].astype(full)
        for k in range(1, deep):
            total = total + r.q_far[h, k - 1].astype(full)
        r.q_sum[h] = total
        head_three(h).start()
        r.out_q[h, x] = r.q_sum[h, x]

    def head_finish(h):
        head_three(h).wait()
        r.out_q[h, 1 - x] = r.q_in[h]

    band = 4 * share
    chunk = r.grads.shape[5]

    def make_grad(c, left_t, right, lanes):
        part = dot_nn(left_t[...], right[:, lanes]).astype(low)
        r.grads[c] = part.reshape(deep, 2, 2, share, chunk)

    plan = iter(schedule)

    def vec_copy(n):
        peer = x_peer if n == 0 else y_peer if n == 1 else z_peers[n - 2]
        return send(r.vec.at[min(n, 2)], r.vec_in.at[n], r.vec_s.at[n], r.vec_r.at[n], peer)

    def act_on(events):
        for kind, c in events:
            if kind == BEGIN:
                stage_one(kit_a, c, flips[c]).start()
            if kind == TURN:
                to_two(kit_a, c, flips[c])
            if kind == CLIMB:
                to_three(kit_a, c, flips[c])
            if kind == HEAD_CLIMB:
                head_to_two(c)
            if kind == HEAD_MEET:
                head_to_three(c)
            if kind == ENTS_TURN:
                to_two(kit_e, 0, False)
            if kind == ENTS_CLIMB:
                to_three(kit_e, 0, False)
            if kind == VEC_TURN:
                vec_copy(0).wait()
                r.vec[1] = r.vec[0] + r.vec_in[0]
                vec_copy(1).start()
            if kind == VEC_CLIMB:
                vec_copy(1).wait()
                r.vec[2] = r.vec[1] + r.vec_in[1]
                for k in range(1, deep):
                    vec_copy(1 + k).start()

    def tick():
        act_on(next(plan))

    downs = hidden // chunk
    r.grad_t[...] = r.grad_low[...].T
    for c in range(downs):
        make_grad(c, r.grad_t, r.act, slice(c * chunk, (c + 1) * chunk))
        tick()

    def fill_dup(lanes, j):
        grad_act = dot_nt(r.grad_low[...], r.w_down[lanes, :])
        grad_up = (grad_act * r.slope_up[:, lanes]).astype(low)
        r.grad_up[:, lanes] = grad_up
        vec[pl.ds(8 + j // (width // wide), 1), aligned(lax.rem(j, width // wide), wide)] = row_sum(
            grad_up.astype(full)
        )

    columns(hidden, fill_dup)
    tick()

    def fill_back(lanes, j):
        r.mail_out[0, 0:rows, lanes] = dot_nt(r.grad_up[...], r.w_up[lanes, :])
        strip(0, 2, j).start()

    columns(width, fill_back)
    tick()
    r.first_t[...] = r.first[...].T
    r.out_words[...] = r.final[pl.ds(pl.multiple_of(t * (half_words // 2), half_words // 2), half_words // 2), :]
    r.out_ents[...] = r.final[
        pl.ds(pl.multiple_of(half_words + t * (half_ents // 2), half_ents // 2), half_ents // 2), :
    ]
    for c in range(downs):
        make_grad(downs + c, r.first_t, r.grad_up, slice(c * chunk, (c + 1) * chunk))
        tick()
    wait_strips(0, 2)

    def first_back(here):
        grad = r.grad_second[here, :] + r.mail_out[0, here, :] + r.mail_in[0, here, :]
        normed = r.normed[here, :]
        vec[1:2, :] += row_sum(grad * normed)
        vec[4:5, :] += row_sum(grad)
        back = normalize_back(grad, normed, r.scale[here, 0:1], r.gain[1:2, :])
        r.grad_first[here, :] = back
        r.grad_low[here, :] = back.astype(low)
        vec[6:7, :] += row_sum(back.astype(low).astype(full))

    over_rows(first_back)
    tick()
    near_rows = aligned(x, side)
    far_rows = aligned(1 - x, side)
    r.back_far[...] = dot_nt(r.grad_low[...], r.w_out[far_rows, :]).astype(low)
    mine = [(aligned(x, half_words), 0, half_words)]
    mine.append((pl.ds(pl.multiple_of(words + x * half_ents, half_ents), half_ents), half_words, half_ents))
    back_copies = [
        send(
            r.back_far.at[pl.ds(first, count), :], r.back_heads.at[place, :],
            r.pair_s.at[3 + n], r.pair_r.at[3 + n], x_peer,
        )
        for n, (place, first, count) in enumerate(mine)
    ]
    for copy in back_copies:
        copy.start()
    near = dot_nt(r.grad_low[...], r.w_out[near_rows, :]).astype(low)
    for place, first, count in mine:
        r.back_heads[place, :] = near[first : first + count, :]
    r.grad_t[...] = r.grad_low[...].T
    outs = 2 * downs
    make_grad(outs, r.grad_t, r.heads_all, slice(0, chunk))
    tick()


    pair = 2 * HD
    for h in range(heads):
        base = h * 4 * HD

        def score_back(start):
            def body(i, carry):
                here = pl.ds(pl.multiple_of(start + i * SOFT, SOFT), SOFT)
                prob, grad_prob = r.prob[h, here, :], r.grad_prob[here, :]
                inner = jnp.sum(prob * grad_prob, 1, keepdims=True)
                r.grad_score[here, :] = (prob * (grad_prob - inner)).astype(low)
                r.prob_low[here, :] = prob.astype(low)
                return carry

            return body

        for which in (x, 1 - x):
            if which is not x:
                tick()
            if h == 0 and which is not x:
                for copy in back_copies:
                    copy.wait()
            for here, _ in both_kinds(which):
                r.grad_prob[here, :] = dot_nt(r.back_heads[here, h * HD : (h + 1) * HD], r.value[h])
            lax.fori_loop(0, half_words // SOFT, score_back(which * half_words), 0)
            lax.fori_loop(0, half_ents // SOFT, score_back(words + which * half_ents), 0)
        queries = jnp.concatenate(
            [
                dot_nn(r.grad_score[:, :words], r.key[h, 0:words, :]),
                dot_nn(r.grad_score[:, words:], r.key[h, words:everyone, :]),
            ],
            1,
        )
        r.grad_qkv[:, base : base + pair] = (queries * score_scale).astype(low)
        tick()
        query_t = r.qkv[:, base : base + pair].T
        keys_t = dot_nn(query_t, r.grad_score[...])
        keys_t = jnp.concatenate([keys_t[:HD, :words], keys_t[HD:, words:]], 1)
        values_t = dot_nn(r.back_heads[:, h * HD : (h + 1) * HD].T, r.prob_low[...])
        r.grad_qkv[:, base + pair : base + 2 * pair] = (
            jnp.concatenate([keys_t, values_t], 0).T.astype(low)
        )

        tick()
        keyval = slice(base + pair, base + 2 * pair)
        query = slice(base, base + pair)
        of_words = dot_nn(r.words_t[...], r.grad_qkv[0:words, query])
        of_ents = dot_nn(r.ents_t[...], r.grad_qkv[words:everyone, query])
        of_keyval = dot_nn(r.words_t[...], r.grad_qkv[0:words, keyval])
        of_keyval = of_keyval + dot_nn(r.ents_t[...], r.grad_qkv[words:everyone, keyval])
        for n, part in enumerate([of_words, of_ents, of_keyval]):
            r.q_grads[h, :, :, :, :, n * pair : (n + 1) * pair] = part.astype(low).reshape(
                deep, 2, 2, share, pair
            )
        head_one(h).start()
        sums = jnp.concatenate(
            [
                row_sum(r.grad_qkv[0:words, base : base + pair].astype(full)),
                row_sum(r.grad_qkv[words:everyone, base : base + pair].astype(full)),
                row_sum(r.grad_qkv[:, base + pair : base + 2 * pair].astype(full)),
            ],
            1,
        )
        place = h * 3 * pair
        vec[pl.ds(10 + 2 * x + place // width, 1), place % width : place % width + 3 * pair] = sums
        tick()

    quarter = half_words // 2

    def input_grad(place, weight):
        return dot_nt(r.grad_qkv[place, :], weight[...])

    ents_part = input_grad(slice(words, everyone), r.cat_ents)
    r.mail_out[1, words // 2 :, :] = ents_part
    ents_swap = swap(1, 0, words // 2, 2 * half_ents)
    ents_swap.start()
    tick()
    for n in range(2):
        r.mail_out[1, n * quarter : (n + 1) * quarter, :] = input_grad(
            aligned(2 * n + 1 - t, quarter), r.cat_words
        )
    words_swap = swap(1, 1, 0, words // 2)
    words_swap.start()
    for n in range(2):
        r.input_part[n] = input_grad(aligned(2 * n + t, quarter), r.cat_words)
    tick()
    ents_swap.wait()
    ents_place = pl.multiple_of(words // 2 + (1 - x) * half_ents, half_ents)
    ents_far = pl.ds(ents_place, half_ents)
    ents_near = pl.ds(pl.multiple_of(words // 2 + x * half_ents, half_ents), half_ents)
    r.ents_back[...] = (r.mail_out[1, ents_far, :] + r.mail_in[1, ents_far, :]).astype(low)
    ents_copy = send(r.ents_back, r.ents_in, r.pair_s.at[5], r.pair_r.at[5], x_peer)
    ents_copy.start()
    tick()
    words_swap.wait()
    far_place = aligned(1 - x, quarter)
    r.words_back[...] = (r.input_part[1 - x] + r.mail_in[1, far_place, :]).astype(low)
    words_back_copy = send(r.words_back, r.words_in, r.pair_s.at[6], r.pair_r.at[6], x_peer)
    words_back_copy.start()
    tick()
    ents_copy.wait()

    grad = r.grad_first[half_words:rows, :] + (r.mail_out[1, ents_near, :] + r.mail_in[1, ents_near, :])
    grad = grad + r.ents_in[...].astype(full)
    own_ents = aligned(x, half_ents)
    normed, scale = normalize(r.ent_lin[own_ents, :])
    vec[0:1, :] = row_sum(grad * normed)
    vec[3:4, :] = row_sum(grad)
    lin_low = normalize_back(grad, normed, scale, r.gain[0:1, :]).astype(low)
    slope = dot_nt(lin_low, r.w_entity[...]).astype(low)
    r.slope[...] = dot_nn(r.outbox[...], slope).reshape(owners, capacity, -1)
    r.slopes[flat] = r.slope[flat]
    for k in range(owners - 1):
        slope_copy(k).start()
    looked_half = r.looked[own_ents, aligned(t, 128)]
    r.ents_grad[...] = dot_tn(lin_low, looked_half).astype(low)

    def ents_body(i, carry):
        r.e_grads[0, i] = r.ents_grad[aligned(i, band), :].reshape(2, 2, share, 128)
        return carry

    lax.fori_loop(0, deep, ents_body, 0)
    stage_one(kit_e, 0, False).start()
    vec_copy(0).start()
    words_back_copy.wait()
    r.grad_words[...] = (
        r.grad_first[aligned(t, quarter), :]
        + (r.input_part[x] + r.mail_in[1, aligned(x, quarter), :])
        + r.words_in[...].astype(full)
    )
    tick()
    for k in range(owners - 1):
        slope_copy(k).wait()
    ids_t = r.asked[...].reshape(slots, 128).astype(full).T
    r.ids_out[...] = ids_t[0:8, :].astype(jnp.int32)
    r.slopes_out[...] = r.slopes[...].reshape(slots, -1).astype(low)
    for c in range(2 * downs + 1):
        finish(kit_a, c)
    total = r.vec[2]
    for k in range(1, deep):
        vec_copy(1 + k).wait()
        total = total + r.vec_in[1 + k]
    r.vec_out[...] = total
    r.across_out[...] = pltpu.roll(total[0:8, :], width - flat * share, 1)[:, 0:128]
    finish(kit_e, 0)
    ents_out = send(r.e_sum.at[0], r.e_in, r.pair_s.at[7], r.pair_r.at[7], core)
    ents_out.start()
    r.out_e[t] = r.e_sum[0]
    for h in range(heads):
        head_finish(h)
    ents_out.wait()
    r.out_e[1 - t] = r.e_in[...]


def finish_kernel(names, *refs):
    r = types.SimpleNamespace(**dict(zip(names, refs, strict=True)))
    low, full = jnp.bfloat16, jnp.float32
    table_rows, embed = r.hbm_first.shape
    slots = r.hbm_ids.shape[1]
    steps = r.in_s.shape[1]
    count = table_rows // steps
    chunks, share, chunk = r.hbm_a.shape
    downs = chunks // 2
    heads, side = r.hbm_q.shape[0], r.hbm_q.shape[0] * HD

    pairs = [(r.hbm_ids, r.ids), (r.hbm_slopes, r.slopes)]
    pairs += [(r.hbm_q, r.out_q), (r.hbm_e, r.out_e), (r.hbm_vec, r.vec), (r.hbm_across, r.across)]
    layers = [(r.hbm_a.at[2 * downs], r.out_part)]
    for c in range(downs):
        lanes = slice(c * chunk, (c + 1) * chunk)
        layers.append((r.hbm_a.at[c], r.down_part.at[:, lanes]))
        layers.append((r.hbm_a.at[downs + c], r.up_part.at[:, lanes]))
    layers += [(r.hbm_words, r.words_part), (r.hbm_ents, r.ents_part), (r.hbm_grad, r.grad_part)]
    smalls = [
        pltpu.make_async_copy(source, target, r.small_s.at[n])
        for n, (source, target) in enumerate(pairs + layers)
    ]
    outs = [
        pltpu.make_async_copy(source, target, r.done_s.at[n])
        for n, (source, target) in enumerate(
            [
                (r.out_part, r.red_out),
                (r.down_part, r.red_down),
                (r.up_part, r.red_up),
                (r.words_part, r.words_done.at[0]),
                (r.ents_part, r.ents_done.at[0]),
                (r.grad_part, r.grad_words_done.at[0]),
                (r.query_part, r.red_query),
                (r.keyval_part, r.red_keyval),
            ]
        )
    ]

    def moves(i, inward):
        here = pl.ds(i * count, count)
        if inward:
            ends = [(r.hbm_first, r.first), (r.hbm_second, r.second)]
            flags = r.in_s
        else:
            ends = [(r.update, r.table_update), (r.first, r.new_first), (r.second, r.new_second)]
            flags = r.out_s
        return [
            pltpu.make_async_copy(source.at[here, :], target.at[here, :], flags.at[n, i])
            for n, (source, target) in enumerate(ends)
        ]

    early, late = smalls[:2], smalls[2:]
    for copy in early + moves(0, True) + moves(1, True) + late:
        copy.start()
    for i in range(2, steps):
        for copy in moves(i, True):
            copy.start()
    for copy in early:
        copy.wait()
    r.addends[:, 0:embed] = r.slopes[...]
    r.addends[:, embed:] = jnp.ones((slots, 128), low)

    def adam(i):
        for copy in moves(i, True):
            copy.wait()
        here = pl.ds(i * count, count)
        row = lax.broadcasted_iota(jnp.int32, (count, slots), 0) + i * count
        chosen = jnp.where(row == r.ids[0:1, :], 1.0, 0.0).astype(low)
        total = dot_nn(chosen, r.addends[...])
        touched = total[:, embed:] > 0.0
        for start in range(0, embed, 128):
            lanes = slice(start, start + 128)
            grad = total[:, lanes]
            first, second = r.first[here, lanes], r.second[here, lanes]
            first_next = beta_one * first + (1.0 - beta_one) * grad
            second_next = beta_two * second + (1.0 - beta_two) * grad * grad
            direction = (
                first_next
                * (1.0 / (1.0 - beta_one**adam_steps))
                / (jnp.sqrt(second_next * (1.0 / (1.0 - beta_two**adam_steps))) + adam_eps)
            )
            r.update[here, lanes] = jnp.where(touched, direction, 0.0)
            r.first[here, lanes] = jnp.where(touched, first_next, first)
            r.second[here, lanes] = jnp.where(touched, second_next, second)
        for copy in moves(i, False):
            copy.start()

    def lay_out_rest():
        for copy in late:
            copy.wait()
        for copy in outs[:6]:
            copy.start()
        width = r.vec.shape[1]
        for n in range(2):
            r.red_entity[:, n * 128 : (n + 1) * 128] = r.out_e[n]
            for h in range(heads):
                place = h * 6 * HD
                line = 10 + 2 * n + place // width
                for j in range(6):
                    lanes = slice(n * side + h * HD, n * side + (h + 1) * HD)
                    part = r.out_q[h, n, :, j * HD : (j + 1) * HD]
                    begin = place % width + j * HD
                    line_part = r.vec[line : line + 1, begin : begin + HD]
                    if j < 4:
                        r.query_part[j, :, lanes] = part
                        r.red_query_bias[j : j + 1, lanes] = line_part
                    else:
                        r.keyval_part[j - 4, :, lanes] = part
                    if j == 5:
                        r.value_row[:, lanes] = line_part
        for copy in outs[6:]:
            copy.start()
        r.red_gain[...] = r.across[0:3, 0:share]
        r.red_shift[...] = r.across[3:6, 0:share]
        r.red_value_bias[...] = r.value_row[...].reshape(-1)
        r.red_out_bias[...] = r.across[6:7, 0:share].reshape(-1)
        r.red_down_bias[...] = r.across[7:8, 0:share].reshape(-1)
        for n in range(2):
            r.red_up_bias[n * width : (n + 1) * width] = r.vec[8 + n : 9 + n, :].reshape(-1)

    for i in range(steps):
        adam(i)
        if i == steps // 2:
            lay_out_rest()
    for i in range(steps):
        for copy in moves(i, False):
            copy.wait()
    for copy in outs:
        copy.wait()


SOFT = 32
STEPS = 8
BEGIN, TURN, CLIMB, HEAD_CLIMB, HEAD_MEET, ENTS_TURN, ENTS_CLIMB, VEC_TURN, VEC_CLIMB = range(9)
SCHEDULE = (
    ((BEGIN, 0),),
    (),
    ((BEGIN, 2),),
    (),
    (),
    (),
    (),
    ((BEGIN, 5),),
    (),
    ((BEGIN, 7),),
    ((TURN, 0),),
    ((TURN, 7), (BEGIN, 8),),
    ((BEGIN, 1), (TURN, 5),),
    (),
    ((CLIMB, 0),),
    ((CLIMB, 7),),
    (),
    (),
    ((BEGIN, 4),),
    ((CLIMB, 5),),
    ((TURN, 8),),
    ((HEAD_CLIMB, 0),),
    (),
    (),
    ((HEAD_CLIMB, 1),),
    ((TURN, 2), (BEGIN, 3), (TURN, 4), (BEGIN, 6),),
    ((CLIMB, 8), (HEAD_CLIMB, 2),),
    ((CLIMB, 4), (TURN, 1), (TURN, 3), (CLIMB, 2),),
    ((HEAD_MEET, 0), (TURN, 6), (CLIMB, 1), (ENTS_TURN, 0), (VEC_TURN, 0), (CLIMB, 3), (CLIMB, 6), (HEAD_MEET, 1), (HEAD_MEET, 2), (ENTS_CLIMB, 0), (VEC_CLIMB, 0),),
)
FLIPS = (False, False, True, False, False, False, True, True, False)


def fused_local(
    word_states,
    entity_shard,
    entity_row,
    word_segments,
    entity_segments,
    entity_table,
    adam_first,
    adam_second,
    w_entity,
    norm_gain,
    norm_bias,
    w_query,
    b_query,
    w_keyval,
    b_value,
    w_out,
    b_out,
    w_up,
    b_up,
    w_down,
    b_down,
    cot_words,
    cot_entities,
):
    low, full = jnp.bfloat16, jnp.float32
    _, half_words, width = word_states.shape
    half_ents = entity_row.shape[2]
    rows, everyone = half_words + half_ents, 2 * (half_words + half_ents)
    words, ents = 2 * half_words, 2 * half_ents
    table_rows, embed = entity_table.shape
    local_width, hidden = w_query.shape[2], w_up.shape[1]
    owners = lax.axis_size(("dp", "stream"))
    deep = lax.axis_size("dp") // 2
    share = width // owners
    capacity = 2 * half_ents // owners
    side = local_width // 2
    heads = side // HD
    chunk = local_width
    chunks = 2 * (hidden // chunk) + 1

    operands = dict(
        shard=entity_shard.reshape(1, half_ents),
        row=entity_row.reshape(1, half_ents),
        word_seg=word_segments,
        ent_seg=entity_segments,
        gain=norm_gain,
        shift=norm_bias,
        b_query=b_query,
        b_value=b_value,
        b_out=b_out,
        b_up=b_up,
        b_down=b_down,
    )
    streamed = dict(
        hbm_words=word_states,
        hbm_cot_words=cot_words,
        hbm_cot_ents=cot_entities,
        hbm_query=w_query,
        hbm_keyval=w_keyval,
        hbm_table=entity_table,
        hbm_entity=w_entity,
        hbm_out=w_out,
        hbm_up=w_up,
        hbm_down=w_down,
    )
    results = dict(
        out_words=((half_words // 2, width), low),
        out_ents=((half_ents // 2, width), low),
        grad_words=((half_words // 2, width), full),
        out_a=((chunks, share, chunk), full),
        out_e=((2, share, 128), full),
        out_q=((heads, 2, share, chunk), full),
        vec_out=((16, width), full),
        across_out=((8, 128), full),
        ids_out=((8, owners * capacity), jnp.int32),
        slopes_out=((owners * capacity, embed), low),
    )
    mail_rows = max(rows, words // 2 + ents)
    dma = pltpu.SemaphoreType.DMA
    scratch = dict(
        w_query=(w_query.shape, low),
        w_keyval=(w_keyval.shape, low),
        table=(entity_table.shape, low),
        w_entity=(w_entity.shape, low),
        w_out=(w_out.shape, low),
        w_up=(w_up.shape, low),
        w_down=(w_down.shape, low),
        cat_words=((width, 4 * side), low),
        cat_ents=((width, 4 * side), low),
        bias_words=((1, 4 * side), full),
        bias_ents=((1, 4 * side), full),
        cotangent=((rows, width), low),
        ask=((owners, capacity, 128), jnp.int32),
        asked=((owners, capacity, 128), jnp.int32),
        outbox=((owners * capacity, half_ents), low),
        select=((ents, owners * 2 * capacity), low),
        found=((owners // 2, 2 * capacity, embed), low),
        answer=((owners, 2 * capacity, embed), low),
        looked=((ents, embed), low),
        ent_lin=((ents, width), full),
        x_ent=((ents, width), full),
        x_all=((everyone, width), low),
        x_own=((rows, width), full),
        words_t=((width, words), low),
        ents_t=((width, ents), low),
        mask=((everyone, everyone), low),
        qkv=((everyone, 4 * side), low),
        key=((heads, everyone, HD), low),
        value=((heads, everyone, HD), low),
        prob=((heads, everyone, everyone), full),
        heads_far=((rows, side), low),
        heads_near=((rows, side), low),
        heads_in=((rows, side), low),
        heads_all=((rows, 2 * side), low),
        mail_out=((2, mail_rows, width), full),
        mail_in=((2, mail_rows, width), full),
        normed=((rows, width), full),
        scale=((rows, 128), full),
        first=((rows, width), low),
        first_t=((width, rows), low),
        act=((rows, hidden), low),
        slope_up=((rows, hidden), full),
        final=((rows, width), low),
        grad_second=((rows, width), full),
        grad_low=((rows, width), low),
        grad_t=((width, rows), low),
        grad_up=((rows, hidden), low),
        grad_first=((rows, width), full),
        back_far=((rows, side), low),
        back_heads=((everyone, side), low),
        grad_prob=((everyone, everyone), full),
        grad_score=((everyone, everyone), low),
        prob_low=((everyone, everyone), low),
        grad_qkv=((everyone, 4 * side), low),
        input_part=((2, half_words // 2, width), full),
        ents_back=((half_ents, width), low),
        ents_in=((half_ents, width), low),
        words_back=((half_words // 2, width), low),
        words_in=((half_words // 2, width), low),
        slope=((owners, capacity, embed), full),
        slopes=((owners, capacity, embed), full),
        ents_grad=((width, 128), low),
        e_sum=((1, share, 128), full),
        e_in=((share, 128), full),
        vec=((3, 16, width), full),
        vec_in=((deep + 1, 16, width), full),
        grads=((chunks, deep, 2, 2, share, chunk), low),
        near=((chunks, deep, 2, share, chunk), low),
        next=((chunks, deep, share, chunk), low),
        far=((chunks, deep - 1, share, chunk), low),
        e_grads=((1, deep, 2, 2, share, 128), low),
        e_near=((1, deep, 2, share, 128), low),
        e_next=((1, deep, share, 128), low),
        e_far=((1, deep - 1, share, 128), low),
        q_grads=((heads, deep, 2, 2, share, chunk), low),
        q_near=((heads, deep, 2, share, chunk), low),
        q_far=((heads, deep - 1, 2, share, chunk), low),
        q_sum=((heads, 2, share, chunk), full),
        q_in=((heads, share, chunk), full),
    )
    signals = dict(
        load_s=(10,),
        ask_s=(owners - 1,),
        ask_r=(owners - 1,),
        answer_s=(owners - 1,),
        answer_r=(owners - 1,),
        slope_s=(owners - 1,),
        slope_r=(owners - 1,),
        pair_s=(8,),
        pair_r=(8,),
        strip_s=(3, width // 256),
        strip_r=(3, width // 256),
        swap_s=(2,),
        swap_r=(2,),
        vec_s=(deep + 1,),
        vec_r=(deep + 1,),
    )
    one, many = (1,), (1, deep - 1)
    signals.update(e_s1=one, e_r1=one, e_s2=one, e_r2=one, e_s3=many, e_r3=many)
    one, many = (chunks,), (chunks, deep - 1)
    signals.update(a_s1=one, a_r1=one, a_s2=one, a_r2=one, a_s3=many, a_r3=many)
    one, many = (heads,), (heads, deep - 1)
    signals.update(q_s1=one, q_r1=one, q_s2=many, q_r2=many, q_s3=one, q_r3=one)
    names = [*operands, *streamed, *results, *scratch, *signals]
    kernel = functools.partial(layer_kernel, names, FLIPS, SCHEDULE)
    made = pl.pallas_call(
        kernel,
        name="layer",
        out_shape=[jax.ShapeDtypeStruct(*item) for item in results.values()],
        in_specs=[pl.BlockSpec(memory_space=pltpu.VMEM)] * len(operands)
        + [pl.BlockSpec(memory_space=pl.ANY)] * len(streamed),
        out_specs=[pl.BlockSpec(memory_space=pltpu.VMEM)] * len(results),
        scratch_shapes=[pltpu.VMEM(*item) for item in scratch.values()]
        + [dma(shape) for shape in signals.values()],
        compiler_params=pltpu.CompilerParams(
            collective_id=0, has_side_effects=True, vmem_limit_bytes=67_043_328
        ),
    )(*operands.values(), *streamed.values())
    got = types.SimpleNamespace(**dict(zip(results, made, strict=True)))

    given = dict(
        hbm_first=adam_first,
        hbm_second=adam_second,
        hbm_ids=got.ids_out,
        hbm_slopes=got.slopes_out,
        hbm_a=got.out_a,
        hbm_e=got.out_e,
        hbm_q=got.out_q,
        hbm_vec=got.vec_out,
        hbm_across=got.across_out,
        hbm_words=got.out_words,
        hbm_ents=got.out_ents,
        hbm_grad=got.grad_words,
    )
    final = dict(
        words_done=(1, half_words // 2, width),
        ents_done=(1, half_ents // 2, width),
        grad_words_done=(1, half_words // 2, width),
        red_entity=(share, embed),
        red_gain=(3, share),
        red_shift=(3, share),
        red_query=(4, share, local_width),
        red_query_bias=(4, local_width),
        red_keyval=(2, share, local_width),
        red_value_bias=(local_width,),
        red_out=(share, local_width),
        red_out_bias=(share,),
        red_up=(share, hidden),
        red_up_bias=(hidden,),
        red_down=(share, hidden),
        red_down_bias=(share,),
        table_update=adam_first.shape,
        new_first=adam_first.shape,
        new_second=adam_first.shape,
    )
    room = dict(
        value_row=((1, local_width), full),
        ids=(got.ids_out.shape, jnp.int32),
        slopes=(got.slopes_out.shape, low),
        addends=((owners * capacity, embed + 128), low),
        out_e=(got.out_e.shape, full),
        out_q=(got.out_q.shape, full),
        vec=(got.vec_out.shape, full),
        across=(got.across_out.shape, full),
        first=(adam_first.shape, full),
        second=(adam_first.shape, full),
        update=(adam_first.shape, full),
        out_part=((share, local_width), full),
        down_part=((share, hidden), full),
        up_part=((share, hidden), full),
        words_part=(got.out_words.shape, low),
        ents_part=(got.out_ents.shape, low),
        grad_part=(got.grad_words.shape, full),
        query_part=((4, share, local_width), full),
        keyval_part=((2, share, local_width), full),
    )
    flags = dict(small_s=(chunks + 9,), done_s=(8,), in_s=(2, STEPS), out_s=(3, STEPS))
    in_place, in_vmem = (pl.BlockSpec(memory_space=space) for space in (pl.ANY, pltpu.VMEM))
    manual = set(dict(words_done=0, ents_done=0, grad_words_done=0, red_query=0, red_keyval=0))
    manual |= set(dict(red_out=0, red_up=0, red_down=0, table_update=0, new_first=0, new_second=0))
    finished = pl.pallas_call(
        functools.partial(finish_kernel, [*given, *final, *room, *flags]),
        name="finish",
        out_shape=[
            jax.ShapeDtypeStruct(shape, low if n < 2 else full)
            for n, shape in enumerate(final.values())
        ],
        in_specs=[in_place] * len(given),
        out_specs=[in_place if name in manual else in_vmem for name in final],
        scratch_shapes=[pltpu.VMEM(*item) for item in room.values()]
        + [dma(shape) for shape in flags.values()],
        compiler_params=pltpu.CompilerParams(vmem_limit_bytes=67_043_328),
    )(*given.values())
    done = dict(zip(final, finished, strict=True))
    return tuple(
        item.T if name in ("red_entity", "red_out", "red_down") else item
        for name, item in done.items()
    )


def plain_local(
    word_states,
    entity_shard,
    entity_row,
    word_segments,
    entity_segments,
    entity_table,
    adam_first,
    adam_second,
    w_entity,
    norm_gain,
    norm_bias,
    w_query,
    b_query,
    w_keyval,
    b_value,
    w_out,
    b_out,
    w_up,
    b_up,
    w_down,
    b_down,
    cot_words,
    cot_entities,
):
    seq_count, half_words, width = word_states.shape
    half_ents = entity_row.shape[2]
    table_rows, embed_width = entity_table.shape
    local_width = w_query.shape[2]
    local_heads = local_width // HD
    owners = lax.axis_size(("dp", "stream"))
    stream_index = lax.axis_index("stream")
    parts = lax.axis_size("tensor")
    part_index = lax.axis_index("tensor")
    word_part = half_words // parts
    ent_part = half_ents // parts
    ent_count = seq_count * half_ents
    word_count = seq_count * half_words
    local_rows = half_words + half_ents
    share_words = seq_count * word_part
    owner_flat = entity_shard.reshape(ent_count)
    row_flat = entity_row.reshape(ent_count)

    def pick(block, count):
        shaped = block.reshape(seq_count, parts, count // parts, block.shape[-1])
        return lax.dynamic_index_in_dim(shaped, part_index, 1, keepdims=False).reshape(
            seq_count * (count // parts), block.shape[-1]
        )

    def own_share(rows):
        return jnp.concatenate(
            [pick(rows[:word_count], half_words), pick(rows[word_count:], half_ents)], 0
        )

    capacity = 2 * ent_count // owners
    owner_hits = (owner_flat[:, None] == jnp.arange(owners, dtype=jnp.int32)[None, :]).astype(
        jnp.int32
    )
    before = jnp.cumsum(owner_hits, 0) - owner_hits
    ranking = jnp.sum(before * owner_hits, 1)
    slot_index = owner_flat * capacity + ranking
    request = (
        jnp.full((owners * capacity,), -1, jnp.int32)
        .at[slot_index]
        .set(row_flat)
        .reshape(owners, capacity)
    )
    asked_ids = lax.all_to_all(request, ("dp", "stream"), split_axis=0, concat_axis=0, tiled=True)
    present = asked_ids >= 0
    found_rows = jnp.take(entity_table, jnp.clip(asked_ids, 0, table_rows - 1), axis=0)
    found_rows = jnp.where(present[..., None], found_rows, jnp.zeros_like(found_rows))
    found_rows, asked_rows = (found_rows, asked_ids)
    answered = lax.all_to_all(found_rows, ("dp", "stream"), split_axis=0, concat_axis=0, tiled=True)
    looked = answered.reshape(owners * capacity, embed_width)[slot_index]
    ent_lin = matmul(looked, w_entity)
    x_entity, entity_norm_back = jax.vjp(layer_norm, ent_lin, norm_gain[0], norm_bias[0])
    entity_low = x_entity.astype(jnp.bfloat16)
    word_low = word_states.reshape(word_count, width)
    query_words = (
        jnp.einsum("rd,jdc->jrc", word_low, w_query[:2], preferred_element_type=jnp.float32)
        + b_query[:2, None, :]
    ).astype(jnp.bfloat16)
    query_ents = (
        jnp.einsum("rd,jdc->jrc", entity_low, w_query[2:], preferred_element_type=jnp.float32)
        + b_query[2:, None, :]
    ).astype(jnp.bfloat16)
    value_shift = jnp.stack([jnp.zeros_like(b_value), b_value])[:, None, :]
    keyval_words = (
        jnp.einsum("rd,jdc->jrc", word_low, w_keyval, preferred_element_type=jnp.float32)
        + value_shift
    ).astype(jnp.bfloat16)
    keyval_ents = (
        jnp.einsum("rd,jdc->jrc", entity_low, w_keyval, preferred_element_type=jnp.float32)
        + value_shift
    ).astype(jnp.bfloat16)
    far_words, far_ents = from_partner((keyval_words, keyval_ents), "stream", 0)

    def by_heads(block, count):
        return block.reshape(block.shape[0], seq_count, count, local_heads, HD)

    queries = jnp.concatenate(
        [by_heads(query_words, half_words), by_heads(query_ents, half_ents)], 2
    )
    keyval_w = jnp.concatenate(
        [by_heads(keyval_words, half_words), by_heads(far_words, half_words)], 2
    )
    keyval_e = jnp.concatenate([by_heads(keyval_ents, half_ents), by_heads(far_ents, half_ents)], 2)
    own_wseg = lax.dynamic_slice_in_dim(word_segments, stream_index * half_words, half_words, 1)
    far_wseg = lax.dynamic_slice_in_dim(
        word_segments, (1 - stream_index) * half_words, half_words, 1
    )
    own_eseg = lax.dynamic_slice_in_dim(entity_segments, stream_index * half_ents, half_ents, 1)
    far_eseg = lax.dynamic_slice_in_dim(
        entity_segments, (1 - stream_index) * half_ents, half_ents, 1
    )
    query_seg = jnp.concatenate([own_wseg, own_eseg], 1)
    key_wseg = jnp.concatenate([own_wseg, far_wseg], 1)
    key_eseg = jnp.concatenate([own_eseg, far_eseg], 1)
    allow_words = query_seg[:, None, :, None] == key_wseg[:, None, None, :]
    allow_ents = query_seg[:, None, :, None] == key_eseg[:, None, None, :]

    def scores_of():
        raw_words = (
            jnp.einsum(
                "sqhd,skhd->shqk", queries[0], keyval_w[0], preferred_element_type=jnp.float32
            )
            * score_scale
        )
        raw_ents = (
            jnp.einsum(
                "sqhd,skhd->shqk", queries[1], keyval_e[0], preferred_element_type=jnp.float32
            )
            * score_scale
        )
        return (
            jnp.where(allow_words, raw_words, masked_score),
            jnp.where(allow_ents, raw_ents, masked_score),
        )

    score_words, score_ents = scores_of()
    highest = jnp.maximum(
        jnp.max(score_words, -1, keepdims=True), jnp.max(score_ents, -1, keepdims=True)
    )
    totals = jnp.sum(jnp.exp(score_words - highest), -1, keepdims=True) + jnp.sum(
        jnp.exp(score_ents - highest), -1, keepdims=True
    )
    log_total = highest + jnp.log(totals)
    low_words = jnp.exp(score_words - log_total).astype(jnp.bfloat16)
    low_ents = jnp.exp(score_ents - log_total).astype(jnp.bfloat16)
    heads_out = jnp.einsum(
        "shqk,skhd->sqhd", low_words, keyval_w[1], preferred_element_type=jnp.float32
    )
    heads_out = heads_out + jnp.einsum(
        "shqk,skhd->sqhd", low_ents, keyval_e[1], preferred_element_type=jnp.float32
    )
    heads_out = heads_out.astype(jnp.bfloat16).reshape(seq_count, local_rows, local_width)
    heads_dense = jnp.concatenate(
        [
            heads_out[:, :half_words].reshape(word_count, local_width),
            heads_out[:, half_words:].reshape(ent_count, local_width),
        ],
        0,
    )
    resid_in = jnp.concatenate([word_low.astype(jnp.float32), x_entity], 0)
    cotangent = jnp.concatenate(
        [cot_words.reshape(word_count, width), cot_entities.reshape(ent_count, width)], 0
    ).astype(jnp.float32)
    attn_out = tensor_total(matmul(heads_dense, w_out)) + b_out
    first_norm, first_back = jax.vjp(layer_norm, resid_in + attn_out, norm_gain[1], norm_bias[1])
    first_low = first_norm.astype(jnp.bfloat16)
    up_value = matmul(first_low, w_up) + b_up
    active, gelu_back = jax.vjp(gelu_exact, up_value)
    active_low = active.astype(jnp.bfloat16)
    ffn_out = tensor_total(matmul(active_low, w_down)) + b_down
    final_norm, final_back = jax.vjp(layer_norm, first_norm + ffn_out, norm_gain[2], norm_bias[2])
    final_share = own_share(final_norm)
    grad_final, gain_final, shift_final = final_back(cotangent)
    grad_ffn = grad_final.astype(jnp.bfloat16)
    out_words = final_share[:share_words].reshape(seq_count, word_part, width).astype(jnp.bfloat16)
    out_entities = (
        final_share[share_words:].reshape(seq_count, ent_part, width).astype(jnp.bfloat16)
    )
    grad_down = jnp.einsum("rf,rd->fd", active_low, grad_ffn, preferred_element_type=jnp.float32)
    grad_down_bias = jnp.sum(grad_ffn.astype(jnp.float32), 0)
    (grad_pre,) = gelu_back(
        jnp.einsum("rd,fd->rf", grad_ffn, w_down, preferred_element_type=jnp.float32)
    )
    grad_up_low = grad_pre.astype(jnp.bfloat16)
    grad_up = jnp.einsum("rd,rf->df", first_low, grad_up_low, preferred_element_type=jnp.float32)
    grad_up_bias = jnp.sum(grad_up_low.astype(jnp.float32), 0)
    ffn_term = jnp.einsum("rf,df->rd", grad_up_low, w_up, preferred_element_type=jnp.float32)
    grad_first, gain_first, shift_first = first_back(grad_final + tensor_total(ffn_term))
    grad_attn = grad_first.astype(jnp.bfloat16)
    grad_out = jnp.einsum("rc,rd->cd", heads_dense, grad_attn, preferred_element_type=jnp.float32)
    grad_out_bias = jnp.sum(grad_attn.astype(jnp.float32), 0)
    grad_heads = jnp.einsum(
        "rd,cd->rc", grad_attn, w_out, preferred_element_type=jnp.float32
    ).astype(jnp.bfloat16)
    grad_heads = jnp.concatenate(
        [
            grad_heads[:word_count].reshape(seq_count, half_words, local_heads, HD),
            grad_heads[word_count:].reshape(seq_count, half_ents, local_heads, HD),
        ],
        1,
    )
    score_words, score_ents = scores_of()
    prob_words = jnp.exp(score_words - log_total)
    prob_ents = jnp.exp(score_ents - log_total)
    low_words = prob_words.astype(jnp.bfloat16)
    low_ents = prob_ents.astype(jnp.bfloat16)
    dprob_words = jnp.einsum(
        "sqhd,skhd->shqk", grad_heads, keyval_w[1], preferred_element_type=jnp.float32
    )
    dprob_ents = jnp.einsum(
        "sqhd,skhd->shqk", grad_heads, keyval_e[1], preferred_element_type=jnp.float32
    )
    inner_sum = jnp.sum(prob_words * dprob_words, -1, keepdims=True) + jnp.sum(
        prob_ents * dprob_ents, -1, keepdims=True
    )
    dscore_words = (prob_words * (dprob_words - inner_sum)).astype(jnp.bfloat16)
    dscore_ents = (prob_ents * (dprob_ents - inner_sum)).astype(jnp.bfloat16)
    grad_to_words = (
        jnp.einsum("shqk,skhd->sqhd", dscore_words, keyval_w[0], preferred_element_type=jnp.float32)
        * score_scale
    ).astype(jnp.bfloat16)
    grad_to_ents = (
        jnp.einsum("shqk,skhd->sqhd", dscore_ents, keyval_e[0], preferred_element_type=jnp.float32)
        * score_scale
    ).astype(jnp.bfloat16)
    kv_grad_words = jnp.stack(
        [
            jnp.einsum(
                "shqk,sqhd->skhd", dscore_words, queries[0], preferred_element_type=jnp.float32
            )
            * score_scale,
            jnp.einsum(
                "shqk,sqhd->skhd", low_words, grad_heads, preferred_element_type=jnp.float32
            ),
        ]
    )
    kv_grad_ents = jnp.stack(
        [
            jnp.einsum(
                "shqk,sqhd->skhd", dscore_ents, queries[1], preferred_element_type=jnp.float32
            )
            * score_scale,
            jnp.einsum("shqk,sqhd->skhd", low_ents, grad_heads, preferred_element_type=jnp.float32),
        ]
    )
    back_words, back_ents = (
        from_partner(kv_grad_words[:, :, half_words:].astype(jnp.bfloat16), "stream", 0).astype(
            jnp.float32
        ),
        from_partner(kv_grad_ents[:, :, half_ents:].astype(jnp.bfloat16), "stream", 0).astype(
            jnp.float32
        ),
    )
    grad_kv_words = (
        (kv_grad_words[:, :, :half_words] + back_words)
        .reshape(2, word_count, local_width)
        .astype(jnp.bfloat16)
    )
    grad_kv_ents = (
        (kv_grad_ents[:, :, :half_ents] + back_ents)
        .reshape(2, ent_count, local_width)
        .astype(jnp.bfloat16)
    )
    grad_q_words = jnp.stack([grad_to_words[:, :half_words], grad_to_ents[:, :half_words]]).reshape(
        2, word_count, local_width
    )
    grad_q_ents = jnp.stack([grad_to_words[:, half_words:], grad_to_ents[:, half_words:]]).reshape(
        2, ent_count, local_width
    )
    grad_query = jnp.concatenate(
        [
            jnp.einsum("rd,jrc->jdc", word_low, grad_q_words, preferred_element_type=jnp.float32),
            jnp.einsum("rd,jrc->jdc", entity_low, grad_q_ents, preferred_element_type=jnp.float32),
        ],
        0,
    )
    grad_query_bias = jnp.concatenate(
        [jnp.sum(grad_q_words.astype(jnp.float32), 1), jnp.sum(grad_q_ents.astype(jnp.float32), 1)],
        0,
    )
    grad_keyval = jnp.einsum(
        "rd,jrc->jdc", word_low, grad_kv_words, preferred_element_type=jnp.float32
    ) + jnp.einsum("rd,jrc->jdc", entity_low, grad_kv_ents, preferred_element_type=jnp.float32)
    grad_value_bias = jnp.sum(grad_kv_words[1].astype(jnp.float32), 0) + jnp.sum(
        grad_kv_ents[1].astype(jnp.float32), 0
    )
    input_words = jnp.einsum(
        "jrc,jdc->rd", grad_q_words, w_query[:2], preferred_element_type=jnp.float32
    ) + jnp.einsum("jrc,jdc->rd", grad_kv_words, w_keyval, preferred_element_type=jnp.float32)
    input_ents = jnp.einsum(
        "jrc,jdc->rd", grad_q_ents, w_query[2:], preferred_element_type=jnp.float32
    ) + jnp.einsum("jrc,jdc->rd", grad_kv_ents, w_keyval, preferred_element_type=jnp.float32)
    input_term = jnp.concatenate([input_words, input_ents], 0)
    grad_input = grad_first + tensor_total(input_term)
    grad_share = own_share(grad_input)
    grad_lin, gain_entity, shift_entity = entity_norm_back(grad_input[word_count:])
    grad_lin_low = grad_lin.astype(jnp.bfloat16)
    gain_grads = jnp.stack([gain_entity, gain_first, gain_final])
    shift_grads = jnp.stack([shift_entity, shift_first, shift_final])
    grad_words = grad_share[:share_words].reshape(seq_count, word_part, width)
    grad_entity = jnp.einsum("re,rd->ed", looked, grad_lin_low, preferred_element_type=jnp.float32)
    grad_looked = jnp.einsum(
        "rd,ed->re", grad_lin_low, w_entity, preferred_element_type=jnp.float32
    )
    outgoing = (
        jnp.zeros((owners * capacity, embed_width), jnp.float32)
        .at[slot_index]
        .set(grad_looked)
        .reshape(owners, capacity, embed_width)
    )
    incoming = lax.all_to_all(
        outgoing.astype(jnp.bfloat16), ("dp", "stream"), split_axis=0, concat_axis=0, tiled=True
    ).astype(outgoing.dtype)
    target = jnp.where(asked_rows >= 0, asked_rows, table_rows).reshape(-1)
    gradient_sum = (
        jnp.zeros((table_rows, embed_width), jnp.float32)
        .at[target]
        .add(incoming.reshape(-1, embed_width), mode="drop")
    )
    use_count = jnp.zeros((table_rows,), jnp.float32).at[target].add(1.0, mode="drop")
    touched = (use_count > 0.0)[:, None]
    first_next = beta_one * adam_first + (1.0 - beta_one) * gradient_sum
    second_next = beta_two * adam_second + (1.0 - beta_two) * gradient_sum * gradient_sum
    direction = (
        first_next
        / (1.0 - beta_one**adam_steps)
        / (jnp.sqrt(second_next / (1.0 - beta_two**adam_steps)) + adam_eps)
    )
    table_update = jnp.where(touched, direction, jnp.zeros_like(direction))
    new_first = jnp.where(touched, first_next, adam_first)
    new_second = jnp.where(touched, second_next, adam_second)
    (
        red_entity,
        red_gain,
        red_shift,
        red_query,
        red_keyval,
        red_out,
        red_out_bias,
        red_up,
        red_down,
        red_down_bias,
    ) = (
        lax.psum_scatter(grad_entity, ("dp", "stream"), scatter_dimension=1, tiled=True),
        lax.psum_scatter(gain_grads, ("dp", "stream"), scatter_dimension=1, tiled=True),
        lax.psum_scatter(shift_grads, ("dp", "stream"), scatter_dimension=1, tiled=True),
        lax.psum_scatter(grad_query, ("dp", "stream"), scatter_dimension=1, tiled=True),
        lax.psum_scatter(grad_keyval, ("dp", "stream"), scatter_dimension=1, tiled=True),
        lax.psum_scatter(grad_out, ("dp", "stream"), scatter_dimension=1, tiled=True),
        lax.psum_scatter(grad_out_bias, ("dp", "stream"), scatter_dimension=0, tiled=True),
        lax.psum_scatter(grad_up, ("dp", "stream"), scatter_dimension=0, tiled=True),
        lax.psum_scatter(grad_down, ("dp", "stream"), scatter_dimension=1, tiled=True),
        lax.psum_scatter(grad_down_bias, ("dp", "stream"), scatter_dimension=0, tiled=True),
    )
    red_query_bias, red_value_bias, red_up_bias = lax.psum(
        (grad_query_bias, grad_value_bias, grad_up_bias), ("dp", "stream")
    )
    return (
        out_words,
        out_entities,
        grad_words,
        red_entity,
        red_gain,
        red_shift,
        red_query,
        red_query_bias,
        red_keyval,
        red_value_bias,
        red_out,
        red_out_bias,
        red_up,
        red_up_bias,
        red_down,
        red_down_bias,
        table_update,
        new_first,
        new_second,
    )


def solution(mesh):
    placed = (
        P("dp", "stream", None),
        P("stream", "dp", None, None),
        P("stream", "dp", None),
        P("dp", None),
        P("dp", None),
        P(("dp", "stream"), None),
        P(("dp", "stream"), None),
        P(("dp", "stream"), None),
        P(),
        P(),
        P(),
        P(None, None, "tensor"),
        P(None, "tensor"),
        P(None, None, "tensor"),
        P("tensor"),
        P("tensor", None),
        P(),
        P(None, "tensor"),
        P("tensor"),
        P("tensor", None),
        P(),
        P("dp", "stream", None),
        P("dp", "stream", None),
    )
    fits = mesh.shape["stream"] == 2 and mesh.shape["tensor"] == 2 and mesh.shape["dp"] % 2 == 0

    def local(*blocks):
        width, owners = blocks[0].shape[2], mesh.shape["dp"] * mesh.shape["stream"]
        if fits and width % (16 * owners) == 0 and blocks[0].shape[0] == 1:
            return fused_local(*blocks)
        return plain_local(*blocks)

    return jax.shard_map(
        local,
        mesh=mesh,
        in_specs=placed,
        out_specs=(
            P("dp", ("stream", "tensor"), None),
            P("dp", ("stream", "tensor"), None),
            P("dp", ("stream", "tensor"), None),
            P(None, ("dp", "stream")),
            P(None, ("dp", "stream")),
            P(None, ("dp", "stream")),
            P(None, ("dp", "stream"), "tensor"),
            P(None, "tensor"),
            P(None, ("dp", "stream"), "tensor"),
            P("tensor"),
            P("tensor", ("dp", "stream")),
            P(("dp", "stream")),
            P(("dp", "stream"), "tensor"),
            P("tensor"),
            P("tensor", ("dp", "stream")),
            P(("dp", "stream")),
            P(("dp", "stream"), None),
            P(("dp", "stream"), None),
            P(("dp", "stream"), None),
        ),
        check_vma=False,
    )
```

```python
import functools
import math
import types

import jax
import jax.numpy as jnp
from jax import lax
from jax.experimental import pallas as pl
from jax.experimental.pallas import tpu as pltpu
from jax.sharding import PartitionSpec as P

HD = 64
MESH_ID = pl.DeviceIdType.MESH


norm_eps = 1e-05
score_scale = 0.125
masked_score = -1e30
beta_one = 0.9
beta_two = 0.99
adam_steps = 10
adam_eps = 1e-08


def from_partner(block, axis, apart):
    count = lax.axis_size(axis)
    route = []
    for low in range(count):
        high = low | 1 << apart
        if high != low and high < count:
            route += [(low, high), (high, low)]
    return lax.ppermute(block, axis, route)


def layer_norm(values_in, gain_row, shift_row):
    center = values_in - jnp.mean(values_in, -1, keepdims=True)
    spread = jnp.mean(center * center, -1, keepdims=True)
    return center * lax.rsqrt(spread + norm_eps) * gain_row + shift_row


def gelu_exact(values_in):
    return jax.nn.gelu(values_in, approximate=False)


def matmul(matrix_a, matrix_b):
    return jnp.dot(matrix_a, matrix_b, preferred_element_type=jnp.float32)


def tensor_total(values_in):
    return lax.psum(values_in, "tensor")


def send(source, target, send_sem, recv_sem, peer):
    return pltpu.make_async_remote_copy(
        src_ref=source,
        dst_ref=target,
        send_sem=send_sem,
        recv_sem=recv_sem,
        device_id=peer,
        device_id_type=MESH_ID,
    )


def row_sum(block):
    return jnp.sum(block, 0, keepdims=True)


def lane_mean(block):
    return jnp.mean(block, -1, keepdims=True)


def dot_nn(left, right):
    return jnp.dot(left, right, preferred_element_type=jnp.float32)


def dot_nt(left, right):
    return lax.dot_general(
        left, right, (((1,), (1,)), ((), ())), preferred_element_type=jnp.float32
    )


def dot_tn(left, right):
    return lax.dot_general(
        left, right, (((0,), (0,)), ((), ())), preferred_element_type=jnp.float32
    )


def normalize(rows):
    center = rows - lane_mean(rows)
    scale = lax.rsqrt(lane_mean(center * center) + norm_eps)
    return center * scale, scale


def normalize_back(grad, normed, scale, gain):
    inner = grad * gain
    return scale * (inner - lane_mean(inner) - normed * lane_mean(inner * normed))


def aligned(index, step):
    return pl.ds(pl.multiple_of(index * step, step), step)


def layer_kernel(names, orders, schedule, *refs):
    r = types.SimpleNamespace(**dict(zip(names, refs, strict=True)))
    low, full = jnp.bfloat16, jnp.float32
    dp, x, t = lax.axis_index("dp"), lax.axis_index("stream"), lax.axis_index("tensor")
    y, z = lax.rem(dp, 2), dp // 2
    owners = lax.axis_size("dp") * 2
    _, half_words, width = r.hbm_words.shape
    half_ents = r.shard.shape[1]
    rows, words = half_words + half_ents, 2 * half_words
    everyone = 2 * rows
    capacity = r.ask.shape[1]
    slots = owners * capacity
    heads = r.prob.shape[0]
    share = width // owners
    side = heads * HD
    hidden = r.w_up.shape[1]
    block = half_ents
    blocks = rows // block
    word_blocks = half_words // block
    wide = 256

    core, x_peer, y_peer = {"tensor": 1 - t}, {"stream": 1 - x}, {"dp": z * 2 + 1 - y}
    z_low, z_high = lax.rem(z, 2), z // 2
    near_peer = {"dp": (z + 1 - 2 * z_low) * 2 + y}
    far_peer = {"dp": (z + 2 - 4 * z_high) * 2 + y}
    mine_on = (z_high, z_low, y, x)
    peer_on = (far_peer, near_peer, y_peer, x_peer)
    flat = dp * 2 + x
    others = []
    for k in range(1, owners):
        other = lax.rem(flat + k, owners)
        others.append((other, {"dp": other // 2, "stream": lax.rem(other, 2)}))

    loads = {}
    barrier = pltpu.get_barrier_semaphore()
    for peer in [core] + [peer for _, peer in others]:
        pl.semaphore_signal(barrier, inc=1, device_id=peer, device_id_type=MESH_ID)

    def load(source, target):
        loads[id(target)] = pltpu.make_async_copy(source, target, r.load_s.at[len(loads)])
        loads[id(target)].start()

    def loaded(target):
        loads.pop(id(target)).wait()

    load(r.hbm_shard, r.shard)
    load(r.hbm_row, r.row)
    my_words = r.x_all.at[aligned(x, half_words), :]
    load(r.hbm_words.at[0], my_words)
    load(r.hbm_query, r.w_query)
    load(r.hbm_keyval, r.w_keyval)
    smalls = [
        (r.hbm_b_query, r.b_query), (r.hbm_b_value, r.b_value), (r.hbm_word_seg, r.word_seg),
        (r.hbm_ent_seg, r.ent_seg), (r.hbm_gain, r.gain), (r.hbm_shift, r.shift),
        (r.hbm_b_out, r.b_out), (r.hbm_b_up, r.b_up), (r.hbm_b_down, r.b_down),
    ]
    for source, target in smalls:
        load(source, target)
    load(r.hbm_table, r.table)
    load(r.hbm_entity, r.w_entity)
    cot_words, cot_ents = r.cotangent.at[0:half_words, :], r.cotangent.at[half_words:rows, :]
    load(r.hbm_cot_words.at[0], cot_words)
    load(r.hbm_cot_ents.at[0], cot_ents)
    load(r.hbm_out, r.w_out)
    load(r.hbm_up, r.w_up)
    load(r.hbm_down, r.w_down)

    flushes = []

    def flush(source, target):
        flushes.append(pltpu.make_async_copy(source, target, r.flush_s.at[len(flushes)]))
        flushes[-1].start()

    loaded(r.shard)
    loaded(r.row)
    shard_row = r.shard[...]
    shard_all = jnp.broadcast_to(shard_row.astype(full), (half_ents, half_ents)).T
    shard_all = shard_all.astype(jnp.int32)
    shard_col = shard_all[:, 0:1]
    below = lax.broadcasted_iota(jnp.int32, (half_ents, half_ents), 0)
    beside = lax.broadcasted_iota(jnp.int32, (half_ents, half_ents), 1)
    same = shard_all == shard_row
    rank_row = row_sum(jnp.where(same & (below < beside), 1.0, 0.0)).astype(jnp.int32)
    rank_col = jnp.sum(jnp.where(same & (beside < below), 1.0, 0.0), 1, keepdims=True)
    rank_col = rank_col.astype(jnp.int32)
    slot_row = shard_row * capacity + rank_row
    in_slot = lax.broadcasted_iota(jnp.int32, (slots, half_ents), 0) == slot_row
    wanted = jnp.sum(
        jnp.where(in_slot, (r.row[...] + 1).astype(full), 0.0), 1, keepdims=True
    )
    wanted = wanted.astype(jnp.int32) - 1
    r.ask[...] = jnp.broadcast_to(wanted, (slots, 128)).reshape(owners, capacity, 128)
    r.outbox[...] = jnp.where(in_slot, 1.0, 0.0).astype(low)
    answer_col = shard_col * (2 * capacity) + x * capacity + rank_col
    answer_lane = lax.broadcasted_iota(jnp.int32, (half_ents, 2 * slots), 1)
    r.select[aligned(x, half_ents), :] = jnp.where(answer_lane == answer_col, 1.0, 0.0).astype(low)
    r.asked[flat] = r.ask[flat]
    r.vec[0] = jnp.zeros(r.vec.shape[1:], full)

    loaded(r.w_query)
    loaded(r.w_keyval)
    for _, target in smalls:
        loaded(target)

    def gather_columns(which):
        for h in range(heads):
            own = slice(which * side + h * HD, which * side + (h + 1) * HD)
            for place, words_part, ents_part in (
                (0, r.w_query[0, :, own], r.w_query[2, :, own]),
                (1, r.w_query[1, :, own], r.w_query[3, :, own]),
                (2, r.w_keyval[0, :, own], None),
                (3, r.w_keyval[1, :, own], None),
            ):
                lanes = slice((4 * h + place) * HD, (4 * h + place + 1) * HD)
                r.cat_words[:, lanes] = words_part
                r.cat_ents[:, lanes] = words_part if ents_part is None else ents_part
            zero = jnp.zeros((1, HD), full)
            value = r.b_value[...].reshape(1, -1)[:, own]
            query = r.b_query[:, own]
            lanes = slice(4 * h * HD, 4 * (h + 1) * HD)
            r.bias_words[:, lanes] = jnp.concatenate([query[0:1], query[1:2], zero, value], 1)
            r.bias_ents[:, lanes] = jnp.concatenate([query[2:3], query[3:4], zero, value], 1)

    for which in range(2):

        @pl.when(x == which)
        def _(which=which):
            gather_columns(which)

    loaded(my_words)
    r.x_own[0:half_words, :] = my_words[...].astype(full)
    pl.semaphore_wait(barrier, owners)

    def ask_copy(k):
        other, peer = others[k]
        return send(r.ask.at[other], r.asked.at[flat], r.ask_s.at[k], r.ask_r.at[k], peer)

    def answer_copy(k):
        other, peer = others[k]
        return send(
            r.found.at[other // 2], r.answer.at[flat], r.answer_s.at[k], r.answer_r.at[k], peer
        )

    def slope_copy(k):
        other, peer = others[k]
        return send(r.slope.at[other], r.slopes.at[flat], r.slope_s.at[k], r.slope_r.at[k], peer)

    for k in range(owners - 1):
        ask_copy(k).start()
    my_select = r.select.at[aligned(x, half_ents), :]
    select_copy = send(my_select, my_select, r.pair_s.at[0], r.pair_r.at[0], x_peer)
    select_copy.start()
    half = half_words // 2
    my_half = r.x_all.at[aligned(2 * x + t, half), :]
    words_copy = send(my_half, my_half, r.pair_s.at[1], r.pair_r.at[1], x_peer)
    words_copy.start()

    is_query = lax.broadcasted_iota(jnp.int32, (1, 4 * HD), 1) < 2 * HD
    scaling = jnp.where(is_query, score_scale, 1.0)

    def project(start, count, weight, bias):
        def body(h, carry):
            lanes = aligned(h, 4 * HD)
            total = dot_nn(r.x_all[pl.ds(start, count), :], weight[:, lanes]) + bias[:, lanes]
            r.qkv[pl.ds(start, count), lanes] = (total * scaling).astype(low)
            return carry

        lax.fori_loop(0, heads, body, 0)

    project(pl.multiple_of(x * half_words, half_words), half_words, r.cat_words, r.bias_words)

    segments = jnp.concatenate([r.word_seg[...], r.ent_seg[...]], 1)
    for i in range(everyone // 128):
        own_seg = jnp.broadcast_to(segments[:, i * 128 : (i + 1) * 128].astype(full), (128, 128)).T
        equal = own_seg[:, 0:1].astype(jnp.int32) == segments
        r.mask[i * 128 : (i + 1) * 128, :] = jnp.where(equal, 0.0, masked_score).astype(low)

    words_copy.wait()
    far_half = r.x_all.at[aligned(2 * (1 - x) + t, half), :]
    relay = send(far_half, far_half, r.pair_s.at[8], r.pair_r.at[8], core)
    relay.start()

    for k in range(owners - 1):
        ask_copy(k).wait()
    ids = r.asked[...].reshape(slots, 128)
    lane = lax.broadcasted_iota(jnp.int32, (slots, 128), 1)
    loaded(r.table)
    piece = 4 * 128

    def pick_body(j, found):
        ones = [jnp.where(ids == lane + (j * piece + n * 128), 1.0, 0.0) for n in range(4)]
        return found + dot_nn(jnp.concatenate(ones, 1).astype(low), r.table[aligned(j, piece), :])

    found = jnp.zeros((slots, r.table.shape[1]), full)
    found = lax.fori_loop(0, r.table.shape[0] // piece, pick_body, found).astype(low)
    r.found[...] = found.reshape(r.found.shape)
    r.answer[flat] = r.found[dp]
    for k in range(owners - 1):
        answer_copy(k).start()

    relay.wait()
    project(pl.multiple_of((1 - x) * half_words, half_words), half_words, r.cat_words, r.bias_words)

    def take_heads(here):
        for h in range(heads):
            r.key[h, here, :] = r.qkv[here, h * 4 * HD + 2 * HD : h * 4 * HD + 3 * HD]
            r.value[h, here, :] = r.qkv[here, h * 4 * HD + 3 * HD : h * 4 * HD + 4 * HD]

    of_words, of_ents = slice(0, words), slice(words, everyone)
    take_heads(of_words)
    for h in range(heads):
        query = r.qkv[of_words, h * 4 * HD : h * 4 * HD + HD]
        r.prob[h, of_words, of_words] = dot_nt(query, r.key[h, of_words, :])

    def mass_lanes(which, h):
        return pl.ds(pl.multiple_of((which * heads + h) * 128, 128), 128)

    def soften_words(which):
        def body(i, carry):
            here = pl.ds(pl.multiple_of(which * half_words + i * SOFT, SOFT), SOFT)
            bias = r.mask[here, of_words].astype(full)
            for h in range(heads):
                score = r.prob[h, here, of_words] + bias
                peak = jnp.max(score, 1, keepdims=True)
                power = jnp.exp(score - peak)
                r.prob[h, here, of_words] = power
                r.factor[h, here, :] = jnp.broadcast_to(peak, (SOFT, 128))
                mass = jnp.broadcast_to(jnp.sum(power, 1, keepdims=True), (SOFT, 128))
                r.mail_out[1, aligned(i, SOFT), mass_lanes(which, h)] = mass
            return carry

        lax.fori_loop(0, half_words // SOFT, body, 0)

    soften_words(0)
    soften_words(1)
    for h in range(heads):
        weights = r.prob[h, of_words, of_words].astype(low)
        r.grad_prob[of_words, h * 128 : h * 128 + HD] = dot_nn(weights, r.value[h, of_words, :])
        r.factor[h, of_ents, :] = jnp.ones((2 * half_ents, 128), full)

    select_copy.wait()
    for k in range(owners - 1):
        answer_copy(k).wait()
    looked = dot_nn(r.select[...], r.answer[...].reshape(2 * slots, r.table.shape[1])).astype(low)
    r.looked[...] = looked
    loaded(r.w_entity)
    ent_lin = dot_nn(looked, r.w_entity[...])
    normed, _ = normalize(ent_lin)
    x_entity = normed * r.gain[0:1, :] + r.shift[0:1, :]
    r.ent_lin[...] = ent_lin
    r.x_ent[...] = x_entity
    r.x_all[words:everyone, :] = x_entity.astype(low)
    r.x_own[half_words:rows, :] = r.x_ent[aligned(x, half_ents), :]
    project(words, 2 * half_ents, r.cat_ents, r.bias_ents)
    take_heads(of_ents)

    def both_kinds(which):
        near_words = pl.ds(pl.multiple_of(which * half_words, half_words), half_words)
        near_ents = pl.ds(pl.multiple_of(words + which * half_ents, half_ents), half_ents)
        return (near_words, slice(0, half_words)), (near_ents, slice(half_words, rows))

    def soften_ents(here):
        bias = r.mask[here, :].astype(full)
        for h in range(heads):
            score = r.prob[h, here, :] + bias
            power = jnp.exp(score - jnp.max(score, 1, keepdims=True))
            r.prob[h, here, :] = power * (1.0 / jnp.sum(power, 1, keepdims=True))

    def complete_words(which, here):
        bias = r.mask[here, of_ents].astype(full)
        for h in range(heads):
            score = r.prob[h, here, of_ents] + bias
            peak = r.factor[h, here, :]
            best = jnp.broadcast_to(jnp.max(score, 1, keepdims=True), (half_words, 128))
            top = jnp.maximum(peak, best)
            power, shrink = jnp.exp(score - top), jnp.exp(peak - top)
            added = jnp.broadcast_to(jnp.sum(power, 1, keepdims=True), (half_words, 128))
            mass = r.mail_out[1, 0:half_words, mass_lanes(which, h)]
            share_of = 1.0 / (mass * shrink + added)
            r.prob[h, here, of_ents] = power * share_of
            r.factor[h, here, :] = shrink * share_of

    def attend_words(which, target):
        (here, there), _ = both_kinds(which)
        for h in range(heads):
            query = r.qkv[here, h * 4 * HD + HD : h * 4 * HD + 2 * HD]
            r.prob[h, here, of_ents] = dot_nt(query, r.key[h, of_ents, :])
        complete_words(which, here)
        for h in range(heads):
            out = r.grad_prob[here, h * 128 : h * 128 + HD] * r.factor[h, here, 0:HD]
            out = out + dot_nn(r.prob[h, here, of_ents].astype(low), r.value[h, of_ents, :])
            target[there, h * HD : (h + 1) * HD] = out.astype(low)

    def attend_ents(which, target):
        _, (here, there) = both_kinds(which)
        for h in range(heads):
            query = r.qkv[here, h * 4 * HD : h * 4 * HD + 2 * HD]
            r.prob[h, here, of_words] = dot_nt(query[:, :HD], r.key[h, of_words, :])
            r.prob[h, here, of_ents] = dot_nt(query[:, HD:], r.key[h, of_ents, :])
        soften_ents(here)
        for h in range(heads):
            out = dot_nn(r.prob[h, here, :].astype(low), r.value[h])
            target[there, h * HD : (h + 1) * HD] = out.astype(low)

    def heads_part(n, part):
        return send(
            r.heads_far.at[part, :], r.heads_in.at[part, :], r.heads_s.at[n], r.heads_r.at[n], x_peer
        )

    attend_words(1 - x, r.heads_far)
    heads_copies = [heads_part(0, slice(0, half_words))]
    heads_copies[0].start()
    attend_ents(1 - x, r.heads_far)
    heads_copies.append(heads_part(1, slice(half_words, rows)))
    heads_copies[1].start()
    attend_words(x, r.heads_near)
    attend_ents(x, r.heads_near)
    r.words_t[...] = r.x_all[of_words, :].T
    r.ents_t[...] = r.x_all[of_ents, :].T
    for copy in heads_copies:
        copy.wait()

    @pl.when(x == 0)
    def _():
        r.heads_all[:, 0:side] = r.heads_near[...]
        r.heads_all[:, side:] = r.heads_in[...]

    @pl.when(x == 1)
    def _():
        r.heads_all[:, 0:side] = r.heads_in[...]
        r.heads_all[:, side:] = r.heads_near[...]

    def strip(which, turn, j):
        part = (which, slice(0, rows), aligned(j, wide))
        return send(
            r.mail_out.at[part], r.mail_in.at[part], r.strip_s.at[turn, j], r.strip_r.at[turn, j], core
        )

    def wait_strips(which, turn):
        for j in range(width // wide):
            strip(which, turn, j).wait()

    def swap(which, turn, first, count):
        part = pl.ds(first, count)
        return send(
            r.mail_out.at[which, part], r.mail_in.at[which, part], r.swap_s.at[turn],
            r.swap_r.at[turn], core,
        )

    def columns(count, fill):
        def body(j, carry):
            fill(aligned(j, wide), j)
            return carry

        lax.fori_loop(0, count // wide, body, 0)

    def fill_attn(lanes, j):
        r.mail_out[0, 0:rows, lanes] = dot_nn(r.heads_all[...], r.w_out[:, lanes])
        strip(0, 0, j).start()

    loaded(r.w_out)
    columns(width, fill_attn)
    wait_strips(0, 0)

    def over_rows(body):
        def step(i, carry):
            body(aligned(i, block))
            return carry

        lax.fori_loop(0, blocks, step, 0)

    def first_norm(here):
        attn = r.mail_out[0, here, :] + r.mail_in[0, here, :] + r.b_out[...].reshape(1, -1)
        normed, scale = normalize(r.x_own[here, :] + attn)
        r.normed[here, :] = normed
        r.scale[here, :] = jnp.broadcast_to(scale, (block, 128))
        r.first[here, :] = (normed * r.gain[1:2, :] + r.shift[1:2, :]).astype(low)

    over_rows(first_norm)

    def fill_up(lanes, _):
        up = dot_nn(r.first[...], r.w_up[:, lanes]) + r.b_up[lanes].reshape(1, -1)
        chance = 0.5 + 0.5 * lax.erf(up * (0.5**0.5))
        r.act[:, lanes] = (up * chance).astype(low)
        r.slope_up[:, lanes] = chance + up * (jnp.exp(-0.5 * up * up) * (0.5 / math.pi) ** 0.5)

    loaded(r.w_up)
    columns(hidden, fill_up)

    def fill_down(lanes, j):
        r.mail_out[1, 0:rows, lanes] = dot_nn(r.act[...], r.w_down[:, lanes])
        strip(1, 1, j).start()

    loaded(r.w_down)
    columns(width, fill_down)
    wait_strips(1, 1)

    vec = r.vec.at[0]

    def second_norm(here):
        ffn = r.mail_out[1, here, :] + r.mail_in[1, here, :] + r.b_down[...].reshape(1, -1)
        entering = r.normed[here, :] * r.gain[1:2, :] + r.shift[1:2, :]
        normed, scale = normalize(entering + ffn)
        r.final[here, :] = (normed * r.gain[2:3, :] + r.shift[2:3, :]).astype(low)
        grad = r.cotangent[here, :].astype(full)
        vec[2:3, :] += row_sum(grad * normed)
        vec[5:6, :] += row_sum(grad)
        back = normalize_back(grad, normed, scale, r.gain[2:3, :])
        r.grad_second[here, :] = back
        r.grad_low[here, :] = back.astype(low)
        vec[7:8, :] += row_sum(back.astype(low).astype(full))

    loaded(cot_words)
    loaded(cot_ents)
    over_rows(second_norm)

    def halved(ref, place, index):
        return ref.at[(slice(None),) * place + (index,)]

    def stage(kit, c, order, n):
        left = [axis for axis in range(4) if axis not in order[:n]]
        axis, place = order[n], left.index(order[n])
        held = kit.held[n].at[c]
        copy = send(
            halved(held, place, 1 - mine_on[axis]), kit.held[n + 1].at[c],
            kit.sent.at[c, n], kit.got.at[c, n], peer_on[axis],
        )
        return copy, halved(held, place, mine_on[axis])

    def advance(kit, c, order, n):
        copy, own = stage(kit, c, order, n - 1)
        copy.wait()
        total = kit.held[n].at[c]

        def body(i, carry):
            total[i] = own[i] + total[i]
            return carry

        lax.fori_loop(0, 2, body, 0)
        stage(kit, c, order, n)[0].start()

    def finish(kit, c, order):
        copy, own = stage(kit, c, order, 3)
        copy.wait()
        kit.out[c] = own[...].astype(full) + kit.held[4][c].astype(full)

    kit_a = types.SimpleNamespace(
        held=(r.grads, r.near, r.next, r.far, r.last), out=r.out_a, sent=r.a_s, got=r.a_r
    )
    kit_e = types.SimpleNamespace(
        held=(r.e_grads, r.e_near, r.e_next, r.e_far, r.e_last), out=r.e_sum, sent=r.e_s, got=r.e_r
    )
    along = dict(zip(range(3), ((3, 2, 1, 0), (2, 3, 1, 0), (1, 0, 3, 2))))

    kit_q = types.SimpleNamespace(held=(r.q_grads, r.q_near, r.q_next, r.q_far), sent=r.q_s, got=r.q_r)
    head_order = (2, 1, 0, 3)

    def head_start(h):
        stage(kit_q, h, head_order, 0)[0].start()

    def head_meet(h):
        return send(r.q_sum.at[h, 1 - x], r.q_in.at[h], r.q_s.at[h, 3], r.q_r.at[h, 3], x_peer)

    def head_advance(h, n):
        if n < 3:
            advance(kit_q, h, head_order, n)
            return
        copy, own = stage(kit_q, h, head_order, 2)
        copy.wait()
        r.q_sum[h] = own[...].astype(full) + r.q_far[h].astype(full)
        head_meet(h).start()
        r.out_q[h, x] = r.q_sum[h, x]

    def head_finish(h):
        head_meet(h).wait()
        r.out_q[h, 1 - x] = r.q_in[h]

    def vec_copy(n):
        return send(r.vec.at[n], r.vec_in.at[n], r.vec_s.at[n], r.vec_r.at[n], peer_on[3 - n])

    def vec_advance(n):
        vec_copy(n - 1).wait()
        r.vec[n] = r.vec[n - 1] + r.vec_in[n - 1]
        if n < 4:
            vec_copy(n).start()

    chunk = r.grads.shape[-1]

    def make_grad(c, left_t, right, lanes):
        part = dot_nn(left_t[...], right[:, lanes]).astype(low)
        r.grads[c] = part.reshape(2, 2, 2, 2, share, chunk)

    plan = iter(schedule)

    def tick():
        for what, c, n in next(plan):
            if what == CHUNK and n == 0:
                stage(kit_a, c, along[orders[c]], 0)[0].start()
            elif what == CHUNK:
                advance(kit_a, c, along[orders[c]], n)
            elif what == HEAD:
                head_advance(c, n)
            elif what == ENTS:
                advance(kit_e, c, along[0], n)
            else:
                vec_advance(n)

    downs = hidden // chunk
    r.grad_t[...] = r.grad_low[...].T
    for c in range(downs):
        make_grad(c, r.grad_t, r.act, slice(c * chunk, (c + 1) * chunk))
        tick()

    def fill_dup(lanes, j):
        grad_act = dot_nt(r.grad_low[...], r.w_down[lanes, :])
        grad_up = (grad_act * r.slope_up[:, lanes]).astype(low)
        r.grad_up[:, lanes] = grad_up
        vec[pl.ds(8 + j // (width // wide), 1), aligned(lax.rem(j, width // wide), wide)] = row_sum(
            grad_up.astype(full)
        )

    columns(hidden, fill_dup)
    tick()

    def fill_back(lanes, j):
        r.mail_out[0, 0:rows, lanes] = dot_nt(r.grad_up[...], r.w_up[lanes, :])
        strip(0, 2, j).start()

    columns(width, fill_back)
    tick()
    r.first_t[...] = r.first[...].T
    flush(r.final.at[aligned(t, half_words // 2), :], r.to_out_words)
    ents_share = pl.multiple_of(half_words + t * (half_ents // 2), half_ents // 2)
    flush(r.final.at[pl.ds(ents_share, half_ents // 2), :], r.to_out_ents)
    for c in range(downs):
        make_grad(downs + c, r.first_t, r.grad_up, slice(c * chunk, (c + 1) * chunk))
        tick()
    wait_strips(0, 2)

    def first_back(here):
        grad = r.grad_second[here, :] + r.mail_out[0, here, :] + r.mail_in[0, here, :]
        normed = r.normed[here, :]
        vec[1:2, :] += row_sum(grad * normed)
        vec[4:5, :] += row_sum(grad)
        back = normalize_back(grad, normed, r.scale[here, 0:1], r.gain[1:2, :])
        r.grad_first[here, :] = back
        r.grad_low[here, :] = back.astype(low)
        vec[6:7, :] += row_sum(back.astype(low).astype(full))

    over_rows(first_back)
    tick()
    near_rows = aligned(x, side)
    far_rows = aligned(1 - x, side)
    r.back_far[...] = dot_nt(r.grad_low[...], r.w_out[far_rows, :]).astype(low)
    mine = [(aligned(x, half_words), 0, half_words)]
    mine.append((pl.ds(pl.multiple_of(words + x * half_ents, half_ents), half_ents), half_words, half_ents))
    back_copies = [
        send(
            r.back_far.at[pl.ds(first, count), :], r.back_heads.at[place, :],
            r.pair_s.at[3 + n], r.pair_r.at[3 + n], x_peer,
        )
        for n, (place, first, count) in enumerate(mine)
    ]
    for copy in back_copies:
        copy.start()
    near = dot_nt(r.grad_low[...], r.w_out[near_rows, :]).astype(low)
    for place, first, count in mine:
        r.back_heads[place, :] = near[first : first + count, :]
    r.grad_t[...] = r.grad_low[...].T
    outs = 2 * downs
    make_grad(outs, r.grad_t, r.heads_all, slice(0, chunk))
    tick()


    pair = 2 * HD
    for h in range(heads):
        base = h * 4 * HD

        def score_back(start):
            def body(i, carry):
                here = pl.ds(pl.multiple_of(start + i * SOFT, SOFT), SOFT)
                factor = jnp.concatenate([r.factor[h, here, :]] * (words // 128), 1)
                scaled = r.prob[h, here, of_words] * factor
                prob = jnp.concatenate([scaled, r.prob[h, here, of_ents]], 1)
                grad_prob = r.grad_prob[here, :]
                inner = jnp.sum(prob * grad_prob, 1, keepdims=True)
                r.grad_score[here, :] = (prob * (grad_prob - inner)).astype(low)
                r.prob_low[here, :] = prob.astype(low)
                return carry

            return body

        for which in (x, 1 - x):
            if which is not x:
                tick()
            if h == 0 and which is not x:
                for copy in back_copies:
                    copy.wait()
            for here, _ in both_kinds(which):
                r.grad_prob[here, :] = dot_nt(r.back_heads[here, h * HD : (h + 1) * HD], r.value[h])
            lax.fori_loop(0, half_words // SOFT, score_back(which * half_words), 0)
            lax.fori_loop(0, half_ents // SOFT, score_back(words + which * half_ents), 0)
        queries = jnp.concatenate(
            [
                dot_nn(r.grad_score[:, :words], r.key[h, 0:words, :]),
                dot_nn(r.grad_score[:, words:], r.key[h, words:everyone, :]),
            ],
            1,
        )
        r.grad_qkv[:, base : base + pair] = (queries * score_scale).astype(low)
        tick()
        query_t = r.qkv[:, base : base + pair].T
        keys_t = dot_nn(query_t, r.grad_score[...])
        keys_t = jnp.concatenate([keys_t[:HD, :words], keys_t[HD:, words:]], 1)
        values_t = dot_nn(r.back_heads[:, h * HD : (h + 1) * HD].T, r.prob_low[...])
        r.grad_qkv[:, base + pair : base + 2 * pair] = (
            jnp.concatenate([keys_t, values_t], 0).T.astype(low)
        )

        tick()
        keyval = slice(base + pair, base + 2 * pair)
        query = slice(base, base + pair)
        by_words = dot_nn(r.words_t[...], r.grad_qkv[0:words, query])
        by_ents = dot_nn(r.ents_t[...], r.grad_qkv[words:everyone, query])
        by_keyval = dot_nn(r.words_t[...], r.grad_qkv[0:words, keyval])
        by_keyval = by_keyval + dot_nn(r.ents_t[...], r.grad_qkv[words:everyone, keyval])
        for n, part in enumerate([by_words, by_ents, by_keyval]):
            r.q_grads[h, :, :, :, :, :, n * pair : (n + 1) * pair] = part.astype(low).reshape(
                2, 2, 2, 2, share, pair
            )
        head_start(h)
        sums = jnp.concatenate(
            [
                row_sum(r.grad_qkv[0:words, base : base + pair].astype(full)),
                row_sum(r.grad_qkv[words:everyone, base : base + pair].astype(full)),
                row_sum(r.grad_qkv[:, base + pair : base + 2 * pair].astype(full)),
            ],
            1,
        )
        place = h * 3 * pair
        vec[pl.ds(10 + 2 * x + place // width, 1), place % width : place % width + 3 * pair] = sums
        tick()

    quarter = half_words // 2

    def input_grad(place, weight):
        return dot_nt(r.grad_qkv[place, :], weight[...])

    ents_part = input_grad(slice(words, everyone), r.cat_ents)
    r.mail_out[1, words // 2 :, :] = ents_part
    ents_swap = swap(1, 0, words // 2, 2 * half_ents)
    ents_swap.start()
    tick()
    for n in range(2):
        r.mail_out[1, n * quarter : (n + 1) * quarter, :] = input_grad(
            aligned(2 * n + 1 - t, quarter), r.cat_words
        )
    words_swap = swap(1, 1, 0, words // 2)
    words_swap.start()
    for n in range(2):
        r.input_part[n] = input_grad(aligned(2 * n + t, quarter), r.cat_words)
    tick()
    ents_swap.wait()
    ents_place = pl.multiple_of(words // 2 + (1 - x) * half_ents, half_ents)
    ents_far = pl.ds(ents_place, half_ents)
    ents_near = pl.ds(pl.multiple_of(words // 2 + x * half_ents, half_ents), half_ents)
    r.ents_back[...] = (r.mail_out[1, ents_far, :] + r.mail_in[1, ents_far, :]).astype(low)
    ents_copy = send(r.ents_back, r.ents_in, r.pair_s.at[5], r.pair_r.at[5], x_peer)
    ents_copy.start()
    tick()
    words_swap.wait()
    far_place = aligned(1 - x, quarter)
    r.words_back[...] = (r.input_part[1 - x] + r.mail_in[1, far_place, :]).astype(low)
    words_back_copy = send(r.words_back, r.words_in, r.pair_s.at[6], r.pair_r.at[6], x_peer)
    words_back_copy.start()
    tick()
    ents_copy.wait()

    grad = r.grad_first[half_words:rows, :] + (r.mail_out[1, ents_near, :] + r.mail_in[1, ents_near, :])
    grad = grad + r.ents_in[...].astype(full)
    own_ents = aligned(x, half_ents)
    normed, scale = normalize(r.ent_lin[own_ents, :])
    vec[0:1, :] = row_sum(grad * normed)
    vec[3:4, :] = row_sum(grad)
    lin_low = normalize_back(grad, normed, scale, r.gain[0:1, :]).astype(low)
    slope = dot_nt(lin_low, r.w_entity[...]).astype(low)
    r.slope[...] = dot_nn(r.outbox[...], slope).reshape(owners, capacity, -1)
    r.slopes[flat] = r.slope[flat]
    for k in range(owners - 1):
        slope_copy(k).start()
    looked_half = r.looked[own_ents, aligned(t, 128)]
    ents_grad = dot_tn(lin_low, looked_half).astype(low)
    r.e_grads[0] = ents_grad.reshape(2, 2, 2, 2, share, 128)
    stage(kit_e, 0, along[0], 0)[0].start()
    vec_copy(0).start()
    words_back_copy.wait()
    r.grad_words[...] = (
        r.grad_first[aligned(t, quarter), :]
        + (r.input_part[x] + r.mail_in[1, aligned(x, quarter), :])
        + r.words_in[...].astype(full)
    )
    flush(r.grad_words, r.to_grad_words)
    tick()
    for k in range(owners - 1):
        slope_copy(k).wait()
    ids_t = r.asked[...].reshape(slots, 128).astype(full).T
    r.ids_out[...] = ids_t[0:8, :].astype(jnp.int32)
    r.slopes_out[...] = r.slopes[...].reshape(slots, -1).astype(low)
    flush(r.ids_out, r.to_ids_out)
    flush(r.slopes_out, r.to_slopes_out)
    for c in range(2 * downs + 1):
        finish(kit_a, c, along[orders[c]])
        flush(r.out_a.at[c], r.to_out_a.at[c])
    vec_advance(4)
    total = r.vec[4]
    flush(r.vec.at[4], r.to_vec_out)
    r.across_out[...] = pltpu.roll(total[0:8, :], width - flat * share, 1)[:, 0:128]
    flush(r.across_out, r.to_across_out)
    finish(kit_e, 0, along[0])
    ents_out = send(r.e_sum.at[0], r.e_in, r.pair_s.at[7], r.pair_r.at[7], core)
    ents_out.start()
    r.out_e[t] = r.e_sum[0]
    for h in range(heads):
        head_finish(h)
        flush(r.out_q.at[h], r.to_out_q.at[h])
    ents_out.wait()
    r.out_e[1 - t] = r.e_in[...]
    flush(r.out_e, r.to_out_e)
    for copy in flushes:
        copy.wait()


def finish_kernel(names, *refs):
    r = types.SimpleNamespace(**dict(zip(names, refs, strict=True)))
    low, full = jnp.bfloat16, jnp.float32
    table_rows, embed = r.hbm_first.shape
    slots = r.hbm_ids.shape[1]
    steps = r.in_s.shape[1]
    count = table_rows // steps
    chunks, share, chunk = r.hbm_a.shape
    downs = chunks // 2
    heads, side = r.hbm_q.shape[0], r.hbm_q.shape[0] * HD

    pairs = [(r.hbm_ids, r.ids), (r.hbm_slopes, r.slopes)]
    pairs += [(r.hbm_q, r.out_q), (r.hbm_e, r.out_e), (r.hbm_vec, r.vec), (r.hbm_across, r.across)]
    layers = [(r.hbm_a.at[2 * downs], r.out_part)]
    for c in range(downs):
        lanes = slice(c * chunk, (c + 1) * chunk)
        layers.append((r.hbm_a.at[c], r.down_part.at[:, lanes]))
        layers.append((r.hbm_a.at[downs + c], r.up_part.at[:, lanes]))
    layers += [(r.hbm_words, r.words_part), (r.hbm_ents, r.ents_part), (r.hbm_grad, r.grad_part)]
    smalls = [
        pltpu.make_async_copy(source, target, r.small_s.at[n])
        for n, (source, target) in enumerate(pairs + layers)
    ]
    outs = [
        pltpu.make_async_copy(source, target, r.done_s.at[n])
        for n, (source, target) in enumerate(
            [
                (r.out_part, r.red_out),
                (r.down_part, r.red_down),
                (r.up_part, r.red_up),
                (r.words_part, r.words_done.at[0]),
                (r.ents_part, r.ents_done.at[0]),
                (r.grad_part, r.grad_words_done.at[0]),
                (r.query_part, r.red_query),
                (r.keyval_part, r.red_keyval),
            ]
        )
    ]

    def moves(i, inward):
        here = pl.ds(i * count, count)
        if inward:
            ends = [(r.hbm_first, r.first), (r.hbm_second, r.second)]
            flags = r.in_s
        else:
            ends = [(r.update, r.table_update), (r.first, r.new_first), (r.second, r.new_second)]
            flags = r.out_s
        return [
            pltpu.make_async_copy(source.at[here, :], target.at[here, :], flags.at[n, i])
            for n, (source, target) in enumerate(ends)
        ]

    early, late = smalls[:2], smalls[2:]
    for copy in early + moves(0, True) + moves(1, True) + late:
        copy.start()
    for i in range(2, steps):
        for copy in moves(i, True):
            copy.start()
    for copy in early:
        copy.wait()
    r.addends[:, 0:embed] = r.slopes[...]
    r.addends[:, embed:] = jnp.ones((slots, 128), low)

    def adam(i):
        for copy in moves(i, True):
            copy.wait()
        here = pl.ds(i * count, count)
        row = lax.broadcasted_iota(jnp.int32, (count, slots), 0) + i * count
        chosen = jnp.where(row == r.ids[0:1, :], 1.0, 0.0).astype(low)
        total = dot_nn(chosen, r.addends[...])
        touched = total[:, embed:] > 0.0
        for start in range(0, embed, 128):
            lanes = slice(start, start + 128)
            grad = total[:, lanes]
            first, second = r.first[here, lanes], r.second[here, lanes]
            first_next = beta_one * first + (1.0 - beta_one) * grad
            second_next = beta_two * second + (1.0 - beta_two) * grad * grad
            direction = (
                first_next
                * (1.0 / (1.0 - beta_one**adam_steps))
                / (jnp.sqrt(second_next * (1.0 / (1.0 - beta_two**adam_steps))) + adam_eps)
            )
            r.update[here, lanes] = jnp.where(touched, direction, 0.0)
            r.first[here, lanes] = jnp.where(touched, first_next, first)
            r.second[here, lanes] = jnp.where(touched, second_next, second)
        for copy in moves(i, False):
            copy.start()

    def lay_out_rest():
        for copy in late:
            copy.wait()
        for copy in outs[:6]:
            copy.start()
        width = r.vec.shape[1]
        for n in range(2):
            r.red_entity[:, n * 128 : (n + 1) * 128] = r.out_e[n]
            for h in range(heads):
                place = h * 6 * HD
                line = 10 + 2 * n + place // width
                for j in range(6):
                    lanes = slice(n * side + h * HD, n * side + (h + 1) * HD)
                    part = r.out_q[h, n, :, j * HD : (j + 1) * HD]
                    begin = place % width + j * HD
                    line_part = r.vec[line : line + 1, begin : begin + HD]
                    if j < 4:
                        r.query_part[j, :, lanes] = part
                        r.red_query_bias[j : j + 1, lanes] = line_part
                    else:
                        r.keyval_part[j - 4, :, lanes] = part
                    if j == 5:
                        r.value_row[:, lanes] = line_part
        for copy in outs[6:]:
            copy.start()
        r.red_gain[...] = r.across[0:3, 0:share]
        r.red_shift[...] = r.across[3:6, 0:share]
        r.red_value_bias[...] = r.value_row[...].reshape(-1)
        r.red_out_bias[...] = r.across[6:7, 0:share].reshape(-1)
        r.red_down_bias[...] = r.across[7:8, 0:share].reshape(-1)
        for n in range(2):
            r.red_up_bias[n * width : (n + 1) * width] = r.vec[8 + n : 9 + n, :].reshape(-1)

    for i in range(steps):
        adam(i)
        if i == steps // 2:
            lay_out_rest()
    for i in range(steps):
        for copy in moves(i, False):
            copy.wait()
    for copy in outs:
        copy.wait()


SOFT = 32
STEPS = 8
CHUNK, HEAD, ENTS, VEC = range(4)
SCHEDULE = (
    (),
    ((CHUNK, 1, 0), (CHUNK, 0, 0),),
    (),
    ((CHUNK, 3, 0),),
    (),
    (),
    ((CHUNK, 4, 0),),
    (),
    (),
    ((CHUNK, 2, 0),),
    ((CHUNK, 7, 0), (CHUNK, 0, 1),),
    ((CHUNK, 1, 1), (CHUNK, 8, 0), (CHUNK, 6, 0), (CHUNK, 4, 1),),
    ((CHUNK, 2, 1), (CHUNK, 3, 1),),
    (),
    (),
    (),
    (),
    ((CHUNK, 7, 1),),
    ((CHUNK, 2, 2), (CHUNK, 5, 0),),
    ((CHUNK, 0, 2), (CHUNK, 8, 1),),
    (),
    (),
    ((HEAD, 0, 1),),
    ((CHUNK, 0, 3), (CHUNK, 3, 2),),
    ((CHUNK, 2, 3),),
    ((CHUNK, 4, 2), (CHUNK, 7, 2),),
    ((CHUNK, 1, 2), (CHUNK, 6, 1), (HEAD, 0, 2), (CHUNK, 5, 1),),
    ((HEAD, 1, 1), (CHUNK, 4, 3), (CHUNK, 7, 3), (HEAD, 2, 1),),
    ((CHUNK, 1, 3), (HEAD, 1, 2), (CHUNK, 8, 2), (CHUNK, 5, 2), (ENTS, 0, 1), (HEAD, 0, 3), (HEAD, 2, 2), (CHUNK, 6, 2), (VEC, 0, 1), (ENTS, 0, 2), (CHUNK, 5, 3), (CHUNK, 8, 3), (VEC, 0, 2), (CHUNK, 3, 3), (HEAD, 1, 3), (CHUNK, 6, 3), (HEAD, 2, 3), (ENTS, 0, 3), (VEC, 0, 3),),
)
ORDERS = (0, 2, 0, 1, 2, 0, 0, 1, 2)


def fused_local(
    word_states,
    entity_shard,
    entity_row,
    word_segments,
    entity_segments,
    entity_table,
    adam_first,
    adam_second,
    w_entity,
    norm_gain,
    norm_bias,
    w_query,
    b_query,
    w_keyval,
    b_value,
    w_out,
    b_out,
    w_up,
    b_up,
    w_down,
    b_down,
    cot_words,
    cot_entities,
):
    low, full = jnp.bfloat16, jnp.float32
    _, half_words, width = word_states.shape
    half_ents = entity_row.shape[2]
    rows, everyone = half_words + half_ents, 2 * (half_words + half_ents)
    words, ents = 2 * half_words, 2 * half_ents
    table_rows, embed = entity_table.shape
    local_width, hidden = w_query.shape[2], w_up.shape[1]
    owners = lax.axis_size(("dp", "stream"))
    share = width // owners
    capacity = 2 * half_ents // owners
    side = local_width // 2
    heads = side // HD
    chunk = local_width
    chunks = 2 * (hidden // chunk) + 1

    operands = dict(
        hbm_shard=entity_shard.reshape(1, half_ents),
        hbm_row=entity_row.reshape(1, half_ents),
        hbm_word_seg=word_segments,
        hbm_ent_seg=entity_segments,
        hbm_gain=norm_gain,
        hbm_shift=norm_bias,
        hbm_b_query=b_query,
        hbm_b_value=b_value,
        hbm_b_out=b_out,
        hbm_b_up=b_up,
        hbm_b_down=b_down,
        hbm_words=word_states,
        hbm_cot_words=cot_words,
        hbm_cot_ents=cot_entities,
        hbm_query=w_query,
        hbm_keyval=w_keyval,
        hbm_table=entity_table,
        hbm_entity=w_entity,
        hbm_out=w_out,
        hbm_up=w_up,
        hbm_down=w_down,
    )
    results = dict(
        to_out_words=((half_words // 2, width), low),
        to_out_ents=((half_ents // 2, width), low),
        to_grad_words=((half_words // 2, width), full),
        to_out_a=((chunks, share, chunk), full),
        to_out_e=((2, share, 128), full),
        to_out_q=((heads, 2, share, chunk), full),
        to_vec_out=((16, width), full),
        to_across_out=((8, 128), full),
        to_ids_out=((8, owners * capacity), jnp.int32),
        to_slopes_out=((owners * capacity, embed), low),
    )
    mail_rows = max(rows, words // 2 + ents)
    dma = pltpu.SemaphoreType.DMA
    scratch = dict(
        shard=((1, half_ents), jnp.int32),
        row=((1, half_ents), jnp.int32),
        word_seg=(word_segments.shape, jnp.int32),
        ent_seg=(entity_segments.shape, jnp.int32),
        gain=(norm_gain.shape, full),
        shift=(norm_bias.shape, full),
        b_query=(b_query.shape, full),
        b_value=(b_value.shape, full),
        b_out=(b_out.shape, full),
        b_up=(b_up.shape, full),
        b_down=(b_down.shape, full),
        grad_words=((half_words // 2, width), full),
        out_a=((chunks, share, chunk), full),
        out_e=((2, share, 128), full),
        out_q=((heads, 2, share, chunk), full),
        across_out=((8, 128), full),
        ids_out=((8, owners * capacity), jnp.int32),
        slopes_out=((owners * capacity, embed), low),
        w_query=(w_query.shape, low),
        w_keyval=(w_keyval.shape, low),
        table=(entity_table.shape, low),
        w_entity=(w_entity.shape, low),
        w_out=(w_out.shape, low),
        w_up=(w_up.shape, low),
        w_down=(w_down.shape, low),
        cat_words=((width, 4 * side), low),
        cat_ents=((width, 4 * side), low),
        bias_words=((1, 4 * side), full),
        bias_ents=((1, 4 * side), full),
        cotangent=((rows, width), low),
        ask=((owners, capacity, 128), jnp.int32),
        asked=((owners, capacity, 128), jnp.int32),
        outbox=((owners * capacity, half_ents), low),
        select=((ents, owners * 2 * capacity), low),
        found=((owners // 2, 2 * capacity, embed), low),
        answer=((owners, 2 * capacity, embed), low),
        looked=((ents, embed), low),
        ent_lin=((ents, width), full),
        x_ent=((ents, width), full),
        x_all=((everyone, width), low),
        x_own=((rows, width), full),
        words_t=((width, words), low),
        ents_t=((width, ents), low),
        mask=((everyone, everyone), low),
        qkv=((everyone, 4 * side), low),
        key=((heads, everyone, HD), low),
        value=((heads, everyone, HD), low),
        prob=((heads, everyone, everyone), full),
        factor=((heads, everyone, 128), full),
        heads_far=((rows, side), low),
        heads_near=((rows, side), low),
        heads_in=((rows, side), low),
        heads_all=((rows, 2 * side), low),
        mail_out=((2, mail_rows, width), full),
        mail_in=((2, mail_rows, width), full),
        normed=((rows, width), full),
        scale=((rows, 128), full),
        first=((rows, width), low),
        first_t=((width, rows), low),
        act=((rows, hidden), low),
        slope_up=((rows, hidden), full),
        final=((rows, width), low),
        grad_second=((rows, width), full),
        grad_low=((rows, width), low),
        grad_t=((width, rows), low),
        grad_up=((rows, hidden), low),
        grad_first=((rows, width), full),
        back_far=((rows, side), low),
        back_heads=((everyone, side), low),
        grad_prob=((everyone, everyone), full),
        grad_score=((everyone, everyone), low),
        prob_low=((everyone, everyone), low),
        grad_qkv=((everyone, 4 * side), low),
        input_part=((2, half_words // 2, width), full),
        ents_back=((half_ents, width), low),
        ents_in=((half_ents, width), low),
        words_back=((half_words // 2, width), low),
        words_in=((half_words // 2, width), low),
        slope=((owners, capacity, embed), full),
        slopes=((owners, capacity, embed), full),
        e_sum=((1, share, 128), full),
        e_in=((share, 128), full),
        vec=((5, 16, width), full),
        vec_in=((4, 16, width), full),
        grads=((chunks, 2, 2, 2, 2, share, chunk), low),
        near=((chunks, 2, 2, 2, share, chunk), low),
        next=((chunks, 2, 2, share, chunk), low),
        far=((chunks, 2, share, chunk), low),
        last=((chunks, share, chunk), low),
        e_grads=((1, 2, 2, 2, 2, share, 128), low),
        e_near=((1, 2, 2, 2, share, 128), low),
        e_next=((1, 2, 2, share, 128), low),
        e_far=((1, 2, share, 128), low),
        e_last=((1, share, 128), low),
        q_grads=((heads, 2, 2, 2, 2, share, chunk), low),
        q_near=((heads, 2, 2, 2, share, chunk), low),
        q_next=((heads, 2, 2, share, chunk), low),
        q_far=((heads, 2, share, chunk), low),
        q_sum=((heads, 2, share, chunk), full),
        q_in=((heads, share, chunk), full),
    )
    signals = dict(
        load_s=(len(operands),),
        flush_s=(len(results) + chunks + heads,),
        ask_s=(owners - 1,),
        ask_r=(owners - 1,),
        answer_s=(owners - 1,),
        answer_r=(owners - 1,),
        slope_s=(owners - 1,),
        slope_r=(owners - 1,),
        heads_s=(2,),
        heads_r=(2,),
        pair_s=(9,),
        pair_r=(9,),
        strip_s=(3, width // 256),
        strip_r=(3, width // 256),
        swap_s=(2,),
        swap_r=(2,),
        vec_s=(4,),
        vec_r=(4,),
        a_s=(chunks, 4),
        a_r=(chunks, 4),
        e_s=(1, 4),
        e_r=(1, 4),
        q_s=(heads, 4),
        q_r=(heads, 4),
    )
    names = [*operands, *results, *scratch, *signals]
    kernel = functools.partial(layer_kernel, names, ORDERS, SCHEDULE)
    made = pl.pallas_call(
        kernel,
        name="layer",
        out_shape=[jax.ShapeDtypeStruct(*item) for item in results.values()],
        in_specs=[pl.BlockSpec(memory_space=pl.ANY)] * len(operands),
        out_specs=[pl.BlockSpec(memory_space=pl.ANY)] * len(results),
        scratch_shapes=[pltpu.VMEM(*item) for item in scratch.values()]
        + [dma(shape) for shape in signals.values()],
        compiler_params=pltpu.CompilerParams(
            collective_id=0, has_side_effects=True, vmem_limit_bytes=67_043_328
        ),
    )(*operands.values())
    got = types.SimpleNamespace(**dict(zip(results, made, strict=True)))

    given = dict(
        hbm_first=adam_first,
        hbm_second=adam_second,
        hbm_ids=got.to_ids_out,
        hbm_slopes=got.to_slopes_out,
        hbm_a=got.to_out_a,
        hbm_e=got.to_out_e,
        hbm_q=got.to_out_q,
        hbm_vec=got.to_vec_out,
        hbm_across=got.to_across_out,
        hbm_words=got.to_out_words,
        hbm_ents=got.to_out_ents,
        hbm_grad=got.to_grad_words,
    )
    final = dict(
        words_done=(1, half_words // 2, width),
        ents_done=(1, half_ents // 2, width),
        grad_words_done=(1, half_words // 2, width),
        red_entity=(share, embed),
        red_gain=(3, share),
        red_shift=(3, share),
        red_query=(4, share, local_width),
        red_query_bias=(4, local_width),
        red_keyval=(2, share, local_width),
        red_value_bias=(local_width,),
        red_out=(share, local_width),
        red_out_bias=(share,),
        red_up=(share, hidden),
        red_up_bias=(hidden,),
        red_down=(share, hidden),
        red_down_bias=(share,),
        table_update=adam_first.shape,
        new_first=adam_first.shape,
        new_second=adam_first.shape,
    )
    room = dict(
        value_row=((1, local_width), full),
        ids=(got.to_ids_out.shape, jnp.int32),
        slopes=(got.to_slopes_out.shape, low),
        addends=((owners * capacity, embed + 128), low),
        out_e=(got.to_out_e.shape, full),
        out_q=(got.to_out_q.shape, full),
        vec=(got.to_vec_out.shape, full),
        across=(got.to_across_out.shape, full),
        first=(adam_first.shape, full),
        second=(adam_first.shape, full),
        update=(adam_first.shape, full),
        out_part=((share, local_width), full),
        down_part=((share, hidden), full),
        up_part=((share, hidden), full),
        words_part=(got.to_out_words.shape, low),
        ents_part=(got.to_out_ents.shape, low),
        grad_part=(got.to_grad_words.shape, full),
        query_part=((4, share, local_width), full),
        keyval_part=((2, share, local_width), full),
    )
    flags = dict(small_s=(chunks + 9,), done_s=(8,), in_s=(2, STEPS), out_s=(3, STEPS))
    in_place, in_vmem = (pl.BlockSpec(memory_space=space) for space in (pl.ANY, pltpu.VMEM))
    manual = set(dict(words_done=0, ents_done=0, grad_words_done=0, red_query=0, red_keyval=0))
    manual |= set(dict(red_out=0, red_up=0, red_down=0, table_update=0, new_first=0, new_second=0))
    finished = pl.pallas_call(
        functools.partial(finish_kernel, [*given, *final, *room, *flags]),
        name="finish",
        out_shape=[
            jax.ShapeDtypeStruct(shape, low if n < 2 else full)
            for n, shape in enumerate(final.values())
        ],
        in_specs=[in_place] * len(given),
        out_specs=[in_place if name in manual else in_vmem for name in final],
        scratch_shapes=[pltpu.VMEM(*item) for item in room.values()]
        + [dma(shape) for shape in flags.values()],
        compiler_params=pltpu.CompilerParams(vmem_limit_bytes=67_043_328),
    )(*given.values())
    done = dict(zip(final, finished, strict=True))
    return tuple(
        item.T if name in ("red_entity", "red_out", "red_down") else item
        for name, item in done.items()
    )


def plain_local(
    word_states,
    entity_shard,
    entity_row,
    word_segments,
    entity_segments,
    entity_table,
    adam_first,
    adam_second,
    w_entity,
    norm_gain,
    norm_bias,
    w_query,
    b_query,
    w_keyval,
    b_value,
    w_out,
    b_out,
    w_up,
    b_up,
    w_down,
    b_down,
    cot_words,
    cot_entities,
):
    seq_count, half_words, width = word_states.shape
    half_ents = entity_row.shape[2]
    table_rows, embed_width = entity_table.shape
    local_width = w_query.shape[2]
    local_heads = local_width // HD
    owners = lax.axis_size(("dp", "stream"))
    stream_index = lax.axis_index("stream")
    parts = lax.axis_size("tensor")
    part_index = lax.axis_index("tensor")
    word_part = half_words // parts
    ent_part = half_ents // parts
    ent_count = seq_count * half_ents
    word_count = seq_count * half_words
    local_rows = half_words + half_ents
    share_words = seq_count * word_part
    owner_flat = entity_shard.reshape(ent_count)
    row_flat = entity_row.reshape(ent_count)

    def pick(block, count):
        shaped = block.reshape(seq_count, parts, count // parts, block.shape[-1])
        return lax.dynamic_index_in_dim(shaped, part_index, 1, keepdims=False).reshape(
            seq_count * (count // parts), block.shape[-1]
        )

    def own_share(rows):
        return jnp.concatenate(
            [pick(rows[:word_count], half_words), pick(rows[word_count:], half_ents)], 0
        )

    capacity = 2 * ent_count // owners
    owner_hits = (owner_flat[:, None] == jnp.arange(owners, dtype=jnp.int32)[None, :]).astype(
        jnp.int32
    )
    before = jnp.cumsum(owner_hits, 0) - owner_hits
    ranking = jnp.sum(before * owner_hits, 1)
    slot_index = owner_flat * capacity + ranking
    request = (
        jnp.full((owners * capacity,), -1, jnp.int32)
        .at[slot_index]
        .set(row_flat)
        .reshape(owners, capacity)
    )
    asked_ids = lax.all_to_all(request, ("dp", "stream"), split_axis=0, concat_axis=0, tiled=True)
    present = asked_ids >= 0
    found_rows = jnp.take(entity_table, jnp.clip(asked_ids, 0, table_rows - 1), axis=0)
    found_rows = jnp.where(present[..., None], found_rows, jnp.zeros_like(found_rows))
    found_rows, asked_rows = (found_rows, asked_ids)
    answered = lax.all_to_all(found_rows, ("dp", "stream"), split_axis=0, concat_axis=0, tiled=True)
    looked = answered.reshape(owners * capacity, embed_width)[slot_index]
    ent_lin = matmul(looked, w_entity)
    x_entity, entity_norm_back = jax.vjp(layer_norm, ent_lin, norm_gain[0], norm_bias[0])
    entity_low = x_entity.astype(jnp.bfloat16)
    word_low = word_states.reshape(word_count, width)
    query_words = (
        jnp.einsum("rd,jdc->jrc", word_low, w_query[:2], preferred_element_type=jnp.float32)
        + b_query[:2, None, :]
    ).astype(jnp.bfloat16)
    query_ents = (
        jnp.einsum("rd,jdc->jrc", entity_low, w_query[2:], preferred_element_type=jnp.float32)
        + b_query[2:, None, :]
    ).astype(jnp.bfloat16)
    value_shift = jnp.stack([jnp.zeros_like(b_value), b_value])[:, None, :]
    keyval_words = (
        jnp.einsum("rd,jdc->jrc", word_low, w_keyval, preferred_element_type=jnp.float32)
        + value_shift
    ).astype(jnp.bfloat16)
    keyval_ents = (
        jnp.einsum("rd,jdc->jrc", entity_low, w_keyval, preferred_element_type=jnp.float32)
        + value_shift
    ).astype(jnp.bfloat16)
    far_words, far_ents = from_partner((keyval_words, keyval_ents), "stream", 0)

    def by_heads(block, count):
        return block.reshape(block.shape[0], seq_count, count, local_heads, HD)

    queries = jnp.concatenate(
        [by_heads(query_words, half_words), by_heads(query_ents, half_ents)], 2
    )
    keyval_w = jnp.concatenate(
        [by_heads(keyval_words, half_words), by_heads(far_words, half_words)], 2
    )
    keyval_e = jnp.concatenate([by_heads(keyval_ents, half_ents), by_heads(far_ents, half_ents)], 2)
    own_wseg = lax.dynamic_slice_in_dim(word_segments, stream_index * half_words, half_words, 1)
    far_wseg = lax.dynamic_slice_in_dim(
        word_segments, (1 - stream_index) * half_words, half_words, 1
    )
    own_eseg = lax.dynamic_slice_in_dim(entity_segments, stream_index * half_ents, half_ents, 1)
    far_eseg = lax.dynamic_slice_in_dim(
        entity_segments, (1 - stream_index) * half_ents, half_ents, 1
    )
    query_seg = jnp.concatenate([own_wseg, own_eseg], 1)
    key_wseg = jnp.concatenate([own_wseg, far_wseg], 1)
    key_eseg = jnp.concatenate([own_eseg, far_eseg], 1)
    allow_words = query_seg[:, None, :, None] == key_wseg[:, None, None, :]
    allow_ents = query_seg[:, None, :, None] == key_eseg[:, None, None, :]

    def scores_of():
        raw_words = (
            jnp.einsum(
                "sqhd,skhd->shqk", queries[0], keyval_w[0], preferred_element_type=jnp.float32
            )
            * score_scale
        )
        raw_ents = (
            jnp.einsum(
                "sqhd,skhd->shqk", queries[1], keyval_e[0], preferred_element_type=jnp.float32
            )
            * score_scale
        )
        return (
            jnp.where(allow_words, raw_words, masked_score),
            jnp.where(allow_ents, raw_ents, masked_score),
        )

    score_words, score_ents = scores_of()
    highest = jnp.maximum(
        jnp.max(score_words, -1, keepdims=True), jnp.max(score_ents, -1, keepdims=True)
    )
    totals = jnp.sum(jnp.exp(score_words - highest), -1, keepdims=True) + jnp.sum(
        jnp.exp(score_ents - highest), -1, keepdims=True
    )
    log_total = highest + jnp.log(totals)
    low_words = jnp.exp(score_words - log_total).astype(jnp.bfloat16)
    low_ents = jnp.exp(score_ents - log_total).astype(jnp.bfloat16)
    heads_out = jnp.einsum(
        "shqk,skhd->sqhd", low_words, keyval_w[1], preferred_element_type=jnp.float32
    )
    heads_out = heads_out + jnp.einsum(
        "shqk,skhd->sqhd", low_ents, keyval_e[1], preferred_element_type=jnp.float32
    )
    heads_out = heads_out.astype(jnp.bfloat16).reshape(seq_count, local_rows, local_width)
    heads_dense = jnp.concatenate(
        [
            heads_out[:, :half_words].reshape(word_count, local_width),
            heads_out[:, half_words:].reshape(ent_count, local_width),
        ],
        0,
    )
    resid_in = jnp.concatenate([word_low.astype(jnp.float32), x_entity], 0)
    cotangent = jnp.concatenate(
        [cot_words.reshape(word_count, width), cot_entities.reshape(ent_count, width)], 0
    ).astype(jnp.float32)
    attn_out = tensor_total(matmul(heads_dense, w_out)) + b_out
    first_norm, first_back = jax.vjp(layer_norm, resid_in + attn_out, norm_gain[1], norm_bias[1])
    first_low = first_norm.astype(jnp.bfloat16)
    up_value = matmul(first_low, w_up) + b_up
    active, gelu_back = jax.vjp(gelu_exact, up_value)
    active_low = active.astype(jnp.bfloat16)
    ffn_out = tensor_total(matmul(active_low, w_down)) + b_down
    final_norm, final_back = jax.vjp(layer_norm, first_norm + ffn_out, norm_gain[2], norm_bias[2])
    final_share = own_share(final_norm)
    grad_final, gain_final, shift_final = final_back(cotangent)
    grad_ffn = grad_final.astype(jnp.bfloat16)
    out_words = final_share[:share_words].reshape(seq_count, word_part, width).astype(jnp.bfloat16)
    out_entities = (
        final_share[share_words:].reshape(seq_count, ent_part, width).astype(jnp.bfloat16)
    )
    grad_down = jnp.einsum("rf,rd->fd", active_low, grad_ffn, preferred_element_type=jnp.float32)
    grad_down_bias = jnp.sum(grad_ffn.astype(jnp.float32), 0)
    (grad_pre,) = gelu_back(
        jnp.einsum("rd,fd->rf", grad_ffn, w_down, preferred_element_type=jnp.float32)
    )
    grad_up_low = grad_pre.astype(jnp.bfloat16)
    grad_up = jnp.einsum("rd,rf->df", first_low, grad_up_low, preferred_element_type=jnp.float32)
    grad_up_bias = jnp.sum(grad_up_low.astype(jnp.float32), 0)
    ffn_term = jnp.einsum("rf,df->rd", grad_up_low, w_up, preferred_element_type=jnp.float32)
    grad_first, gain_first, shift_first = first_back(grad_final + tensor_total(ffn_term))
    grad_attn = grad_first.astype(jnp.bfloat16)
    grad_out = jnp.einsum("rc,rd->cd", heads_dense, grad_attn, preferred_element_type=jnp.float32)
    grad_out_bias = jnp.sum(grad_attn.astype(jnp.float32), 0)
    grad_heads = jnp.einsum(
        "rd,cd->rc", grad_attn, w_out, preferred_element_type=jnp.float32
    ).astype(jnp.bfloat16)
    grad_heads = jnp.concatenate(
        [
            grad_heads[:word_count].reshape(seq_count, half_words, local_heads, HD),
            grad_heads[word_count:].reshape(seq_count, half_ents, local_heads, HD),
        ],
        1,
    )
    score_words, score_ents = scores_of()
    prob_words = jnp.exp(score_words - log_total)
    prob_ents = jnp.exp(score_ents - log_total)
    low_words = prob_words.astype(jnp.bfloat16)
    low_ents = prob_ents.astype(jnp.bfloat16)
    dprob_words = jnp.einsum(
        "sqhd,skhd->shqk", grad_heads, keyval_w[1], preferred_element_type=jnp.float32
    )
    dprob_ents = jnp.einsum(
        "sqhd,skhd->shqk", grad_heads, keyval_e[1], preferred_element_type=jnp.float32
    )
    inner_sum = jnp.sum(prob_words * dprob_words, -1, keepdims=True) + jnp.sum(
        prob_ents * dprob_ents, -1, keepdims=True
    )
    dscore_words = (prob_words * (dprob_words - inner_sum)).astype(jnp.bfloat16)
    dscore_ents = (prob_ents * (dprob_ents - inner_sum)).astype(jnp.bfloat16)
    grad_to_words = (
        jnp.einsum("shqk,skhd->sqhd", dscore_words, keyval_w[0], preferred_element_type=jnp.float32)
        * score_scale
    ).astype(jnp.bfloat16)
    grad_to_ents = (
        jnp.einsum("shqk,skhd->sqhd", dscore_ents, keyval_e[0], preferred_element_type=jnp.float32)
        * score_scale
    ).astype(jnp.bfloat16)
    kv_grad_words = jnp.stack(
        [
            jnp.einsum(
                "shqk,sqhd->skhd", dscore_words, queries[0], preferred_element_type=jnp.float32
            )
            * score_scale,
            jnp.einsum(
                "shqk,sqhd->skhd", low_words, grad_heads, preferred_element_type=jnp.float32
            ),
        ]
    )
    kv_grad_ents = jnp.stack(
        [
            jnp.einsum(
                "shqk,sqhd->skhd", dscore_ents, queries[1], preferred_element_type=jnp.float32
            )
            * score_scale,
            jnp.einsum("shqk,sqhd->skhd", low_ents, grad_heads, preferred_element_type=jnp.float32),
        ]
    )
    back_words, back_ents = (
        from_partner(kv_grad_words[:, :, half_words:].astype(jnp.bfloat16), "stream", 0).astype(
            jnp.float32
        ),
        from_partner(kv_grad_ents[:, :, half_ents:].astype(jnp.bfloat16), "stream", 0).astype(
            jnp.float32
        ),
    )
    grad_kv_words = (
        (kv_grad_words[:, :, :half_words] + back_words)
        .reshape(2, word_count, local_width)
        .astype(jnp.bfloat16)
    )
    grad_kv_ents = (
        (kv_grad_ents[:, :, :half_ents] + back_ents)
        .reshape(2, ent_count, local_width)
        .astype(jnp.bfloat16)
    )
    grad_q_words = jnp.stack([grad_to_words[:, :half_words], grad_to_ents[:, :half_words]]).reshape(
        2, word_count, local_width
    )
    grad_q_ents = jnp.stack([grad_to_words[:, half_words:], grad_to_ents[:, half_words:]]).reshape(
        2, ent_count, local_width
    )
    grad_query = jnp.concatenate(
        [
            jnp.einsum("rd,jrc->jdc", word_low, grad_q_words, preferred_element_type=jnp.float32),
            jnp.einsum("rd,jrc->jdc", entity_low, grad_q_ents, preferred_element_type=jnp.float32),
        ],
        0,
    )
    grad_query_bias = jnp.concatenate(
        [jnp.sum(grad_q_words.astype(jnp.float32), 1), jnp.sum(grad_q_ents.astype(jnp.float32), 1)],
        0,
    )
    grad_keyval = jnp.einsum(
        "rd,jrc->jdc", word_low, grad_kv_words, preferred_element_type=jnp.float32
    ) + jnp.einsum("rd,jrc->jdc", entity_low, grad_kv_ents, preferred_element_type=jnp.float32)
    grad_value_bias = jnp.sum(grad_kv_words[1].astype(jnp.float32), 0) + jnp.sum(
        grad_kv_ents[1].astype(jnp.float32), 0
    )
    input_words = jnp.einsum(
        "jrc,jdc->rd", grad_q_words, w_query[:2], preferred_element_type=jnp.float32
    ) + jnp.einsum("jrc,jdc->rd", grad_kv_words, w_keyval, preferred_element_type=jnp.float32)
    input_ents = jnp.einsum(
        "jrc,jdc->rd", grad_q_ents, w_query[2:], preferred_element_type=jnp.float32
    ) + jnp.einsum("jrc,jdc->rd", grad_kv_ents, w_keyval, preferred_element_type=jnp.float32)
    input_term = jnp.concatenate([input_words, input_ents], 0)
    grad_input = grad_first + tensor_total(input_term)
    grad_share = own_share(grad_input)
    grad_lin, gain_entity, shift_entity = entity_norm_back(grad_input[word_count:])
    grad_lin_low = grad_lin.astype(jnp.bfloat16)
    gain_grads = jnp.stack([gain_entity, gain_first, gain_final])
    shift_grads = jnp.stack([shift_entity, shift_first, shift_final])
    grad_words = grad_share[:share_words].reshape(seq_count, word_part, width)
    grad_entity = jnp.einsum("re,rd->ed", looked, grad_lin_low, preferred_element_type=jnp.float32)
    grad_looked = jnp.einsum(
        "rd,ed->re", grad_lin_low, w_entity, preferred_element_type=jnp.float32
    )
    outgoing = (
        jnp.zeros((owners * capacity, embed_width), jnp.float32)
        .at[slot_index]
        .set(grad_looked)
        .reshape(owners, capacity, embed_width)
    )
    incoming = lax.all_to_all(
        outgoing.astype(jnp.bfloat16), ("dp", "stream"), split_axis=0, concat_axis=0, tiled=True
    ).astype(outgoing.dtype)
    target = jnp.where(asked_rows >= 0, asked_rows, table_rows).reshape(-1)
    gradient_sum = (
        jnp.zeros((table_rows, embed_width), jnp.float32)
        .at[target]
        .add(incoming.reshape(-1, embed_width), mode="drop")
    )
    use_count = jnp.zeros((table_rows,), jnp.float32).at[target].add(1.0, mode="drop")
    touched = (use_count > 0.0)[:, None]
    first_next = beta_one * adam_first + (1.0 - beta_one) * gradient_sum
    second_next = beta_two * adam_second + (1.0 - beta_two) * gradient_sum * gradient_sum
    direction = (
        first_next
        / (1.0 - beta_one**adam_steps)
        / (jnp.sqrt(second_next / (1.0 - beta_two**adam_steps)) + adam_eps)
    )
    table_update = jnp.where(touched, direction, jnp.zeros_like(direction))
    new_first = jnp.where(touched, first_next, adam_first)
    new_second = jnp.where(touched, second_next, adam_second)
    (
        red_entity,
        red_gain,
        red_shift,
        red_query,
        red_keyval,
        red_out,
        red_out_bias,
        red_up,
        red_down,
        red_down_bias,
    ) = (
        lax.psum_scatter(grad_entity, ("dp", "stream"), scatter_dimension=1, tiled=True),
        lax.psum_scatter(gain_grads, ("dp", "stream"), scatter_dimension=1, tiled=True),
        lax.psum_scatter(shift_grads, ("dp", "stream"), scatter_dimension=1, tiled=True),
        lax.psum_scatter(grad_query, ("dp", "stream"), scatter_dimension=1, tiled=True),
        lax.psum_scatter(grad_keyval, ("dp", "stream"), scatter_dimension=1, tiled=True),
        lax.psum_scatter(grad_out, ("dp", "stream"), scatter_dimension=1, tiled=True),
        lax.psum_scatter(grad_out_bias, ("dp", "stream"), scatter_dimension=0, tiled=True),
        lax.psum_scatter(grad_up, ("dp", "stream"), scatter_dimension=0, tiled=True),
        lax.psum_scatter(grad_down, ("dp", "stream"), scatter_dimension=1, tiled=True),
        lax.psum_scatter(grad_down_bias, ("dp", "stream"), scatter_dimension=0, tiled=True),
    )
    red_query_bias, red_value_bias, red_up_bias = lax.psum(
        (grad_query_bias, grad_value_bias, grad_up_bias), ("dp", "stream")
    )
    return (
        out_words,
        out_entities,
        grad_words,
        red_entity,
        red_gain,
        red_shift,
        red_query,
        red_query_bias,
        red_keyval,
        red_value_bias,
        red_out,
        red_out_bias,
        red_up,
        red_up_bias,
        red_down,
        red_down_bias,
        table_update,
        new_first,
        new_second,
    )


def solution(mesh):
    placed = (
        P("dp", "stream", None),
        P("stream", "dp", None, None),
        P("stream", "dp", None),
        P("dp", None),
        P("dp", None),
        P(("dp", "stream"), None),
        P(("dp", "stream"), None),
        P(("dp", "stream"), None),
        P(),
        P(),
        P(),
        P(None, None, "tensor"),
        P(None, "tensor"),
        P(None, None, "tensor"),
        P("tensor"),
        P("tensor", None),
        P(),
        P(None, "tensor"),
        P("tensor"),
        P("tensor", None),
        P(),
        P("dp", "stream", None),
        P("dp", "stream", None),
    )
    fits = mesh.shape["stream"] == 2 and mesh.shape["tensor"] == 2 and mesh.shape["dp"] == 8

    def local(*blocks):
        width, owners = blocks[0].shape[2], mesh.shape["dp"] * mesh.shape["stream"]
        if fits and width % (16 * owners) == 0 and blocks[0].shape[0] == 1:
            return fused_local(*blocks)
        return plain_local(*blocks)

    return jax.shard_map(
        local,
        mesh=mesh,
        in_specs=placed,
        out_specs=(
            P("dp", ("stream", "tensor"), None),
            P("dp", ("stream", "tensor"), None),
            P("dp", ("stream", "tensor"), None),
            P(None, ("dp", "stream")),
            P(None, ("dp", "stream")),
            P(None, ("dp", "stream")),
            P(None, ("dp", "stream"), "tensor"),
            P(None, "tensor"),
            P(None, ("dp", "stream"), "tensor"),
            P("tensor"),
            P("tensor", ("dp", "stream")),
            P(("dp", "stream")),
            P(("dp", "stream"), "tensor"),
            P("tensor"),
            P("tensor", ("dp", "stream")),
            P(("dp", "stream")),
            P(("dp", "stream"), None),
            P(("dp", "stream"), None),
            P(("dp", "stream"), None),
        ),
        check_vma=False,
    )
```

```python
import functools
import math
import types

import jax
import jax.numpy as jnp
from jax import lax
from jax.experimental import pallas as pl
from jax.experimental.pallas import tpu as pltpu
from jax.sharding import PartitionSpec as P

HD = 64
MESH_ID = pl.DeviceIdType.MESH


norm_eps = 1e-05
score_scale = 0.125
masked_score = -1e30
beta_one = 0.9
beta_two = 0.99
adam_steps = 10
adam_eps = 1e-08


def from_partner(block, axis, apart):
    count = lax.axis_size(axis)
    route = []
    for low in range(count):
        high = low | 1 << apart
        if high != low and high < count:
            route += [(low, high), (high, low)]
    return lax.ppermute(block, axis, route)


def layer_norm(values_in, gain_row, shift_row):
    center = values_in - jnp.mean(values_in, -1, keepdims=True)
    spread = jnp.mean(center * center, -1, keepdims=True)
    return center * lax.rsqrt(spread + norm_eps) * gain_row + shift_row


def gelu_exact(values_in):
    return jax.nn.gelu(values_in, approximate=False)


def matmul(matrix_a, matrix_b):
    return jnp.dot(matrix_a, matrix_b, preferred_element_type=jnp.float32)


def tensor_total(values_in):
    return lax.psum(values_in, "tensor")


def send(source, target, send_sem, recv_sem, peer):
    return pltpu.make_async_remote_copy(
        src_ref=source,
        dst_ref=target,
        send_sem=send_sem,
        recv_sem=recv_sem,
        device_id=peer,
        device_id_type=MESH_ID,
    )


def row_sum(block):
    return jnp.sum(block, 0, keepdims=True)


def lane_mean(block):
    return jnp.mean(block, -1, keepdims=True)


def dot_nn(left, right):
    return jnp.dot(left, right, preferred_element_type=jnp.float32)


def dot_nt(left, right):
    return lax.dot_general(
        left, right, (((1,), (1,)), ((), ())), preferred_element_type=jnp.float32
    )


def dot_tn(left, right):
    return lax.dot_general(
        left, right, (((0,), (0,)), ((), ())), preferred_element_type=jnp.float32
    )


def normalize(rows):
    center = rows - lane_mean(rows)
    scale = lax.rsqrt(lane_mean(center * center) + norm_eps)
    return center * scale, scale


def normalize_back(grad, normed, scale, gain):
    inner = grad * gain
    return scale * (inner - lane_mean(inner) - normed * lane_mean(inner * normed))


def aligned(index, step):
    return pl.ds(pl.multiple_of(index * step, step), step)


def layer_kernel(names, orders, ents_order, vec_order, schedule, *refs):
    r = types.SimpleNamespace(**dict(zip(names, refs, strict=True)))
    low, full = jnp.bfloat16, jnp.float32
    dp, x, t = lax.axis_index("dp"), lax.axis_index("stream"), lax.axis_index("tensor")
    y, z = lax.rem(dp, 2), dp // 2
    owners = lax.axis_size("dp") * 2
    _, half_words, width = r.hbm_words.shape
    half_ents = r.shard.shape[1]
    rows, words = half_words + half_ents, 2 * half_words
    everyone = 2 * rows
    capacity = r.ask.shape[1]
    slots = owners * capacity
    heads = r.prob.shape[0]
    share = width // owners
    side = heads * HD
    hidden = r.w_up.shape[1]
    block = half_ents
    blocks = rows // block
    word_blocks = half_words // block
    wide = 256

    core, x_peer, y_peer = {"tensor": 1 - t}, {"stream": 1 - x}, {"dp": z * 2 + 1 - y}
    z_low, z_high = lax.rem(z, 2), z // 2
    near_peer = {"dp": (z + 1 - 2 * z_low) * 2 + y}
    far_peer = {"dp": (z + 2 - 4 * z_high) * 2 + y}
    mine_on = (z_high, z_low, y, x)
    peer_on = (far_peer, near_peer, y_peer, x_peer)
    flat = dp * 2 + x
    others = []
    for k in range(1, owners):
        other = lax.rem(flat + k, owners)
        others.append((other, {"dp": other // 2, "stream": lax.rem(other, 2)}))

    loads = {}
    barrier = pltpu.get_barrier_semaphore()
    for peer in [core] + [peer for _, peer in others]:
        pl.semaphore_signal(barrier, inc=1, device_id=peer, device_id_type=MESH_ID)

    def load(source, target):
        loads[id(target)] = pltpu.make_async_copy(source, target, r.load_s.at[len(loads)])
        loads[id(target)].start()

    def loaded(target):
        loads.pop(id(target)).wait()

    load(r.hbm_shard, r.shard)
    load(r.hbm_row, r.row)
    my_words = r.x_all.at[aligned(x, half_words), :]
    load(r.hbm_words.at[0], my_words)
    load(r.hbm_query, r.w_query)
    load(r.hbm_keyval, r.w_keyval)
    smalls = [
        (r.hbm_b_query, r.b_query), (r.hbm_b_value, r.b_value), (r.hbm_word_seg, r.word_seg),
        (r.hbm_ent_seg, r.ent_seg), (r.hbm_gain, r.gain), (r.hbm_shift, r.shift),
        (r.hbm_b_out, r.b_out), (r.hbm_b_up, r.b_up), (r.hbm_b_down, r.b_down),
    ]
    for source, target in smalls:
        load(source, target)
    load(r.hbm_table, r.table)
    load(r.hbm_entity, r.w_entity)
    cot_words, cot_ents = r.cotangent.at[0:half_words, :], r.cotangent.at[half_words:rows, :]
    load(r.hbm_cot_words.at[0], cot_words)
    load(r.hbm_cot_ents.at[0], cot_ents)
    load(r.hbm_out, r.w_out)
    load(r.hbm_up, r.w_up)
    load(r.hbm_down, r.w_down)

    flushes = []

    def flush(source, target):
        flushes.append(pltpu.make_async_copy(source, target, r.flush_s.at[len(flushes)]))
        flushes[-1].start()

    loaded(r.shard)
    loaded(r.row)
    shard_row = r.shard[...]
    shard_all = jnp.broadcast_to(shard_row.astype(full), (half_ents, half_ents)).T
    shard_all = shard_all.astype(jnp.int32)
    shard_col = shard_all[:, 0:1]
    below = lax.broadcasted_iota(jnp.int32, (half_ents, half_ents), 0)
    beside = lax.broadcasted_iota(jnp.int32, (half_ents, half_ents), 1)
    same = shard_all == shard_row
    rank_row = row_sum(jnp.where(same & (below < beside), 1.0, 0.0)).astype(jnp.int32)
    rank_col = jnp.sum(jnp.where(same & (beside < below), 1.0, 0.0), 1, keepdims=True)
    rank_col = rank_col.astype(jnp.int32)
    slot_row = shard_row * capacity + rank_row
    in_slot = lax.broadcasted_iota(jnp.int32, (slots, half_ents), 0) == slot_row
    wanted = jnp.sum(
        jnp.where(in_slot, (r.row[...] + 1).astype(full), 0.0), 1, keepdims=True
    )
    wanted = wanted.astype(jnp.int32) - 1
    r.ask[...] = jnp.broadcast_to(wanted, (slots, 128)).reshape(owners, capacity, 128)
    r.outbox[...] = jnp.where(in_slot, 1.0, 0.0).astype(low)
    answer_col = shard_col * (2 * capacity) + x * capacity + rank_col
    answer_lane = lax.broadcasted_iota(jnp.int32, (half_ents, 2 * slots), 1)
    r.select[aligned(x, half_ents), :] = jnp.where(answer_lane == answer_col, 1.0, 0.0).astype(low)
    r.asked[flat] = r.ask[flat]
    r.vec[0] = jnp.zeros(r.vec.shape[1:], full)

    loaded(r.w_query)
    loaded(r.w_keyval)
    for _, target in smalls:
        loaded(target)

    def gather_columns(which):
        for h in range(heads):
            own = slice(which * side + h * HD, which * side + (h + 1) * HD)
            for place, words_part, ents_part in (
                (0, r.w_query[0, :, own], r.w_query[2, :, own]),
                (1, r.w_query[1, :, own], r.w_query[3, :, own]),
                (2, r.w_keyval[0, :, own], None),
                (3, r.w_keyval[1, :, own], None),
            ):
                lanes = slice((4 * h + place) * HD, (4 * h + place + 1) * HD)
                r.cat_words[:, lanes] = words_part
                r.cat_ents[:, lanes] = words_part if ents_part is None else ents_part
            zero = jnp.zeros((1, HD), full)
            value = r.b_value[...].reshape(1, -1)[:, own]
            query = r.b_query[:, own]
            lanes = slice(4 * h * HD, 4 * (h + 1) * HD)
            r.bias_words[:, lanes] = jnp.concatenate([query[0:1], query[1:2], zero, value], 1)
            r.bias_ents[:, lanes] = jnp.concatenate([query[2:3], query[3:4], zero, value], 1)

    for which in range(2):

        @pl.when(x == which)
        def _(which=which):
            gather_columns(which)

    loaded(my_words)
    r.x_own[0:half_words, :] = my_words[...].astype(full)
    pl.semaphore_wait(barrier, owners)

    def ask_copy(k):
        other, peer = others[k]
        return send(r.ask.at[other], r.asked.at[flat], r.ask_s.at[k], r.ask_r.at[k], peer)

    def answer_copy(k):
        other, peer = others[k]
        return send(
            r.found.at[other // 2], r.answer.at[flat], r.answer_s.at[k], r.answer_r.at[k], peer
        )

    def slope_copy(k):
        other, peer = others[k]
        return send(r.slope.at[other], r.slopes.at[flat], r.slope_s.at[k], r.slope_r.at[k], peer)

    for k in range(owners - 1):
        ask_copy(k).start()
    my_select = r.select.at[aligned(x, half_ents), :]
    select_copy = send(my_select, my_select, r.pair_s.at[0], r.pair_r.at[0], x_peer)
    select_copy.start()
    half = half_words // 2
    my_half = r.x_all.at[aligned(2 * x + t, half), :]
    words_copy = send(my_half, my_half, r.pair_s.at[1], r.pair_r.at[1], x_peer)
    words_copy.start()

    is_query = lax.broadcasted_iota(jnp.int32, (1, 4 * HD), 1) < 2 * HD
    scaling = jnp.where(is_query, score_scale, 1.0)

    def project(start, count, weight, bias):
        def body(h, carry):
            lanes = aligned(h, 4 * HD)
            total = dot_nn(r.x_all[pl.ds(start, count), :], weight[:, lanes]) + bias[:, lanes]
            r.qkv[pl.ds(start, count), lanes] = (total * scaling).astype(low)
            return carry

        lax.fori_loop(0, heads, body, 0)

    project(pl.multiple_of(x * half_words, half_words), half_words, r.cat_words, r.bias_words)

    segments = jnp.concatenate([r.word_seg[...], r.ent_seg[...]], 1)
    for i in range(everyone // 128):
        own_seg = jnp.broadcast_to(segments[:, i * 128 : (i + 1) * 128].astype(full), (128, 128)).T
        equal = own_seg[:, 0:1].astype(jnp.int32) == segments
        r.mask[i * 128 : (i + 1) * 128, :] = jnp.where(equal, 0.0, masked_score).astype(low)

    for k in range(owners - 1):
        ask_copy(k).wait()
    ids = r.asked[...].reshape(slots, 128)
    lane = lax.broadcasted_iota(jnp.int32, (slots, 128), 1)
    loaded(r.table)
    piece = 4 * 128

    def pick_body(j, found):
        ones = [jnp.where(ids == lane + (j * piece + n * 128), 1.0, 0.0) for n in range(4)]
        return found + dot_nn(jnp.concatenate(ones, 1).astype(low), r.table[aligned(j, piece), :])

    found = jnp.zeros((slots, r.table.shape[1]), full)
    found = lax.fori_loop(0, r.table.shape[0] // piece, pick_body, found, unroll=True).astype(low)
    r.found[...] = found.reshape(r.found.shape)
    r.answer[flat] = r.found[dp]
    for k in range(owners - 1):
        answer_copy(k).start()

    words_copy.wait()
    far_half = r.x_all.at[aligned(2 * (1 - x) + t, half), :]
    relay = send(far_half, far_half, r.pair_s.at[8], r.pair_r.at[8], core)
    relay.start()
    relay.wait()
    project(pl.multiple_of((1 - x) * half_words, half_words), half_words, r.cat_words, r.bias_words)

    def take_heads(here):
        for h in range(heads):
            r.key[h, here, :] = r.qkv[here, h * 4 * HD + 2 * HD : h * 4 * HD + 3 * HD]
            r.value[h, here, :] = r.qkv[here, h * 4 * HD + 3 * HD : h * 4 * HD + 4 * HD]

    of_words, of_ents = slice(0, words), slice(words, everyone)
    take_heads(of_words)
    for h in range(heads):
        query = r.qkv[of_words, h * 4 * HD : h * 4 * HD + HD]
        r.prob[h, of_words, of_words] = dot_nt(query, r.key[h, of_words, :])

    def soften_words(which):
        def body(i, carry):
            here = pl.ds(pl.multiple_of(which * half_words + i * SOFT, SOFT), SOFT)
            bias = r.mask[here, of_words].astype(full)
            for h in range(heads):
                score = r.prob[h, here, of_words] + bias
                peak = jnp.max(score, 1, keepdims=True)
                power = jnp.exp(score - peak)
                r.prob[h, here, of_words] = power
                r.factor[h, here, :] = jnp.broadcast_to(peak, (SOFT, 128))
                mass = jnp.broadcast_to(jnp.sum(power, 1, keepdims=True), (SOFT, 128))
                r.mass[h, here, :] = mass
            return carry

        lax.fori_loop(0, half_words // SOFT, body, 0)

    soften_words(0)
    soften_words(1)
    for h in range(heads):
        weights = r.prob[h, of_words, of_words].astype(low)
        r.grad_prob[of_words, h * 128 : h * 128 + HD] = dot_nn(weights, r.value[h, of_words, :])
        r.factor[h, of_ents, :] = jnp.ones((2 * half_ents, 128), full)

    select_copy.wait()
    for k in range(owners - 1):
        answer_copy(k).wait()
    looked = dot_nn(r.select[...], r.answer[...].reshape(2 * slots, r.table.shape[1])).astype(low)
    r.looked[...] = looked
    loaded(r.w_entity)
    ent_lin = dot_nn(looked, r.w_entity[...])
    normed, _ = normalize(ent_lin)
    x_entity = normed * r.gain[0:1, :] + r.shift[0:1, :]
    r.ent_lin[...] = ent_lin
    r.x_ent[...] = x_entity
    r.x_all[words:everyone, :] = x_entity.astype(low)
    r.x_own[half_words:rows, :] = r.x_ent[aligned(x, half_ents), :]
    project(words, 2 * half_ents, r.cat_ents, r.bias_ents)
    take_heads(of_ents)

    def both_kinds(which):
        near_words = pl.ds(pl.multiple_of(which * half_words, half_words), half_words)
        near_ents = pl.ds(pl.multiple_of(words + which * half_ents, half_ents), half_ents)
        return (near_words, slice(0, half_words)), (near_ents, slice(half_words, rows))

    def soften_ents(here):
        bias = r.mask[here, :].astype(full)
        for h in range(heads):
            score = r.prob[h, here, :] + bias
            power = jnp.exp(score - jnp.max(score, 1, keepdims=True))
            r.prob[h, here, :] = power * (1.0 / jnp.sum(power, 1, keepdims=True))

    def complete_words(here):
        bias = r.mask[here, of_ents].astype(full)
        for h in range(heads):
            score = r.prob[h, here, of_ents] + bias
            peak = r.factor[h, here, :]
            best = jnp.broadcast_to(jnp.max(score, 1, keepdims=True), (half_words, 128))
            top = jnp.maximum(peak, best)
            power, shrink = jnp.exp(score - top), jnp.exp(peak - top)
            added = jnp.broadcast_to(jnp.sum(power, 1, keepdims=True), (half_words, 128))
            share_of = 1.0 / (r.mass[h, here, :] * shrink + added)
            r.prob[h, here, of_ents] = power * share_of
            r.factor[h, here, :] = shrink * share_of

    def attend_words(which, target):
        (here, there), _ = both_kinds(which)
        for h in range(heads):
            query = r.qkv[here, h * 4 * HD + HD : h * 4 * HD + 2 * HD]
            r.prob[h, here, of_ents] = dot_nt(query, r.key[h, of_ents, :])
        complete_words(here)
        for h in range(heads):
            out = r.grad_prob[here, h * 128 : h * 128 + HD] * r.factor[h, here, 0:HD]
            out = out + dot_nn(r.prob[h, here, of_ents].astype(low), r.value[h, of_ents, :])
            target[there, h * HD : (h + 1) * HD] = out.astype(low)

    def attend_ents(which, target):
        _, (here, there) = both_kinds(which)
        for h in range(heads):
            query = r.qkv[here, h * 4 * HD : h * 4 * HD + 2 * HD]
            r.prob[h, here, of_words] = dot_nt(query[:, :HD], r.key[h, of_words, :])
            r.prob[h, here, of_ents] = dot_nt(query[:, HD:], r.key[h, of_ents, :])
        soften_ents(here)
        for h in range(heads):
            out = dot_nn(r.prob[h, here, :].astype(low), r.value[h])
            target[there, h * HD : (h + 1) * HD] = out.astype(low)

    def heads_part(n, part):
        return send(
            r.heads_far.at[part, :], r.heads_in.at[part, :], r.heads_s.at[n], r.heads_r.at[n], x_peer
        )

    attend_words(1 - x, r.heads_far)
    heads_copies = [heads_part(0, slice(0, half_words))]
    heads_copies[0].start()
    attend_ents(1 - x, r.heads_far)
    heads_copies.append(heads_part(1, slice(half_words, rows)))
    heads_copies[1].start()
    attend_words(x, r.heads_near)
    attend_ents(x, r.heads_near)
    r.words_t[...] = r.x_all[of_words, :].T
    r.ents_t[...] = r.x_all[of_ents, :].T
    for copy in heads_copies:
        copy.wait()

    @pl.when(x == 0)
    def _():
        r.heads_all[:, 0:side] = r.heads_near[...]
        r.heads_all[:, side:] = r.heads_in[...]

    @pl.when(x == 1)
    def _():
        r.heads_all[:, 0:side] = r.heads_in[...]
        r.heads_all[:, side:] = r.heads_near[...]

    def strip(which, turn, j):
        part = (which, slice(0, rows), aligned(j, wide))
        return send(
            r.mail_out.at[part], r.mail_in.at[part], r.strip_s.at[turn, j], r.strip_r.at[turn, j], core
        )

    def arrived(which, here):
        return r.mail_out[which, here, :].astype(full) + r.mail_in[which, here, :].astype(full)

    def wait_strips(which, turn):
        for j in range(width // wide):
            strip(which, turn, j).wait()

    def swap(which, turn, first, count):
        part = pl.ds(first, count)
        return send(
            r.mail_out.at[which, part], r.mail_in.at[which, part], r.swap_s.at[turn],
            r.swap_r.at[turn], core,
        )

    def columns(count, fill):
        def body(j, carry):
            fill(aligned(j, wide), j)
            return carry

        lax.fori_loop(0, count // wide, body, 0)

    def fill_attn(lanes, j):
        r.mail_out[0, 0:rows, lanes] = dot_nn(r.heads_all[...], r.w_out[:, lanes]).astype(low)
        strip(0, 0, j).start()

    loaded(r.w_out)
    columns(width, fill_attn)
    wait_strips(0, 0)

    def over_rows(body):
        def step(i, carry):
            body(aligned(i, block))
            return carry

        lax.fori_loop(0, blocks, step, 0)

    def first_norm(here):
        attn = arrived(0, here) + r.b_out[...].reshape(1, -1)
        normed, scale = normalize(r.x_own[here, :] + attn)
        r.normed[here, :] = normed
        r.scale[here, :] = jnp.broadcast_to(scale, (block, 128))
        r.first[here, :] = (normed * r.gain[1:2, :] + r.shift[1:2, :]).astype(low)

    over_rows(first_norm)

    def fill_up(lanes, _):
        up = dot_nn(r.first[...], r.w_up[:, lanes]) + r.b_up[lanes].reshape(1, -1)
        chance = 0.5 + 0.5 * lax.erf(up * (0.5**0.5))
        r.act[:, lanes] = (up * chance).astype(low)
        r.slope_up[:, lanes] = chance + up * (jnp.exp(-0.5 * up * up) * (0.5 / math.pi) ** 0.5)

    loaded(r.w_up)
    columns(hidden, fill_up)

    def fill_down(lanes, j):
        r.mail_out[1, 0:rows, lanes] = dot_nn(r.act[...], r.w_down[:, lanes]).astype(low)
        strip(1, 1, j).start()

    loaded(r.w_down)
    columns(width, fill_down)
    wait_strips(1, 1)

    vec = r.vec.at[0]

    def second_norm(here):
        ffn = arrived(1, here) + r.b_down[...].reshape(1, -1)
        entering = r.normed[here, :] * r.gain[1:2, :] + r.shift[1:2, :]
        normed, scale = normalize(entering + ffn)
        r.final[here, :] = (normed * r.gain[2:3, :] + r.shift[2:3, :]).astype(low)
        grad = r.cotangent[here, :].astype(full)
        vec[2:3, :] += row_sum(grad * normed)
        vec[5:6, :] += row_sum(grad)
        back = normalize_back(grad, normed, scale, r.gain[2:3, :])
        r.grad_second[here, :] = back
        r.grad_low[here, :] = back.astype(low)
        vec[7:8, :] += row_sum(back.astype(low).astype(full))

    loaded(cot_words)
    loaded(cot_ents)
    over_rows(second_norm)

    def halved(ref, place, index):
        return ref.at[(slice(None),) * place + (index,)]

    def stage(kit, c, order, n):
        left = [axis for axis in range(4) if axis not in order[:n]]
        axis, place = order[n], left.index(order[n])
        held = kit.held[n].at[c]
        copy = send(
            halved(held, place, 1 - mine_on[axis]), kit.held[n + 1].at[c],
            kit.sent.at[c, n], kit.got.at[c, n], peer_on[axis],
        )
        return copy, halved(held, place, mine_on[axis])

    def advance(kit, c, order, n):
        copy, own = stage(kit, c, order, n - 1)
        copy.wait()
        total = kit.held[n].at[c]

        def body(i, carry):
            total[i] = own[i] + total[i]
            return carry

        lax.fori_loop(0, 2, body, 0)
        stage(kit, c, order, n)[0].start()

    def finish(kit, c, order):
        copy, own = stage(kit, c, order, 3)
        copy.wait()
        kit.out[c] = own[...].astype(full) + kit.held[4][c].astype(full)

    kit_a = types.SimpleNamespace(
        held=(r.grads, r.near, r.next, r.far, r.last), out=r.out_a, sent=r.a_s, got=r.a_r
    )
    kit_e = types.SimpleNamespace(
        held=(r.e_grads, r.e_near, r.e_next, r.e_far, r.e_last), out=r.e_sum, sent=r.e_s, got=r.e_r
    )
    along = dict(zip(range(3), ((3, 2, 1, 0), (2, 3, 1, 0), (1, 0, 3, 2))))

    kit_q = types.SimpleNamespace(held=(r.q_grads, r.q_near, r.q_next, r.q_far), sent=r.q_s, got=r.q_r)
    head_order = (2, 1, 0, 3)

    def head_start(h):
        stage(kit_q, h, head_order, 0)[0].start()

    def head_meet(h):
        return send(r.q_away.at[h], r.q_in.at[h], r.q_s.at[h, 3], r.q_r.at[h, 3], x_peer)

    def head_advance(h, n):
        if n < 3:
            advance(kit_q, h, head_order, n)
            return
        copy, own = stage(kit_q, h, head_order, 2)
        copy.wait()
        away = own[1 - x].astype(full) + r.q_far[h, 1 - x].astype(full)
        r.q_away[h] = away.astype(low)
        head_meet(h).start()
        r.out_q[h, x] = own[x].astype(full) + r.q_far[h, x].astype(full)

    def head_finish(h):
        head_meet(h).wait()
        r.out_q[h, 1 - x] = r.q_in[h].astype(full)

    def vec_copy(n):
        peer = peer_on[along[vec_order][n]]
        return send(r.vec.at[n], r.vec_in.at[n], r.vec_s.at[n], r.vec_r.at[n], peer)

    def vec_advance(n):
        vec_copy(n - 1).wait()
        r.vec[n] = r.vec[n - 1] + r.vec_in[n - 1]
        if n < 4:
            vec_copy(n).start()

    chunk = r.grads.shape[-1]

    def make_grad(c, left_t, right, lanes):
        part = dot_nn(left_t[...], right[:, lanes]).astype(low)
        r.grads[c] = part.reshape(2, 2, 2, 2, share, chunk)

    plan = iter(schedule)

    def tick():
        for what, c, n in next(plan):
            if what == CHUNK and n == 0:
                stage(kit_a, c, along[orders[c]], 0)[0].start()
            elif what == CHUNK:
                advance(kit_a, c, along[orders[c]], n)
            elif what == HEAD:
                head_advance(c, n)
            elif what == ENTS:
                advance(kit_e, c, along[ents_order], n)
            elif what == WORDS:
                words_back_copy.start()
            else:
                vec_advance(n)

    downs = hidden // chunk
    r.grad_t[...] = r.grad_low[...].T
    for c in range(downs):
        make_grad(c, r.grad_t, r.act, slice(c * chunk, (c + 1) * chunk))
        tick()

    def fill_dup(lanes, j):
        grad_act = dot_nt(r.grad_low[...], r.w_down[lanes, :])
        grad_up = (grad_act * r.slope_up[:, lanes]).astype(low)
        r.grad_up[:, lanes] = grad_up
        vec[pl.ds(8 + j // (width // wide), 1), aligned(lax.rem(j, width // wide), wide)] = row_sum(
            grad_up.astype(full)
        )

    columns(hidden, fill_dup)
    tick()

    def fill_back(lanes, j):
        r.mail_out[0, 0:rows, lanes] = dot_nt(r.grad_up[...], r.w_up[lanes, :]).astype(low)
        strip(0, 2, j).start()

    columns(width, fill_back)
    tick()
    r.first_t[...] = r.first[...].T
    flush(r.final.at[aligned(t, half_words // 2), :], r.to_out_words)
    ents_share = pl.multiple_of(half_words + t * (half_ents // 2), half_ents // 2)
    flush(r.final.at[pl.ds(ents_share, half_ents // 2), :], r.to_out_ents)
    for c in range(downs):
        make_grad(downs + c, r.first_t, r.grad_up, slice(c * chunk, (c + 1) * chunk))
        tick()
    wait_strips(0, 2)

    def first_back(here):
        grad = r.grad_second[here, :] + arrived(0, here)
        normed = r.normed[here, :]
        vec[1:2, :] += row_sum(grad * normed)
        vec[4:5, :] += row_sum(grad)
        back = normalize_back(grad, normed, r.scale[here, 0:1], r.gain[1:2, :])
        r.grad_first[here, :] = back
        r.grad_low[here, :] = back.astype(low)
        vec[6:7, :] += row_sum(back.astype(low).astype(full))

    over_rows(first_back)
    tick()
    near_rows = aligned(x, side)
    far_rows = aligned(1 - x, side)
    r.back_far[...] = dot_nt(r.grad_low[...], r.w_out[far_rows, :]).astype(low)
    mine = [(aligned(x, half_words), 0, half_words)]
    mine.append((pl.ds(pl.multiple_of(words + x * half_ents, half_ents), half_ents), half_words, half_ents))
    back_copies = [
        send(
            r.back_far.at[pl.ds(first, count), :], r.back_heads.at[place, :],
            r.pair_s.at[3 + n], r.pair_r.at[3 + n], x_peer,
        )
        for n, (place, first, count) in enumerate(mine)
    ]
    for copy in back_copies:
        copy.start()
    near = dot_nt(r.grad_low[...], r.w_out[near_rows, :]).astype(low)
    for place, first, count in mine:
        r.back_heads[place, :] = near[first : first + count, :]
    r.grad_t[...] = r.grad_low[...].T
    outs = 2 * downs
    make_grad(outs, r.grad_t, r.heads_all, slice(0, chunk))
    tick()


    pair = 2 * HD
    for h in range(heads):
        base = h * 4 * HD

        def score_back(start, size):
            def body(i, carry):
                here = pl.ds(pl.multiple_of(start + i * size, size), size)
                factor = jnp.concatenate([r.factor[h, here, :]] * (words // 128), 1)
                scaled = r.prob[h, here, of_words] * factor
                prob = jnp.concatenate([scaled, r.prob[h, here, of_ents]], 1)
                grad_prob = r.grad_prob[here, :]
                inner = jnp.sum(prob * grad_prob, 1, keepdims=True)
                r.grad_score[here, :] = (prob * (grad_prob - inner)).astype(low)
                r.prob_low[here, :] = prob.astype(low)
                return carry

            return body

        for which in (x, 1 - x):
            if which is not x:
                tick()
            if h == 0 and which is not x:
                for copy in back_copies:
                    copy.wait()
            for here, _ in both_kinds(which):
                r.grad_prob[here, :] = dot_nt(r.back_heads[here, h * HD : (h + 1) * HD], r.value[h])
            lax.fori_loop(0, half_words // SOFT, score_back(which * half_words, SOFT), 0)
            score_back(words + which * half_ents, half_ents)(0, 0)
        queries = jnp.concatenate(
            [
                dot_nn(r.grad_score[:, :words], r.key[h, 0:words, :]),
                dot_nn(r.grad_score[:, words:], r.key[h, words:everyone, :]),
            ],
            1,
        )
        r.grad_qkv[:, base : base + pair] = (queries * score_scale).astype(low)
        tick()
        query_t = r.qkv[:, base : base + pair].T
        keys_t = dot_nn(query_t, r.grad_score[...])
        keys_t = jnp.concatenate([keys_t[:HD, :words], keys_t[HD:, words:]], 1)
        values_t = dot_nn(r.back_heads[:, h * HD : (h + 1) * HD].T, r.prob_low[...])
        r.grad_qkv[:, base + pair : base + 2 * pair] = (
            jnp.concatenate([keys_t, values_t], 0).T.astype(low)
        )

        tick()
        keyval = slice(base + pair, base + 2 * pair)
        query = slice(base, base + pair)
        by_words = dot_nn(r.words_t[...], r.grad_qkv[0:words, query])
        by_ents = dot_nn(r.ents_t[...], r.grad_qkv[words:everyone, query])
        by_keyval = dot_nn(r.words_t[...], r.grad_qkv[0:words, keyval])
        by_keyval = by_keyval + dot_nn(r.ents_t[...], r.grad_qkv[words:everyone, keyval])
        for n, part in enumerate([by_words, by_ents, by_keyval]):
            r.q_grads[h, :, :, :, :, :, n * pair : (n + 1) * pair] = part.astype(low).reshape(
                2, 2, 2, 2, share, pair
            )
        head_start(h)
        sums = jnp.concatenate(
            [
                row_sum(r.grad_qkv[0:words, base : base + pair].astype(full)),
                row_sum(r.grad_qkv[words:everyone, base : base + pair].astype(full)),
                row_sum(r.grad_qkv[:, base + pair : base + 2 * pair].astype(full)),
            ],
            1,
        )
        place = h * 3 * pair
        vec[pl.ds(10 + 2 * x + place // width, 1), place % width : place % width + 3 * pair] = sums
        tick()

    quarter = half_words // 2

    def input_grad(place, weight):
        return dot_nt(r.grad_qkv[place, :], weight[...])

    ents_part = input_grad(slice(words, everyone), r.cat_ents)
    r.mail_out[1, words // 2 :, :] = ents_part.astype(low)
    ents_swap = swap(1, 0, words // 2, 2 * half_ents)
    ents_swap.start()
    tick()
    for n in range(2):
        r.mail_out[1, n * quarter : (n + 1) * quarter, :] = input_grad(
            aligned(2 * n + 1 - t, quarter), r.cat_words
        ).astype(low)
    words_swap = swap(1, 1, 0, words // 2)
    words_swap.start()
    for n in range(2):
        r.input_part[n] = input_grad(aligned(2 * n + t, quarter), r.cat_words)
    tick()
    ents_swap.wait()
    ents_place = pl.multiple_of(words // 2 + (1 - x) * half_ents, half_ents)
    ents_far = pl.ds(ents_place, half_ents)
    ents_near = pl.ds(pl.multiple_of(words // 2 + x * half_ents, half_ents), half_ents)
    r.ents_back[...] = arrived(1, ents_far).astype(low)
    ents_copy = send(r.ents_back, r.ents_in, r.pair_s.at[5], r.pair_r.at[5], x_peer)
    ents_copy.start()
    tick()
    words_swap.wait()
    far_place = aligned(1 - x, quarter)
    r.words_back[...] = (r.input_part[1 - x] + r.mail_in[1, far_place, :].astype(full)).astype(low)
    words_back_copy = send(r.words_back, r.words_in, r.pair_s.at[6], r.pair_r.at[6], x_peer)
    tick()
    ents_copy.wait()

    grad = r.grad_first[half_words:rows, :] + arrived(1, ents_near)
    grad = grad + r.ents_in[...].astype(full)
    own_ents = aligned(x, half_ents)
    normed, scale = normalize(r.ent_lin[own_ents, :])
    vec[0:1, :] = row_sum(grad * normed)
    vec[3:4, :] = row_sum(grad)
    lin_low = normalize_back(grad, normed, scale, r.gain[0:1, :]).astype(low)
    slope = dot_nt(lin_low, r.w_entity[...]).astype(low)
    r.slope[...] = dot_nn(r.outbox[...], slope).reshape(owners, capacity, -1)
    r.slopes[flat] = r.slope[flat]
    for k in range(owners - 1):
        slope_copy(k).start()
    looked_half = r.looked[own_ents, aligned(t, 128)]
    ents_grad = dot_tn(lin_low, looked_half).astype(low)
    r.e_grads[0] = ents_grad.reshape(2, 2, 2, 2, share, 128)
    stage(kit_e, 0, along[ents_order], 0)[0].start()
    vec_copy(0).start()
    tick()
    for k in range(owners - 1):
        slope_copy(k).wait()
    ids_t = r.asked[...].reshape(slots, 128).astype(full).T
    r.ids_out[...] = ids_t[0:8, :].astype(jnp.int32)
    r.slopes_out[...] = r.slopes[...].reshape(slots, -1).astype(low)
    flush(r.ids_out, r.to_ids_out)
    flush(r.slopes_out, r.to_slopes_out)
    words_back_copy.wait()
    r.grad_words[...] = (
        r.grad_first[aligned(t, quarter), :]
        + (r.input_part[x] + r.mail_in[1, aligned(x, quarter), :].astype(full))
        + r.words_in[...].astype(full)
    )
    flush(r.grad_words, r.to_grad_words)
    for c in range(2 * downs + 1):
        finish(kit_a, c, along[orders[c]])
        flush(r.out_a.at[c], r.to_out_a.at[c])
    vec_advance(4)
    total = r.vec[4]
    flush(r.vec.at[4], r.to_vec_out)
    r.across_out[...] = pltpu.roll(total[0:8, :], width - flat * share, 1)[:, 0:128]
    flush(r.across_out, r.to_across_out)
    finish(kit_e, 0, along[ents_order])
    ents_out = send(r.e_sum.at[0], r.e_in, r.pair_s.at[7], r.pair_r.at[7], core)
    ents_out.start()
    r.out_e[t] = r.e_sum[0]
    for h in range(heads):
        head_finish(h)
        flush(r.out_q.at[h], r.to_out_q.at[h])
    ents_out.wait()
    r.out_e[1 - t] = r.e_in[...]
    flush(r.out_e, r.to_out_e)
    for copy in flushes:
        copy.wait()


def finish_kernel(names, *refs):
    r = types.SimpleNamespace(**dict(zip(names, refs, strict=True)))
    low, full = jnp.bfloat16, jnp.float32
    table_rows, embed = r.hbm_first.shape
    slots = r.hbm_ids.shape[1]
    steps = r.in_s.shape[1]
    count = table_rows // steps
    chunks, share, chunk = r.hbm_a.shape
    downs = chunks // 2
    heads, side = r.hbm_q.shape[0], r.hbm_q.shape[0] * HD

    pairs = [(r.hbm_ids, r.ids), (r.hbm_slopes, r.slopes)]
    pairs += [(r.hbm_q, r.out_q), (r.hbm_e, r.out_e), (r.hbm_vec, r.vec), (r.hbm_across, r.across)]
    layers = [(r.hbm_a.at[2 * downs], r.out_part)]
    for c in range(downs):
        lanes = slice(c * chunk, (c + 1) * chunk)
        layers.append((r.hbm_a.at[c], r.down_part.at[:, lanes]))
        layers.append((r.hbm_a.at[downs + c], r.up_part.at[:, lanes]))
    layers += [(r.hbm_words, r.words_part), (r.hbm_ents, r.ents_part), (r.hbm_grad, r.grad_part)]
    smalls = [
        pltpu.make_async_copy(source, target, r.small_s.at[n])
        for n, (source, target) in enumerate(pairs + layers)
    ]
    outs = [
        pltpu.make_async_copy(source, target, r.done_s.at[n])
        for n, (source, target) in enumerate(
            [
                (r.out_part, r.red_out),
                (r.down_part, r.red_down),
                (r.up_part, r.red_up),
                (r.words_part, r.words_done.at[0]),
                (r.ents_part, r.ents_done.at[0]),
                (r.grad_part, r.grad_words_done.at[0]),
                (r.query_part, r.red_query),
                (r.keyval_part, r.red_keyval),
            ]
        )
    ]

    def moves(i, inward):
        here = pl.ds(i * count, count)
        if inward:
            ends = [(r.hbm_first, r.first), (r.hbm_second, r.second)]
            flags = r.in_s
        else:
            ends = [(r.update, r.table_update), (r.first, r.new_first), (r.second, r.new_second)]
            flags = r.out_s
        return [
            pltpu.make_async_copy(source.at[here, :], target.at[here, :], flags.at[n, i])
            for n, (source, target) in enumerate(ends)
        ]

    early, late = smalls[:2], smalls[2:]
    for copy in early + moves(0, True) + moves(1, True) + late:
        copy.start()
    for i in range(2, steps):
        for copy in moves(i, True):
            copy.start()
    for copy in early:
        copy.wait()
    r.addends[:, 0:embed] = r.slopes[...]
    r.addends[:, embed:] = jnp.ones((slots, 128), low)

    def adam(i):
        for copy in moves(i, True):
            copy.wait()
        here = pl.ds(i * count, count)
        row = lax.broadcasted_iota(jnp.int32, (count, slots), 0) + i * count
        chosen = jnp.where(row == r.ids[0:1, :], 1.0, 0.0).astype(low)
        total = dot_nn(chosen, r.addends[...])
        touched = total[:, embed:] > 0.0
        for start in range(0, embed, 128):
            lanes = slice(start, start + 128)
            grad = total[:, lanes]
            first, second = r.first[here, lanes], r.second[here, lanes]
            first_next = beta_one * first + (1.0 - beta_one) * grad
            second_next = beta_two * second + (1.0 - beta_two) * grad * grad
            direction = (
                first_next
                * (1.0 / (1.0 - beta_one**adam_steps))
                / (jnp.sqrt(second_next * (1.0 / (1.0 - beta_two**adam_steps))) + adam_eps)
            )
            r.update[here, lanes] = jnp.where(touched, direction, 0.0)
            r.first[here, lanes] = jnp.where(touched, first_next, first)
            r.second[here, lanes] = jnp.where(touched, second_next, second)
        for copy in moves(i, False):
            copy.start()

    def lay_out_rest():
        for copy in late:
            copy.wait()
        for copy in outs[:6]:
            copy.start()
        width = r.vec.shape[1]
        for n in range(2):
            r.red_entity[:, n * 128 : (n + 1) * 128] = r.out_e[n]
            for h in range(heads):
                place = h * 6 * HD
                line = 10 + 2 * n + place // width
                for j in range(6):
                    lanes = slice(n * side + h * HD, n * side + (h + 1) * HD)
                    part = r.out_q[h, n, :, j * HD : (j + 1) * HD]
                    begin = place % width + j * HD
                    line_part = r.vec[line : line + 1, begin : begin + HD]
                    if j < 4:
                        r.query_part[j, :, lanes] = part
                        r.red_query_bias[j : j + 1, lanes] = line_part
                    else:
                        r.keyval_part[j - 4, :, lanes] = part
                    if j == 5:
                        r.value_row[:, lanes] = line_part
        for copy in outs[6:]:
            copy.start()
        r.red_gain[...] = r.across[0:3, 0:share]
        r.red_shift[...] = r.across[3:6, 0:share]
        r.red_value_bias[...] = r.value_row[...].reshape(-1)
        r.red_out_bias[...] = r.across[6:7, 0:share].reshape(-1)
        r.red_down_bias[...] = r.across[7:8, 0:share].reshape(-1)
        for n in range(2):
            r.red_up_bias[n * width : (n + 1) * width] = r.vec[8 + n : 9 + n, :].reshape(-1)

    for i in range(steps):
        adam(i)
        if i == steps // 2:
            lay_out_rest()
    for i in range(steps):
        for copy in moves(i, False):
            copy.wait()
    for copy in outs:
        copy.wait()


SOFT = 256
STEPS = 8
CHUNK, HEAD, ENTS, VEC, WORDS = range(5)
SCHEDULE = (
    ((CHUNK, 0, 0),),
    ((CHUNK, 1, 0),),
    ((CHUNK, 2, 0),),
    (),
    (),
    (),
    (),
    ((CHUNK, 3, 0),),
    (),
    ((CHUNK, 7, 0),),
    (),
    ((CHUNK, 0, 1), (CHUNK, 4, 0), (CHUNK, 6, 0),),
    ((CHUNK, 1, 1),),
    (),
    (),
    (),
    ((CHUNK, 2, 1),),
    ((CHUNK, 3, 1), (CHUNK, 8, 0), (CHUNK, 5, 0),),
    ((CHUNK, 7, 1),),
    ((CHUNK, 2, 2), (HEAD, 0, 1),),
    ((CHUNK, 6, 1),),
    (),
    (),
    ((HEAD, 1, 1),),
    ((HEAD, 0, 2),),
    ((CHUNK, 8, 1), (CHUNK, 0, 2), (CHUNK, 1, 2),),
    ((CHUNK, 4, 1), (CHUNK, 3, 2), (CHUNK, 2, 3), (HEAD, 2, 1), (HEAD, 1, 2), (CHUNK, 5, 1), (CHUNK, 0, 3), (CHUNK, 6, 2),),
    ((CHUNK, 8, 2), (CHUNK, 1, 3),),
    ((WORDS, 0, 0), (CHUNK, 4, 2), (CHUNK, 3, 3), (HEAD, 2, 2), (CHUNK, 5, 2), (CHUNK, 8, 3), (ENTS, 0, 1), (VEC, 0, 1), (CHUNK, 7, 2), (CHUNK, 6, 3), (ENTS, 0, 2), (CHUNK, 5, 3), (VEC, 0, 2), (CHUNK, 4, 3), (CHUNK, 7, 3), (HEAD, 0, 3), (HEAD, 1, 3), (HEAD, 2, 3), (ENTS, 0, 3), (VEC, 0, 3),),
)
ORDERS = (2, 0, 1, 2, 0, 0, 2, 1, 0)
VEC_ORDER = 1
ENTS_ORDER = 0


def fused_local(
    word_states,
    entity_shard,
    entity_row,
    word_segments,
    entity_segments,
    entity_table,
    adam_first,
    adam_second,
    w_entity,
    norm_gain,
    norm_bias,
    w_query,
    b_query,
    w_keyval,
    b_value,
    w_out,
    b_out,
    w_up,
    b_up,
    w_down,
    b_down,
    cot_words,
    cot_entities,
):
    low, full = jnp.bfloat16, jnp.float32
    _, half_words, width = word_states.shape
    half_ents = entity_row.shape[2]
    rows, everyone = half_words + half_ents, 2 * (half_words + half_ents)
    words, ents = 2 * half_words, 2 * half_ents
    table_rows, embed = entity_table.shape
    local_width, hidden = w_query.shape[2], w_up.shape[1]
    owners = lax.axis_size(("dp", "stream"))
    share = width // owners
    capacity = 2 * half_ents // owners
    side = local_width // 2
    heads = side // HD
    chunk = local_width
    chunks = 2 * (hidden // chunk) + 1

    operands = dict(
        hbm_shard=entity_shard.reshape(1, half_ents),
        hbm_row=entity_row.reshape(1, half_ents),
        hbm_word_seg=word_segments,
        hbm_ent_seg=entity_segments,
        hbm_gain=norm_gain,
        hbm_shift=norm_bias,
        hbm_b_query=b_query,
        hbm_b_value=b_value,
        hbm_b_out=b_out,
        hbm_b_up=b_up,
        hbm_b_down=b_down,
        hbm_words=word_states,
        hbm_cot_words=cot_words,
        hbm_cot_ents=cot_entities,
        hbm_query=w_query,
        hbm_keyval=w_keyval,
        hbm_table=entity_table,
        hbm_entity=w_entity,
        hbm_out=w_out,
        hbm_up=w_up,
        hbm_down=w_down,
    )
    results = dict(
        to_out_words=((half_words // 2, width), low),
        to_out_ents=((half_ents // 2, width), low),
        to_grad_words=((half_words // 2, width), full),
        to_out_a=((chunks, share, chunk), full),
        to_out_e=((2, share, 128), full),
        to_out_q=((heads, 2, share, chunk), full),
        to_vec_out=((16, width), full),
        to_across_out=((8, 128), full),
        to_ids_out=((8, owners * capacity), jnp.int32),
        to_slopes_out=((owners * capacity, embed), low),
    )
    mail_rows = max(rows, words // 2 + ents)
    dma = pltpu.SemaphoreType.DMA
    scratch = dict(
        shard=((1, half_ents), jnp.int32),
        row=((1, half_ents), jnp.int32),
        word_seg=(word_segments.shape, jnp.int32),
        ent_seg=(entity_segments.shape, jnp.int32),
        gain=(norm_gain.shape, full),
        shift=(norm_bias.shape, full),
        b_query=(b_query.shape, full),
        b_value=(b_value.shape, full),
        b_out=(b_out.shape, full),
        b_up=(b_up.shape, full),
        b_down=(b_down.shape, full),
        grad_words=((half_words // 2, width), full),
        out_a=((chunks, share, chunk), full),
        out_e=((2, share, 128), full),
        out_q=((heads, 2, share, chunk), full),
        across_out=((8, 128), full),
        ids_out=((8, owners * capacity), jnp.int32),
        slopes_out=((owners * capacity, embed), low),
        w_query=(w_query.shape, low),
        w_keyval=(w_keyval.shape, low),
        table=(entity_table.shape, low),
        w_entity=(w_entity.shape, low),
        w_out=(w_out.shape, low),
        w_up=(w_up.shape, low),
        w_down=(w_down.shape, low),
        cat_words=((width, 4 * side), low),
        cat_ents=((width, 4 * side), low),
        bias_words=((1, 4 * side), full),
        bias_ents=((1, 4 * side), full),
        cotangent=((rows, width), low),
        ask=((owners, capacity, 128), jnp.int32),
        asked=((owners, capacity, 128), jnp.int32),
        outbox=((owners * capacity, half_ents), low),
        select=((ents, owners * 2 * capacity), low),
        found=((owners // 2, 2 * capacity, embed), low),
        answer=((owners, 2 * capacity, embed), low),
        looked=((ents, embed), low),
        ent_lin=((ents, width), full),
        x_ent=((ents, width), full),
        x_all=((everyone, width), low),
        x_own=((rows, width), full),
        words_t=((width, words), low),
        ents_t=((width, ents), low),
        mask=((everyone, everyone), low),
        qkv=((everyone, 4 * side), low),
        key=((heads, everyone, HD), low),
        value=((heads, everyone, HD), low),
        prob=((heads, everyone, everyone), full),
        factor=((heads, everyone, 128), full),
        mass=((heads, words, 128), full),
        heads_far=((rows, side), low),
        heads_near=((rows, side), low),
        heads_in=((rows, side), low),
        heads_all=((rows, 2 * side), low),
        mail_out=((2, mail_rows, width), low),
        mail_in=((2, mail_rows, width), low),
        normed=((rows, width), full),
        scale=((rows, 128), full),
        first=((rows, width), low),
        first_t=((width, rows), low),
        act=((rows, hidden), low),
        slope_up=((rows, hidden), full),
        final=((rows, width), low),
        grad_second=((rows, width), full),
        grad_low=((rows, width), low),
        grad_t=((width, rows), low),
        grad_up=((rows, hidden), low),
        grad_first=((rows, width), full),
        back_far=((rows, side), low),
        back_heads=((everyone, side), low),
        grad_prob=((everyone, everyone), full),
        grad_score=((everyone, everyone), low),
        prob_low=((everyone, everyone), low),
        grad_qkv=((everyone, 4 * side), low),
        input_part=((2, half_words // 2, width), full),
        ents_back=((half_ents, width), low),
        ents_in=((half_ents, width), low),
        words_back=((half_words // 2, width), low),
        words_in=((half_words // 2, width), low),
        slope=((owners, capacity, embed), full),
        slopes=((owners, capacity, embed), full),
        e_sum=((1, share, 128), full),
        e_in=((share, 128), full),
        vec=((5, 16, width), full),
        vec_in=((4, 16, width), full),
        grads=((chunks, 2, 2, 2, 2, share, chunk), low),
        near=((chunks, 2, 2, 2, share, chunk), low),
        next=((chunks, 2, 2, share, chunk), low),
        far=((chunks, 2, share, chunk), low),
        last=((chunks, share, chunk), low),
        e_grads=((1, 2, 2, 2, 2, share, 128), low),
        e_near=((1, 2, 2, 2, share, 128), low),
        e_next=((1, 2, 2, share, 128), low),
        e_far=((1, 2, share, 128), low),
        e_last=((1, share, 128), low),
        q_grads=((heads, 2, 2, 2, 2, share, chunk), low),
        q_near=((heads, 2, 2, 2, share, chunk), low),
        q_next=((heads, 2, 2, share, chunk), low),
        q_far=((heads, 2, share, chunk), low),
        q_away=((heads, share, chunk), low),
        q_in=((heads, share, chunk), low),
    )
    signals = dict(
        load_s=(len(operands),),
        flush_s=(len(results) + chunks + heads,),
        ask_s=(owners - 1,),
        ask_r=(owners - 1,),
        answer_s=(owners - 1,),
        answer_r=(owners - 1,),
        slope_s=(owners - 1,),
        slope_r=(owners - 1,),
        heads_s=(2,),
        heads_r=(2,),
        pair_s=(9,),
        pair_r=(9,),
        strip_s=(3, width // 256),
        strip_r=(3, width // 256),
        swap_s=(2,),
        swap_r=(2,),
        vec_s=(4,),
        vec_r=(4,),
        a_s=(chunks, 4),
        a_r=(chunks, 4),
        e_s=(1, 4),
        e_r=(1, 4),
        q_s=(heads, 4),
        q_r=(heads, 4),
    )
    names = [*operands, *results, *scratch, *signals]
    kernel = functools.partial(layer_kernel, names, ORDERS, ENTS_ORDER, VEC_ORDER, SCHEDULE)
    made = pl.pallas_call(
        kernel,
        name="layer",
        out_shape=[jax.ShapeDtypeStruct(*item) for item in results.values()],
        in_specs=[pl.BlockSpec(memory_space=pl.ANY)] * len(operands),
        out_specs=[pl.BlockSpec(memory_space=pl.ANY)] * len(results),
        scratch_shapes=[pltpu.VMEM(*item) for item in scratch.values()]
        + [dma(shape) for shape in signals.values()],
        compiler_params=pltpu.CompilerParams(
            collective_id=0, has_side_effects=True, vmem_limit_bytes=67_043_328
        ),
    )(*operands.values())
    got = types.SimpleNamespace(**dict(zip(results, made, strict=True)))

    given = dict(
        hbm_first=adam_first,
        hbm_second=adam_second,
        hbm_ids=got.to_ids_out,
        hbm_slopes=got.to_slopes_out,
        hbm_a=got.to_out_a,
        hbm_e=got.to_out_e,
        hbm_q=got.to_out_q,
        hbm_vec=got.to_vec_out,
        hbm_across=got.to_across_out,
        hbm_words=got.to_out_words,
        hbm_ents=got.to_out_ents,
        hbm_grad=got.to_grad_words,
    )
    final = dict(
        words_done=(1, half_words // 2, width),
        ents_done=(1, half_ents // 2, width),
        grad_words_done=(1, half_words // 2, width),
        red_entity=(share, embed),
        red_gain=(3, share),
        red_shift=(3, share),
        red_query=(4, share, local_width),
        red_query_bias=(4, local_width),
        red_keyval=(2, share, local_width),
        red_value_bias=(local_width,),
        red_out=(share, local_width),
        red_out_bias=(share,),
        red_up=(share, hidden),
        red_up_bias=(hidden,),
        red_down=(share, hidden),
        red_down_bias=(share,),
        table_update=adam_first.shape,
        new_first=adam_first.shape,
        new_second=adam_first.shape,
    )
    room = dict(
        value_row=((1, local_width), full),
        ids=(got.to_ids_out.shape, jnp.int32),
        slopes=(got.to_slopes_out.shape, low),
        addends=((owners * capacity, embed + 128), low),
        out_e=(got.to_out_e.shape, full),
        out_q=(got.to_out_q.shape, full),
        vec=(got.to_vec_out.shape, full),
        across=(got.to_across_out.shape, full),
        first=(adam_first.shape, full),
        second=(adam_first.shape, full),
        update=(adam_first.shape, full),
        out_part=((share, local_width), full),
        down_part=((share, hidden), full),
        up_part=((share, hidden), full),
        words_part=(got.to_out_words.shape, low),
        ents_part=(got.to_out_ents.shape, low),
        grad_part=(got.to_grad_words.shape, full),
        query_part=((4, share, local_width), full),
        keyval_part=((2, share, local_width), full),
    )
    flags = dict(small_s=(chunks + 9,), done_s=(8,), in_s=(2, STEPS), out_s=(3, STEPS))
    in_place, in_vmem = (pl.BlockSpec(memory_space=space) for space in (pl.ANY, pltpu.VMEM))
    manual = set(dict(words_done=0, ents_done=0, grad_words_done=0, red_query=0, red_keyval=0))
    manual |= set(dict(red_out=0, red_up=0, red_down=0, table_update=0, new_first=0, new_second=0))
    finished = pl.pallas_call(
        functools.partial(finish_kernel, [*given, *final, *room, *flags]),
        name="finish",
        out_shape=[
            jax.ShapeDtypeStruct(shape, low if n < 2 else full)
            for n, shape in enumerate(final.values())
        ],
        in_specs=[in_place] * len(given),
        out_specs=[in_place if name in manual else in_vmem for name in final],
        scratch_shapes=[pltpu.VMEM(*item) for item in room.values()]
        + [dma(shape) for shape in flags.values()],
        compiler_params=pltpu.CompilerParams(vmem_limit_bytes=67_043_328),
    )(*given.values())
    done = dict(zip(final, finished, strict=True))
    return tuple(
        item.T if name in ("red_entity", "red_out", "red_down") else item
        for name, item in done.items()
    )


def plain_local(
    word_states,
    entity_shard,
    entity_row,
    word_segments,
    entity_segments,
    entity_table,
    adam_first,
    adam_second,
    w_entity,
    norm_gain,
    norm_bias,
    w_query,
    b_query,
    w_keyval,
    b_value,
    w_out,
    b_out,
    w_up,
    b_up,
    w_down,
    b_down,
    cot_words,
    cot_entities,
):
    seq_count, half_words, width = word_states.shape
    half_ents = entity_row.shape[2]
    table_rows, embed_width = entity_table.shape
    local_width = w_query.shape[2]
    local_heads = local_width // HD
    owners = lax.axis_size(("dp", "stream"))
    stream_index = lax.axis_index("stream")
    parts = lax.axis_size("tensor")
    part_index = lax.axis_index("tensor")
    word_part = half_words // parts
    ent_part = half_ents // parts
    ent_count = seq_count * half_ents
    word_count = seq_count * half_words
    local_rows = half_words + half_ents
    share_words = seq_count * word_part
    owner_flat = entity_shard.reshape(ent_count)
    row_flat = entity_row.reshape(ent_count)

    def pick(block, count):
        shaped = block.reshape(seq_count, parts, count // parts, block.shape[-1])
        return lax.dynamic_index_in_dim(shaped, part_index, 1, keepdims=False).reshape(
            seq_count * (count // parts), block.shape[-1]
        )

    def own_share(rows):
        return jnp.concatenate(
            [pick(rows[:word_count], half_words), pick(rows[word_count:], half_ents)], 0
        )

    capacity = 2 * ent_count // owners
    owner_hits = (owner_flat[:, None] == jnp.arange(owners, dtype=jnp.int32)[None, :]).astype(
        jnp.int32
    )
    before = jnp.cumsum(owner_hits, 0) - owner_hits
    ranking = jnp.sum(before * owner_hits, 1)
    slot_index = owner_flat * capacity + ranking
    request = (
        jnp.full((owners * capacity,), -1, jnp.int32)
        .at[slot_index]
        .set(row_flat)
        .reshape(owners, capacity)
    )
    asked_ids = lax.all_to_all(request, ("dp", "stream"), split_axis=0, concat_axis=0, tiled=True)
    present = asked_ids >= 0
    found_rows = jnp.take(entity_table, jnp.clip(asked_ids, 0, table_rows - 1), axis=0)
    found_rows = jnp.where(present[..., None], found_rows, jnp.zeros_like(found_rows))
    found_rows, asked_rows = (found_rows, asked_ids)
    answered = lax.all_to_all(found_rows, ("dp", "stream"), split_axis=0, concat_axis=0, tiled=True)
    looked = answered.reshape(owners * capacity, embed_width)[slot_index]
    ent_lin = matmul(looked, w_entity)
    x_entity, entity_norm_back = jax.vjp(layer_norm, ent_lin, norm_gain[0], norm_bias[0])
    entity_low = x_entity.astype(jnp.bfloat16)
    word_low = word_states.reshape(word_count, width)
    query_words = (
        jnp.einsum("rd,jdc->jrc", word_low, w_query[:2], preferred_element_type=jnp.float32)
        + b_query[:2, None, :]
    ).astype(jnp.bfloat16)
    query_ents = (
        jnp.einsum("rd,jdc->jrc", entity_low, w_query[2:], preferred_element_type=jnp.float32)
        + b_query[2:, None, :]
    ).astype(jnp.bfloat16)
    value_shift = jnp.stack([jnp.zeros_like(b_value), b_value])[:, None, :]
    keyval_words = (
        jnp.einsum("rd,jdc->jrc", word_low, w_keyval, preferred_element_type=jnp.float32)
        + value_shift
    ).astype(jnp.bfloat16)
    keyval_ents = (
        jnp.einsum("rd,jdc->jrc", entity_low, w_keyval, preferred_element_type=jnp.float32)
        + value_shift
    ).astype(jnp.bfloat16)
    far_words, far_ents = from_partner((keyval_words, keyval_ents), "stream", 0)

    def by_heads(block, count):
        return block.reshape(block.shape[0], seq_count, count, local_heads, HD)

    queries = jnp.concatenate(
        [by_heads(query_words, half_words), by_heads(query_ents, half_ents)], 2
    )
    keyval_w = jnp.concatenate(
        [by_heads(keyval_words, half_words), by_heads(far_words, half_words)], 2
    )
    keyval_e = jnp.concatenate([by_heads(keyval_ents, half_ents), by_heads(far_ents, half_ents)], 2)
    own_wseg = lax.dynamic_slice_in_dim(word_segments, stream_index * half_words, half_words, 1)
    far_wseg = lax.dynamic_slice_in_dim(
        word_segments, (1 - stream_index) * half_words, half_words, 1
    )
    own_eseg = lax.dynamic_slice_in_dim(entity_segments, stream_index * half_ents, half_ents, 1)
    far_eseg = lax.dynamic_slice_in_dim(
        entity_segments, (1 - stream_index) * half_ents, half_ents, 1
    )
    query_seg = jnp.concatenate([own_wseg, own_eseg], 1)
    key_wseg = jnp.concatenate([own_wseg, far_wseg], 1)
    key_eseg = jnp.concatenate([own_eseg, far_eseg], 1)
    allow_words = query_seg[:, None, :, None] == key_wseg[:, None, None, :]
    allow_ents = query_seg[:, None, :, None] == key_eseg[:, None, None, :]

    def scores_of():
        raw_words = (
            jnp.einsum(
                "sqhd,skhd->shqk", queries[0], keyval_w[0], preferred_element_type=jnp.float32
            )
            * score_scale
        )
        raw_ents = (
            jnp.einsum(
                "sqhd,skhd->shqk", queries[1], keyval_e[0], preferred_element_type=jnp.float32
            )
            * score_scale
        )
        return (
            jnp.where(allow_words, raw_words, masked_score),
            jnp.where(allow_ents, raw_ents, masked_score),
        )

    score_words, score_ents = scores_of()
    highest = jnp.maximum(
        jnp.max(score_words, -1, keepdims=True), jnp.max(score_ents, -1, keepdims=True)
    )
    totals = jnp.sum(jnp.exp(score_words - highest), -1, keepdims=True) + jnp.sum(
        jnp.exp(score_ents - highest), -1, keepdims=True
    )
    log_total = highest + jnp.log(totals)
    low_words = jnp.exp(score_words - log_total).astype(jnp.bfloat16)
    low_ents = jnp.exp(score_ents - log_total).astype(jnp.bfloat16)
    heads_out = jnp.einsum(
        "shqk,skhd->sqhd", low_words, keyval_w[1], preferred_element_type=jnp.float32
    )
    heads_out = heads_out + jnp.einsum(
        "shqk,skhd->sqhd", low_ents, keyval_e[1], preferred_element_type=jnp.float32
    )
    heads_out = heads_out.astype(jnp.bfloat16).reshape(seq_count, local_rows, local_width)
    heads_dense = jnp.concatenate(
        [
            heads_out[:, :half_words].reshape(word_count, local_width),
            heads_out[:, half_words:].reshape(ent_count, local_width),
        ],
        0,
    )
    resid_in = jnp.concatenate([word_low.astype(jnp.float32), x_entity], 0)
    cotangent = jnp.concatenate(
        [cot_words.reshape(word_count, width), cot_entities.reshape(ent_count, width)], 0
    ).astype(jnp.float32)
    attn_out = tensor_total(matmul(heads_dense, w_out)) + b_out
    first_norm, first_back = jax.vjp(layer_norm, resid_in + attn_out, norm_gain[1], norm_bias[1])
    first_low = first_norm.astype(jnp.bfloat16)
    up_value = matmul(first_low, w_up) + b_up
    active, gelu_back = jax.vjp(gelu_exact, up_value)
    active_low = active.astype(jnp.bfloat16)
    ffn_out = tensor_total(matmul(active_low, w_down)) + b_down
    final_norm, final_back = jax.vjp(layer_norm, first_norm + ffn_out, norm_gain[2], norm_bias[2])
    final_share = own_share(final_norm)
    grad_final, gain_final, shift_final = final_back(cotangent)
    grad_ffn = grad_final.astype(jnp.bfloat16)
    out_words = final_share[:share_words].reshape(seq_count, word_part, width).astype(jnp.bfloat16)
    out_entities = (
        final_share[share_words:].reshape(seq_count, ent_part, width).astype(jnp.bfloat16)
    )
    grad_down = jnp.einsum("rf,rd->fd", active_low, grad_ffn, preferred_element_type=jnp.float32)
    grad_down_bias = jnp.sum(grad_ffn.astype(jnp.float32), 0)
    (grad_pre,) = gelu_back(
        jnp.einsum("rd,fd->rf", grad_ffn, w_down, preferred_element_type=jnp.float32)
    )
    grad_up_low = grad_pre.astype(jnp.bfloat16)
    grad_up = jnp.einsum("rd,rf->df", first_low, grad_up_low, preferred_element_type=jnp.float32)
    grad_up_bias = jnp.sum(grad_up_low.astype(jnp.float32), 0)
    ffn_term = jnp.einsum("rf,df->rd", grad_up_low, w_up, preferred_element_type=jnp.float32)
    grad_first, gain_first, shift_first = first_back(grad_final + tensor_total(ffn_term))
    grad_attn = grad_first.astype(jnp.bfloat16)
    grad_out = jnp.einsum("rc,rd->cd", heads_dense, grad_attn, preferred_element_type=jnp.float32)
    grad_out_bias = jnp.sum(grad_attn.astype(jnp.float32), 0)
    grad_heads = jnp.einsum(
        "rd,cd->rc", grad_attn, w_out, preferred_element_type=jnp.float32
    ).astype(jnp.bfloat16)
    grad_heads = jnp.concatenate(
        [
            grad_heads[:word_count].reshape(seq_count, half_words, local_heads, HD),
            grad_heads[word_count:].reshape(seq_count, half_ents, local_heads, HD),
        ],
        1,
    )
    score_words, score_ents = scores_of()
    prob_words = jnp.exp(score_words - log_total)
    prob_ents = jnp.exp(score_ents - log_total)
    low_words = prob_words.astype(jnp.bfloat16)
    low_ents = prob_ents.astype(jnp.bfloat16)
    dprob_words = jnp.einsum(
        "sqhd,skhd->shqk", grad_heads, keyval_w[1], preferred_element_type=jnp.float32
    )
    dprob_ents = jnp.einsum(
        "sqhd,skhd->shqk", grad_heads, keyval_e[1], preferred_element_type=jnp.float32
    )
    inner_sum = jnp.sum(prob_words * dprob_words, -1, keepdims=True) + jnp.sum(
        prob_ents * dprob_ents, -1, keepdims=True
    )
    dscore_words = (prob_words * (dprob_words - inner_sum)).astype(jnp.bfloat16)
    dscore_ents = (prob_ents * (dprob_ents - inner_sum)).astype(jnp.bfloat16)
    grad_to_words = (
        jnp.einsum("shqk,skhd->sqhd", dscore_words, keyval_w[0], preferred_element_type=jnp.float32)
        * score_scale
    ).astype(jnp.bfloat16)
    grad_to_ents = (
        jnp.einsum("shqk,skhd->sqhd", dscore_ents, keyval_e[0], preferred_element_type=jnp.float32)
        * score_scale
    ).astype(jnp.bfloat16)
    kv_grad_words = jnp.stack(
        [
            jnp.einsum(
                "shqk,sqhd->skhd", dscore_words, queries[0], preferred_element_type=jnp.float32
            )
            * score_scale,
            jnp.einsum(
                "shqk,sqhd->skhd", low_words, grad_heads, preferred_element_type=jnp.float32
            ),
        ]
    )
    kv_grad_ents = jnp.stack(
        [
            jnp.einsum(
                "shqk,sqhd->skhd", dscore_ents, queries[1], preferred_element_type=jnp.float32
            )
            * score_scale,
            jnp.einsum("shqk,sqhd->skhd", low_ents, grad_heads, preferred_element_type=jnp.float32),
        ]
    )
    back_words, back_ents = (
        from_partner(kv_grad_words[:, :, half_words:].astype(jnp.bfloat16), "stream", 0).astype(
            jnp.float32
        ),
        from_partner(kv_grad_ents[:, :, half_ents:].astype(jnp.bfloat16), "stream", 0).astype(
            jnp.float32
        ),
    )
    grad_kv_words = (
        (kv_grad_words[:, :, :half_words] + back_words)
        .reshape(2, word_count, local_width)
        .astype(jnp.bfloat16)
    )
    grad_kv_ents = (
        (kv_grad_ents[:, :, :half_ents] + back_ents)
        .reshape(2, ent_count, local_width)
        .astype(jnp.bfloat16)
    )
    grad_q_words = jnp.stack([grad_to_words[:, :half_words], grad_to_ents[:, :half_words]]).reshape(
        2, word_count, local_width
    )
    grad_q_ents = jnp.stack([grad_to_words[:, half_words:], grad_to_ents[:, half_words:]]).reshape(
        2, ent_count, local_width
    )
    grad_query = jnp.concatenate(
        [
            jnp.einsum("rd,jrc->jdc", word_low, grad_q_words, preferred_element_type=jnp.float32),
            jnp.einsum("rd,jrc->jdc", entity_low, grad_q_ents, preferred_element_type=jnp.float32),
        ],
        0,
    )
    grad_query_bias = jnp.concatenate(
        [jnp.sum(grad_q_words.astype(jnp.float32), 1), jnp.sum(grad_q_ents.astype(jnp.float32), 1)],
        0,
    )
    grad_keyval = jnp.einsum(
        "rd,jrc->jdc", word_low, grad_kv_words, preferred_element_type=jnp.float32
    ) + jnp.einsum("rd,jrc->jdc", entity_low, grad_kv_ents, preferred_element_type=jnp.float32)
    grad_value_bias = jnp.sum(grad_kv_words[1].astype(jnp.float32), 0) + jnp.sum(
        grad_kv_ents[1].astype(jnp.float32), 0
    )
    input_words = jnp.einsum(
        "jrc,jdc->rd", grad_q_words, w_query[:2], preferred_element_type=jnp.float32
    ) + jnp.einsum("jrc,jdc->rd", grad_kv_words, w_keyval, preferred_element_type=jnp.float32)
    input_ents = jnp.einsum(
        "jrc,jdc->rd", grad_q_ents, w_query[2:], preferred_element_type=jnp.float32
    ) + jnp.einsum("jrc,jdc->rd", grad_kv_ents, w_keyval, preferred_element_type=jnp.float32)
    input_term = jnp.concatenate([input_words, input_ents], 0)
    grad_input = grad_first + tensor_total(input_term)
    grad_share = own_share(grad_input)
    grad_lin, gain_entity, shift_entity = entity_norm_back(grad_input[word_count:])
    grad_lin_low = grad_lin.astype(jnp.bfloat16)
    gain_grads = jnp.stack([gain_entity, gain_first, gain_final])
    shift_grads = jnp.stack([shift_entity, shift_first, shift_final])
    grad_words = grad_share[:share_words].reshape(seq_count, word_part, width)
    grad_entity = jnp.einsum("re,rd->ed", looked, grad_lin_low, preferred_element_type=jnp.float32)
    grad_looked = jnp.einsum(
        "rd,ed->re", grad_lin_low, w_entity, preferred_element_type=jnp.float32
    )
    outgoing = (
        jnp.zeros((owners * capacity, embed_width), jnp.float32)
        .at[slot_index]
        .set(grad_looked)
        .reshape(owners, capacity, embed_width)
    )
    incoming = lax.all_to_all(
        outgoing.astype(jnp.bfloat16), ("dp", "stream"), split_axis=0, concat_axis=0, tiled=True
    ).astype(outgoing.dtype)
    target = jnp.where(asked_rows >= 0, asked_rows, table_rows).reshape(-1)
    gradient_sum = (
        jnp.zeros((table_rows, embed_width), jnp.float32)
        .at[target]
        .add(incoming.reshape(-1, embed_width), mode="drop")
    )
    use_count = jnp.zeros((table_rows,), jnp.float32).at[target].add(1.0, mode="drop")
    touched = (use_count > 0.0)[:, None]
    first_next = beta_one * adam_first + (1.0 - beta_one) * gradient_sum
    second_next = beta_two * adam_second + (1.0 - beta_two) * gradient_sum * gradient_sum
    direction = (
        first_next
        / (1.0 - beta_one**adam_steps)
        / (jnp.sqrt(second_next / (1.0 - beta_two**adam_steps)) + adam_eps)
    )
    table_update = jnp.where(touched, direction, jnp.zeros_like(direction))
    new_first = jnp.where(touched, first_next, adam_first)
    new_second = jnp.where(touched, second_next, adam_second)
    (
        red_entity,
        red_gain,
        red_shift,
        red_query,
        red_keyval,
        red_out,
        red_out_bias,
        red_up,
        red_down,
        red_down_bias,
    ) = (
        lax.psum_scatter(grad_entity, ("dp", "stream"), scatter_dimension=1, tiled=True),
        lax.psum_scatter(gain_grads, ("dp", "stream"), scatter_dimension=1, tiled=True),
        lax.psum_scatter(shift_grads, ("dp", "stream"), scatter_dimension=1, tiled=True),
        lax.psum_scatter(grad_query, ("dp", "stream"), scatter_dimension=1, tiled=True),
        lax.psum_scatter(grad_keyval, ("dp", "stream"), scatter_dimension=1, tiled=True),
        lax.psum_scatter(grad_out, ("dp", "stream"), scatter_dimension=1, tiled=True),
        lax.psum_scatter(grad_out_bias, ("dp", "stream"), scatter_dimension=0, tiled=True),
        lax.psum_scatter(grad_up, ("dp", "stream"), scatter_dimension=0, tiled=True),
        lax.psum_scatter(grad_down, ("dp", "stream"), scatter_dimension=1, tiled=True),
        lax.psum_scatter(grad_down_bias, ("dp", "stream"), scatter_dimension=0, tiled=True),
    )
    red_query_bias, red_value_bias, red_up_bias = lax.psum(
        (grad_query_bias, grad_value_bias, grad_up_bias), ("dp", "stream")
    )
    return (
        out_words,
        out_entities,
        grad_words,
        red_entity,
        red_gain,
        red_shift,
        red_query,
        red_query_bias,
        red_keyval,
        red_value_bias,
        red_out,
        red_out_bias,
        red_up,
        red_up_bias,
        red_down,
        red_down_bias,
        table_update,
        new_first,
        new_second,
    )


def solution(mesh):
    placed = (
        P("dp", "stream", None),
        P("stream", "dp", None, None),
        P("stream", "dp", None),
        P("dp", None),
        P("dp", None),
        P(("dp", "stream"), None),
        P(("dp", "stream"), None),
        P(("dp", "stream"), None),
        P(),
        P(),
        P(),
        P(None, None, "tensor"),
        P(None, "tensor"),
        P(None, None, "tensor"),
        P("tensor"),
        P("tensor", None),
        P(),
        P(None, "tensor"),
        P("tensor"),
        P("tensor", None),
        P(),
        P("dp", "stream", None),
        P("dp", "stream", None),
    )
    fits = mesh.shape["stream"] == 2 and mesh.shape["tensor"] == 2 and mesh.shape["dp"] == 8

    def local(*blocks):
        width, owners = blocks[0].shape[2], mesh.shape["dp"] * mesh.shape["stream"]
        if fits and width % (16 * owners) == 0 and blocks[0].shape[0] == 1:
            return fused_local(*blocks)
        return plain_local(*blocks)

    return jax.shard_map(
        local,
        mesh=mesh,
        in_specs=placed,
        out_specs=(
            P("dp", ("stream", "tensor"), None),
            P("dp", ("stream", "tensor"), None),
            P("dp", ("stream", "tensor"), None),
            P(None, ("dp", "stream")),
            P(None, ("dp", "stream")),
            P(None, ("dp", "stream")),
            P(None, ("dp", "stream"), "tensor"),
            P(None, "tensor"),
            P(None, ("dp", "stream"), "tensor"),
            P("tensor"),
            P("tensor", ("dp", "stream")),
            P(("dp", "stream")),
            P(("dp", "stream"), "tensor"),
            P("tensor"),
            P("tensor", ("dp", "stream")),
            P(("dp", "stream")),
            P(("dp", "stream"), None),
            P(("dp", "stream"), None),
            P(("dp", "stream"), None),
        ),
        check_vma=False,
    )
```

```python
import functools
import math
import types

import jax
import jax.numpy as jnp
from jax import lax
from jax.experimental import pallas as pl
from jax.experimental.pallas import tpu as pltpu
from jax.sharding import PartitionSpec as P

HD = 64
MESH_ID = pl.DeviceIdType.MESH


norm_eps = 1e-05
score_scale = 0.125
masked_score = -1e30
beta_one = 0.9
beta_two = 0.99
adam_steps = 10
adam_eps = 1e-08


def from_partner(block, axis, apart):
    count = lax.axis_size(axis)
    route = []
    for low in range(count):
        high = low | 1 << apart
        if high != low and high < count:
            route += [(low, high), (high, low)]
    return lax.ppermute(block, axis, route)


def layer_norm(values_in, gain_row, shift_row):
    center = values_in - jnp.mean(values_in, -1, keepdims=True)
    spread = jnp.mean(center * center, -1, keepdims=True)
    return center * lax.rsqrt(spread + norm_eps) * gain_row + shift_row


def gelu_exact(values_in):
    return jax.nn.gelu(values_in, approximate=False)


def matmul(matrix_a, matrix_b):
    return jnp.dot(matrix_a, matrix_b, preferred_element_type=jnp.float32)


def tensor_total(values_in):
    return lax.psum(values_in, "tensor")


def send(source, target, send_sem, recv_sem, peer):
    return pltpu.make_async_remote_copy(
        src_ref=source,
        dst_ref=target,
        send_sem=send_sem,
        recv_sem=recv_sem,
        device_id=peer,
        device_id_type=MESH_ID,
    )


def row_sum(block):
    return jnp.sum(block, 0, keepdims=True)


def lane_mean(block):
    return jnp.mean(block, -1, keepdims=True)


def dot_nn(left, right):
    return jnp.dot(left, right, preferred_element_type=jnp.float32)


def dot_nt(left, right):
    return lax.dot_general(
        left, right, (((1,), (1,)), ((), ())), preferred_element_type=jnp.float32
    )


def dot_tn(left, right):
    return lax.dot_general(
        left, right, (((0,), (0,)), ((), ())), preferred_element_type=jnp.float32
    )


def normalize(rows):
    center = rows - lane_mean(rows)
    scale = lax.rsqrt(lane_mean(center * center) + norm_eps)
    return center * scale, scale


def normalize_back(grad, normed, scale, gain):
    inner = grad * gain
    return scale * (inner - lane_mean(inner) - normed * lane_mean(inner * normed))


def aligned(index, step):
    return pl.ds(pl.multiple_of(index * step, step), step)


def layer_kernel(names, orders, ents_order, vec_order, schedule, *refs):
    r = types.SimpleNamespace(**dict(zip(names, refs, strict=True)))
    low, full = jnp.bfloat16, jnp.float32
    dp, x, t = lax.axis_index("dp"), lax.axis_index("stream"), lax.axis_index("tensor")
    y, z = lax.rem(dp, 2), dp // 2
    owners = lax.axis_size("dp") * 2
    _, half_words, width = r.hbm_words.shape
    half_ents = r.shard.shape[1]
    rows, words = half_words + half_ents, 2 * half_words
    everyone = 2 * rows
    capacity = r.ask.shape[1]
    slots = owners * capacity
    heads = r.prob.shape[0]
    share = width // owners
    side = heads * HD
    hidden = r.w_up.shape[1]
    block = half_ents
    blocks = rows // block
    word_blocks = half_words // block
    wide = 256

    core, x_peer, y_peer = {"tensor": 1 - t}, {"stream": 1 - x}, {"dp": z * 2 + 1 - y}
    z_low, z_high = lax.rem(z, 2), z // 2
    near_peer = {"dp": (z + 1 - 2 * z_low) * 2 + y}
    far_peer = {"dp": (z + 2 - 4 * z_high) * 2 + y}
    mine_on = (z_high, z_low, y, x)
    peer_on = (far_peer, near_peer, y_peer, x_peer)
    flat = dp * 2 + x
    others = []
    for k in range(1, owners):
        other = lax.rem(flat + k, owners)
        others.append((other, {"dp": other // 2, "stream": lax.rem(other, 2)}))

    loads = {}
    barrier = pltpu.get_barrier_semaphore()
    for peer in [core] + [peer for _, peer in others]:
        pl.semaphore_signal(barrier, inc=1, device_id=peer, device_id_type=MESH_ID)

    def load(source, target):
        loads[id(target)] = pltpu.make_async_copy(source, target, r.load_s.at[len(loads)])
        loads[id(target)].start()

    def loaded(target):
        loads.pop(id(target)).wait()

    load(r.hbm_shard, r.shard)
    load(r.hbm_row, r.row)
    my_words = r.x_all.at[aligned(x, half_words), :]
    load(r.hbm_words.at[0], my_words)
    load(r.hbm_query, r.w_query)
    load(r.hbm_keyval, r.w_keyval)
    smalls = [
        (r.hbm_b_query, r.b_query), (r.hbm_b_value, r.b_value), (r.hbm_word_seg, r.word_seg),
        (r.hbm_ent_seg, r.ent_seg), (r.hbm_gain, r.gain), (r.hbm_shift, r.shift),
        (r.hbm_b_out, r.b_out), (r.hbm_b_up, r.b_up), (r.hbm_b_down, r.b_down),
    ]
    for source, target in smalls:
        load(source, target)
    load(r.hbm_table, r.table)
    load(r.hbm_entity, r.w_entity)
    cot_words, cot_ents = r.cotangent.at[0:half_words, :], r.cotangent.at[half_words:rows, :]
    load(r.hbm_cot_words.at[0], cot_words)
    load(r.hbm_cot_ents.at[0], cot_ents)
    load(r.hbm_out, r.w_out)
    load(r.hbm_up, r.w_up)
    load(r.hbm_down, r.w_down)

    flushes = []

    def flush(source, target):
        flushes.append(pltpu.make_async_copy(source, target, r.flush_s.at[len(flushes)]))
        flushes[-1].start()

    loaded(r.shard)
    loaded(r.row)
    shard_row = r.shard[...]
    shard_all = jnp.broadcast_to(shard_row.astype(full), (half_ents, half_ents)).T
    shard_all = shard_all.astype(jnp.int32)
    shard_col = shard_all[:, 0:1]
    below = lax.broadcasted_iota(jnp.int32, (half_ents, half_ents), 0)
    beside = lax.broadcasted_iota(jnp.int32, (half_ents, half_ents), 1)
    same = shard_all == shard_row
    rank_row = row_sum(jnp.where(same & (below < beside), 1.0, 0.0)).astype(jnp.int32)
    rank_col = jnp.sum(jnp.where(same & (beside < below), 1.0, 0.0), 1, keepdims=True)
    rank_col = rank_col.astype(jnp.int32)
    slot_row = shard_row * capacity + rank_row
    in_slot = lax.broadcasted_iota(jnp.int32, (slots, half_ents), 0) == slot_row
    wanted = jnp.sum(
        jnp.where(in_slot, (r.row[...] + 1).astype(full), 0.0), 1, keepdims=True
    )
    wanted = wanted.astype(jnp.int32) - 1
    r.ask[...] = jnp.broadcast_to(wanted, (slots, 128)).reshape(owners, capacity, 128)
    r.outbox[...] = jnp.where(in_slot, 1.0, 0.0).astype(low)
    answer_col = shard_col * (2 * capacity) + x * capacity + rank_col
    answer_lane = lax.broadcasted_iota(jnp.int32, (half_ents, 2 * slots), 1)
    r.select[aligned(x, half_ents), :] = jnp.where(answer_lane == answer_col, 1.0, 0.0).astype(low)
    r.asked[flat] = r.ask[flat]
    r.vec[0] = jnp.zeros(r.vec.shape[1:], full)

    loaded(r.w_query)
    loaded(r.w_keyval)
    for _, target in smalls:
        loaded(target)

    def gather_columns(which):
        for h in range(heads):
            own = slice(which * side + h * HD, which * side + (h + 1) * HD)
            for place, words_part, ents_part in (
                (0, r.w_query[0, :, own], r.w_query[2, :, own]),
                (1, r.w_query[1, :, own], r.w_query[3, :, own]),
                (2, r.w_keyval[0, :, own], None),
                (3, r.w_keyval[1, :, own], None),
            ):
                lanes = slice((4 * h + place) * HD, (4 * h + place + 1) * HD)
                r.cat_words[:, lanes] = words_part
                r.cat_ents[:, lanes] = words_part if ents_part is None else ents_part
            zero = jnp.zeros((1, HD), full)
            value = r.b_value[...].reshape(1, -1)[:, own]
            query = r.b_query[:, own]
            lanes = slice(4 * h * HD, 4 * (h + 1) * HD)
            r.bias_words[:, lanes] = jnp.concatenate([query[0:1], query[1:2], zero, value], 1)
            r.bias_ents[:, lanes] = jnp.concatenate([query[2:3], query[3:4], zero, value], 1)

    for which in range(2):

        @pl.when(x == which)
        def _(which=which):
            gather_columns(which)

    loaded(my_words)
    r.x_own[0:half_words, :] = my_words[...].astype(full)
    pl.semaphore_wait(barrier, owners)

    def ask_copy(k):
        other, peer = others[k]
        return send(r.ask.at[other], r.asked.at[flat], r.ask_s.at[k], r.ask_r.at[k], peer)

    def answer_copy(k):
        other, peer = others[k]
        return send(
            r.found.at[other // 2], r.answer.at[flat], r.answer_s.at[k], r.answer_r.at[k], peer
        )

    def slope_copy(k):
        other, peer = others[k]
        return send(r.slope.at[other], r.slopes.at[flat], r.slope_s.at[k], r.slope_r.at[k], peer)

    for k in range(owners - 1):
        ask_copy(k).start()
    my_select = r.select.at[aligned(x, half_ents), :]
    select_copy = send(my_select, my_select, r.pair_s.at[0], r.pair_r.at[0], x_peer)
    select_copy.start()
    half = half_words // 2
    my_half = r.x_all.at[aligned(2 * x + t, half), :]
    words_copy = send(my_half, my_half, r.pair_s.at[1], r.pair_r.at[1], x_peer)
    words_copy.start()

    is_query = lax.broadcasted_iota(jnp.int32, (1, 4 * HD), 1) < 2 * HD
    scaling = jnp.where(is_query, score_scale, 1.0)

    def project(start, count, weight, bias):
        def body(h, carry):
            lanes = aligned(h, 4 * HD)
            total = dot_nn(r.x_all[pl.ds(start, count), :], weight[:, lanes]) + bias[:, lanes]
            r.qkv[pl.ds(start, count), lanes] = (total * scaling).astype(low)
            return carry

        lax.fori_loop(0, heads, body, 0, unroll=True)

    project(pl.multiple_of(x * half_words, half_words), half_words, r.cat_words, r.bias_words)

    segments = jnp.concatenate([r.word_seg[...], r.ent_seg[...]], 1)
    for i in range(everyone // 128):
        own_seg = jnp.broadcast_to(segments[:, i * 128 : (i + 1) * 128].astype(full), (128, 128)).T
        equal = own_seg[:, 0:1].astype(jnp.int32) == segments
        r.mask[i * 128 : (i + 1) * 128, :] = jnp.where(equal, 0.0, masked_score).astype(low)

    for k in range(owners - 1):
        ask_copy(k).wait()
    ids = r.asked[...].reshape(slots, 128)
    lane = lax.broadcasted_iota(jnp.int32, (slots, 128), 1)
    loaded(r.table)
    piece = 4 * 128

    def pick_body(j, found):
        ones = [jnp.where(ids == lane + (j * piece + n * 128), 1.0, 0.0) for n in range(4)]
        return found + dot_nn(jnp.concatenate(ones, 1).astype(low), r.table[aligned(j, piece), :])

    found = jnp.zeros((slots, r.table.shape[1]), full)
    found = lax.fori_loop(0, r.table.shape[0] // piece, pick_body, found, unroll=True).astype(low)
    r.found[...] = found.reshape(r.found.shape)
    r.answer[flat] = r.found[dp]
    for k in range(owners - 1):
        answer_copy(k).start()

    words_copy.wait()
    far_half = r.x_all.at[aligned(2 * (1 - x) + t, half), :]
    relay = send(far_half, far_half, r.pair_s.at[8], r.pair_r.at[8], core)
    relay.start()
    relay.wait()
    project(pl.multiple_of((1 - x) * half_words, half_words), half_words, r.cat_words, r.bias_words)

    def take_heads(here):
        for h in range(heads):
            r.key[h, here, :] = r.qkv[here, h * 4 * HD + 2 * HD : h * 4 * HD + 3 * HD]
            r.value[h, here, :] = r.qkv[here, h * 4 * HD + 3 * HD : h * 4 * HD + 4 * HD]

    of_words, of_ents = slice(0, words), slice(words, everyone)
    take_heads(of_words)
    for h in range(heads):
        query = r.qkv[of_words, h * 4 * HD : h * 4 * HD + HD]
        r.prob[h, of_words, of_words] = dot_nt(query, r.key[h, of_words, :])

    def soften_words(which):
        def body(i, carry):
            here = pl.ds(pl.multiple_of(which * half_words + i * SOFT, SOFT), SOFT)
            bias = r.mask[here, of_words].astype(full)
            for h in range(heads):
                score = r.prob[h, here, of_words] + bias
                peak = jnp.max(score, 1, keepdims=True)
                power = jnp.exp(score - peak)
                r.prob[h, here, of_words] = power
                r.factor[h, here, :] = jnp.broadcast_to(peak, (SOFT, 128))
                mass = jnp.broadcast_to(jnp.sum(power, 1, keepdims=True), (SOFT, 128))
                r.mass[h, here, :] = mass
            return carry

        lax.fori_loop(0, half_words // SOFT, body, 0)

    soften_words(0)
    soften_words(1)
    for h in range(heads):
        weights = r.prob[h, of_words, of_words].astype(low)
        r.grad_prob[of_words, h * 128 : h * 128 + HD] = dot_nn(weights, r.value[h, of_words, :])
        r.factor[h, of_ents, :] = jnp.ones((2 * half_ents, 128), full)

    select_copy.wait()
    for k in range(owners - 1):
        answer_copy(k).wait()
    looked = dot_nn(r.select[...], r.answer[...].reshape(2 * slots, r.table.shape[1])).astype(low)
    r.looked[...] = looked
    loaded(r.w_entity)
    ent_lin = dot_nn(looked, r.w_entity[...])
    normed, _ = normalize(ent_lin)
    x_entity = normed * r.gain[0:1, :] + r.shift[0:1, :]
    r.ent_lin[...] = ent_lin
    r.x_ent[...] = x_entity
    r.x_all[words:everyone, :] = x_entity.astype(low)
    r.x_own[half_words:rows, :] = r.x_ent[aligned(x, half_ents), :]
    project(words, 2 * half_ents, r.cat_ents, r.bias_ents)
    take_heads(of_ents)

    def both_kinds(which):
        near_words = pl.ds(pl.multiple_of(which * half_words, half_words), half_words)
        near_ents = pl.ds(pl.multiple_of(words + which * half_ents, half_ents), half_ents)
        return (near_words, slice(0, half_words)), (near_ents, slice(half_words, rows))

    def soften_ents(here):
        bias = r.mask[here, :].astype(full)
        for h in range(heads):
            score = r.prob[h, here, :] + bias
            power = jnp.exp(score - jnp.max(score, 1, keepdims=True))
            r.prob[h, here, :] = power * (1.0 / jnp.sum(power, 1, keepdims=True))

    def complete_words(here):
        bias = r.mask[here, of_ents].astype(full)
        for h in range(heads):
            score = r.prob[h, here, of_ents] + bias
            peak = r.factor[h, here, :]
            best = jnp.broadcast_to(jnp.max(score, 1, keepdims=True), (half_words, 128))
            top = jnp.maximum(peak, best)
            power, shrink = jnp.exp(score - top), jnp.exp(peak - top)
            added = jnp.broadcast_to(jnp.sum(power, 1, keepdims=True), (half_words, 128))
            share_of = 1.0 / (r.mass[h, here, :] * shrink + added)
            r.prob[h, here, of_ents] = power * share_of
            r.factor[h, here, :] = shrink * share_of

    def attend_words(which, target):
        (here, there), _ = both_kinds(which)
        for h in range(heads):
            query = r.qkv[here, h * 4 * HD + HD : h * 4 * HD + 2 * HD]
            r.prob[h, here, of_ents] = dot_nt(query, r.key[h, of_ents, :])
        complete_words(here)
        for h in range(heads):
            out = r.grad_prob[here, h * 128 : h * 128 + HD] * r.factor[h, here, 0:HD]
            out = out + dot_nn(r.prob[h, here, of_ents].astype(low), r.value[h, of_ents, :])
            target[there, h * HD : (h + 1) * HD] = out.astype(low)

    def attend_ents(which, target):
        _, (here, there) = both_kinds(which)
        for h in range(heads):
            query = r.qkv[here, h * 4 * HD : h * 4 * HD + 2 * HD]
            r.prob[h, here, of_words] = dot_nt(query[:, :HD], r.key[h, of_words, :])
            r.prob[h, here, of_ents] = dot_nt(query[:, HD:], r.key[h, of_ents, :])
        soften_ents(here)
        for h in range(heads):
            out = dot_nn(r.prob[h, here, :].astype(low), r.value[h])
            target[there, h * HD : (h + 1) * HD] = out.astype(low)

    def heads_part(n, part):
        return send(
            r.heads_far.at[part, :], r.heads_in.at[part, :], r.heads_s.at[n], r.heads_r.at[n], x_peer
        )

    attend_words(1 - x, r.heads_far)
    heads_copies = [heads_part(0, slice(0, half_words))]
    heads_copies[0].start()
    attend_ents(1 - x, r.heads_far)
    heads_copies.append(heads_part(1, slice(half_words, rows)))
    heads_copies[1].start()
    attend_words(x, r.heads_near)
    attend_ents(x, r.heads_near)
    r.words_t[...] = r.x_all[of_words, :].T
    r.ents_t[...] = r.x_all[of_ents, :].T
    for copy in heads_copies:
        copy.wait()

    @pl.when(x == 0)
    def _():
        r.heads_all[:, 0:side] = r.heads_near[...]
        r.heads_all[:, side:] = r.heads_in[...]

    @pl.when(x == 1)
    def _():
        r.heads_all[:, 0:side] = r.heads_in[...]
        r.heads_all[:, side:] = r.heads_near[...]

    def strip(which, turn, j):
        part = (which, slice(0, rows), aligned(j, wide))
        return send(
            r.mail_out.at[part], r.mail_in.at[part], r.strip_s.at[turn, j], r.strip_r.at[turn, j], core
        )

    def arrived(which, here):
        return r.mail_out[which, here, :].astype(full) + r.mail_in[which, here, :].astype(full)

    def wait_strips(which, turn):
        for j in range(width // wide):
            strip(which, turn, j).wait()

    def swap(which, turn, first, count):
        part = pl.ds(first, count)
        return send(
            r.mail_out.at[which, part], r.mail_in.at[which, part], r.swap_s.at[turn],
            r.swap_r.at[turn], core,
        )

    def columns(count, fill):
        def body(j, carry):
            fill(aligned(j, wide), j)
            return carry

        lax.fori_loop(0, count // wide, body, 0, unroll=True)

    def fill_attn(lanes, j):
        r.mail_out[0, 0:rows, lanes] = dot_nn(r.heads_all[...], r.w_out[:, lanes]).astype(low)
        strip(0, 0, j).start()

    loaded(r.w_out)
    columns(width, fill_attn)
    wait_strips(0, 0)

    tall = rows // 1

    def over_rows(body):
        def step(i, carry):
            body(aligned(i, tall))
            return carry

        lax.fori_loop(0, rows // tall, step, 0)

    def first_norm(here):
        attn = arrived(0, here) + r.b_out[...].reshape(1, -1)
        normed, scale = normalize(r.x_own[here, :] + attn)
        r.normed[here, :] = normed
        r.scale[here, :] = jnp.broadcast_to(scale, (tall, 128))
        r.first[here, :] = (normed * r.gain[1:2, :] + r.shift[1:2, :]).astype(low)

    over_rows(first_norm)

    def fill_up(lanes, _):
        up = dot_nn(r.first[...], r.w_up[:, lanes]) + r.b_up[lanes].reshape(1, -1)
        chance = 0.5 + 0.5 * lax.erf(up * (0.5**0.5))
        r.act[:, lanes] = (up * chance).astype(low)
        r.slope_up[:, lanes] = chance + up * (jnp.exp(-0.5 * up * up) * (0.5 / math.pi) ** 0.5)

    loaded(r.w_up)
    columns(hidden, fill_up)

    def fill_down(lanes, j):
        r.mail_out[1, 0:rows, lanes] = dot_nn(r.act[...], r.w_down[:, lanes]).astype(low)
        strip(1, 1, j).start()

    loaded(r.w_down)
    columns(width, fill_down)
    wait_strips(1, 1)

    vec = r.vec.at[0]

    def second_norm(here):
        ffn = arrived(1, here) + r.b_down[...].reshape(1, -1)
        entering = r.normed[here, :] * r.gain[1:2, :] + r.shift[1:2, :]
        normed, scale = normalize(entering + ffn)
        r.final[here, :] = (normed * r.gain[2:3, :] + r.shift[2:3, :]).astype(low)
        grad = r.cotangent[here, :].astype(full)
        vec[2:3, :] += row_sum(grad * normed)
        vec[5:6, :] += row_sum(grad)
        back = normalize_back(grad, normed, scale, r.gain[2:3, :])
        r.grad_second[here, :] = back
        r.grad_low[here, :] = back.astype(low)
        vec[7:8, :] += row_sum(back.astype(low).astype(full))

    loaded(cot_words)
    loaded(cot_ents)
    over_rows(second_norm)

    def halved(ref, place, index):
        return ref.at[(slice(None),) * place + (index,)]

    def stage(kit, c, order, n):
        left = [axis for axis in range(4) if axis not in order[:n]]
        axis, place = order[n], left.index(order[n])
        held = kit.held[n].at[c]
        copy = send(
            halved(held, place, 1 - mine_on[axis]), kit.held[n + 1].at[c],
            kit.sent.at[c, n], kit.got.at[c, n], peer_on[axis],
        )
        return copy, halved(held, place, mine_on[axis])

    def advance(kit, c, order, n):
        copy, own = stage(kit, c, order, n - 1)
        copy.wait()
        total = kit.held[n].at[c]

        def body(i, carry):
            total[i] = own[i] + total[i]
            return carry

        lax.fori_loop(0, 2, body, 0)
        stage(kit, c, order, n)[0].start()

    def finish(kit, c, order):
        copy, own = stage(kit, c, order, 3)
        copy.wait()
        kit.out[c] = own[...].astype(full) + kit.held[4][c].astype(full)

    kit_a = types.SimpleNamespace(
        held=(r.grads, r.near, r.next, r.far, r.last), out=r.out_a, sent=r.a_s, got=r.a_r
    )
    kit_e = types.SimpleNamespace(
        held=(r.e_grads, r.e_near, r.e_next, r.e_far, r.e_last), out=r.e_sum, sent=r.e_s, got=r.e_r
    )
    along = dict(zip(range(3), ((3, 2, 1, 0), (2, 3, 1, 0), (1, 0, 3, 2))))

    kit_q = types.SimpleNamespace(held=(r.q_grads, r.q_near, r.q_next, r.q_far), sent=r.q_s, got=r.q_r)
    head_order = (2, 1, 0, 3)

    def head_start(h):
        stage(kit_q, h, head_order, 0)[0].start()

    def head_meet(h):
        return send(r.q_away.at[h], r.q_in.at[h], r.q_s.at[h, 3], r.q_r.at[h, 3], x_peer)

    def head_advance(h, n):
        if n < 3:
            advance(kit_q, h, head_order, n)
            return
        copy, own = stage(kit_q, h, head_order, 2)
        copy.wait()
        away = own[1 - x].astype(full) + r.q_far[h, 1 - x].astype(full)
        r.q_away[h] = away.astype(low)
        head_meet(h).start()
        r.out_q[h, x] = own[x].astype(full) + r.q_far[h, x].astype(full)

    def head_finish(h):
        head_meet(h).wait()
        r.out_q[h, 1 - x] = r.q_in[h].astype(full)

    def vec_copy(n):
        peer = peer_on[along[vec_order][n]]
        return send(r.vec.at[n], r.vec_in.at[n], r.vec_s.at[n], r.vec_r.at[n], peer)

    def vec_advance(n):
        vec_copy(n - 1).wait()
        r.vec[n] = r.vec[n - 1] + r.vec_in[n - 1]
        if n < 4:
            vec_copy(n).start()

    chunk = r.grads.shape[-1]

    def make_grad(c, left_t, right, lanes):
        part = dot_nn(left_t[...], right[:, lanes]).astype(low)
        r.grads[c] = part.reshape(2, 2, 2, 2, share, chunk)

    plan = iter(schedule)

    def tick():
        for what, c, n in next(plan):
            if what == CHUNK and n == 0:
                stage(kit_a, c, along[orders[c]], 0)[0].start()
            elif what == CHUNK:
                advance(kit_a, c, along[orders[c]], n)
            elif what == HEAD:
                head_advance(c, n)
            elif what == ENTS:
                advance(kit_e, c, along[ents_order], n)
            elif what == WORDS:
                words_back_copy.start()
            else:
                vec_advance(n)

    downs = hidden // chunk
    r.grad_t[...] = r.grad_low[...].T
    for c in range(downs):
        make_grad(c, r.grad_t, r.act, slice(c * chunk, (c + 1) * chunk))
        tick()

    def fill_dup(lanes, j):
        grad_act = dot_nt(r.grad_low[...], r.w_down[lanes, :])
        grad_up = (grad_act * r.slope_up[:, lanes]).astype(low)
        r.grad_up[:, lanes] = grad_up
        vec[pl.ds(8 + j // (width // wide), 1), aligned(lax.rem(j, width // wide), wide)] = row_sum(
            grad_up.astype(full)
        )

    columns(hidden, fill_dup)
    tick()

    def fill_back(lanes, j):
        r.mail_out[0, 0:rows, lanes] = dot_nt(r.grad_up[...], r.w_up[lanes, :]).astype(low)
        strip(0, 2, j).start()

    columns(width, fill_back)
    tick()
    r.first_t[...] = r.first[...].T
    flush(r.final.at[aligned(t, half_words // 2), :], r.to_out_words)
    ents_share = pl.multiple_of(half_words + t * (half_ents // 2), half_ents // 2)
    flush(r.final.at[pl.ds(ents_share, half_ents // 2), :], r.to_out_ents)
    for c in range(downs):
        make_grad(downs + c, r.first_t, r.grad_up, slice(c * chunk, (c + 1) * chunk))
        tick()
    wait_strips(0, 2)

    def first_back(here):
        grad = r.grad_second[here, :] + arrived(0, here)
        normed = r.normed[here, :]
        vec[1:2, :] += row_sum(grad * normed)
        vec[4:5, :] += row_sum(grad)
        back = normalize_back(grad, normed, r.scale[here, 0:1], r.gain[1:2, :])
        r.grad_first[here, :] = back
        r.grad_low[here, :] = back.astype(low)
        vec[6:7, :] += row_sum(back.astype(low).astype(full))

    over_rows(first_back)
    tick()
    near_rows = aligned(x, side)
    far_rows = aligned(1 - x, side)
    r.back_far[...] = dot_nt(r.grad_low[...], r.w_out[far_rows, :]).astype(low)
    mine = [(aligned(x, half_words), 0, half_words)]
    mine.append((pl.ds(pl.multiple_of(words + x * half_ents, half_ents), half_ents), half_words, half_ents))
    back_copies = [
        send(
            r.back_far.at[pl.ds(first, count), :], r.back_heads.at[place, :],
            r.pair_s.at[3 + n], r.pair_r.at[3 + n], x_peer,
        )
        for n, (place, first, count) in enumerate(mine)
    ]
    for copy in back_copies:
        copy.start()
    near = dot_nt(r.grad_low[...], r.w_out[near_rows, :]).astype(low)
    for place, first, count in mine:
        r.back_heads[place, :] = near[first : first + count, :]
    r.grad_t[...] = r.grad_low[...].T
    outs = 2 * downs
    make_grad(outs, r.grad_t, r.heads_all, slice(0, chunk))
    tick()


    pair = 2 * HD
    for h in range(heads):
        base = h * 4 * HD

        def score_back(start, size):
            def body(i, carry):
                here = pl.ds(pl.multiple_of(start + i * size, size), size)
                factor = jnp.concatenate([r.factor[h, here, :]] * (words // 128), 1)
                scaled = r.prob[h, here, of_words] * factor
                prob = jnp.concatenate([scaled, r.prob[h, here, of_ents]], 1)
                grad_prob = r.grad_prob[here, :]
                inner = jnp.sum(prob * grad_prob, 1, keepdims=True)
                r.grad_score[here, :] = (prob * (grad_prob - inner)).astype(low)
                r.prob_low[here, :] = prob.astype(low)
                return carry

            return body

        for which in (x, 1 - x):
            if which is not x:
                tick()
            if h == 0 and which is not x:
                for copy in back_copies:
                    copy.wait()
            for here, _ in both_kinds(which):
                r.grad_prob[here, :] = dot_nt(r.back_heads[here, h * HD : (h + 1) * HD], r.value[h])
            lax.fori_loop(0, half_words // SOFT, score_back(which * half_words, SOFT), 0)
            score_back(words + which * half_ents, half_ents)(0, 0)
        queries = jnp.concatenate(
            [
                dot_nn(r.grad_score[:, :words], r.key[h, 0:words, :]),
                dot_nn(r.grad_score[:, words:], r.key[h, words:everyone, :]),
            ],
            1,
        )
        r.grad_qkv[:, base : base + pair] = (queries * score_scale).astype(low)
        tick()
        query_t = r.qkv[:, base : base + pair].T
        keys_t = dot_nn(query_t, r.grad_score[...])
        keys_t = jnp.concatenate([keys_t[:HD, :words], keys_t[HD:, words:]], 1)
        values_t = dot_nn(r.back_heads[:, h * HD : (h + 1) * HD].T, r.prob_low[...])
        r.grad_qkv[:, base + pair : base + 2 * pair] = (
            jnp.concatenate([keys_t, values_t], 0).T.astype(low)
        )

        tick()
        keyval = slice(base + pair, base + 2 * pair)
        query = slice(base, base + pair)
        by_words = dot_nn(r.words_t[...], r.grad_qkv[0:words, query])
        by_ents = dot_nn(r.ents_t[...], r.grad_qkv[words:everyone, query])
        by_keyval = dot_nn(r.words_t[...], r.grad_qkv[0:words, keyval])
        by_keyval = by_keyval + dot_nn(r.ents_t[...], r.grad_qkv[words:everyone, keyval])
        for n, part in enumerate([by_words, by_ents, by_keyval]):
            r.q_grads[h, :, :, :, :, :, n * pair : (n + 1) * pair] = part.astype(low).reshape(
                2, 2, 2, 2, share, pair
            )
        head_start(h)
        sums = jnp.concatenate(
            [
                row_sum(r.grad_qkv[0:words, base : base + pair].astype(full)),
                row_sum(r.grad_qkv[words:everyone, base : base + pair].astype(full)),
                row_sum(r.grad_qkv[:, base + pair : base + 2 * pair].astype(full)),
            ],
            1,
        )
        place = h * 3 * pair
        vec[pl.ds(10 + 2 * x + place // width, 1), place % width : place % width + 3 * pair] = sums
        tick()

    quarter = half_words // 2

    def input_grad(place, weight):
        return dot_nt(r.grad_qkv[place, :], weight[...])

    ents_part = input_grad(slice(words, everyone), r.cat_ents)
    r.mail_out[1, words // 2 :, :] = ents_part.astype(low)
    ents_swap = swap(1, 0, words // 2, 2 * half_ents)
    ents_swap.start()
    tick()
    for n in range(2):
        r.mail_out[1, n * quarter : (n + 1) * quarter, :] = input_grad(
            aligned(2 * n + 1 - t, quarter), r.cat_words
        ).astype(low)
    words_swap = swap(1, 1, 0, words // 2)
    words_swap.start()
    for n in range(2):
        r.input_part[n] = input_grad(aligned(2 * n + t, quarter), r.cat_words)
    tick()
    ents_swap.wait()
    ents_place = pl.multiple_of(words // 2 + (1 - x) * half_ents, half_ents)
    ents_far = pl.ds(ents_place, half_ents)
    ents_near = pl.ds(pl.multiple_of(words // 2 + x * half_ents, half_ents), half_ents)
    r.ents_back[...] = arrived(1, ents_far).astype(low)
    ents_copy = send(r.ents_back, r.ents_in, r.pair_s.at[5], r.pair_r.at[5], x_peer)
    ents_copy.start()
    tick()
    words_swap.wait()
    far_place = aligned(1 - x, quarter)
    r.words_back[...] = (r.input_part[1 - x] + r.mail_in[1, far_place, :].astype(full)).astype(low)
    words_back_copy = send(r.words_back, r.words_in, r.pair_s.at[6], r.pair_r.at[6], x_peer)
    tick()
    ents_copy.wait()

    grad = r.grad_first[half_words:rows, :] + arrived(1, ents_near)
    grad = grad + r.ents_in[...].astype(full)
    own_ents = aligned(x, half_ents)
    normed, scale = normalize(r.ent_lin[own_ents, :])
    vec[0:1, :] = row_sum(grad * normed)
    vec[3:4, :] = row_sum(grad)
    lin_low = normalize_back(grad, normed, scale, r.gain[0:1, :]).astype(low)
    slope = dot_nt(lin_low, r.w_entity[...]).astype(low)
    r.slope[...] = dot_nn(r.outbox[...], slope).reshape(owners, capacity, -1)
    r.slopes[flat] = r.slope[flat]
    for k in range(owners - 1):
        slope_copy(k).start()
    looked_half = r.looked[own_ents, aligned(t, 128)]
    ents_grad = dot_tn(lin_low, looked_half).astype(low)
    r.e_grads[0] = ents_grad.reshape(2, 2, 2, 2, share, 128)
    stage(kit_e, 0, along[ents_order], 0)[0].start()
    vec_copy(0).start()
    tick()
    for k in range(owners - 1):
        slope_copy(k).wait()
    ids_t = r.asked[...].reshape(slots, 128).astype(full).T
    r.ids_out[...] = ids_t[0:8, :].astype(jnp.int32)
    r.slopes_out[...] = r.slopes[...].reshape(slots, -1).astype(low)
    flush(r.ids_out, r.to_ids_out)
    flush(r.slopes_out, r.to_slopes_out)
    words_back_copy.wait()
    r.grad_words[...] = (
        r.grad_first[aligned(t, quarter), :]
        + (r.input_part[x] + r.mail_in[1, aligned(x, quarter), :].astype(full))
        + r.words_in[...].astype(full)
    )
    flush(r.grad_words, r.to_grad_words)
    for c in range(2 * downs + 1):
        finish(kit_a, c, along[orders[c]])
        flush(r.out_a.at[c], r.to_out_a.at[c])
    vec_advance(4)
    total = r.vec[4]
    flush(r.vec.at[4], r.to_vec_out)
    r.across_out[...] = pltpu.roll(total[0:8, :], width - flat * share, 1)[:, 0:128]
    flush(r.across_out, r.to_across_out)
    finish(kit_e, 0, along[ents_order])
    ents_out = send(r.e_sum.at[0], r.e_in, r.pair_s.at[7], r.pair_r.at[7], core)
    ents_out.start()
    r.out_e[t] = r.e_sum[0]
    for h in range(heads):
        head_finish(h)
        flush(r.out_q.at[h], r.to_out_q.at[h])
    ents_out.wait()
    r.out_e[1 - t] = r.e_in[...]
    flush(r.out_e, r.to_out_e)
    for copy in flushes:
        copy.wait()


def finish_kernel(names, *refs):
    r = types.SimpleNamespace(**dict(zip(names, refs, strict=True)))
    low, full = jnp.bfloat16, jnp.float32
    table_rows, embed = r.hbm_first.shape
    slots = r.hbm_ids.shape[1]
    steps = r.in_s.shape[1]
    count = table_rows // steps
    chunks, share, chunk = r.hbm_a.shape
    downs = chunks // 2
    heads, side = r.hbm_q.shape[0], r.hbm_q.shape[0] * HD

    pairs = [(r.hbm_ids, r.ids), (r.hbm_slopes, r.slopes)]
    pairs += [(r.hbm_q, r.out_q), (r.hbm_e, r.out_e), (r.hbm_vec, r.vec), (r.hbm_across, r.across)]
    layers = [(r.hbm_a.at[2 * downs], r.out_part)]
    for c in range(downs):
        lanes = slice(c * chunk, (c + 1) * chunk)
        layers.append((r.hbm_a.at[c], r.down_part.at[:, lanes]))
        layers.append((r.hbm_a.at[downs + c], r.up_part.at[:, lanes]))
    layers += [(r.hbm_words, r.words_part), (r.hbm_ents, r.ents_part), (r.hbm_grad, r.grad_part)]
    smalls = [
        pltpu.make_async_copy(source, target, r.small_s.at[n])
        for n, (source, target) in enumerate(pairs + layers)
    ]
    outs = [
        pltpu.make_async_copy(source, target, r.done_s.at[n])
        for n, (source, target) in enumerate(
            [
                (r.out_part, r.red_out),
                (r.down_part, r.red_down),
                (r.up_part, r.red_up),
                (r.words_part, r.words_done.at[0]),
                (r.ents_part, r.ents_done.at[0]),
                (r.grad_part, r.grad_words_done.at[0]),
                (r.query_part, r.red_query),
                (r.keyval_part, r.red_keyval),
            ]
        )
    ]

    def moves(i, inward):
        here = pl.ds(i * count, count)
        if inward:
            ends = [(r.hbm_first, r.first), (r.hbm_second, r.second)]
            flags = r.in_s
        else:
            ends = [(r.update, r.table_update), (r.first, r.new_first), (r.second, r.new_second)]
            flags = r.out_s
        return [
            pltpu.make_async_copy(source.at[here, :], target.at[here, :], flags.at[n, i])
            for n, (source, target) in enumerate(ends)
        ]

    early, late = smalls[:2], smalls[2:]
    for copy in early + moves(0, True) + moves(1, True) + late:
        copy.start()
    for i in range(2, steps):
        for copy in moves(i, True):
            copy.start()
    for copy in early:
        copy.wait()
    r.addends[:, 0:embed] = r.slopes[...]
    r.addends[:, embed:] = jnp.ones((slots, 128), low)

    def adam(i):
        for copy in moves(i, True):
            copy.wait()
        here = pl.ds(i * count, count)
        row = lax.broadcasted_iota(jnp.int32, (count, slots), 0) + i * count
        chosen = jnp.where(row == r.ids[0:1, :], 1.0, 0.0).astype(low)
        total = dot_nn(chosen, r.addends[...])
        touched = total[:, embed:] > 0.0
        for start in range(0, embed, 128):
            lanes = slice(start, start + 128)
            grad = total[:, lanes]
            first, second = r.first[here, lanes], r.second[here, lanes]
            first_next = beta_one * first + (1.0 - beta_one) * grad
            second_next = beta_two * second + (1.0 - beta_two) * grad * grad
            direction = (
                first_next
                * (1.0 / (1.0 - beta_one**adam_steps))
                / (jnp.sqrt(second_next * (1.0 / (1.0 - beta_two**adam_steps))) + adam_eps)
            )
            r.update[here, lanes] = jnp.where(touched, direction, 0.0)
            r.first[here, lanes] = jnp.where(touched, first_next, first)
            r.second[here, lanes] = jnp.where(touched, second_next, second)
        for copy in moves(i, False):
            copy.start()

    def lay_out_rest():
        for copy in late:
            copy.wait()
        for copy in outs[:6]:
            copy.start()
        width = r.vec.shape[1]
        for n in range(2):
            r.red_entity[:, n * 128 : (n + 1) * 128] = r.out_e[n]
            for h in range(heads):
                place = h * 6 * HD
                line = 10 + 2 * n + place // width
                for j in range(6):
                    lanes = slice(n * side + h * HD, n * side + (h + 1) * HD)
                    part = r.out_q[h, n, :, j * HD : (j + 1) * HD]
                    begin = place % width + j * HD
                    line_part = r.vec[line : line + 1, begin : begin + HD]
                    if j < 4:
                        r.query_part[j, :, lanes] = part
                        r.red_query_bias[j : j + 1, lanes] = line_part
                    else:
                        r.keyval_part[j - 4, :, lanes] = part
                    if j == 5:
                        r.value_row[:, lanes] = line_part
        for copy in outs[6:]:
            copy.start()
        r.red_gain[...] = r.across[0:3, 0:share]
        r.red_shift[...] = r.across[3:6, 0:share]
        r.red_value_bias[...] = r.value_row[...].reshape(-1)
        r.red_out_bias[...] = r.across[6:7, 0:share].reshape(-1)
        r.red_down_bias[...] = r.across[7:8, 0:share].reshape(-1)
        for n in range(2):
            r.red_up_bias[n * width : (n + 1) * width] = r.vec[8 + n : 9 + n, :].reshape(-1)

    for i in range(steps):
        adam(i)
        if i == steps // 2:
            lay_out_rest()
    for i in range(steps):
        for copy in moves(i, False):
            copy.wait()
    for copy in outs:
        copy.wait()


SOFT = 256
STEPS = 8
CHUNK, HEAD, ENTS, VEC, WORDS = range(5)
SCHEDULE = (
    ((CHUNK, 0, 0),),
    ((CHUNK, 1, 0),),
    (),
    ((CHUNK, 2, 0),),
    (),
    (),
    (),
    (),
    ((CHUNK, 5, 0),),
    (),
    (),
    ((CHUNK, 4, 0), (CHUNK, 6, 0), (CHUNK, 0, 1),),
    (),
    ((CHUNK, 2, 1),),
    ((CHUNK, 5, 1),),
    (),
    ((CHUNK, 1, 1), (CHUNK, 0, 2),),
    ((CHUNK, 6, 1),),
    (),
    ((CHUNK, 8, 0), (CHUNK, 7, 0),),
    ((CHUNK, 5, 2),),
    ((HEAD, 0, 1),),
    ((CHUNK, 4, 1), (CHUNK, 0, 3),),
    (),
    ((CHUNK, 1, 2),),
    (),
    ((CHUNK, 5, 3), (CHUNK, 3, 0), (HEAD, 1, 1), (CHUNK, 8, 1), (CHUNK, 2, 2), (HEAD, 0, 2), (CHUNK, 4, 2), (CHUNK, 1, 3),),
    ((HEAD, 1, 2),),
    ((CHUNK, 7, 1), (HEAD, 2, 1), (VEC, 0, 1), (CHUNK, 3, 1), (CHUNK, 6, 2), (CHUNK, 8, 2), (WORDS, 0, 0), (CHUNK, 4, 3), (CHUNK, 7, 2), (ENTS, 0, 1), (CHUNK, 2, 3), (HEAD, 2, 2), (CHUNK, 3, 2), (VEC, 0, 2), (ENTS, 0, 2), (CHUNK, 6, 3), (CHUNK, 7, 3), (CHUNK, 8, 3), (HEAD, 1, 3), (VEC, 0, 3), (ENTS, 0, 3), (CHUNK, 3, 3), (HEAD, 0, 3), (HEAD, 2, 3),),
)
ORDERS = (0, 1, 2, 0, 0, 1, 2, 0, 0)
VEC_ORDER = 2
ENTS_ORDER = 0


def fused_local(
    word_states,
    entity_shard,
    entity_row,
    word_segments,
    entity_segments,
    entity_table,
    adam_first,
    adam_second,
    w_entity,
    norm_gain,
    norm_bias,
    w_query,
    b_query,
    w_keyval,
    b_value,
    w_out,
    b_out,
    w_up,
    b_up,
    w_down,
    b_down,
    cot_words,
    cot_entities,
):
    low, full = jnp.bfloat16, jnp.float32
    _, half_words, width = word_states.shape
    half_ents = entity_row.shape[2]
    rows, everyone = half_words + half_ents, 2 * (half_words + half_ents)
    words, ents = 2 * half_words, 2 * half_ents
    table_rows, embed = entity_table.shape
    local_width, hidden = w_query.shape[2], w_up.shape[1]
    owners = lax.axis_size(("dp", "stream"))
    share = width // owners
    capacity = 2 * half_ents // owners
    side = local_width // 2
    heads = side // HD
    chunk = local_width
    chunks = 2 * (hidden // chunk) + 1

    operands = dict(
        hbm_shard=entity_shard.reshape(1, half_ents),
        hbm_row=entity_row.reshape(1, half_ents),
        hbm_word_seg=word_segments,
        hbm_ent_seg=entity_segments,
        hbm_gain=norm_gain,
        hbm_shift=norm_bias,
        hbm_b_query=b_query,
        hbm_b_value=b_value,
        hbm_b_out=b_out,
        hbm_b_up=b_up,
        hbm_b_down=b_down,
        hbm_words=word_states,
        hbm_cot_words=cot_words,
        hbm_cot_ents=cot_entities,
        hbm_query=w_query,
        hbm_keyval=w_keyval,
        hbm_table=entity_table,
        hbm_entity=w_entity,
        hbm_out=w_out,
        hbm_up=w_up,
        hbm_down=w_down,
    )
    results = dict(
        to_out_words=((half_words // 2, width), low),
        to_out_ents=((half_ents // 2, width), low),
        to_grad_words=((half_words // 2, width), full),
        to_out_a=((chunks, share, chunk), full),
        to_out_e=((2, share, 128), full),
        to_out_q=((heads, 2, share, chunk), full),
        to_vec_out=((16, width), full),
        to_across_out=((8, 128), full),
        to_ids_out=((8, owners * capacity), jnp.int32),
        to_slopes_out=((owners * capacity, embed), low),
    )
    mail_rows = max(rows, words // 2 + ents)
    dma = pltpu.SemaphoreType.DMA
    scratch = dict(
        shard=((1, half_ents), jnp.int32),
        row=((1, half_ents), jnp.int32),
        word_seg=(word_segments.shape, jnp.int32),
        ent_seg=(entity_segments.shape, jnp.int32),
        gain=(norm_gain.shape, full),
        shift=(norm_bias.shape, full),
        b_query=(b_query.shape, full),
        b_value=(b_value.shape, full),
        b_out=(b_out.shape, full),
        b_up=(b_up.shape, full),
        b_down=(b_down.shape, full),
        grad_words=((half_words // 2, width), full),
        out_a=((chunks, share, chunk), full),
        out_e=((2, share, 128), full),
        out_q=((heads, 2, share, chunk), full),
        across_out=((8, 128), full),
        ids_out=((8, owners * capacity), jnp.int32),
        slopes_out=((owners * capacity, embed), low),
        w_query=(w_query.shape, low),
        w_keyval=(w_keyval.shape, low),
        table=(entity_table.shape, low),
        w_entity=(w_entity.shape, low),
        w_out=(w_out.shape, low),
        w_up=(w_up.shape, low),
        w_down=(w_down.shape, low),
        cat_words=((width, 4 * side), low),
        cat_ents=((width, 4 * side), low),
        bias_words=((1, 4 * side), full),
        bias_ents=((1, 4 * side), full),
        cotangent=((rows, width), low),
        ask=((owners, capacity, 128), jnp.int32),
        asked=((owners, capacity, 128), jnp.int32),
        outbox=((owners * capacity, half_ents), low),
        select=((ents, owners * 2 * capacity), low),
        found=((owners // 2, 2 * capacity, embed), low),
        answer=((owners, 2 * capacity, embed), low),
        looked=((ents, embed), low),
        ent_lin=((ents, width), full),
        x_ent=((ents, width), full),
        x_all=((everyone, width), low),
        x_own=((rows, width), full),
        words_t=((width, words), low),
        ents_t=((width, ents), low),
        mask=((everyone, everyone), low),
        qkv=((everyone, 4 * side), low),
        key=((heads, everyone, HD), low),
        value=((heads, everyone, HD), low),
        prob=((heads, everyone, everyone), full),
        factor=((heads, everyone, 128), full),
        mass=((heads, words, 128), full),
        heads_far=((rows, side), low),
        heads_near=((rows, side), low),
        heads_in=((rows, side), low),
        heads_all=((rows, 2 * side), low),
        mail_out=((2, mail_rows, width), low),
        mail_in=((2, mail_rows, width), low),
        normed=((rows, width), full),
        scale=((rows, 128), full),
        first=((rows, width), low),
        first_t=((width, rows), low),
        act=((rows, hidden), low),
        slope_up=((rows, hidden), full),
        final=((rows, width), low),
        grad_second=((rows, width), full),
        grad_low=((rows, width), low),
        grad_t=((width, rows), low),
        grad_up=((rows, hidden), low),
        grad_first=((rows, width), full),
        back_far=((rows, side), low),
        back_heads=((everyone, side), low),
        grad_prob=((everyone, everyone), full),
        grad_score=((everyone, everyone), low),
        prob_low=((everyone, everyone), low),
        grad_qkv=((everyone, 4 * side), low),
        input_part=((2, half_words // 2, width), full),
        ents_back=((half_ents, width), low),
        ents_in=((half_ents, width), low),
        words_back=((half_words // 2, width), low),
        words_in=((half_words // 2, width), low),
        slope=((owners, capacity, embed), full),
        slopes=((owners, capacity, embed), full),
        e_sum=((1, share, 128), full),
        e_in=((share, 128), full),
        vec=((5, 16, width), full),
        vec_in=((4, 16, width), full),
        grads=((chunks, 2, 2, 2, 2, share, chunk), low),
        near=((chunks, 2, 2, 2, share, chunk), low),
        next=((chunks, 2, 2, share, chunk), low),
        far=((chunks, 2, share, chunk), low),
        last=((chunks, share, chunk), low),
        e_grads=((1, 2, 2, 2, 2, share, 128), low),
        e_near=((1, 2, 2, 2, share, 128), low),
        e_next=((1, 2, 2, share, 128), low),
        e_far=((1, 2, share, 128), low),
        e_last=((1, share, 128), low),
        q_grads=((heads, 2, 2, 2, 2, share, chunk), low),
        q_near=((heads, 2, 2, 2, share, chunk), low),
        q_next=((heads, 2, 2, share, chunk), low),
        q_far=((heads, 2, share, chunk), low),
        q_away=((heads, share, chunk), low),
        q_in=((heads, share, chunk), low),
    )
    signals = dict(
        load_s=(len(operands),),
        flush_s=(len(results) + chunks + heads,),
        ask_s=(owners - 1,),
        ask_r=(owners - 1,),
        answer_s=(owners - 1,),
        answer_r=(owners - 1,),
        slope_s=(owners - 1,),
        slope_r=(owners - 1,),
        heads_s=(2,),
        heads_r=(2,),
        pair_s=(9,),
        pair_r=(9,),
        strip_s=(3, width // 256),
        strip_r=(3, width // 256),
        swap_s=(2,),
        swap_r=(2,),
        vec_s=(4,),
        vec_r=(4,),
        a_s=(chunks, 4),
        a_r=(chunks, 4),
        e_s=(1, 4),
        e_r=(1, 4),
        q_s=(heads, 4),
        q_r=(heads, 4),
    )
    names = [*operands, *results, *scratch, *signals]
    kernel = functools.partial(layer_kernel, names, ORDERS, ENTS_ORDER, VEC_ORDER, SCHEDULE)
    made = pl.pallas_call(
        kernel,
        name="layer",
        out_shape=[jax.ShapeDtypeStruct(*item) for item in results.values()],
        in_specs=[pl.BlockSpec(memory_space=pl.ANY)] * len(operands),
        out_specs=[pl.BlockSpec(memory_space=pl.ANY)] * len(results),
        scratch_shapes=[pltpu.VMEM(*item) for item in scratch.values()]
        + [dma(shape) for shape in signals.values()],
        compiler_params=pltpu.CompilerParams(
            collective_id=0, has_side_effects=True, vmem_limit_bytes=67_043_328
        ),
    )(*operands.values())
    got = types.SimpleNamespace(**dict(zip(results, made, strict=True)))

    given = dict(
        hbm_first=adam_first,
        hbm_second=adam_second,
        hbm_ids=got.to_ids_out,
        hbm_slopes=got.to_slopes_out,
        hbm_a=got.to_out_a,
        hbm_e=got.to_out_e,
        hbm_q=got.to_out_q,
        hbm_vec=got.to_vec_out,
        hbm_across=got.to_across_out,
        hbm_words=got.to_out_words,
        hbm_ents=got.to_out_ents,
        hbm_grad=got.to_grad_words,
    )
    final = dict(
        words_done=(1, half_words // 2, width),
        ents_done=(1, half_ents // 2, width),
        grad_words_done=(1, half_words // 2, width),
        red_entity=(share, embed),
        red_gain=(3, share),
        red_shift=(3, share),
        red_query=(4, share, local_width),
        red_query_bias=(4, local_width),
        red_keyval=(2, share, local_width),
        red_value_bias=(local_width,),
        red_out=(share, local_width),
        red_out_bias=(share,),
        red_up=(share, hidden),
        red_up_bias=(hidden,),
        red_down=(share, hidden),
        red_down_bias=(share,),
        table_update=adam_first.shape,
        new_first=adam_first.shape,
        new_second=adam_first.shape,
    )
    room = dict(
        value_row=((1, local_width), full),
        ids=(got.to_ids_out.shape, jnp.int32),
        slopes=(got.to_slopes_out.shape, low),
        addends=((owners * capacity, embed + 128), low),
        out_e=(got.to_out_e.shape, full),
        out_q=(got.to_out_q.shape, full),
        vec=(got.to_vec_out.shape, full),
        across=(got.to_across_out.shape, full),
        first=(adam_first.shape, full),
        second=(adam_first.shape, full),
        update=(adam_first.shape, full),
        out_part=((share, local_width), full),
        down_part=((share, hidden), full),
        up_part=((share, hidden), full),
        words_part=(got.to_out_words.shape, low),
        ents_part=(got.to_out_ents.shape, low),
        grad_part=(got.to_grad_words.shape, full),
        query_part=((4, share, local_width), full),
        keyval_part=((2, share, local_width), full),
    )
    flags = dict(small_s=(chunks + 9,), done_s=(8,), in_s=(2, STEPS), out_s=(3, STEPS))
    in_place, in_vmem = (pl.BlockSpec(memory_space=space) for space in (pl.ANY, pltpu.VMEM))
    manual = set(dict(words_done=0, ents_done=0, grad_words_done=0, red_query=0, red_keyval=0))
    manual |= set(dict(red_out=0, red_up=0, red_down=0, table_update=0, new_first=0, new_second=0))
    finished = pl.pallas_call(
        functools.partial(finish_kernel, [*given, *final, *room, *flags]),
        name="finish",
        out_shape=[
            jax.ShapeDtypeStruct(shape, low if n < 2 else full)
            for n, shape in enumerate(final.values())
        ],
        in_specs=[in_place] * len(given),
        out_specs=[in_place if name in manual else in_vmem for name in final],
        scratch_shapes=[pltpu.VMEM(*item) for item in room.values()]
        + [dma(shape) for shape in flags.values()],
        compiler_params=pltpu.CompilerParams(vmem_limit_bytes=67_043_328),
    )(*given.values())
    done = dict(zip(final, finished, strict=True))
    return tuple(
        item.T if name in ("red_entity", "red_out", "red_down") else item
        for name, item in done.items()
    )


def plain_local(
    word_states,
    entity_shard,
    entity_row,
    word_segments,
    entity_segments,
    entity_table,
    adam_first,
    adam_second,
    w_entity,
    norm_gain,
    norm_bias,
    w_query,
    b_query,
    w_keyval,
    b_value,
    w_out,
    b_out,
    w_up,
    b_up,
    w_down,
    b_down,
    cot_words,
    cot_entities,
):
    seq_count, half_words, width = word_states.shape
    half_ents = entity_row.shape[2]
    table_rows, embed_width = entity_table.shape
    local_width = w_query.shape[2]
    local_heads = local_width // HD
    owners = lax.axis_size(("dp", "stream"))
    stream_index = lax.axis_index("stream")
    parts = lax.axis_size("tensor")
    part_index = lax.axis_index("tensor")
    word_part = half_words // parts
    ent_part = half_ents // parts
    ent_count = seq_count * half_ents
    word_count = seq_count * half_words
    local_rows = half_words + half_ents
    share_words = seq_count * word_part
    owner_flat = entity_shard.reshape(ent_count)
    row_flat = entity_row.reshape(ent_count)

    def pick(block, count):
        shaped = block.reshape(seq_count, parts, count // parts, block.shape[-1])
        return lax.dynamic_index_in_dim(shaped, part_index, 1, keepdims=False).reshape(
            seq_count * (count // parts), block.shape[-1]
        )

    def own_share(rows):
        return jnp.concatenate(
            [pick(rows[:word_count], half_words), pick(rows[word_count:], half_ents)], 0
        )

    capacity = 2 * ent_count // owners
    owner_hits = (owner_flat[:, None] == jnp.arange(owners, dtype=jnp.int32)[None, :]).astype(
        jnp.int32
    )
    before = jnp.cumsum(owner_hits, 0) - owner_hits
    ranking = jnp.sum(before * owner_hits, 1)
    slot_index = owner_flat * capacity + ranking
    request = (
        jnp.full((owners * capacity,), -1, jnp.int32)
        .at[slot_index]
        .set(row_flat)
        .reshape(owners, capacity)
    )
    asked_ids = lax.all_to_all(request, ("dp", "stream"), split_axis=0, concat_axis=0, tiled=True)
    present = asked_ids >= 0
    found_rows = jnp.take(entity_table, jnp.clip(asked_ids, 0, table_rows - 1), axis=0)
    found_rows = jnp.where(present[..., None], found_rows, jnp.zeros_like(found_rows))
    found_rows, asked_rows = (found_rows, asked_ids)
    answered = lax.all_to_all(found_rows, ("dp", "stream"), split_axis=0, concat_axis=0, tiled=True)
    looked = answered.reshape(owners * capacity, embed_width)[slot_index]
    ent_lin = matmul(looked, w_entity)
    x_entity, entity_norm_back = jax.vjp(layer_norm, ent_lin, norm_gain[0], norm_bias[0])
    entity_low = x_entity.astype(jnp.bfloat16)
    word_low = word_states.reshape(word_count, width)
    query_words = (
        jnp.einsum("rd,jdc->jrc", word_low, w_query[:2], preferred_element_type=jnp.float32)
        + b_query[:2, None, :]
    ).astype(jnp.bfloat16)
    query_ents = (
        jnp.einsum("rd,jdc->jrc", entity_low, w_query[2:], preferred_element_type=jnp.float32)
        + b_query[2:, None, :]
    ).astype(jnp.bfloat16)
    value_shift = jnp.stack([jnp.zeros_like(b_value), b_value])[:, None, :]
    keyval_words = (
        jnp.einsum("rd,jdc->jrc", word_low, w_keyval, preferred_element_type=jnp.float32)
        + value_shift
    ).astype(jnp.bfloat16)
    keyval_ents = (
        jnp.einsum("rd,jdc->jrc", entity_low, w_keyval, preferred_element_type=jnp.float32)
        + value_shift
    ).astype(jnp.bfloat16)
    far_words, far_ents = from_partner((keyval_words, keyval_ents), "stream", 0)

    def by_heads(block, count):
        return block.reshape(block.shape[0], seq_count, count, local_heads, HD)

    queries = jnp.concatenate(
        [by_heads(query_words, half_words), by_heads(query_ents, half_ents)], 2
    )
    keyval_w = jnp.concatenate(
        [by_heads(keyval_words, half_words), by_heads(far_words, half_words)], 2
    )
    keyval_e = jnp.concatenate([by_heads(keyval_ents, half_ents), by_heads(far_ents, half_ents)], 2)
    own_wseg = lax.dynamic_slice_in_dim(word_segments, stream_index * half_words, half_words, 1)
    far_wseg = lax.dynamic_slice_in_dim(
        word_segments, (1 - stream_index) * half_words, half_words, 1
    )
    own_eseg = lax.dynamic_slice_in_dim(entity_segments, stream_index * half_ents, half_ents, 1)
    far_eseg = lax.dynamic_slice_in_dim(
        entity_segments, (1 - stream_index) * half_ents, half_ents, 1
    )
    query_seg = jnp.concatenate([own_wseg, own_eseg], 1)
    key_wseg = jnp.concatenate([own_wseg, far_wseg], 1)
    key_eseg = jnp.concatenate([own_eseg, far_eseg], 1)
    allow_words = query_seg[:, None, :, None] == key_wseg[:, None, None, :]
    allow_ents = query_seg[:, None, :, None] == key_eseg[:, None, None, :]

    def scores_of():
        raw_words = (
            jnp.einsum(
                "sqhd,skhd->shqk", queries[0], keyval_w[0], preferred_element_type=jnp.float32
            )
            * score_scale
        )
        raw_ents = (
            jnp.einsum(
                "sqhd,skhd->shqk", queries[1], keyval_e[0], preferred_element_type=jnp.float32
            )
            * score_scale
        )
        return (
            jnp.where(allow_words, raw_words, masked_score),
            jnp.where(allow_ents, raw_ents, masked_score),
        )

    score_words, score_ents = scores_of()
    highest = jnp.maximum(
        jnp.max(score_words, -1, keepdims=True), jnp.max(score_ents, -1, keepdims=True)
    )
    totals = jnp.sum(jnp.exp(score_words - highest), -1, keepdims=True) + jnp.sum(
        jnp.exp(score_ents - highest), -1, keepdims=True
    )
    log_total = highest + jnp.log(totals)
    low_words = jnp.exp(score_words - log_total).astype(jnp.bfloat16)
    low_ents = jnp.exp(score_ents - log_total).astype(jnp.bfloat16)
    heads_out = jnp.einsum(
        "shqk,skhd->sqhd", low_words, keyval_w[1], preferred_element_type=jnp.float32
    )
    heads_out = heads_out + jnp.einsum(
        "shqk,skhd->sqhd", low_ents, keyval_e[1], preferred_element_type=jnp.float32
    )
    heads_out = heads_out.astype(jnp.bfloat16).reshape(seq_count, local_rows, local_width)
    heads_dense = jnp.concatenate(
        [
            heads_out[:, :half_words].reshape(word_count, local_width),
            heads_out[:, half_words:].reshape(ent_count, local_width),
        ],
        0,
    )
    resid_in = jnp.concatenate([word_low.astype(jnp.float32), x_entity], 0)
    cotangent = jnp.concatenate(
        [cot_words.reshape(word_count, width), cot_entities.reshape(ent_count, width)], 0
    ).astype(jnp.float32)
    attn_out = tensor_total(matmul(heads_dense, w_out)) + b_out
    first_norm, first_back = jax.vjp(layer_norm, resid_in + attn_out, norm_gain[1], norm_bias[1])
    first_low = first_norm.astype(jnp.bfloat16)
    up_value = matmul(first_low, w_up) + b_up
    active, gelu_back = jax.vjp(gelu_exact, up_value)
    active_low = active.astype(jnp.bfloat16)
    ffn_out = tensor_total(matmul(active_low, w_down)) + b_down
    final_norm, final_back = jax.vjp(layer_norm, first_norm + ffn_out, norm_gain[2], norm_bias[2])
    final_share = own_share(final_norm)
    grad_final, gain_final, shift_final = final_back(cotangent)
    grad_ffn = grad_final.astype(jnp.bfloat16)
    out_words = final_share[:share_words].reshape(seq_count, word_part, width).astype(jnp.bfloat16)
    out_entities = (
        final_share[share_words:].reshape(seq_count, ent_part, width).astype(jnp.bfloat16)
    )
    grad_down = jnp.einsum("rf,rd->fd", active_low, grad_ffn, preferred_element_type=jnp.float32)
    grad_down_bias = jnp.sum(grad_ffn.astype(jnp.float32), 0)
    (grad_pre,) = gelu_back(
        jnp.einsum("rd,fd->rf", grad_ffn, w_down, preferred_element_type=jnp.float32)
    )
    grad_up_low = grad_pre.astype(jnp.bfloat16)
    grad_up = jnp.einsum("rd,rf->df", first_low, grad_up_low, preferred_element_type=jnp.float32)
    grad_up_bias = jnp.sum(grad_up_low.astype(jnp.float32), 0)
    ffn_term = jnp.einsum("rf,df->rd", grad_up_low, w_up, preferred_element_type=jnp.float32)
    grad_first, gain_first, shift_first = first_back(grad_final + tensor_total(ffn_term))
    grad_attn = grad_first.astype(jnp.bfloat16)
    grad_out = jnp.einsum("rc,rd->cd", heads_dense, grad_attn, preferred_element_type=jnp.float32)
    grad_out_bias = jnp.sum(grad_attn.astype(jnp.float32), 0)
    grad_heads = jnp.einsum(
        "rd,cd->rc", grad_attn, w_out, preferred_element_type=jnp.float32
    ).astype(jnp.bfloat16)
    grad_heads = jnp.concatenate(
        [
            grad_heads[:word_count].reshape(seq_count, half_words, local_heads, HD),
            grad_heads[word_count:].reshape(seq_count, half_ents, local_heads, HD),
        ],
        1,
    )
    score_words, score_ents = scores_of()
    prob_words = jnp.exp(score_words - log_total)
    prob_ents = jnp.exp(score_ents - log_total)
    low_words = prob_words.astype(jnp.bfloat16)
    low_ents = prob_ents.astype(jnp.bfloat16)
    dprob_words = jnp.einsum(
        "sqhd,skhd->shqk", grad_heads, keyval_w[1], preferred_element_type=jnp.float32
    )
    dprob_ents = jnp.einsum(
        "sqhd,skhd->shqk", grad_heads, keyval_e[1], preferred_element_type=jnp.float32
    )
    inner_sum = jnp.sum(prob_words * dprob_words, -1, keepdims=True) + jnp.sum(
        prob_ents * dprob_ents, -1, keepdims=True
    )
    dscore_words = (prob_words * (dprob_words - inner_sum)).astype(jnp.bfloat16)
    dscore_ents = (prob_ents * (dprob_ents - inner_sum)).astype(jnp.bfloat16)
    grad_to_words = (
        jnp.einsum("shqk,skhd->sqhd", dscore_words, keyval_w[0], preferred_element_type=jnp.float32)
        * score_scale
    ).astype(jnp.bfloat16)
    grad_to_ents = (
        jnp.einsum("shqk,skhd->sqhd", dscore_ents, keyval_e[0], preferred_element_type=jnp.float32)
        * score_scale
    ).astype(jnp.bfloat16)
    kv_grad_words = jnp.stack(
        [
            jnp.einsum(
                "shqk,sqhd->skhd", dscore_words, queries[0], preferred_element_type=jnp.float32
            )
            * score_scale,
            jnp.einsum(
                "shqk,sqhd->skhd", low_words, grad_heads, preferred_element_type=jnp.float32
            ),
        ]
    )
    kv_grad_ents = jnp.stack(
        [
            jnp.einsum(
                "shqk,sqhd->skhd", dscore_ents, queries[1], preferred_element_type=jnp.float32
            )
            * score_scale,
            jnp.einsum("shqk,sqhd->skhd", low_ents, grad_heads, preferred_element_type=jnp.float32),
        ]
    )
    back_words, back_ents = (
        from_partner(kv_grad_words[:, :, half_words:].astype(jnp.bfloat16), "stream", 0).astype(
            jnp.float32
        ),
        from_partner(kv_grad_ents[:, :, half_ents:].astype(jnp.bfloat16), "stream", 0).astype(
            jnp.float32
        ),
    )
    grad_kv_words = (
        (kv_grad_words[:, :, :half_words] + back_words)
        .reshape(2, word_count, local_width)
        .astype(jnp.bfloat16)
    )
    grad_kv_ents = (
        (kv_grad_ents[:, :, :half_ents] + back_ents)
        .reshape(2, ent_count, local_width)
        .astype(jnp.bfloat16)
    )
    grad_q_words = jnp.stack([grad_to_words[:, :half_words], grad_to_ents[:, :half_words]]).reshape(
        2, word_count, local_width
    )
    grad_q_ents = jnp.stack([grad_to_words[:, half_words:], grad_to_ents[:, half_words:]]).reshape(
        2, ent_count, local_width
    )
    grad_query = jnp.concatenate(
        [
            jnp.einsum("rd,jrc->jdc", word_low, grad_q_words, preferred_element_type=jnp.float32),
            jnp.einsum("rd,jrc->jdc", entity_low, grad_q_ents, preferred_element_type=jnp.float32),
        ],
        0,
    )
    grad_query_bias = jnp.concatenate(
        [jnp.sum(grad_q_words.astype(jnp.float32), 1), jnp.sum(grad_q_ents.astype(jnp.float32), 1)],
        0,
    )
    grad_keyval = jnp.einsum(
        "rd,jrc->jdc", word_low, grad_kv_words, preferred_element_type=jnp.float32
    ) + jnp.einsum("rd,jrc->jdc", entity_low, grad_kv_ents, preferred_element_type=jnp.float32)
    grad_value_bias = jnp.sum(grad_kv_words[1].astype(jnp.float32), 0) + jnp.sum(
        grad_kv_ents[1].astype(jnp.float32), 0
    )
    input_words = jnp.einsum(
        "jrc,jdc->rd", grad_q_words, w_query[:2], preferred_element_type=jnp.float32
    ) + jnp.einsum("jrc,jdc->rd", grad_kv_words, w_keyval, preferred_element_type=jnp.float32)
    input_ents = jnp.einsum(
        "jrc,jdc->rd", grad_q_ents, w_query[2:], preferred_element_type=jnp.float32
    ) + jnp.einsum("jrc,jdc->rd", grad_kv_ents, w_keyval, preferred_element_type=jnp.float32)
    input_term = jnp.concatenate([input_words, input_ents], 0)
    grad_input = grad_first + tensor_total(input_term)
    grad_share = own_share(grad_input)
    grad_lin, gain_entity, shift_entity = entity_norm_back(grad_input[word_count:])
    grad_lin_low = grad_lin.astype(jnp.bfloat16)
    gain_grads = jnp.stack([gain_entity, gain_first, gain_final])
    shift_grads = jnp.stack([shift_entity, shift_first, shift_final])
    grad_words = grad_share[:share_words].reshape(seq_count, word_part, width)
    grad_entity = jnp.einsum("re,rd->ed", looked, grad_lin_low, preferred_element_type=jnp.float32)
    grad_looked = jnp.einsum(
        "rd,ed->re", grad_lin_low, w_entity, preferred_element_type=jnp.float32
    )
    outgoing = (
        jnp.zeros((owners * capacity, embed_width), jnp.float32)
        .at[slot_index]
        .set(grad_looked)
        .reshape(owners, capacity, embed_width)
    )
    incoming = lax.all_to_all(
        outgoing.astype(jnp.bfloat16), ("dp", "stream"), split_axis=0, concat_axis=0, tiled=True
    ).astype(outgoing.dtype)
    target = jnp.where(asked_rows >= 0, asked_rows, table_rows).reshape(-1)
    gradient_sum = (
        jnp.zeros((table_rows, embed_width), jnp.float32)
        .at[target]
        .add(incoming.reshape(-1, embed_width), mode="drop")
    )
    use_count = jnp.zeros((table_rows,), jnp.float32).at[target].add(1.0, mode="drop")
    touched = (use_count > 0.0)[:, None]
    first_next = beta_one * adam_first + (1.0 - beta_one) * gradient_sum
    second_next = beta_two * adam_second + (1.0 - beta_two) * gradient_sum * gradient_sum
    direction = (
        first_next
        / (1.0 - beta_one**adam_steps)
        / (jnp.sqrt(second_next / (1.0 - beta_two**adam_steps)) + adam_eps)
    )
    table_update = jnp.where(touched, direction, jnp.zeros_like(direction))
    new_first = jnp.where(touched, first_next, adam_first)
    new_second = jnp.where(touched, second_next, adam_second)
    (
        red_entity,
        red_gain,
        red_shift,
        red_query,
        red_keyval,
        red_out,
        red_out_bias,
        red_up,
        red_down,
        red_down_bias,
    ) = (
        lax.psum_scatter(grad_entity, ("dp", "stream"), scatter_dimension=1, tiled=True),
        lax.psum_scatter(gain_grads, ("dp", "stream"), scatter_dimension=1, tiled=True),
        lax.psum_scatter(shift_grads, ("dp", "stream"), scatter_dimension=1, tiled=True),
        lax.psum_scatter(grad_query, ("dp", "stream"), scatter_dimension=1, tiled=True),
        lax.psum_scatter(grad_keyval, ("dp", "stream"), scatter_dimension=1, tiled=True),
        lax.psum_scatter(grad_out, ("dp", "stream"), scatter_dimension=1, tiled=True),
        lax.psum_scatter(grad_out_bias, ("dp", "stream"), scatter_dimension=0, tiled=True),
        lax.psum_scatter(grad_up, ("dp", "stream"), scatter_dimension=0, tiled=True),
        lax.psum_scatter(grad_down, ("dp", "stream"), scatter_dimension=1, tiled=True),
        lax.psum_scatter(grad_down_bias, ("dp", "stream"), scatter_dimension=0, tiled=True),
    )
    red_query_bias, red_value_bias, red_up_bias = lax.psum(
        (grad_query_bias, grad_value_bias, grad_up_bias), ("dp", "stream")
    )
    return (
        out_words,
        out_entities,
        grad_words,
        red_entity,
        red_gain,
        red_shift,
        red_query,
        red_query_bias,
        red_keyval,
        red_value_bias,
        red_out,
        red_out_bias,
        red_up,
        red_up_bias,
        red_down,
        red_down_bias,
        table_update,
        new_first,
        new_second,
    )


def solution(mesh):
    placed = (
        P("dp", "stream", None),
        P("stream", "dp", None, None),
        P("stream", "dp", None),
        P("dp", None),
        P("dp", None),
        P(("dp", "stream"), None),
        P(("dp", "stream"), None),
        P(("dp", "stream"), None),
        P(),
        P(),
        P(),
        P(None, None, "tensor"),
        P(None, "tensor"),
        P(None, None, "tensor"),
        P("tensor"),
        P("tensor", None),
        P(),
        P(None, "tensor"),
        P("tensor"),
        P("tensor", None),
        P(),
        P("dp", "stream", None),
        P("dp", "stream", None),
    )
    fits = mesh.shape["stream"] == 2 and mesh.shape["tensor"] == 2 and mesh.shape["dp"] == 8

    def local(*blocks):
        width, owners = blocks[0].shape[2], mesh.shape["dp"] * mesh.shape["stream"]
        if fits and width % (16 * owners) == 0 and blocks[0].shape[0] == 1:
            return fused_local(*blocks)
        return plain_local(*blocks)

    return jax.shard_map(
        local,
        mesh=mesh,
        in_specs=placed,
        out_specs=(
            P("dp", ("stream", "tensor"), None),
            P("dp", ("stream", "tensor"), None),
            P("dp", ("stream", "tensor"), None),
            P(None, ("dp", "stream")),
            P(None, ("dp", "stream")),
            P(None, ("dp", "stream")),
            P(None, ("dp", "stream"), "tensor"),
            P(None, "tensor"),
            P(None, ("dp", "stream"), "tensor"),
            P("tensor"),
            P("tensor", ("dp", "stream")),
            P(("dp", "stream")),
            P(("dp", "stream"), "tensor"),
            P("tensor"),
            P("tensor", ("dp", "stream")),
            P(("dp", "stream")),
            P(("dp", "stream"), None),
            P(("dp", "stream"), None),
            P(("dp", "stream"), None),
        ),
        check_vma=False,
    )
```

```python
import functools
import math
import types

import jax
import jax.numpy as jnp
from jax import lax
from jax.experimental import pallas as pl
from jax.experimental.pallas import tpu as pltpu
from jax.sharding import PartitionSpec as P

HD = 64
MESH_ID = pl.DeviceIdType.MESH


norm_eps = 1e-05
score_scale = 0.125
masked_score = -1e30
beta_one = 0.9
beta_two = 0.99
adam_steps = 10
adam_eps = 1e-08


def from_partner(block, axis, apart):
    count = lax.axis_size(axis)
    route = []
    for low in range(count):
        high = low | 1 << apart
        if high != low and high < count:
            route += [(low, high), (high, low)]
    return lax.ppermute(block, axis, route)


def layer_norm(values_in, gain_row, shift_row):
    center = values_in - jnp.mean(values_in, -1, keepdims=True)
    spread = jnp.mean(center * center, -1, keepdims=True)
    return center * lax.rsqrt(spread + norm_eps) * gain_row + shift_row


def gelu_exact(values_in):
    return jax.nn.gelu(values_in, approximate=False)


def matmul(matrix_a, matrix_b):
    return jnp.dot(matrix_a, matrix_b, preferred_element_type=jnp.float32)


def tensor_total(values_in):
    return lax.psum(values_in, "tensor")


def send(source, target, send_sem, recv_sem, peer):
    return pltpu.make_async_remote_copy(
        src_ref=source,
        dst_ref=target,
        send_sem=send_sem,
        recv_sem=recv_sem,
        device_id=peer,
        device_id_type=MESH_ID,
    )


def row_sum(block):
    return jnp.sum(block, 0, keepdims=True)


def lane_mean(block):
    return jnp.mean(block, -1, keepdims=True)


def dot_nn(left, right):
    return jnp.dot(left, right, preferred_element_type=jnp.float32)


def dot_nt(left, right):
    return lax.dot_general(
        left, right, (((1,), (1,)), ((), ())), preferred_element_type=jnp.float32
    )


def dot_tn(left, right):
    return lax.dot_general(
        left, right, (((0,), (0,)), ((), ())), preferred_element_type=jnp.float32
    )


def normalize(rows):
    center = rows - lane_mean(rows)
    scale = lax.rsqrt(lane_mean(center * center) + norm_eps)
    return center * scale, scale


def normalize_back(grad, normed, scale, gain):
    inner = grad * gain
    return scale * (inner - lane_mean(inner) - normed * lane_mean(inner * normed))


def aligned(index, step):
    return pl.ds(pl.multiple_of(index * step, step), step)


def layer_kernel(names, orders, ents_order, vec_order, schedule, *refs):
    r = types.SimpleNamespace(**dict(zip(names, refs, strict=True)))
    low, full = jnp.bfloat16, jnp.float32
    dp, x, t = lax.axis_index("dp"), lax.axis_index("stream"), lax.axis_index("tensor")
    y, z = lax.rem(dp, 2), dp // 2
    owners = lax.axis_size("dp") * 2
    _, half_words, width = r.hbm_words.shape
    half_ents = r.shard.shape[1]
    rows, words = half_words + half_ents, 2 * half_words
    everyone = 2 * rows
    capacity = r.ask.shape[1]
    slots = owners * capacity
    heads = r.prob.shape[0]
    share = width // owners
    side = heads * HD
    hidden = r.w_up.shape[1]
    block = half_ents
    blocks = rows // block
    word_blocks = half_words // block
    wide = 256

    core, x_peer, y_peer = {"tensor": 1 - t}, {"stream": 1 - x}, {"dp": z * 2 + 1 - y}
    z_low, z_high = lax.rem(z, 2), z // 2
    near_peer = {"dp": (z + 1 - 2 * z_low) * 2 + y}
    far_peer = {"dp": (z + 2 - 4 * z_high) * 2 + y}
    mine_on = (z_high, z_low, y, x)
    peer_on = (far_peer, near_peer, y_peer, x_peer)
    flat = dp * 2 + x
    others = []
    for k in range(1, owners):
        other = lax.rem(flat + k, owners)
        others.append((other, {"dp": other // 2, "stream": lax.rem(other, 2)}))

    loads = {}
    barrier = pltpu.get_barrier_semaphore()
    for peer in [core] + [peer for _, peer in others]:
        pl.semaphore_signal(barrier, inc=1, device_id=peer, device_id_type=MESH_ID)

    def load(source, target):
        loads[id(target)] = pltpu.make_async_copy(source, target, r.load_s.at[len(loads)])
        loads[id(target)].start()

    def loaded(target):
        loads.pop(id(target)).wait()

    load(r.hbm_shard, r.shard)
    load(r.hbm_row, r.row)
    my_words = r.x_all.at[aligned(x, half_words), :]
    load(r.hbm_words.at[0], my_words)
    load(r.hbm_query, r.w_query)
    load(r.hbm_keyval, r.w_keyval)
    smalls = [
        (r.hbm_b_query, r.b_query), (r.hbm_b_value, r.b_value), (r.hbm_word_seg, r.word_seg),
        (r.hbm_ent_seg, r.ent_seg), (r.hbm_gain, r.gain), (r.hbm_shift, r.shift),
        (r.hbm_b_out, r.b_out), (r.hbm_b_up, r.b_up), (r.hbm_b_down, r.b_down),
    ]
    for source, target in smalls:
        load(source, target)
    load(r.hbm_table, r.table)
    load(r.hbm_entity, r.w_entity)
    cot_words, cot_ents = r.cotangent.at[0:half_words, :], r.cotangent.at[half_words:rows, :]
    load(r.hbm_cot_words.at[0], cot_words)
    load(r.hbm_cot_ents.at[0], cot_ents)
    load(r.hbm_out, r.w_out)
    load(r.hbm_up, r.w_up)
    load(r.hbm_down, r.w_down)

    flushes = []

    def flush(source, target):
        flushes.append(pltpu.make_async_copy(source, target, r.flush_s.at[len(flushes)]))
        flushes[-1].start()

    loaded(r.shard)
    loaded(r.row)
    shard_row = r.shard[...]
    shard_all = jnp.broadcast_to(shard_row.astype(full), (half_ents, half_ents)).T
    shard_all = shard_all.astype(jnp.int32)
    shard_col = shard_all[:, 0:1]
    below = lax.broadcasted_iota(jnp.int32, (half_ents, half_ents), 0)
    beside = lax.broadcasted_iota(jnp.int32, (half_ents, half_ents), 1)
    same = shard_all == shard_row
    rank_row = row_sum(jnp.where(same & (below < beside), 1.0, 0.0)).astype(jnp.int32)
    rank_col = jnp.sum(jnp.where(same & (beside < below), 1.0, 0.0), 1, keepdims=True)
    rank_col = rank_col.astype(jnp.int32)
    slot_row = shard_row * capacity + rank_row
    in_slot = lax.broadcasted_iota(jnp.int32, (slots, half_ents), 0) == slot_row
    wanted = jnp.sum(
        jnp.where(in_slot, (r.row[...] + 1).astype(full), 0.0), 1, keepdims=True
    )
    wanted = wanted.astype(jnp.int32) - 1
    r.ask[...] = jnp.broadcast_to(wanted, (slots, 128)).reshape(owners, capacity, 128)
    r.outbox[...] = jnp.where(in_slot, 1.0, 0.0).astype(low)
    answer_col = shard_col * (2 * capacity) + x * capacity + rank_col
    answer_lane = lax.broadcasted_iota(jnp.int32, (half_ents, 2 * slots), 1)
    r.select[aligned(x, half_ents), :] = jnp.where(answer_lane == answer_col, 1.0, 0.0).astype(low)
    r.asked[flat] = r.ask[flat]
    r.vec[0] = jnp.zeros(r.vec.shape[1:], full)

    loaded(r.w_query)
    loaded(r.w_keyval)
    for _, target in smalls:
        loaded(target)

    def gather_columns(which):
        for h in range(heads):
            own = slice(which * side + h * HD, which * side + (h + 1) * HD)
            for place, words_part, ents_part in (
                (0, r.w_query[0, :, own], r.w_query[2, :, own]),
                (1, r.w_query[1, :, own], r.w_query[3, :, own]),
                (2, r.w_keyval[0, :, own], None),
                (3, r.w_keyval[1, :, own], None),
            ):
                lanes = slice((4 * h + place) * HD, (4 * h + place + 1) * HD)
                r.cat_words[:, lanes] = words_part
                r.cat_ents[:, lanes] = words_part if ents_part is None else ents_part
            zero = jnp.zeros((1, HD), full)
            value = r.b_value[...].reshape(1, -1)[:, own]
            query = r.b_query[:, own]
            lanes = slice(4 * h * HD, 4 * (h + 1) * HD)
            r.bias_words[:, lanes] = jnp.concatenate([query[0:1], query[1:2], zero, value], 1)
            r.bias_ents[:, lanes] = jnp.concatenate([query[2:3], query[3:4], zero, value], 1)

    for which in range(2):

        @pl.when(x == which)
        def _(which=which):
            gather_columns(which)

    loaded(my_words)
    r.x_own[0:half_words, :] = my_words[...].astype(full)
    pl.semaphore_wait(barrier, owners)

    def ask_copy(k):
        other, peer = others[k]
        return send(r.ask.at[other], r.asked.at[flat], r.ask_s.at[k], r.ask_r.at[k], peer)

    def answer_copy(k):
        other, peer = others[k]
        return send(
            r.found.at[other // 2], r.answer.at[flat], r.answer_s.at[k], r.answer_r.at[k], peer
        )

    def slope_copy(k):
        other, peer = others[k]
        return send(r.slope.at[other], r.slopes.at[flat], r.slope_s.at[k], r.slope_r.at[k], peer)

    for k in range(owners - 1):
        ask_copy(k).start()
    my_select = r.select.at[aligned(x, half_ents), :]
    select_copy = send(my_select, my_select, r.pair_s.at[0], r.pair_r.at[0], x_peer)
    select_copy.start()
    half = half_words // 2
    my_half = r.x_all.at[aligned(2 * x + t, half), :]
    words_copy = send(my_half, my_half, r.pair_s.at[1], r.pair_r.at[1], x_peer)
    words_copy.start()

    is_query = lax.broadcasted_iota(jnp.int32, (1, 4 * HD), 1) < 2 * HD
    scaling = jnp.where(is_query, score_scale, 1.0)

    def project(start, count, weight, bias):
        def body(h, carry):
            lanes = aligned(h, 4 * HD)
            total = dot_nn(r.x_all[pl.ds(start, count), :], weight[:, lanes]) + bias[:, lanes]
            r.qkv[pl.ds(start, count), lanes] = (total * scaling).astype(low)
            return carry

        lax.fori_loop(0, heads, body, 0, unroll=True)

    project(pl.multiple_of(x * half_words, half_words), half_words, r.cat_words, r.bias_words)

    segments = jnp.concatenate([r.word_seg[...], r.ent_seg[...]], 1)
    for i in range(everyone // 128):
        own_seg = jnp.broadcast_to(segments[:, i * 128 : (i + 1) * 128].astype(full), (128, 128)).T
        equal = own_seg[:, 0:1].astype(jnp.int32) == segments
        r.mask[i * 128 : (i + 1) * 128, :] = jnp.where(equal, 0.0, masked_score).astype(low)

    for k in range(owners - 1):
        ask_copy(k).wait()
    ids = r.asked[...].reshape(slots, 128)
    lane = lax.broadcasted_iota(jnp.int32, (slots, 128), 1)
    loaded(r.table)
    piece = 4 * 128

    def pick_body(j, found):
        ones = [jnp.where(ids == lane + (j * piece + n * 128), 1.0, 0.0) for n in range(4)]
        return found + dot_nn(jnp.concatenate(ones, 1).astype(low), r.table[aligned(j, piece), :])

    found = jnp.zeros((slots, r.table.shape[1]), full)
    found = lax.fori_loop(0, r.table.shape[0] // piece, pick_body, found, unroll=True).astype(low)
    r.found[...] = found.reshape(r.found.shape)
    r.answer[flat] = r.found[dp]
    for k in range(owners - 1):
        answer_copy(k).start()

    words_copy.wait()
    far_half = r.x_all.at[aligned(2 * (1 - x) + t, half), :]
    relay = send(far_half, far_half, r.pair_s.at[8], r.pair_r.at[8], core)
    relay.start()
    relay.wait()
    project(pl.multiple_of((1 - x) * half_words, half_words), half_words, r.cat_words, r.bias_words)

    def take_heads(here):
        for h in range(heads):
            r.key[h, here, :] = r.qkv[here, h * 4 * HD + 2 * HD : h * 4 * HD + 3 * HD]
            r.value[h, here, :] = r.qkv[here, h * 4 * HD + 3 * HD : h * 4 * HD + 4 * HD]

    of_words, of_ents = slice(0, words), slice(words, everyone)
    take_heads(of_words)
    for h in range(heads):
        query = r.qkv[of_words, h * 4 * HD : h * 4 * HD + HD]
        r.prob[h, of_words, of_words] = dot_nt(query, r.key[h, of_words, :])

    def soften_words(which):
        def body(i, carry):
            here = pl.ds(pl.multiple_of(which * half_words + i * SOFT, SOFT), SOFT)
            bias = r.mask[here, of_words].astype(full)
            for h in range(heads):
                score = r.prob[h, here, of_words] + bias
                peak = jnp.max(score, 1, keepdims=True)
                power = jnp.exp(score - peak)
                r.prob[h, here, of_words] = power
                r.factor[h, here, :] = jnp.broadcast_to(peak, (SOFT, 128))
                mass = jnp.broadcast_to(jnp.sum(power, 1, keepdims=True), (SOFT, 128))
                r.mass[h, here, :] = mass
            return carry

        lax.fori_loop(0, half_words // SOFT, body, 0)

    soften_words(0)
    soften_words(1)
    for h in range(heads):
        weights = r.prob[h, of_words, of_words].astype(low)
        r.grad_prob[of_words, h * 128 : h * 128 + HD] = dot_nn(weights, r.value[h, of_words, :])
        r.factor[h, of_ents, :] = jnp.ones((2 * half_ents, 128), full)

    select_copy.wait()
    for k in range(owners - 1):
        answer_copy(k).wait()
    looked = dot_nn(r.select[...], r.answer[...].reshape(2 * slots, r.table.shape[1])).astype(low)
    r.looked[...] = looked
    loaded(r.w_entity)
    ent_lin = dot_nn(looked, r.w_entity[...])
    normed, _ = normalize(ent_lin)
    x_entity = normed * r.gain[0:1, :] + r.shift[0:1, :]
    r.ent_lin[...] = ent_lin
    r.x_ent[...] = x_entity
    r.x_all[words:everyone, :] = x_entity.astype(low)
    r.x_own[half_words:rows, :] = r.x_ent[aligned(x, half_ents), :]
    project(words, 2 * half_ents, r.cat_ents, r.bias_ents)
    take_heads(of_ents)

    def both_kinds(which):
        near_words = pl.ds(pl.multiple_of(which * half_words, half_words), half_words)
        near_ents = pl.ds(pl.multiple_of(words + which * half_ents, half_ents), half_ents)
        return (near_words, slice(0, half_words)), (near_ents, slice(half_words, rows))

    def soften_ents(here):
        bias = r.mask[here, :].astype(full)
        for h in range(heads):
            score = r.prob[h, here, :] + bias
            power = jnp.exp(score - jnp.max(score, 1, keepdims=True))
            r.prob[h, here, :] = power * (1.0 / jnp.sum(power, 1, keepdims=True))

    def complete_words(here):
        bias = r.mask[here, of_ents].astype(full)
        for h in range(heads):
            score = r.prob[h, here, of_ents] + bias
            peak = r.factor[h, here, :]
            best = jnp.broadcast_to(jnp.max(score, 1, keepdims=True), (half_words, 128))
            top = jnp.maximum(peak, best)
            power, shrink = jnp.exp(score - top), jnp.exp(peak - top)
            added = jnp.broadcast_to(jnp.sum(power, 1, keepdims=True), (half_words, 128))
            share_of = 1.0 / (r.mass[h, here, :] * shrink + added)
            r.prob[h, here, of_ents] = power * share_of
            r.factor[h, here, :] = shrink * share_of

    def attend_words(which, target):
        (here, there), _ = both_kinds(which)
        for h in range(heads):
            query = r.qkv[here, h * 4 * HD + HD : h * 4 * HD + 2 * HD]
            r.prob[h, here, of_ents] = dot_nt(query, r.key[h, of_ents, :])
        complete_words(here)
        for h in range(heads):
            out = r.grad_prob[here, h * 128 : h * 128 + HD] * r.factor[h, here, 0:HD]
            out = out + dot_nn(r.prob[h, here, of_ents].astype(low), r.value[h, of_ents, :])
            target[there, h * HD : (h + 1) * HD] = out.astype(low)

    def attend_ents(which, target):
        _, (here, there) = both_kinds(which)
        for h in range(heads):
            query = r.qkv[here, h * 4 * HD : h * 4 * HD + 2 * HD]
            r.prob[h, here, of_words] = dot_nt(query[:, :HD], r.key[h, of_words, :])
            r.prob[h, here, of_ents] = dot_nt(query[:, HD:], r.key[h, of_ents, :])
        soften_ents(here)
        for h in range(heads):
            out = dot_nn(r.prob[h, here, :].astype(low), r.value[h])
            target[there, h * HD : (h + 1) * HD] = out.astype(low)

    def heads_part(n, part):
        return send(
            r.heads_far.at[part, :], r.heads_in.at[part, :], r.heads_s.at[n], r.heads_r.at[n], x_peer
        )

    attend_words(1 - x, r.heads_far)
    heads_copies = [heads_part(0, slice(0, half_words))]
    heads_copies[0].start()
    attend_ents(1 - x, r.heads_far)
    heads_copies.append(heads_part(1, slice(half_words, rows)))
    heads_copies[1].start()
    attend_words(x, r.heads_near)
    attend_ents(x, r.heads_near)
    r.words_t[...] = r.x_all[of_words, :].T
    r.ents_t[...] = r.x_all[of_ents, :].T
    for copy in heads_copies:
        copy.wait()

    @pl.when(x == 0)
    def _():
        r.heads_all[:, 0:side] = r.heads_near[...]
        r.heads_all[:, side:] = r.heads_in[...]

    @pl.when(x == 1)
    def _():
        r.heads_all[:, 0:side] = r.heads_in[...]
        r.heads_all[:, side:] = r.heads_near[...]

    def strip(which, turn, j):
        part = (which, slice(0, rows), aligned(j, wide))
        return send(
            r.mail_out.at[part], r.mail_in.at[part], r.strip_s.at[turn, j], r.strip_r.at[turn, j], core
        )

    def arrived(which, here):
        return r.mail_out[which, here, :].astype(full) + r.mail_in[which, here, :].astype(full)

    def wait_strips(which, turn):
        for j in range(width // wide):
            strip(which, turn, j).wait()

    def swap(which, turn, first, count):
        part = pl.ds(first, count)
        return send(
            r.mail_out.at[which, part], r.mail_in.at[which, part], r.swap_s.at[turn],
            r.swap_r.at[turn], core,
        )

    def columns(count, fill):
        def body(j, carry):
            fill(aligned(j, wide), j)
            return carry

        lax.fori_loop(0, count // wide, body, 0, unroll=True)

    def fill_attn(lanes, j):
        r.mail_out[0, 0:rows, lanes] = dot_nn(r.heads_all[...], r.w_out[:, lanes]).astype(low)
        strip(0, 0, j).start()

    loaded(r.w_out)
    columns(width, fill_attn)
    wait_strips(0, 0)

    tall = rows // 1

    def over_rows(body):
        def step(i, carry):
            body(aligned(i, tall))
            return carry

        lax.fori_loop(0, rows // tall, step, 0)

    def first_norm(here):
        attn = arrived(0, here) + r.b_out[...].reshape(1, -1)
        normed, scale = normalize(r.x_own[here, :] + attn)
        r.normed[here, :] = normed
        r.scale[here, :] = jnp.broadcast_to(scale, (tall, 128))
        r.first[here, :] = (normed * r.gain[1:2, :] + r.shift[1:2, :]).astype(low)

    over_rows(first_norm)

    def fill_up(lanes, _):
        up = dot_nn(r.first[...], r.w_up[:, lanes]) + r.b_up[lanes].reshape(1, -1)
        chance = 0.5 + 0.5 * lax.erf(up * (0.5**0.5))
        r.act[:, lanes] = (up * chance).astype(low)
        r.up[:, lanes] = up
        r.chance[:, lanes] = chance

    loaded(r.w_up)
    columns(hidden, fill_up)

    def fill_down(lanes, j):
        r.mail_out[1, 0:rows, lanes] = dot_nn(r.act[...], r.w_down[:, lanes]).astype(low)
        strip(1, 1, j).start()

    loaded(r.w_down)
    columns(width, fill_down)
    wait_strips(1, 1)

    vec = r.vec.at[0]

    def second_norm(here):
        ffn = arrived(1, here) + r.b_down[...].reshape(1, -1)
        entering = r.normed[here, :] * r.gain[1:2, :] + r.shift[1:2, :]
        normed, scale = normalize(entering + ffn)
        r.final[here, :] = (normed * r.gain[2:3, :] + r.shift[2:3, :]).astype(low)
        grad = r.cotangent[here, :].astype(full)
        vec[2:3, :] += row_sum(grad * normed)
        vec[5:6, :] += row_sum(grad)
        back = normalize_back(grad, normed, scale, r.gain[2:3, :])
        r.grad_second[here, :] = back
        r.grad_low[here, :] = back.astype(low)
        vec[7:8, :] += row_sum(back.astype(low).astype(full))

    loaded(cot_words)
    loaded(cot_ents)
    over_rows(second_norm)

    def halved(ref, place, index):
        return ref.at[(slice(None),) * place + (index,)]

    def stage(kit, c, order, n):
        left = [axis for axis in range(4) if axis not in order[:n]]
        axis, place = order[n], left.index(order[n])
        held = kit.held[n].at[c]
        copy = send(
            halved(held, place, 1 - mine_on[axis]), kit.held[n + 1].at[c],
            kit.sent.at[c, n], kit.got.at[c, n], peer_on[axis],
        )
        return copy, halved(held, place, mine_on[axis])

    def advance(kit, c, order, n):
        copy, own = stage(kit, c, order, n - 1)
        copy.wait()
        total = kit.held[n].at[c]

        def body(i, carry):
            total[i] = own[i] + total[i]
            return carry

        lax.fori_loop(0, 2, body, 0)
        stage(kit, c, order, n)[0].start()

    def finish(kit, c, order):
        copy, own = stage(kit, c, order, 3)
        copy.wait()
        kit.out[c] = own[...].astype(full) + kit.held[4][c].astype(full)

    kit_a = types.SimpleNamespace(
        held=(r.grads, r.near, r.next, r.far, r.last), out=r.out_a, sent=r.a_s, got=r.a_r
    )
    kit_e = types.SimpleNamespace(
        held=(r.e_grads, r.e_near, r.e_next, r.e_far, r.e_last), out=r.e_sum, sent=r.e_s, got=r.e_r
    )
    along = dict(zip(range(3), ((3, 2, 1, 0), (2, 3, 1, 0), (1, 0, 3, 2))))

    kit_q = types.SimpleNamespace(held=(r.q_grads, r.q_near, r.q_next, r.q_far), sent=r.q_s, got=r.q_r)
    head_order = (2, 1, 0, 3)

    def head_start(h):
        stage(kit_q, h, head_order, 0)[0].start()

    def head_meet(h):
        return send(r.q_away.at[h], r.q_in.at[h], r.q_s.at[h, 3], r.q_r.at[h, 3], x_peer)

    def head_advance(h, n):
        if n < 3:
            advance(kit_q, h, head_order, n)
            return
        copy, own = stage(kit_q, h, head_order, 2)
        copy.wait()
        away = own[1 - x].astype(full) + r.q_far[h, 1 - x].astype(full)
        r.q_away[h] = away.astype(low)
        head_meet(h).start()
        r.out_q[h, x] = own[x].astype(full) + r.q_far[h, x].astype(full)

    def head_finish(h):
        head_meet(h).wait()
        r.out_q[h, 1 - x] = r.q_in[h].astype(full)

    def vec_copy(n):
        peer = peer_on[along[vec_order][n]]
        return send(r.vec.at[n], r.vec_in.at[n], r.vec_s.at[n], r.vec_r.at[n], peer)

    def vec_advance(n):
        vec_copy(n - 1).wait()
        r.vec[n] = r.vec[n - 1] + r.vec_in[n - 1]
        if n < 4:
            vec_copy(n).start()

    chunk = r.grads.shape[-1]

    def make_grad(c, left_t, right, lanes):
        part = dot_nn(left_t[...], right[:, lanes]).astype(low)
        r.grads[c] = part.reshape(2, 2, 2, 2, share, chunk)

    plan = iter(schedule)

    def tick():
        for what, c, n in next(plan):
            if what == CHUNK and n == 0:
                stage(kit_a, c, along[orders[c]], 0)[0].start()
            elif what == CHUNK:
                advance(kit_a, c, along[orders[c]], n)
            elif what == HEAD:
                head_advance(c, n)
            elif what == ENTS:
                advance(kit_e, c, along[ents_order], n)
            elif what == WORDS:
                words_back_copy.start()
            else:
                vec_advance(n)

    downs = hidden // chunk
    r.grad_t[...] = r.grad_low[...].T
    for c in range(downs):
        make_grad(c, r.grad_t, r.act, slice(c * chunk, (c + 1) * chunk))
        tick()

    def fill_dup(lanes, j):
        grad_act = dot_nt(r.grad_low[...], r.w_down[lanes, :])
        up = r.up[:, lanes]
        slope = r.chance[:, lanes] + up * (jnp.exp(-0.5 * up * up) * (0.5 / math.pi) ** 0.5)
        grad_up = (grad_act * slope).astype(low)
        r.grad_up[:, lanes] = grad_up
        vec[pl.ds(8 + j // (width // wide), 1), aligned(lax.rem(j, width // wide), wide)] = row_sum(
            grad_up.astype(full)
        )

    columns(hidden, fill_dup)
    tick()

    def fill_back(lanes, j):
        r.mail_out[0, 0:rows, lanes] = dot_nt(r.grad_up[...], r.w_up[lanes, :]).astype(low)
        strip(0, 2, j).start()

    columns(width, fill_back)
    tick()
    r.first_t[...] = r.first[...].T
    flush(r.final.at[aligned(t, half_words // 2), :], r.to_out_words)
    ents_share = pl.multiple_of(half_words + t * (half_ents // 2), half_ents // 2)
    flush(r.final.at[pl.ds(ents_share, half_ents // 2), :], r.to_out_ents)
    for c in range(downs):
        make_grad(downs + c, r.first_t, r.grad_up, slice(c * chunk, (c + 1) * chunk))
        tick()
    wait_strips(0, 2)

    def first_back(here):
        grad = r.grad_second[here, :] + arrived(0, here)
        normed = r.normed[here, :]
        vec[1:2, :] += row_sum(grad * normed)
        vec[4:5, :] += row_sum(grad)
        back = normalize_back(grad, normed, r.scale[here, 0:1], r.gain[1:2, :])
        r.grad_first[here, :] = back
        r.grad_low[here, :] = back.astype(low)
        vec[6:7, :] += row_sum(back.astype(low).astype(full))

    over_rows(first_back)
    tick()
    near_rows = aligned(x, side)
    far_rows = aligned(1 - x, side)
    r.back_far[...] = dot_nt(r.grad_low[...], r.w_out[far_rows, :]).astype(low)
    mine = [(aligned(x, half_words), 0, half_words)]
    mine.append((pl.ds(pl.multiple_of(words + x * half_ents, half_ents), half_ents), half_words, half_ents))
    back_copies = [
        send(
            r.back_far.at[pl.ds(first, count), :], r.back_heads.at[place, :],
            r.pair_s.at[3 + n], r.pair_r.at[3 + n], x_peer,
        )
        for n, (place, first, count) in enumerate(mine)
    ]
    for copy in back_copies:
        copy.start()
    near = dot_nt(r.grad_low[...], r.w_out[near_rows, :]).astype(low)
    for place, first, count in mine:
        r.back_heads[place, :] = near[first : first + count, :]
    r.grad_t[...] = r.grad_low[...].T
    outs = 2 * downs
    make_grad(outs, r.grad_t, r.heads_all, slice(0, chunk))
    tick()


    pair = 2 * HD
    for h in range(heads):
        base = h * 4 * HD

        def score_back(start, size):
            def body(i, carry):
                here = pl.ds(pl.multiple_of(start + i * size, size), size)
                factor = jnp.concatenate([r.factor[h, here, :]] * (words // 128), 1)
                scaled = r.prob[h, here, of_words] * factor
                prob = jnp.concatenate([scaled, r.prob[h, here, of_ents]], 1)
                grad_prob = r.grad_prob[here, :]
                inner = jnp.sum(prob * grad_prob, 1, keepdims=True)
                r.grad_score[here, :] = (prob * (grad_prob - inner)).astype(low)
                r.prob_low[here, :] = prob.astype(low)
                return carry

            return body

        for which in (x, 1 - x):
            if which is not x:
                tick()
            if h == 0 and which is not x:
                for copy in back_copies:
                    copy.wait()
            for here, _ in both_kinds(which):
                r.grad_prob[here, :] = dot_nt(r.back_heads[here, h * HD : (h + 1) * HD], r.value[h])
            lax.fori_loop(0, half_words // SOFT, score_back(which * half_words, SOFT), 0)
            score_back(words + which * half_ents, half_ents)(0, 0)
        queries = jnp.concatenate(
            [
                dot_nn(r.grad_score[:, :words], r.key[h, 0:words, :]),
                dot_nn(r.grad_score[:, words:], r.key[h, words:everyone, :]),
            ],
            1,
        )
        r.grad_qkv[:, base : base + pair] = (queries * score_scale).astype(low)
        tick()
        query_t = r.qkv[:, base : base + pair].T
        keys_t = dot_nn(query_t, r.grad_score[...])
        keys_t = jnp.concatenate([keys_t[:HD, :words], keys_t[HD:, words:]], 1)
        values_t = dot_nn(r.back_heads[:, h * HD : (h + 1) * HD].T, r.prob_low[...])
        r.grad_qkv[:, base + pair : base + 2 * pair] = (
            jnp.concatenate([keys_t, values_t], 0).T.astype(low)
        )

        tick()
        keyval = slice(base + pair, base + 2 * pair)
        query = slice(base, base + pair)
        by_words = dot_nn(r.words_t[...], r.grad_qkv[0:words, query])
        by_ents = dot_nn(r.ents_t[...], r.grad_qkv[words:everyone, query])
        by_keyval = dot_nn(r.words_t[...], r.grad_qkv[0:words, keyval])
        by_keyval = by_keyval + dot_nn(r.ents_t[...], r.grad_qkv[words:everyone, keyval])
        for n, part in enumerate([by_words, by_ents, by_keyval]):
            r.q_grads[h, :, :, :, :, :, n * pair : (n + 1) * pair] = part.astype(low).reshape(
                2, 2, 2, 2, share, pair
            )
        head_start(h)
        sums = jnp.concatenate(
            [
                row_sum(r.grad_qkv[0:words, base : base + pair].astype(full)),
                row_sum(r.grad_qkv[words:everyone, base : base + pair].astype(full)),
                row_sum(r.grad_qkv[:, base + pair : base + 2 * pair].astype(full)),
            ],
            1,
        )
        place = h * 3 * pair
        vec[pl.ds(10 + 2 * x + place // width, 1), place % width : place % width + 3 * pair] = sums
        tick()

    quarter = half_words // 2

    def input_grad(place, weight):
        return dot_nt(r.grad_qkv[place, :], weight[...])

    ents_part = input_grad(slice(words, everyone), r.cat_ents)
    r.mail_out[1, words // 2 :, :] = ents_part.astype(low)
    ents_swap = swap(1, 0, words // 2, 2 * half_ents)
    ents_swap.start()
    tick()
    for n in range(2):
        r.mail_out[1, n * quarter : (n + 1) * quarter, :] = input_grad(
            aligned(2 * n + 1 - t, quarter), r.cat_words
        ).astype(low)
    words_swap = swap(1, 1, 0, words // 2)
    words_swap.start()
    for n in range(2):
        r.input_part[n] = input_grad(aligned(2 * n + t, quarter), r.cat_words)
    tick()
    ents_swap.wait()
    ents_place = pl.multiple_of(words // 2 + (1 - x) * half_ents, half_ents)
    ents_far = pl.ds(ents_place, half_ents)
    ents_near = pl.ds(pl.multiple_of(words // 2 + x * half_ents, half_ents), half_ents)
    r.ents_back[...] = arrived(1, ents_far).astype(low)
    ents_copy = send(r.ents_back, r.ents_in, r.pair_s.at[5], r.pair_r.at[5], x_peer)
    ents_copy.start()
    tick()
    words_swap.wait()
    far_place = aligned(1 - x, quarter)
    r.words_back[...] = (r.input_part[1 - x] + r.mail_in[1, far_place, :].astype(full)).astype(low)
    words_back_copy = send(r.words_back, r.words_in, r.pair_s.at[6], r.pair_r.at[6], x_peer)
    tick()
    ents_copy.wait()

    grad = r.grad_first[half_words:rows, :] + arrived(1, ents_near)
    grad = grad + r.ents_in[...].astype(full)
    own_ents = aligned(x, half_ents)
    normed, scale = normalize(r.ent_lin[own_ents, :])
    vec[0:1, :] = row_sum(grad * normed)
    vec[3:4, :] = row_sum(grad)
    lin_low = normalize_back(grad, normed, scale, r.gain[0:1, :]).astype(low)
    slope = dot_nt(lin_low, r.w_entity[...]).astype(low)
    r.slope[...] = dot_nn(r.outbox[...], slope).reshape(owners, capacity, -1)
    r.slopes[flat] = r.slope[flat]
    for k in range(owners - 1):
        slope_copy(k).start()
    looked_half = r.looked[own_ents, aligned(t, 128)]
    ents_grad = dot_tn(lin_low, looked_half).astype(low)
    r.e_grads[0] = ents_grad.reshape(2, 2, 2, 2, share, 128)
    stage(kit_e, 0, along[ents_order], 0)[0].start()
    vec_copy(0).start()
    tick()
    for k in range(owners - 1):
        slope_copy(k).wait()
    ids_t = r.asked[...].reshape(slots, 128).astype(full).T
    r.ids_out[...] = ids_t[0:8, :].astype(jnp.int32)
    r.slopes_out[...] = r.slopes[...].reshape(slots, -1).astype(low)
    flush(r.ids_out, r.to_ids_out)
    flush(r.slopes_out, r.to_slopes_out)
    words_back_copy.wait()
    r.grad_words[...] = (
        r.grad_first[aligned(t, quarter), :]
        + (r.input_part[x] + r.mail_in[1, aligned(x, quarter), :].astype(full))
        + r.words_in[...].astype(full)
    )
    flush(r.grad_words, r.to_grad_words)
    for c in range(2 * downs + 1):
        finish(kit_a, c, along[orders[c]])
        flush(r.out_a.at[c], r.to_out_a.at[c])
    vec_advance(4)
    total = r.vec[4]
    flush(r.vec.at[4], r.to_vec_out)
    r.across_out[...] = pltpu.roll(total[0:8, :], width - flat * share, 1)[:, 0:128]
    flush(r.across_out, r.to_across_out)
    finish(kit_e, 0, along[ents_order])
    ents_out = send(r.e_sum.at[0], r.e_in, r.pair_s.at[7], r.pair_r.at[7], core)
    ents_out.start()
    r.out_e[t] = r.e_sum[0]
    for h in range(heads):
        head_finish(h)
        flush(r.out_q.at[h], r.to_out_q.at[h])
    ents_out.wait()
    r.out_e[1 - t] = r.e_in[...]
    flush(r.out_e, r.to_out_e)
    for copy in flushes:
        copy.wait()


def finish_kernel(names, *refs):
    r = types.SimpleNamespace(**dict(zip(names, refs, strict=True)))
    low, full = jnp.bfloat16, jnp.float32
    table_rows, embed = r.hbm_first.shape
    slots = r.hbm_ids.shape[1]
    steps = r.in_s.shape[1]
    count = table_rows // steps
    chunks, share, chunk = r.hbm_a.shape
    downs = chunks // 2
    heads, side = r.hbm_q.shape[0], r.hbm_q.shape[0] * HD

    pairs = [(r.hbm_ids, r.ids), (r.hbm_slopes, r.slopes)]
    pairs += [(r.hbm_q, r.out_q), (r.hbm_e, r.out_e), (r.hbm_vec, r.vec), (r.hbm_across, r.across)]
    layers = [(r.hbm_a.at[2 * downs], r.out_part)]
    for c in range(downs):
        lanes = slice(c * chunk, (c + 1) * chunk)
        layers.append((r.hbm_a.at[c], r.down_part.at[:, lanes]))
        layers.append((r.hbm_a.at[downs + c], r.up_part.at[:, lanes]))
    layers += [(r.hbm_words, r.words_part), (r.hbm_ents, r.ents_part), (r.hbm_grad, r.grad_part)]
    smalls = [
        pltpu.make_async_copy(source, target, r.small_s.at[n])
        for n, (source, target) in enumerate(pairs + layers)
    ]
    outs = [
        pltpu.make_async_copy(source, target, r.done_s.at[n])
        for n, (source, target) in enumerate(
            [
                (r.out_part, r.red_out),
                (r.down_part, r.red_down),
                (r.up_part, r.red_up),
                (r.words_part, r.words_done.at[0]),
                (r.ents_part, r.ents_done.at[0]),
                (r.grad_part, r.grad_words_done.at[0]),
                (r.query_part, r.red_query),
                (r.keyval_part, r.red_keyval),
            ]
        )
    ]

    def moves(i, inward):
        here = pl.ds(i * count, count)
        if inward:
            ends = [(r.hbm_first, r.first), (r.hbm_second, r.second)]
            flags = r.in_s
        else:
            ends = [(r.update, r.table_update), (r.first, r.new_first), (r.second, r.new_second)]
            flags = r.out_s
        return [
            pltpu.make_async_copy(source.at[here, :], target.at[here, :], flags.at[n, i])
            for n, (source, target) in enumerate(ends)
        ]

    early, late = smalls[:2], smalls[2:]
    for copy in early + moves(0, True) + moves(1, True) + late:
        copy.start()
    for i in range(2, steps):
        for copy in moves(i, True):
            copy.start()
    for copy in early:
        copy.wait()
    r.addends[:, 0:embed] = r.slopes[...]
    r.addends[:, embed:] = jnp.ones((slots, 128), low)

    def adam(i):
        for copy in moves(i, True):
            copy.wait()
        here = pl.ds(i * count, count)
        row = lax.broadcasted_iota(jnp.int32, (count, slots), 0) + i * count
        chosen = jnp.where(row == r.ids[0:1, :], 1.0, 0.0).astype(low)
        total = dot_nn(chosen, r.addends[...])
        touched = total[:, embed:] > 0.0
        for start in range(0, embed, 128):
            lanes = slice(start, start + 128)
            grad = total[:, lanes]
            first, second = r.first[here, lanes], r.second[here, lanes]
            first_next = beta_one * first + (1.0 - beta_one) * grad
            second_next = beta_two * second + (1.0 - beta_two) * grad * grad
            direction = (
                first_next
                * (1.0 / (1.0 - beta_one**adam_steps))
                / (jnp.sqrt(second_next * (1.0 / (1.0 - beta_two**adam_steps))) + adam_eps)
            )
            r.update[here, lanes] = jnp.where(touched, direction, 0.0)
            r.first[here, lanes] = jnp.where(touched, first_next, first)
            r.second[here, lanes] = jnp.where(touched, second_next, second)
        for copy in moves(i, False):
            copy.start()

    def lay_out_rest():
        for copy in late:
            copy.wait()
        for copy in outs[:6]:
            copy.start()
        width = r.vec.shape[1]
        for n in range(2):
            r.red_entity[:, n * 128 : (n + 1) * 128] = r.out_e[n]
            for h in range(heads):
                place = h * 6 * HD
                line = 10 + 2 * n + place // width
                for j in range(6):
                    lanes = slice(n * side + h * HD, n * side + (h + 1) * HD)
                    part = r.out_q[h, n, :, j * HD : (j + 1) * HD]
                    begin = place % width + j * HD
                    line_part = r.vec[line : line + 1, begin : begin + HD]
                    if j < 4:
                        r.query_part[j, :, lanes] = part
                        r.red_query_bias[j : j + 1, lanes] = line_part
                    else:
                        r.keyval_part[j - 4, :, lanes] = part
                    if j == 5:
                        r.value_row[:, lanes] = line_part
        for copy in outs[6:]:
            copy.start()
        r.red_gain[...] = r.across[0:3, 0:share]
        r.red_shift[...] = r.across[3:6, 0:share]
        r.red_value_bias[...] = r.value_row[...].reshape(-1)
        r.red_out_bias[...] = r.across[6:7, 0:share].reshape(-1)
        r.red_down_bias[...] = r.across[7:8, 0:share].reshape(-1)
        for n in range(2):
            r.red_up_bias[n * width : (n + 1) * width] = r.vec[8 + n : 9 + n, :].reshape(-1)

    for i in range(steps):
        adam(i)
        if i == steps // 2:
            lay_out_rest()
    for i in range(steps):
        for copy in moves(i, False):
            copy.wait()
    for copy in outs:
        copy.wait()


SOFT = 256
STEPS = 8
CHUNK, HEAD, ENTS, VEC, WORDS = range(5)
SCHEDULE = (
    ((CHUNK, 0, 0),),
    ((CHUNK, 1, 0),),
    (),
    ((CHUNK, 2, 0),),
    (),
    (),
    (),
    (),
    ((CHUNK, 5, 0),),
    (),
    (),
    ((CHUNK, 4, 0), (CHUNK, 6, 0), (CHUNK, 0, 1),),
    (),
    ((CHUNK, 2, 1),),
    ((CHUNK, 5, 1),),
    (),
    ((CHUNK, 1, 1), (CHUNK, 0, 2),),
    ((CHUNK, 6, 1),),
    (),
    ((CHUNK, 8, 0), (CHUNK, 7, 0),),
    ((CHUNK, 5, 2),),
    ((HEAD, 0, 1),),
    ((CHUNK, 4, 1), (CHUNK, 0, 3),),
    (),
    ((CHUNK, 1, 2),),
    (),
    ((CHUNK, 5, 3), (CHUNK, 3, 0), (HEAD, 1, 1), (CHUNK, 8, 1), (CHUNK, 2, 2), (HEAD, 0, 2), (CHUNK, 4, 2), (CHUNK, 1, 3),),
    ((HEAD, 1, 2),),
    ((CHUNK, 7, 1), (HEAD, 2, 1), (VEC, 0, 1), (CHUNK, 3, 1), (CHUNK, 6, 2), (CHUNK, 8, 2), (WORDS, 0, 0), (CHUNK, 4, 3), (CHUNK, 7, 2), (ENTS, 0, 1), (CHUNK, 2, 3), (HEAD, 2, 2), (CHUNK, 3, 2), (VEC, 0, 2), (ENTS, 0, 2), (CHUNK, 6, 3), (CHUNK, 7, 3), (CHUNK, 8, 3), (HEAD, 1, 3), (VEC, 0, 3), (ENTS, 0, 3), (CHUNK, 3, 3), (HEAD, 0, 3), (HEAD, 2, 3),),
)
ORDERS = (0, 1, 2, 0, 0, 1, 2, 0, 0)
VEC_ORDER = 2
ENTS_ORDER = 0


def fused_local(
    word_states,
    entity_shard,
    entity_row,
    word_segments,
    entity_segments,
    entity_table,
    adam_first,
    adam_second,
    w_entity,
    norm_gain,
    norm_bias,
    w_query,
    b_query,
    w_keyval,
    b_value,
    w_out,
    b_out,
    w_up,
    b_up,
    w_down,
    b_down,
    cot_words,
    cot_entities,
):
    low, full = jnp.bfloat16, jnp.float32
    _, half_words, width = word_states.shape
    half_ents = entity_row.shape[2]
    rows, everyone = half_words + half_ents, 2 * (half_words + half_ents)
    words, ents = 2 * half_words, 2 * half_ents
    table_rows, embed = entity_table.shape
    local_width, hidden = w_query.shape[2], w_up.shape[1]
    owners = lax.axis_size(("dp", "stream"))
    share = width // owners
    capacity = 2 * half_ents // owners
    side = local_width // 2
    heads = side // HD
    chunk = local_width
    chunks = 2 * (hidden // chunk) + 1

    operands = dict(
        hbm_shard=entity_shard.reshape(1, half_ents),
        hbm_row=entity_row.reshape(1, half_ents),
        hbm_word_seg=word_segments,
        hbm_ent_seg=entity_segments,
        hbm_gain=norm_gain,
        hbm_shift=norm_bias,
        hbm_b_query=b_query,
        hbm_b_value=b_value,
        hbm_b_out=b_out,
        hbm_b_up=b_up,
        hbm_b_down=b_down,
        hbm_words=word_states,
        hbm_cot_words=cot_words,
        hbm_cot_ents=cot_entities,
        hbm_query=w_query,
        hbm_keyval=w_keyval,
        hbm_table=entity_table,
        hbm_entity=w_entity,
        hbm_out=w_out,
        hbm_up=w_up,
        hbm_down=w_down,
    )
    results = dict(
        to_out_words=((half_words // 2, width), low),
        to_out_ents=((half_ents // 2, width), low),
        to_grad_words=((half_words // 2, width), full),
        to_out_a=((chunks, share, chunk), full),
        to_out_e=((2, share, 128), full),
        to_out_q=((heads, 2, share, chunk), full),
        to_vec_out=((16, width), full),
        to_across_out=((8, 128), full),
        to_ids_out=((8, owners * capacity), jnp.int32),
        to_slopes_out=((owners * capacity, embed), low),
    )
    mail_rows = max(rows, words // 2 + ents)
    dma = pltpu.SemaphoreType.DMA
    scratch = dict(
        shard=((1, half_ents), jnp.int32),
        row=((1, half_ents), jnp.int32),
        word_seg=(word_segments.shape, jnp.int32),
        ent_seg=(entity_segments.shape, jnp.int32),
        gain=(norm_gain.shape, full),
        shift=(norm_bias.shape, full),
        b_query=(b_query.shape, full),
        b_value=(b_value.shape, full),
        b_out=(b_out.shape, full),
        b_up=(b_up.shape, full),
        b_down=(b_down.shape, full),
        grad_words=((half_words // 2, width), full),
        out_a=((chunks, share, chunk), full),
        out_e=((2, share, 128), full),
        out_q=((heads, 2, share, chunk), full),
        across_out=((8, 128), full),
        ids_out=((8, owners * capacity), jnp.int32),
        slopes_out=((owners * capacity, embed), low),
        w_query=(w_query.shape, low),
        w_keyval=(w_keyval.shape, low),
        table=(entity_table.shape, low),
        w_entity=(w_entity.shape, low),
        w_out=(w_out.shape, low),
        w_up=(w_up.shape, low),
        w_down=(w_down.shape, low),
        cat_words=((width, 4 * side), low),
        cat_ents=((width, 4 * side), low),
        bias_words=((1, 4 * side), full),
        bias_ents=((1, 4 * side), full),
        cotangent=((rows, width), low),
        ask=((owners, capacity, 128), jnp.int32),
        asked=((owners, capacity, 128), jnp.int32),
        outbox=((owners * capacity, half_ents), low),
        select=((ents, owners * 2 * capacity), low),
        found=((owners // 2, 2 * capacity, embed), low),
        answer=((owners, 2 * capacity, embed), low),
        looked=((ents, embed), low),
        ent_lin=((ents, width), full),
        x_ent=((ents, width), full),
        x_all=((everyone, width), low),
        x_own=((rows, width), full),
        words_t=((width, words), low),
        ents_t=((width, ents), low),
        mask=((everyone, everyone), low),
        qkv=((everyone, 4 * side), low),
        key=((heads, everyone, HD), low),
        value=((heads, everyone, HD), low),
        prob=((heads, everyone, everyone), full),
        factor=((heads, everyone, 128), full),
        mass=((heads, words, 128), full),
        heads_far=((rows, side), low),
        heads_near=((rows, side), low),
        heads_in=((rows, side), low),
        heads_all=((rows, 2 * side), low),
        mail_out=((2, mail_rows, width), low),
        mail_in=((2, mail_rows, width), low),
        normed=((rows, width), full),
        scale=((rows, 128), full),
        first=((rows, width), low),
        first_t=((width, rows), low),
        act=((rows, hidden), low),
        up=((rows, hidden), full),
        chance=((rows, hidden), full),
        final=((rows, width), low),
        grad_second=((rows, width), full),
        grad_low=((rows, width), low),
        grad_t=((width, rows), low),
        grad_up=((rows, hidden), low),
        grad_first=((rows, width), full),
        back_far=((rows, side), low),
        back_heads=((everyone, side), low),
        grad_prob=((everyone, everyone), full),
        grad_score=((everyone, everyone), low),
        prob_low=((everyone, everyone), low),
        grad_qkv=((everyone, 4 * side), low),
        input_part=((2, half_words // 2, width), full),
        ents_back=((half_ents, width), low),
        ents_in=((half_ents, width), low),
        words_back=((half_words // 2, width), low),
        words_in=((half_words // 2, width), low),
        slope=((owners, capacity, embed), full),
        slopes=((owners, capacity, embed), full),
        e_sum=((1, share, 128), full),
        e_in=((share, 128), full),
        vec=((5, 16, width), full),
        vec_in=((4, 16, width), full),
        grads=((chunks, 2, 2, 2, 2, share, chunk), low),
        near=((chunks, 2, 2, 2, share, chunk), low),
        next=((chunks, 2, 2, share, chunk), low),
        far=((chunks, 2, share, chunk), low),
        last=((chunks, share, chunk), low),
        e_grads=((1, 2, 2, 2, 2, share, 128), low),
        e_near=((1, 2, 2, 2, share, 128), low),
        e_next=((1, 2, 2, share, 128), low),
        e_far=((1, 2, share, 128), low),
        e_last=((1, share, 128), low),
        q_grads=((heads, 2, 2, 2, 2, share, chunk), low),
        q_near=((heads, 2, 2, 2, share, chunk), low),
        q_next=((heads, 2, 2, share, chunk), low),
        q_far=((heads, 2, share, chunk), low),
        q_away=((heads, share, chunk), low),
        q_in=((heads, share, chunk), low),
    )
    signals = dict(
        load_s=(len(operands),),
        flush_s=(len(results) + chunks + heads,),
        ask_s=(owners - 1,),
        ask_r=(owners - 1,),
        answer_s=(owners - 1,),
        answer_r=(owners - 1,),
        slope_s=(owners - 1,),
        slope_r=(owners - 1,),
        heads_s=(2,),
        heads_r=(2,),
        pair_s=(9,),
        pair_r=(9,),
        strip_s=(3, width // 256),
        strip_r=(3, width // 256),
        swap_s=(2,),
        swap_r=(2,),
        vec_s=(4,),
        vec_r=(4,),
        a_s=(chunks, 4),
        a_r=(chunks, 4),
        e_s=(1, 4),
        e_r=(1, 4),
        q_s=(heads, 4),
        q_r=(heads, 4),
    )
    names = [*operands, *results, *scratch, *signals]
    kernel = functools.partial(layer_kernel, names, ORDERS, ENTS_ORDER, VEC_ORDER, SCHEDULE)
    made = pl.pallas_call(
        kernel,
        name="layer",
        out_shape=[jax.ShapeDtypeStruct(*item) for item in results.values()],
        in_specs=[pl.BlockSpec(memory_space=pl.ANY)] * len(operands),
        out_specs=[pl.BlockSpec(memory_space=pl.ANY)] * len(results),
        scratch_shapes=[pltpu.VMEM(*item) for item in scratch.values()]
        + [dma(shape) for shape in signals.values()],
        compiler_params=pltpu.CompilerParams(
            collective_id=0, has_side_effects=True, vmem_limit_bytes=67_043_328
        ),
    )(*operands.values())
    got = types.SimpleNamespace(**dict(zip(results, made, strict=True)))

    given = dict(
        hbm_first=adam_first,
        hbm_second=adam_second,
        hbm_ids=got.to_ids_out,
        hbm_slopes=got.to_slopes_out,
        hbm_a=got.to_out_a,
        hbm_e=got.to_out_e,
        hbm_q=got.to_out_q,
        hbm_vec=got.to_vec_out,
        hbm_across=got.to_across_out,
        hbm_words=got.to_out_words,
        hbm_ents=got.to_out_ents,
        hbm_grad=got.to_grad_words,
    )
    final = dict(
        words_done=(1, half_words // 2, width),
        ents_done=(1, half_ents // 2, width),
        grad_words_done=(1, half_words // 2, width),
        red_entity=(share, embed),
        red_gain=(3, share),
        red_shift=(3, share),
        red_query=(4, share, local_width),
        red_query_bias=(4, local_width),
        red_keyval=(2, share, local_width),
        red_value_bias=(local_width,),
        red_out=(share, local_width),
        red_out_bias=(share,),
        red_up=(share, hidden),
        red_up_bias=(hidden,),
        red_down=(share, hidden),
        red_down_bias=(share,),
        table_update=adam_first.shape,
        new_first=adam_first.shape,
        new_second=adam_first.shape,
    )
    room = dict(
        value_row=((1, local_width), full),
        ids=(got.to_ids_out.shape, jnp.int32),
        slopes=(got.to_slopes_out.shape, low),
        addends=((owners * capacity, embed + 128), low),
        out_e=(got.to_out_e.shape, full),
        out_q=(got.to_out_q.shape, full),
        vec=(got.to_vec_out.shape, full),
        across=(got.to_across_out.shape, full),
        first=(adam_first.shape, full),
        second=(adam_first.shape, full),
        update=(adam_first.shape, full),
        out_part=((share, local_width), full),
        down_part=((share, hidden), full),
        up_part=((share, hidden), full),
        words_part=(got.to_out_words.shape, low),
        ents_part=(got.to_out_ents.shape, low),
        grad_part=(got.to_grad_words.shape, full),
        query_part=((4, share, local_width), full),
        keyval_part=((2, share, local_width), full),
    )
    flags = dict(small_s=(chunks + 9,), done_s=(8,), in_s=(2, STEPS), out_s=(3, STEPS))
    in_place, in_vmem = (pl.BlockSpec(memory_space=space) for space in (pl.ANY, pltpu.VMEM))
    manual = set(dict(words_done=0, ents_done=0, grad_words_done=0, red_query=0, red_keyval=0))
    manual |= set(dict(red_out=0, red_up=0, red_down=0, table_update=0, new_first=0, new_second=0))
    finished = pl.pallas_call(
        functools.partial(finish_kernel, [*given, *final, *room, *flags]),
        name="finish",
        out_shape=[
            jax.ShapeDtypeStruct(shape, low if n < 2 else full)
            for n, shape in enumerate(final.values())
        ],
        in_specs=[in_place] * len(given),
        out_specs=[in_place if name in manual else in_vmem for name in final],
        scratch_shapes=[pltpu.VMEM(*item) for item in room.values()]
        + [dma(shape) for shape in flags.values()],
        compiler_params=pltpu.CompilerParams(vmem_limit_bytes=67_043_328),
    )(*given.values())
    done = dict(zip(final, finished, strict=True))
    return tuple(
        item.T if name in ("red_entity", "red_out", "red_down") else item
        for name, item in done.items()
    )


def plain_local(
    word_states,
    entity_shard,
    entity_row,
    word_segments,
    entity_segments,
    entity_table,
    adam_first,
    adam_second,
    w_entity,
    norm_gain,
    norm_bias,
    w_query,
    b_query,
    w_keyval,
    b_value,
    w_out,
    b_out,
    w_up,
    b_up,
    w_down,
    b_down,
    cot_words,
    cot_entities,
):
    seq_count, half_words, width = word_states.shape
    half_ents = entity_row.shape[2]
    table_rows, embed_width = entity_table.shape
    local_width = w_query.shape[2]
    local_heads = local_width // HD
    owners = lax.axis_size(("dp", "stream"))
    stream_index = lax.axis_index("stream")
    parts = lax.axis_size("tensor")
    part_index = lax.axis_index("tensor")
    word_part = half_words // parts
    ent_part = half_ents // parts
    ent_count = seq_count * half_ents
    word_count = seq_count * half_words
    local_rows = half_words + half_ents
    share_words = seq_count * word_part
    owner_flat = entity_shard.reshape(ent_count)
    row_flat = entity_row.reshape(ent_count)

    def pick(block, count):
        shaped = block.reshape(seq_count, parts, count // parts, block.shape[-1])
        return lax.dynamic_index_in_dim(shaped, part_index, 1, keepdims=False).reshape(
            seq_count * (count // parts), block.shape[-1]
        )

    def own_share(rows):
        return jnp.concatenate(
            [pick(rows[:word_count], half_words), pick(rows[word_count:], half_ents)], 0
        )

    capacity = 2 * ent_count // owners
    owner_hits = (owner_flat[:, None] == jnp.arange(owners, dtype=jnp.int32)[None, :]).astype(
        jnp.int32
    )
    before = jnp.cumsum(owner_hits, 0) - owner_hits
    ranking = jnp.sum(before * owner_hits, 1)
    slot_index = owner_flat * capacity + ranking
    request = (
        jnp.full((owners * capacity,), -1, jnp.int32)
        .at[slot_index]
        .set(row_flat)
        .reshape(owners, capacity)
    )
    asked_ids = lax.all_to_all(request, ("dp", "stream"), split_axis=0, concat_axis=0, tiled=True)
    present = asked_ids >= 0
    found_rows = jnp.take(entity_table, jnp.clip(asked_ids, 0, table_rows - 1), axis=0)
    found_rows = jnp.where(present[..., None], found_rows, jnp.zeros_like(found_rows))
    found_rows, asked_rows = (found_rows, asked_ids)
    answered = lax.all_to_all(found_rows, ("dp", "stream"), split_axis=0, concat_axis=0, tiled=True)
    looked = answered.reshape(owners * capacity, embed_width)[slot_index]
    ent_lin = matmul(looked, w_entity)
    x_entity, entity_norm_back = jax.vjp(layer_norm, ent_lin, norm_gain[0], norm_bias[0])
    entity_low = x_entity.astype(jnp.bfloat16)
    word_low = word_states.reshape(word_count, width)
    query_words = (
        jnp.einsum("rd,jdc->jrc", word_low, w_query[:2], preferred_element_type=jnp.float32)
        + b_query[:2, None, :]
    ).astype(jnp.bfloat16)
    query_ents = (
        jnp.einsum("rd,jdc->jrc", entity_low, w_query[2:], preferred_element_type=jnp.float32)
        + b_query[2:, None, :]
    ).astype(jnp.bfloat16)
    value_shift = jnp.stack([jnp.zeros_like(b_value), b_value])[:, None, :]
    keyval_words = (
        jnp.einsum("rd,jdc->jrc", word_low, w_keyval, preferred_element_type=jnp.float32)
        + value_shift
    ).astype(jnp.bfloat16)
    keyval_ents = (
        jnp.einsum("rd,jdc->jrc", entity_low, w_keyval, preferred_element_type=jnp.float32)
        + value_shift
    ).astype(jnp.bfloat16)
    far_words, far_ents = from_partner((keyval_words, keyval_ents), "stream", 0)

    def by_heads(block, count):
        return block.reshape(block.shape[0], seq_count, count, local_heads, HD)

    queries = jnp.concatenate(
        [by_heads(query_words, half_words), by_heads(query_ents, half_ents)], 2
    )
    keyval_w = jnp.concatenate(
        [by_heads(keyval_words, half_words), by_heads(far_words, half_words)], 2
    )
    keyval_e = jnp.concatenate([by_heads(keyval_ents, half_ents), by_heads(far_ents, half_ents)], 2)
    own_wseg = lax.dynamic_slice_in_dim(word_segments, stream_index * half_words, half_words, 1)
    far_wseg = lax.dynamic_slice_in_dim(
        word_segments, (1 - stream_index) * half_words, half_words, 1
    )
    own_eseg = lax.dynamic_slice_in_dim(entity_segments, stream_index * half_ents, half_ents, 1)
    far_eseg = lax.dynamic_slice_in_dim(
        entity_segments, (1 - stream_index) * half_ents, half_ents, 1
    )
    query_seg = jnp.concatenate([own_wseg, own_eseg], 1)
    key_wseg = jnp.concatenate([own_wseg, far_wseg], 1)
    key_eseg = jnp.concatenate([own_eseg, far_eseg], 1)
    allow_words = query_seg[:, None, :, None] == key_wseg[:, None, None, :]
    allow_ents = query_seg[:, None, :, None] == key_eseg[:, None, None, :]

    def scores_of():
        raw_words = (
            jnp.einsum(
                "sqhd,skhd->shqk", queries[0], keyval_w[0], preferred_element_type=jnp.float32
            )
            * score_scale
        )
        raw_ents = (
            jnp.einsum(
                "sqhd,skhd->shqk", queries[1], keyval_e[0], preferred_element_type=jnp.float32
            )
            * score_scale
        )
        return (
            jnp.where(allow_words, raw_words, masked_score),
            jnp.where(allow_ents, raw_ents, masked_score),
        )

    score_words, score_ents = scores_of()
    highest = jnp.maximum(
        jnp.max(score_words, -1, keepdims=True), jnp.max(score_ents, -1, keepdims=True)
    )
    totals = jnp.sum(jnp.exp(score_words - highest), -1, keepdims=True) + jnp.sum(
        jnp.exp(score_ents - highest), -1, keepdims=True
    )
    log_total = highest + jnp.log(totals)
    low_words = jnp.exp(score_words - log_total).astype(jnp.bfloat16)
    low_ents = jnp.exp(score_ents - log_total).astype(jnp.bfloat16)
    heads_out = jnp.einsum(
        "shqk,skhd->sqhd", low_words, keyval_w[1], preferred_element_type=jnp.float32
    )
    heads_out = heads_out + jnp.einsum(
        "shqk,skhd->sqhd", low_ents, keyval_e[1], preferred_element_type=jnp.float32
    )
    heads_out = heads_out.astype(jnp.bfloat16).reshape(seq_count, local_rows, local_width)
    heads_dense = jnp.concatenate(
        [
            heads_out[:, :half_words].reshape(word_count, local_width),
            heads_out[:, half_words:].reshape(ent_count, local_width),
        ],
        0,
    )
    resid_in = jnp.concatenate([word_low.astype(jnp.float32), x_entity], 0)
    cotangent = jnp.concatenate(
        [cot_words.reshape(word_count, width), cot_entities.reshape(ent_count, width)], 0
    ).astype(jnp.float32)
    attn_out = tensor_total(matmul(heads_dense, w_out)) + b_out
    first_norm, first_back = jax.vjp(layer_norm, resid_in + attn_out, norm_gain[1], norm_bias[1])
    first_low = first_norm.astype(jnp.bfloat16)
    up_value = matmul(first_low, w_up) + b_up
    active, gelu_back = jax.vjp(gelu_exact, up_value)
    active_low = active.astype(jnp.bfloat16)
    ffn_out = tensor_total(matmul(active_low, w_down)) + b_down
    final_norm, final_back = jax.vjp(layer_norm, first_norm + ffn_out, norm_gain[2], norm_bias[2])
    final_share = own_share(final_norm)
    grad_final, gain_final, shift_final = final_back(cotangent)
    grad_ffn = grad_final.astype(jnp.bfloat16)
    out_words = final_share[:share_words].reshape(seq_count, word_part, width).astype(jnp.bfloat16)
    out_entities = (
        final_share[share_words:].reshape(seq_count, ent_part, width).astype(jnp.bfloat16)
    )
    grad_down = jnp.einsum("rf,rd->fd", active_low, grad_ffn, preferred_element_type=jnp.float32)
    grad_down_bias = jnp.sum(grad_ffn.astype(jnp.float32), 0)
    (grad_pre,) = gelu_back(
        jnp.einsum("rd,fd->rf", grad_ffn, w_down, preferred_element_type=jnp.float32)
    )
    grad_up_low = grad_pre.astype(jnp.bfloat16)
    grad_up = jnp.einsum("rd,rf->df", first_low, grad_up_low, preferred_element_type=jnp.float32)
    grad_up_bias = jnp.sum(grad_up_low.astype(jnp.float32), 0)
    ffn_term = jnp.einsum("rf,df->rd", grad_up_low, w_up, preferred_element_type=jnp.float32)
    grad_first, gain_first, shift_first = first_back(grad_final + tensor_total(ffn_term))
    grad_attn = grad_first.astype(jnp.bfloat16)
    grad_out = jnp.einsum("rc,rd->cd", heads_dense, grad_attn, preferred_element_type=jnp.float32)
    grad_out_bias = jnp.sum(grad_attn.astype(jnp.float32), 0)
    grad_heads = jnp.einsum(
        "rd,cd->rc", grad_attn, w_out, preferred_element_type=jnp.float32
    ).astype(jnp.bfloat16)
    grad_heads = jnp.concatenate(
        [
            grad_heads[:word_count].reshape(seq_count, half_words, local_heads, HD),
            grad_heads[word_count:].reshape(seq_count, half_ents, local_heads, HD),
        ],
        1,
    )
    score_words, score_ents = scores_of()
    prob_words = jnp.exp(score_words - log_total)
    prob_ents = jnp.exp(score_ents - log_total)
    low_words = prob_words.astype(jnp.bfloat16)
    low_ents = prob_ents.astype(jnp.bfloat16)
    dprob_words = jnp.einsum(
        "sqhd,skhd->shqk", grad_heads, keyval_w[1], preferred_element_type=jnp.float32
    )
    dprob_ents = jnp.einsum(
        "sqhd,skhd->shqk", grad_heads, keyval_e[1], preferred_element_type=jnp.float32
    )
    inner_sum = jnp.sum(prob_words * dprob_words, -1, keepdims=True) + jnp.sum(
        prob_ents * dprob_ents, -1, keepdims=True
    )
    dscore_words = (prob_words * (dprob_words - inner_sum)).astype(jnp.bfloat16)
    dscore_ents = (prob_ents * (dprob_ents - inner_sum)).astype(jnp.bfloat16)
    grad_to_words = (
        jnp.einsum("shqk,skhd->sqhd", dscore_words, keyval_w[0], preferred_element_type=jnp.float32)
        * score_scale
    ).astype(jnp.bfloat16)
    grad_to_ents = (
        jnp.einsum("shqk,skhd->sqhd", dscore_ents, keyval_e[0], preferred_element_type=jnp.float32)
        * score_scale
    ).astype(jnp.bfloat16)
    kv_grad_words = jnp.stack(
        [
            jnp.einsum(
                "shqk,sqhd->skhd", dscore_words, queries[0], preferred_element_type=jnp.float32
            )
            * score_scale,
            jnp.einsum(
                "shqk,sqhd->skhd", low_words, grad_heads, preferred_element_type=jnp.float32
            ),
        ]
    )
    kv_grad_ents = jnp.stack(
        [
            jnp.einsum(
                "shqk,sqhd->skhd", dscore_ents, queries[1], preferred_element_type=jnp.float32
            )
            * score_scale,
            jnp.einsum("shqk,sqhd->skhd", low_ents, grad_heads, preferred_element_type=jnp.float32),
        ]
    )
    back_words, back_ents = (
        from_partner(kv_grad_words[:, :, half_words:].astype(jnp.bfloat16), "stream", 0).astype(
            jnp.float32
        ),
        from_partner(kv_grad_ents[:, :, half_ents:].astype(jnp.bfloat16), "stream", 0).astype(
            jnp.float32
        ),
    )
    grad_kv_words = (
        (kv_grad_words[:, :, :half_words] + back_words)
        .reshape(2, word_count, local_width)
        .astype(jnp.bfloat16)
    )
    grad_kv_ents = (
        (kv_grad_ents[:, :, :half_ents] + back_ents)
        .reshape(2, ent_count, local_width)
        .astype(jnp.bfloat16)
    )
    grad_q_words = jnp.stack([grad_to_words[:, :half_words], grad_to_ents[:, :half_words]]).reshape(
        2, word_count, local_width
    )
    grad_q_ents = jnp.stack([grad_to_words[:, half_words:], grad_to_ents[:, half_words:]]).reshape(
        2, ent_count, local_width
    )
    grad_query = jnp.concatenate(
        [
            jnp.einsum("rd,jrc->jdc", word_low, grad_q_words, preferred_element_type=jnp.float32),
            jnp.einsum("rd,jrc->jdc", entity_low, grad_q_ents, preferred_element_type=jnp.float32),
        ],
        0,
    )
    grad_query_bias = jnp.concatenate(
        [jnp.sum(grad_q_words.astype(jnp.float32), 1), jnp.sum(grad_q_ents.astype(jnp.float32), 1)],
        0,
    )
    grad_keyval = jnp.einsum(
        "rd,jrc->jdc", word_low, grad_kv_words, preferred_element_type=jnp.float32
    ) + jnp.einsum("rd,jrc->jdc", entity_low, grad_kv_ents, preferred_element_type=jnp.float32)
    grad_value_bias = jnp.sum(grad_kv_words[1].astype(jnp.float32), 0) + jnp.sum(
        grad_kv_ents[1].astype(jnp.float32), 0
    )
    input_words = jnp.einsum(
        "jrc,jdc->rd", grad_q_words, w_query[:2], preferred_element_type=jnp.float32
    ) + jnp.einsum("jrc,jdc->rd", grad_kv_words, w_keyval, preferred_element_type=jnp.float32)
    input_ents = jnp.einsum(
        "jrc,jdc->rd", grad_q_ents, w_query[2:], preferred_element_type=jnp.float32
    ) + jnp.einsum("jrc,jdc->rd", grad_kv_ents, w_keyval, preferred_element_type=jnp.float32)
    input_term = jnp.concatenate([input_words, input_ents], 0)
    grad_input = grad_first + tensor_total(input_term)
    grad_share = own_share(grad_input)
    grad_lin, gain_entity, shift_entity = entity_norm_back(grad_input[word_count:])
    grad_lin_low = grad_lin.astype(jnp.bfloat16)
    gain_grads = jnp.stack([gain_entity, gain_first, gain_final])
    shift_grads = jnp.stack([shift_entity, shift_first, shift_final])
    grad_words = grad_share[:share_words].reshape(seq_count, word_part, width)
    grad_entity = jnp.einsum("re,rd->ed", looked, grad_lin_low, preferred_element_type=jnp.float32)
    grad_looked = jnp.einsum(
        "rd,ed->re", grad_lin_low, w_entity, preferred_element_type=jnp.float32
    )
    outgoing = (
        jnp.zeros((owners * capacity, embed_width), jnp.float32)
        .at[slot_index]
        .set(grad_looked)
        .reshape(owners, capacity, embed_width)
    )
    incoming = lax.all_to_all(
        outgoing.astype(jnp.bfloat16), ("dp", "stream"), split_axis=0, concat_axis=0, tiled=True
    ).astype(outgoing.dtype)
    target = jnp.where(asked_rows >= 0, asked_rows, table_rows).reshape(-1)
    gradient_sum = (
        jnp.zeros((table_rows, embed_width), jnp.float32)
        .at[target]
        .add(incoming.reshape(-1, embed_width), mode="drop")
    )
    use_count = jnp.zeros((table_rows,), jnp.float32).at[target].add(1.0, mode="drop")
    touched = (use_count > 0.0)[:, None]
    first_next = beta_one * adam_first + (1.0 - beta_one) * gradient_sum
    second_next = beta_two * adam_second + (1.0 - beta_two) * gradient_sum * gradient_sum
    direction = (
        first_next
        / (1.0 - beta_one**adam_steps)
        / (jnp.sqrt(second_next / (1.0 - beta_two**adam_steps)) + adam_eps)
    )
    table_update = jnp.where(touched, direction, jnp.zeros_like(direction))
    new_first = jnp.where(touched, first_next, adam_first)
    new_second = jnp.where(touched, second_next, adam_second)
    (
        red_entity,
        red_gain,
        red_shift,
        red_query,
        red_keyval,
        red_out,
        red_out_bias,
        red_up,
        red_down,
        red_down_bias,
    ) = (
        lax.psum_scatter(grad_entity, ("dp", "stream"), scatter_dimension=1, tiled=True),
        lax.psum_scatter(gain_grads, ("dp", "stream"), scatter_dimension=1, tiled=True),
        lax.psum_scatter(shift_grads, ("dp", "stream"), scatter_dimension=1, tiled=True),
        lax.psum_scatter(grad_query, ("dp", "stream"), scatter_dimension=1, tiled=True),
        lax.psum_scatter(grad_keyval, ("dp", "stream"), scatter_dimension=1, tiled=True),
        lax.psum_scatter(grad_out, ("dp", "stream"), scatter_dimension=1, tiled=True),
        lax.psum_scatter(grad_out_bias, ("dp", "stream"), scatter_dimension=0, tiled=True),
        lax.psum_scatter(grad_up, ("dp", "stream"), scatter_dimension=0, tiled=True),
        lax.psum_scatter(grad_down, ("dp", "stream"), scatter_dimension=1, tiled=True),
        lax.psum_scatter(grad_down_bias, ("dp", "stream"), scatter_dimension=0, tiled=True),
    )
    red_query_bias, red_value_bias, red_up_bias = lax.psum(
        (grad_query_bias, grad_value_bias, grad_up_bias), ("dp", "stream")
    )
    return (
        out_words,
        out_entities,
        grad_words,
        red_entity,
        red_gain,
        red_shift,
        red_query,
        red_query_bias,
        red_keyval,
        red_value_bias,
        red_out,
        red_out_bias,
        red_up,
        red_up_bias,
        red_down,
        red_down_bias,
        table_update,
        new_first,
        new_second,
    )


def solution(mesh):
    placed = (
        P("dp", "stream", None),
        P("stream", "dp", None, None),
        P("stream", "dp", None),
        P("dp", None),
        P("dp", None),
        P(("dp", "stream"), None),
        P(("dp", "stream"), None),
        P(("dp", "stream"), None),
        P(),
        P(),
        P(),
        P(None, None, "tensor"),
        P(None, "tensor"),
        P(None, None, "tensor"),
        P("tensor"),
        P("tensor", None),
        P(),
        P(None, "tensor"),
        P("tensor"),
        P("tensor", None),
        P(),
        P("dp", "stream", None),
        P("dp", "stream", None),
    )
    fits = mesh.shape["stream"] == 2 and mesh.shape["tensor"] == 2 and mesh.shape["dp"] == 8

    def local(*blocks):
        width, owners = blocks[0].shape[2], mesh.shape["dp"] * mesh.shape["stream"]
        if fits and width % (16 * owners) == 0 and blocks[0].shape[0] == 1:
            return fused_local(*blocks)
        return plain_local(*blocks)

    return jax.shard_map(
        local,
        mesh=mesh,
        in_specs=placed,
        out_specs=(
            P("dp", ("stream", "tensor"), None),
            P("dp", ("stream", "tensor"), None),
            P("dp", ("stream", "tensor"), None),
            P(None, ("dp", "stream")),
            P(None, ("dp", "stream")),
            P(None, ("dp", "stream")),
            P(None, ("dp", "stream"), "tensor"),
            P(None, "tensor"),
            P(None, ("dp", "stream"), "tensor"),
            P("tensor"),
            P("tensor", ("dp", "stream")),
            P(("dp", "stream")),
            P(("dp", "stream"), "tensor"),
            P("tensor"),
            P("tensor", ("dp", "stream")),
            P(("dp", "stream")),
            P(("dp", "stream"), None),
            P(("dp", "stream"), None),
            P(("dp", "stream"), None),
        ),
        check_vma=False,
    )
```
